32 devices in a mesh: page: 8 (over z, x), band: 4 (over y, core).
Axes of the slice: x: 2, y: 2, z: 4, core: 2. Of those that a mesh axis runs over, the one named last changes fastest.
Arguments:
- tokens: bfloat16 [32, 512, 768], P('page', 'band'), may hold values from -6 to 6
- band_ids: int32 [32, 512], P('page'), may hold values from 0 to 3, as said below
- band_counts: int32 [32, 4], P('page'), may hold values from 64 to 256, as said below
- page_mask: int32 [32, 512], P('page'), may hold values from 0 to 1, as said below
- w_query: bfloat16 [768, 768], P(('page', 'band')), may hold values from -0.21875 to 0.21875
- b_query: bfloat16 [768], P(('page', 'band')), may hold values from -1.5 to 1.5
- w_key: bfloat16 [768, 768], P(('page', 'band')), may hold values from -0.3125 to 0.3125
- w_value: bfloat16 [768, 768], P(('page', 'band')), may hold values from -0.21875 to 0.21875
- b_value: bfloat16 [768], P(('page', 'band')), may hold values from -0.5 to 0.5
- w_attn_out: bfloat16 [768, 768], P(('page', 'band')), may hold values from -1.25 to 1.25
- b_attn_out: bfloat16 [768], P(('page', 'band')), may hold values from -1 to 1
- attn_gain: bfloat16 [768], P(('page', 'band')), may hold values from 0.5 to 1.5
- attn_shift: bfloat16 [768], P(('page', 'band')), may hold values from -1 to 1
- w_inner: bfloat16 [768, 3072], P(('page', 'band')), may hold values from -0.21875 to 0.21875
- b_inner: bfloat16 [3072], P(('page', 'band')), may hold values from -1 to 1
- w_outer: bfloat16 [3072, 768], P(('page', 'band')), may hold values from -0.109375 to 0.109375
- b_outer: bfloat16 [768], P(('page', 'band')), may hold values from -1 to 1
- ffn_gain: bfloat16 [768], P(('page', 'band')), may hold values from 0.5 to 1.5
- ffn_shift: bfloat16 [768], P(('page', 'band')), may hold values from -1.5 to 1.5
- grad_output: bfloat16 [32, 1024, 768], P('page', 'band'), may hold values from -6 to 6
Outputs:
- layer_out: bfloat16 [32, 1024, 768], P('page', 'band')
- grad_tokens: bfloat16 [32, 512, 768], P('page', 'band')
- grad_w_query: float32 [768, 768], P(('page', 'band'))
- grad_b_query: float32 [768], P(('page', 'band'))
- grad_w_key: float32 [768, 768], P(('page', 'band'))
- grad_w_value: float32 [768, 768], P(('page', 'band'))
- grad_b_value: float32 [768], P(('page', 'band'))
- grad_w_attn_out: float32 [768, 768], P(('page', 'band'))
- grad_b_attn_out: float32 [768], P(('page', 'band'))
- grad_attn_gain: float32 [768], P(('page', 'band'))
- grad_attn_shift: float32 [768], P(('page', 'band'))
- grad_w_inner: float32 [768, 3072], P(('page', 'band'))
- grad_b_inner: float32 [3072], P(('page', 'band'))
- grad_w_outer: float32 [3072, 768], P(('page', 'band'))
- grad_b_outer: float32 [768], P(('page', 'band'))
- grad_ffn_gain: float32 [768], P(('page', 'band'))
- grad_ffn_shift: float32 [768], P(('page', 'band'))
The draws below stay inside these ranges and needn't reach their ends.
Inputs may be any that keep to these rules, and one draw needn't show every extreme that they name: `band_ids`: in each page every band holds between 64 and 256 tokens; one band holds exactly 256 tokens, 64 in each quarter of the page (128 positions in a row), and another holds exactly 64; no band holds more than 64 tokens of one quarter of a page. band_counts[p, b] is the number of tokens of page p whose band id is b. `page_mask`: in each page the ones form a prefix of at least 128 positions, and the page ends with at least one 0.
All inputs are finite; a program needn't handle non-finite values.
Results may differ from the reference program's by a relative error of at most 0.04.
Values may be sent and summed in bfloat16 or wider, within the bound.
A program may use at most 192 MiB of HBM per device.

```python
import math
import jax
import jax.numpy as jnp
from jax import lax

D = 768
HEADS = 12
HEAD_DIM = 64
FF = 3072
PAGE_LEN = 512
BANDS = 4
BAND_CAP = 256
SEND_CAP = 64
PAGES = 32


def band_layout(key):
    base_key = jax.random.fold_in(key, 7)
    page_keys = jax.random.split(base_key, PAGES)

    def one_page(page_key):
        order_key, cut_key, mix_key = jax.random.split(page_key, 3)
        band_order = jax.random.permutation(order_key, BANDS).astype(jnp.int32)
        middle = jax.random.randint(cut_key, (), 0, SEND_CAP + 1, dtype=jnp.int32)
        band_sizes = jnp.stack([jnp.int32(BAND_CAP), jnp.int32(SEND_CAP), SEND_CAP + middle, 2 * SEND_CAP - middle]).astype(jnp.int32)
        counts = jnp.zeros((BANDS,), jnp.int32).at[band_order].set(band_sizes)
        rest_pos = jnp.arange(4 * SEND_CAP, dtype=jnp.int32)
        rest_ids = jnp.where(rest_pos < SEND_CAP, band_order[1], jnp.where(rest_pos < 2 * SEND_CAP + middle, band_order[2], band_order[3]))
        rest_blocks = rest_ids.reshape(4, SEND_CAP)
        big_blocks = jnp.zeros((4, SEND_CAP), jnp.int32) + band_order[0]
        joined = jnp.concatenate([big_blocks, rest_blocks], axis=1)
        mix_keys = jax.random.split(mix_key, 4)
        shuffled = jax.vmap(lambda one_key, block_ids: jax.random.permutation(one_key, block_ids))(mix_keys, joined)
        return (shuffled.reshape(-1).astype(jnp.int32), counts)
    return jax.vmap(one_page)(page_keys)


def draw_band_ids(key, part):
    return band_layout(key)[0]


def draw_band_counts(key, part):
    return band_layout(key)[1]


def draw_page_mask(key, part):
    mask_key = jax.random.fold_in(key, 11)
    live_len = jax.random.randint(mask_key, (PAGES, 1), PAGE_LEN // 4, PAGE_LEN, dtype=jnp.int32)
    return (jnp.arange(PAGE_LEN, dtype=jnp.int32)[None, :] < live_len).astype(jnp.int32)


def block_scale(own_key, extent, pieces, low, top_value):
    factor_of, own = 1.0, jax.random.fold_in(own_key, 6)
    for position, shards_of in pieces:
        heights = jnp.exp(jax.random.uniform(jax.random.fold_in(own, position), (shards_of,), jnp.float32, low / len(pieces), top_value / len(pieces)))
        factor_of = factor_of * jnp.repeat(heights, extent[position] // shards_of).reshape([-1 if axis == position else 1 for axis in range(len(extent))])
    return factor_of


def noise(stream_key, shape, spread, bound, shards=(), kind=jnp.bfloat16):
    values = spread * jax.random.normal(stream_key, shape, jnp.float32)
    if shards:
        values = values * block_scale(stream_key, shape, shards, -0.22, 0.18)
    return jnp.clip(values, -bound, bound).astype(kind)


def setup_inputs(seed: int = 0) -> dict:
    splits = jax.random.split(jax.random.key(seed), 21)
    tokens = noise(splits[0], (PAGES, PAGE_LEN, D), 1.0, 6.0, ((0, 8), (1, 4)))
    band_ids = draw_band_ids(jax.random.fold_in(splits[20], 71), 0)
    band_counts = draw_band_counts(jax.random.fold_in(splits[20], 71), 0)
    page_mask = draw_page_mask(jax.random.fold_in(splits[20], 71), 0)
    w_query = noise(splits[4], (D, D), D ** -0.5, 0.21875, ((0, 32),))
    b_query = noise(splits[5], (D,), 0.3, 1.5, ((0, 32),))
    w_key = noise(splits[6], (D, D), (D // 2) ** -0.5, 0.3125, ((0, 32),))
    w_value = noise(splits[7], (D, D), D ** -0.5, 0.21875, ((0, 32),))
    b_value = noise(splits[8], (D,), 0.1, 0.5, ((0, 32),))
    w_attn_out = noise(splits[9], (D, D), (D // 32) ** -0.5, 1.25, ((0, 32),))
    b_attn_out = noise(splits[10], (D,), 0.2, 1.0, ((0, 32),))
    attn_gain = jnp.clip(1.0 + 0.1 * jax.random.normal(splits[11], (D,), jnp.float32), 0.5, 1.5).astype(jnp.bfloat16)
    attn_shift = noise(splits[12], (D,), 0.2, 1.0, ((0, 32),))
    w_inner = noise(splits[13], (D, FF), D ** -0.5, 0.21875, ((0, 32),))
    b_inner = noise(splits[14], (FF,), 0.2, 1.0, ((0, 32),))
    w_outer = noise(splits[15], (FF, D), FF ** -0.5, 0.109375, ((0, 32),))
    b_outer = noise(splits[16], (D,), 0.2, 1.0, ((0, 32),))
    ffn_gain = jnp.clip(1.0 + 0.1 * jax.random.normal(splits[17], (D,), jnp.float32), 0.5, 1.5).astype(jnp.bfloat16)
    ffn_shift = noise(splits[18], (D,), 0.3, 1.5, ((0, 32),))
    grad_output = noise(splits[19], (PAGES, BANDS * BAND_CAP, D), 1.0, 6.0, ((0, 8), (1, 4)))
    return dict(tokens=tokens, band_ids=band_ids, band_counts=band_counts, page_mask=page_mask, w_query=w_query, b_query=b_query, w_key=w_key, w_value=w_value, b_value=b_value, w_attn_out=w_attn_out, b_attn_out=b_attn_out, attn_gain=attn_gain, attn_shift=attn_shift, w_inner=w_inner, b_inner=b_inner, w_outer=w_outer, b_outer=b_outer, ffn_gain=ffn_gain, ffn_shift=ffn_shift, grad_output=grad_output)


@jax.custom_vjp
def low(v):
    return lax.optimization_barrier(v.astype(jnp.bfloat16)).astype(jnp.float32)

@jax.custom_vjp
def low_back(v):
    return v

def low_keep(v):
    return (low(v), None)

def low_pass(kept, grad):
    return (grad,)

def back_keep(v):
    return (v, None)

def back_low(kept, grad):
    return (low(grad),)
low.defvjp(low_keep, low_pass)
low_back.defvjp(back_keep, back_low)
LN_EPS = 1e-12
NEG_FILL = -1e+30

def layer_norm(values):
    center = values - lax.optimization_barrier(jnp.mean(values, axis=-1, keepdims=True))
    return center * lax.rsqrt(lax.optimization_barrier(jnp.mean(center * center, axis=-1, keepdims=True)) + LN_EPS)

def project(rows_in, weight):
    return jnp.einsum('gld,de->gle', rows_in, weight, precision=lax.Precision.HIGHEST)

def page_layer(params, group_in):
    query_weight, query_bias, key_weight, value_weight, value_bias, out_weight, out_bias, gain_one, shift_one, inner_weight, inner_bias, outer_weight, outer_bias, gain_two, shift_two = params
    page_rows, key_live = group_in
    group_size, page_len, feat_width = page_rows.shape
    score_scale = HEAD_DIM ** (-0.5)
    query_rows = low_back(low(project(page_rows, query_weight) + query_bias)).reshape(group_size, page_len, HEADS, HEAD_DIM)
    key_rows = low_back(low(project(page_rows, key_weight))).reshape(group_size, page_len, HEADS, HEAD_DIM)
    value_rows = low_back(low(project(page_rows, value_weight) + value_bias)).reshape(group_size, page_len, HEADS, HEAD_DIM)
    scores = low_back(jnp.einsum('gqhd,gkhd->ghqk', query_rows, key_rows, precision=lax.Precision.HIGHEST) * score_scale)
    scores = jnp.where(key_live[:, None, None, :], scores, NEG_FILL)
    shifted = jnp.exp(scores - lax.optimization_barrier(jnp.max(scores, axis=-1, keepdims=True)))
    attn_probs = low(shifted / lax.optimization_barrier(jnp.sum(shifted, axis=-1, keepdims=True)))
    mixed_rows = jnp.einsum('ghqk,gkhd->gqhd', attn_probs, value_rows, precision=lax.Precision.HIGHEST)
    attended = low_back(low(mixed_rows.reshape(group_size, page_len, feat_width)))
    branch = low_back(project(attended, out_weight) + out_bias)
    hidden = layer_norm(page_rows + branch) * gain_one + shift_one
    inner_pre = low_back(project(low(hidden), inner_weight) + inner_bias)
    outer = low_back(project(low(jax.nn.gelu(inner_pre, approximate=False)), outer_weight) + outer_bias)
    return layer_norm(hidden + outer) * gain_two + shift_two

def reference(tokens, band_ids, band_counts, page_mask, w_query, b_query, w_key, w_value, b_value, w_attn_out, b_attn_out, attn_gain, attn_shift, w_inner, b_inner, w_outer, b_outer, ffn_gain, ffn_shift, grad_output):
    page_total, page_len = band_ids.shape
    band_range = jnp.arange(BANDS, dtype=jnp.int32)
    onehot = (band_ids[:, :, None] == band_range).astype(jnp.int32)
    page_rank = lax.optimization_barrier(jnp.sum(onehot * (jnp.cumsum(onehot, axis=1) - 1), axis=2))
    slot_index = (band_ids * BAND_CAP + page_rank).astype(jnp.int32)
    grad_rows = jax.vmap(lambda table, picks: table[picks])(grad_output.astype(jnp.float32), slot_index)
    params = tuple((weight.astype(jnp.float32) for weight in (w_query, b_query, w_key, w_value, b_value, w_attn_out, b_attn_out, attn_gain, attn_shift, w_inner, b_inner, w_outer, b_outer, ffn_gain, ffn_shift)))
    group_size = math.gcd(page_total, 8)
    key_live = page_mask > 0

    def forward(rows_in, weights_in):
        blocks = (rows_in.reshape(page_total // group_size, group_size, page_len, D), key_live.reshape(page_total // group_size, group_size, page_len))
        layer_fn = jax.checkpoint(page_layer)
        outs_all = lax.map(lambda block_in: layer_fn(weights_in, block_in), blocks)
        return outs_all.reshape(page_total, page_len, D)
    layer_rows, pullback = jax.vjp(forward, tokens.astype(jnp.float32), params)
    grad_rows_in, grad_params = pullback(grad_rows)
    layer_low = layer_rows.astype(jnp.bfloat16)
    placed = jax.vmap(lambda picks, rows_in: jnp.zeros((BANDS * BAND_CAP, D), jnp.bfloat16).at[picks].set(rows_in))(slot_index, layer_low)
    slot_live = (jnp.arange(BAND_CAP, dtype=jnp.int32)[None, None, :] < band_counts[:, :, None]).reshape(page_total, BANDS * BAND_CAP)
    layer_out = jnp.where(slot_live[:, :, None], placed, jnp.zeros_like(placed))
    return (layer_out, grad_rows_in.astype(jnp.bfloat16), grad_params[0], grad_params[1], grad_params[2], grad_params[3], grad_params[4], grad_params[5], grad_params[6], grad_params[7], grad_params[8], grad_params[9], grad_params[10], grad_params[11], grad_params[12], grad_params[13], grad_params[14])
```

```python
import jax
import jax.numpy as jnp
from jax import lax
from jax.experimental import pallas as pl
from jax.experimental.pallas import tpu as pltpu
from jax.sharding import PartitionSpec as P

HEAD_DIM = 64
LN_EPS = 1e-12
NEG_FILL = -1e30
MESH = pl.DeviceIdType.MESH
F32 = jnp.float32
BF16 = jnp.bfloat16
BOTH = ("page", "band")
VMEM_LIMIT = 60 * 2**20


def my_place():
    page, band = lax.axis_index("page"), lax.axis_index("band")
    return page // 2, page % 2, band // 2, band % 2


def dev(z, x, y, c):
    return (z * 2 + x, y * 2 + c)


def remote(src, dst, send_sem, recv_sem, place):
    return pltpu.make_async_remote_copy(
        src_ref=src,
        dst_ref=dst,
        send_sem=send_sem,
        recv_sem=recv_sem,
        device_id=dev(*place),
        device_id_type=MESH,
    )


def meet(places):
    barrier = pltpu.get_barrier_semaphore()
    for place in places:
        pl.semaphore_signal(barrier, inc=1, device_id=dev(*place), device_id_type=MESH)
    pl.semaphore_wait(barrier, len(places))


def grid_peers(z, x, y, c):
    return [((z + j) % 4, x, y, c) for j in (1, 2, 3)] + [
        (z, 1 - x, y, c),
        (z, x, 1 - y, c),
        (z, x, y, 1 - c),
    ]


def half(ref, which):
    width = ref.shape[-1] // 2
    return ref.at[..., pl.ds(which * width, width)]


def gather_kernel(count, *refs):
    ins, outs = refs[:count], refs[count : 2 * count]
    lsem, zs, zr, ps, pr, qs, qr, cs, cr = refs[2 * count :]
    z, x, y, c = my_place()
    x_peer, y_peer, c_peer = (z, 1 - x, y, c), (z, x, 1 - y, c), (z, x, y, 1 - c)
    meet(grid_peers(z, x, y, c))
    local, z_copies = [], []
    for a in range(count):
        copy = pltpu.make_async_copy(ins[a], outs[a].at[z, x, y, c], lsem.at[a])
        copy.start()
        local.append(copy)
        row = []
        for j in range(3):
            place = ((z + j + 1) % 4, x, y, c)
            row.append(
                remote(ins[a], outs[a].at[z, x, y, c], zs.at[a, j], zr.at[a, j], place)
            )
            row[-1].start()
        z_copies.append(row)
    first, second, last = [], [], []
    for a in range(count):
        local[a].wait()
        for copy in z_copies[a]:
            copy.wait_recv()
        part = outs[a].at[:, x, y, c]
        pair = [
            remote(half(part, h), half(part, h), ps.at[a, h], pr.at[a, h], place)
            for h, place in ((0, x_peer), (1, y_peer))
        ]
        for copy in pair:
            copy.start()
        first.append(pair)
    for a in range(count):
        parts = (half(outs[a].at[:, :, y, c], 0), half(outs[a].at[:, x, :, c], 1))
        pair = []
        for h, place in ((0, y_peer), (1, x_peer)):
            first[a][h].wait_recv()
            pair.append(remote(parts[h], parts[h], qs.at[a, h], qr.at[a, h], place))
            pair[-1].start()
        second.append(pair)
    for a in range(count):
        for copy in second[a]:
            copy.wait_recv()
        part = outs[a].at[:, :, :, c]
        last.append(remote(part, part, cs.at[a], cr.at[a], c_peer))
        last[-1].start()
    for a in range(count):
        last[a].wait_recv()
    for a in range(count):
        for copy in z_copies[a] + first[a] + second[a] + [last[a]]:
            copy.wait_send()


def gather_shards(shards):
    count = len(shards)
    dma = pltpu.SemaphoreType.DMA
    spec = pl.BlockSpec(memory_space=pl.ANY)

    def body(*refs):
        gather_kernel(count, *refs)

    return pl.pallas_call(
        body,
        out_shape=[jax.ShapeDtypeStruct((4, 2, 2, 2) + s.shape, s.dtype) for s in shards],
        in_specs=[spec] * count,
        out_specs=[spec] * count,
        scratch_shapes=[dma((count,)), dma((count, 3)), dma((count, 3))]
        + [dma((count, 2))] * 4
        + [dma((count,))] * 2,
        compiler_params=pltpu.CompilerParams(
            collective_id=0, has_side_effects=True, vmem_limit_bytes=VMEM_LIMIT
        ),
        name="gather",
    )(*shards)


def add_into(dst, src, lead):
    total = 1
    for size in lead:
        total *= size

    def step(flat, _):
        index = []
        for size in reversed(lead):
            index.append(flat % size)
            flat = flat // size
        index = tuple(reversed(index))
        dst[index] = (dst[index].astype(F32) + src[index].astype(F32)).astype(BF16)
        return 0

    lax.fori_loop(0, total, step, 0)


def reduce_kernel(count, *refs):
    parts, outs = refs[:count], refs[count : 2 * count]
    bufs = refs[2 * count : 2 * count + 6 * count]
    cs, cr, ps, pr, qs, qr, zs, zr = refs[8 * count :]
    z, x, y, c = my_place()
    x_peer, y_peer, c_peer = (z, 1 - x, y, c), (z, x, 1 - y, c), (z, x, y, 1 - c)
    meet(grid_peers(z, x, y, c))
    sends, core, first, second, last = [], [], [], [], []
    for a in range(count):
        got = bufs[6 * a]
        core.append(remote(parts[a].at[:, :, :, 1 - c], got, cs.at[a], cr.at[a], c_peer))
        core[-1].start()
    for a in range(count):
        own, got = parts[a].at[:, :, :, c], bufs[6 * a]
        core[a].wait_recv()
        add_into(own, got, (4, 2, 2))
        pair = [
            remote(half(own.at[:, :, 1 - y], 0), bufs[6 * a + 1], ps.at[a, 0], pr.at[a, 0], y_peer),
            remote(half(own.at[:, 1 - x], 1), bufs[6 * a + 2], ps.at[a, 1], pr.at[a, 1], x_peer),
        ]
        for copy in pair:
            copy.start()
        first.append(pair)
    for a in range(count):
        own = parts[a].at[:, :, :, c]
        pair = []
        first[a][0].wait_recv()
        add_into(half(own.at[:, :, y], 0), bufs[6 * a + 1], (4, 2))
        pair.append(
            remote(half(own.at[:, 1 - x, y], 0), bufs[6 * a + 3], qs.at[a, 0], qr.at[a, 0], x_peer)
        )
        pair[-1].start()
        first[a][1].wait_recv()
        add_into(half(own.at[:, x], 1), bufs[6 * a + 2], (4, 2))
        pair.append(
            remote(half(own.at[:, x, 1 - y], 1), bufs[6 * a + 4], qs.at[a, 1], qr.at[a, 1], y_peer)
        )
        pair[-1].start()
        second.append(pair)
    for a in range(count):
        own = parts[a].at[:, x, y, c]
        for h in (0, 1):
            second[a][h].wait_recv()
            add_into(half(own, h), bufs[6 * a + 3 + h], (4,))
        row = []
        for j in range(3):
            there = (z + j + 1) % 4
            row.append(
                remote(
                    own.at[there],
                    bufs[6 * a + 5].at[j],
                    zs.at[a, j],
                    zr.at[a, j],
                    (there, x, y, c),
                )
            )
            row[-1].start()
        last.append(row)
    for a in range(count):
        for copy in last[a]:
            copy.wait_recv()
        total = parts[a][z, x, y, c].astype(F32)
        for j in range(3):
            total = total + bufs[6 * a + 5][j].astype(F32)
        outs[a][...] = total
    for a in range(count):
        for copy in [core[a]] + first[a] + second[a] + last[a]:
            copy.wait_send()


def reduce_shards(parts):
    count = len(parts)
    dma = pltpu.SemaphoreType.DMA
    vmem = pl.BlockSpec(memory_space=pltpu.VMEM)
    bufs = []
    for part in parts:
        rows, width = part.shape[-2:]
        bufs += [
            pltpu.VMEM((4, 2, 2, rows, width), BF16),
            pltpu.VMEM((4, 2, rows, width // 2), BF16),
            pltpu.VMEM((4, 2, rows, width // 2), BF16),
            pltpu.VMEM((4, rows, width // 2), BF16),
            pltpu.VMEM((4, rows, width // 2), BF16),
            pltpu.VMEM((3, rows, width), BF16),
        ]

    def body(*refs):
        reduce_kernel(count, *refs)

    return pl.pallas_call(
        body,
        out_shape=[jax.ShapeDtypeStruct(p.shape[-2:], F32) for p in parts],
        in_specs=[vmem] * count,
        out_specs=[vmem] * count,
        scratch_shapes=bufs
        + [dma((count,))] * 2
        + [dma((count, 2))] * 4
        + [dma((count, 3))] * 2,
        compiler_params=pltpu.CompilerParams(
            collective_id=1, has_side_effects=True, vmem_limit_bytes=VMEM_LIMIT
        ),
        name="reduce",
    )(*parts)


def norm_rows(values):
    center = values - jnp.mean(values, axis=-1, keepdims=True)
    factor = lax.rsqrt(jnp.mean(center * center, axis=-1, keepdims=True) + LN_EPS)
    return (center * factor, factor)


def norm_back(upstream, normed, factor):
    return factor * (
        upstream
        - jnp.mean(upstream, axis=-1, keepdims=True)
        - normed * jnp.mean(upstream * normed, axis=-1, keepdims=True)
    )


def dot(first, second):
    return jnp.dot(first, second, preferred_element_type=F32)


def dot_rows(first, second):
    return lax.dot_general(first, second, (((0,), (0,)), ((), ())), preferred_element_type=F32)


def dot_cols(first, second):
    return lax.dot_general(first, second, (((1,), (1,)), ((), ())), preferred_element_type=F32)


def page_slots(ids, bands, slot_cap):
    onehot = (ids[:, :, None] == jnp.arange(bands, dtype=jnp.int32)).astype(F32)
    length = ids.shape[1]
    before = (jnp.arange(length)[:, None] > jnp.arange(length)[None, :]).astype(F32)
    counts = jnp.einsum("tu,pub->ptb", before, onehot, preferred_element_type=F32)
    rank = jnp.sum(onehot * counts, axis=2).astype(jnp.int32)
    return ids * slot_cap + rank


def layer_pages(rows_in, slots, live, grad_slots, weights):
    (wq, bq, wk, wv, bv, wo, bo, g1, s1, w1, b1, w2, b2, g2, s2) = weights
    pages, length, feat = rows_in.shape
    heads = feat // HEAD_DIM
    scale = HEAD_DIM**-0.5
    x_low = rows_in.reshape(-1, feat)
    select = (slots[:, None, :] == jnp.arange(grad_slots.shape[1])[None, :, None]).astype(BF16)
    grad_layer = jnp.einsum("pst,psd->ptd", select, grad_slots, preferred_element_type=F32)
    grad_layer = grad_layer.reshape(-1, feat)

    def split(flat):
        return flat.reshape(pages, length, heads, HEAD_DIM)

    query = split((dot(x_low, wq) + bq).astype(BF16))
    key = split(dot(x_low, wk).astype(BF16))
    value = split((dot(x_low, wv) + bv).astype(BF16))
    scores = jnp.einsum("pthd,puhd->phtu", query, key, preferred_element_type=F32) * scale
    scores = jnp.where(live[:, None, None, :], scores, NEG_FILL)
    shifted = jnp.exp(scores - jnp.max(scores, axis=-1, keepdims=True))
    probs = shifted / jnp.sum(shifted, axis=-1, keepdims=True)
    probs_low = probs.astype(BF16)
    mixed = jnp.einsum("phtu,puhd->pthd", probs_low, value, preferred_element_type=F32)
    attended = mixed.astype(BF16).reshape(-1, feat)
    normed_one, factor_one = norm_rows(x_low.astype(F32) + dot(attended, wo) + bo)
    hidden = normed_one * g1 + s1
    hidden_low = hidden.astype(BF16)
    inner = dot(hidden_low, w1) + b1
    cdf = 0.5 * (1.0 + lax.erf(inner * (0.5**0.5)))
    act_low = (inner * cdf).astype(BF16)
    slope = cdf + inner * jnp.exp(-0.5 * inner * inner) * ((0.5 / jnp.pi) ** 0.5)
    normed_two, factor_two = norm_rows(hidden + dot(act_low, w2) + b2)
    layer = (normed_two * g2 + s2).astype(BF16).reshape(pages, length, feat)
    layer_slots = jnp.einsum("pst,ptd->psd", select, layer, preferred_element_type=F32).astype(BF16)

    grad_g2 = jnp.sum(grad_layer * normed_two, axis=0)
    grad_s2 = jnp.sum(grad_layer, axis=0)
    grad_second = norm_back(grad_layer * g2, normed_two, factor_two)
    second_low = grad_second.astype(BF16)
    grad_w2 = dot_rows(act_low, second_low)
    grad_b2 = jnp.sum(second_low.astype(F32), axis=0)
    inner_low = (dot_cols(second_low, w2) * slope).astype(BF16)
    grad_w1 = dot_rows(hidden_low, inner_low)
    grad_b1 = jnp.sum(inner_low.astype(F32), axis=0)
    grad_hidden = grad_second + dot_cols(inner_low, w1)
    grad_g1 = jnp.sum(grad_hidden * normed_one, axis=0)
    grad_s1 = jnp.sum(grad_hidden, axis=0)
    grad_first = norm_back(grad_hidden * g1, normed_one, factor_one)
    first_low = grad_first.astype(BF16)
    grad_wo = dot_rows(attended, first_low)
    grad_bo = jnp.sum(first_low.astype(F32), axis=0)
    grad_att = split(dot_cols(first_low, wo).astype(BF16))
    grad_probs = jnp.einsum("pthd,puhd->phtu", grad_att, value, preferred_element_type=F32)
    inner_sum = jnp.sum(probs * grad_probs, axis=-1, keepdims=True)
    grad_scores = (probs * (grad_probs - inner_sum)).astype(BF16)

    def flat(per_head, factor):
        return (per_head * factor).astype(BF16).reshape(-1, feat)

    ein = lambda form, a, b: jnp.einsum(form, a, b, preferred_element_type=F32)
    grad_q = flat(ein("phtu,puhd->pthd", grad_scores, key), scale)
    grad_k = flat(ein("phtu,pthd->puhd", grad_scores, query), scale)
    grad_v = flat(ein("phtu,pthd->puhd", probs_low, grad_att), 1.0)
    grad_wq, grad_wk, grad_wv = (dot_rows(x_low, g) for g in (grad_q, grad_k, grad_v))
    grad_bq = jnp.sum(grad_q.astype(F32), axis=0)
    grad_bv = jnp.sum(grad_v.astype(F32), axis=0)
    grad_in = grad_first + dot_cols(grad_q, wq) + dot_cols(grad_k, wk) + dot_cols(grad_v, wv)
    grad_in = grad_in.astype(BF16).reshape(pages, length, feat)
    return (
        layer_slots,
        grad_in,
        (grad_wq, grad_bq, grad_wk, grad_wv, grad_bv, grad_wo, grad_bo, grad_g1, grad_s1)
        + (grad_w1, grad_b1, grad_w2, grad_b2, grad_g2, grad_s2),
    )


def to_pages(blocks):
    return lax.all_to_all(blocks, "band", split_axis=0, concat_axis=1, tiled=True)


def from_pages(blocks):
    return lax.all_to_all(blocks, "band", split_axis=1, concat_axis=0, tiled=True)


SMALL = (1, 4, 6, 7, 8, 10, 12, 13, 14)
LARGE = (0, 2, 3, 5, 9, 11)


def gather_weights(weights, hand_made):
    if not hand_made:
        return [lax.all_gather(w, BOTH, axis=0, tiled=True) for w in weights]
    sizes = [weights[i].shape[0] for i in SMALL]
    flat = jnp.concatenate([weights[i] for i in SMALL])
    flat = jnp.pad(flat, (0, -flat.shape[0] % 256))
    flat = jnp.broadcast_to(flat[None], (8, flat.shape[0]))
    got = gather_shards([weights[i] for i in LARGE] + [flat])
    full = [None] * len(weights)
    for i, whole in zip(LARGE, got):
        full[i] = whole.reshape(-1, whole.shape[-1])
    small = got[-1].reshape(-1, 8, flat.shape[1])[:, 0]
    start = 0
    for i, size in zip(SMALL, sizes):
        full[i] = small[:, start : start + size].reshape(-1)
        start += size
    return full


def reduce_grads(grads, hand_made):
    if not hand_made:
        return tuple(
            lax.psum_scatter(g, BOTH, scatter_dimension=0, tiled=True) for g in grads
        )
    devices = 32
    small = jnp.concatenate([grads[i].reshape(devices, -1) for i in SMALL], axis=1)
    width = small.shape[1]
    small = jnp.pad(small, ((0, 0), (0, -width % 256)))
    small = jnp.broadcast_to(small[:, None], (devices, 8, small.shape[1]))
    parts = [grads[i].reshape(devices, -1, grads[i].shape[-1]) for i in LARGE] + [small]
    parts = [p.astype(BF16).reshape((4, 2, 2, 2) + p.shape[1:]) for p in parts]
    sums = reduce_shards(parts)
    full = [None] * len(grads)
    for i, total in zip(LARGE, sums):
        full[i] = total
    start = 0
    for i in SMALL:
        size = grads[i].shape[0] // devices
        full[i] = sums[-1][0, start : start + size]
        start += size
    return tuple(full)


def per_device(hand_made, *args):
    tokens, band_ids, band_counts, page_mask = args[:4]
    weights, grad_output = args[4:19], args[19]
    bands = lax.axis_size("band")
    slot_cap = grad_output.shape[1]
    pages = tokens.shape[0] // bands
    full = gather_weights(weights, hand_made)
    first = lax.axis_index("band") * pages
    ids = lax.dynamic_slice_in_dim(band_ids, first, pages, 0)
    live = lax.dynamic_slice_in_dim(page_mask, first, pages, 0) > 0
    slots = page_slots(ids, bands, slot_cap)
    layer_slots, grad_in, grads = layer_pages(
        to_pages(tokens), slots, live, to_pages(grad_output), full
    )
    return (from_pages(layer_slots), from_pages(grad_in)) + reduce_grads(grads, hand_made)


def solution(mesh):
    hand_made = dict(mesh.shape) == {"page": 8, "band": 4}
    shard = P(BOTH)
    rows = P(BOTH, None)
    tokens = P("page", "band", None)
    page = P("page", None)
    weights = (rows, shard, rows, rows, shard, rows, shard, shard, shard)
    weights = weights + (rows, shard, rows, shard, shard, shard)

    def step(*args):
        return per_device(hand_made, *args)

    return jax.shard_map(
        step,
        mesh=mesh,
        in_specs=(tokens, page, page, page) + weights + (tokens,),
        out_specs=(tokens, tokens) + weights,
        check_vma=False,
    )
```

```python
import jax
import jax.numpy as jnp
from jax import lax
from jax.experimental import pallas as pl
from jax.experimental.pallas import tpu as pltpu
from jax.sharding import PartitionSpec as P

HEAD_DIM = 64
LN_EPS = 1e-12
NEG_FILL = -1e30
MESH = pl.DeviceIdType.MESH
DMA = pltpu.SemaphoreType.DMA
F32 = jnp.float32
BF16 = jnp.bfloat16
BOTH = ("page", "band")
VMEM_LIMIT = 60 * 2**20


def my_place():
    page, band = lax.axis_index("page"), lax.axis_index("band")
    return page // 2, page % 2, band // 2, band % 2


def dev(z, x, y, c):
    return (z * 2 + x, y * 2 + c)


def remote(src, dst, send_sem, recv_sem, place):
    return pltpu.make_async_remote_copy(
        src_ref=src,
        dst_ref=dst,
        send_sem=send_sem,
        recv_sem=recv_sem,
        device_id=dev(*place),
        device_id_type=MESH,
    )


def meet(places):
    barrier = pltpu.get_barrier_semaphore()
    for place in places:
        pl.semaphore_signal(barrier, inc=1, device_id=dev(*place), device_id_type=MESH)
    pl.semaphore_wait(barrier, len(places))


def grid_peers(z, x, y, c):
    return [((z + j) % 4, x, y, c) for j in (1, 2, 3)] + [
        (z, 1 - x, y, c),
        (z, x, 1 - y, c),
        (z, x, y, 1 - c),
    ]


def half(ref, which):
    rows, width = ref.shape[-2] // 2, ref.shape[-1] // 2
    if width % 128:
        return ref.at[..., pl.ds(which * rows, rows), :]
    return ref.at[..., pl.ds(which * width, width)]


def norm_rows(values):
    center = values - jnp.mean(values, axis=-1, keepdims=True)
    factor = lax.rsqrt(jnp.mean(center * center, axis=-1, keepdims=True) + LN_EPS)
    return (center * factor, factor)


def norm_back(upstream, normed, factor):
    return factor * (
        upstream
        - jnp.mean(upstream, axis=-1, keepdims=True)
        - normed * jnp.mean(upstream * normed, axis=-1, keepdims=True)
    )


def dot(first, second):
    return jnp.dot(first, second, preferred_element_type=F32)


def dot_rows(first, second):
    return lax.dot_general(first, second, (((0,), (0,)), ((), ())), preferred_element_type=F32)


def dot_cols(first, second):
    return lax.dot_general(first, second, (((1,), (1,)), ((), ())), preferred_element_type=F32)


def page_slots(ids, bands, slot_cap):
    onehot = (ids[:, :, None] == jnp.arange(bands, dtype=jnp.int32)).astype(F32)
    length = ids.shape[1]
    before = (jnp.arange(length)[:, None] > jnp.arange(length)[None, :]).astype(F32)
    counts = jnp.einsum("tu,pub->ptb", before, onehot, preferred_element_type=F32)
    rank = jnp.sum(onehot * counts, axis=2).astype(jnp.int32)
    return ids * slot_cap + rank


def layer_pages(rows_in, slots, live, grad_slots, weights):
    (wq, bq, wk, wv, bv, wo, bo, g1, s1, w1, b1, w2, b2, g2, s2) = weights
    pages, length, feat = rows_in.shape
    heads = feat // HEAD_DIM
    scale = HEAD_DIM**-0.5
    x_low = rows_in.reshape(-1, feat)
    select = (slots[:, None, :] == jnp.arange(grad_slots.shape[1])[None, :, None]).astype(BF16)
    grad_layer = jnp.einsum("pst,psd->ptd", select, grad_slots, preferred_element_type=F32)
    grad_layer = grad_layer.reshape(-1, feat)

    def split(flat):
        return flat.reshape(pages, length, heads, HEAD_DIM)

    query = split((dot(x_low, wq) + bq).astype(BF16))
    key = split(dot(x_low, wk).astype(BF16))
    value = split((dot(x_low, wv) + bv).astype(BF16))
    scores = jnp.einsum("pthd,puhd->phtu", query, key, preferred_element_type=F32) * scale
    scores = jnp.where(live[:, None, None, :], scores, NEG_FILL)
    shifted = jnp.exp(scores - jnp.max(scores, axis=-1, keepdims=True))
    probs = shifted / jnp.sum(shifted, axis=-1, keepdims=True)
    probs_low = probs.astype(BF16)
    mixed = jnp.einsum("phtu,puhd->pthd", probs_low, value, preferred_element_type=F32)
    attended = mixed.astype(BF16).reshape(-1, feat)
    normed_one, factor_one = norm_rows(x_low.astype(F32) + dot(attended, wo) + bo)
    hidden = normed_one * g1 + s1
    hidden_low = hidden.astype(BF16)
    inner = dot(hidden_low, w1) + b1
    cdf = 0.5 * (1.0 + lax.erf(inner * (0.5**0.5)))
    act_low = (inner * cdf).astype(BF16)
    slope = cdf + inner * jnp.exp(-0.5 * inner * inner) * ((0.5 / jnp.pi) ** 0.5)
    normed_two, factor_two = norm_rows(hidden + dot(act_low, w2) + b2)
    layer = (normed_two * g2 + s2).astype(BF16).reshape(pages, length, feat)
    layer_slots = jnp.einsum("pst,ptd->psd", select, layer, preferred_element_type=F32).astype(BF16)

    grad_g2 = jnp.sum(grad_layer * normed_two, axis=0)
    grad_s2 = jnp.sum(grad_layer, axis=0)
    grad_second = norm_back(grad_layer * g2, normed_two, factor_two)
    second_low = grad_second.astype(BF16)
    grad_w2 = dot_rows(act_low, second_low)
    grad_b2 = jnp.sum(second_low.astype(F32), axis=0)
    inner_low = (dot_cols(second_low, w2) * slope).astype(BF16)
    grad_w1 = dot_rows(hidden_low, inner_low)
    grad_b1 = jnp.sum(inner_low.astype(F32), axis=0)
    grad_hidden = grad_second + dot_cols(inner_low, w1)
    grad_g1 = jnp.sum(grad_hidden * normed_one, axis=0)
    grad_s1 = jnp.sum(grad_hidden, axis=0)
    grad_first = norm_back(grad_hidden * g1, normed_one, factor_one)
    first_low = grad_first.astype(BF16)
    grad_wo = dot_rows(attended, first_low)
    grad_bo = jnp.sum(first_low.astype(F32), axis=0)
    grad_att = split(dot_cols(first_low, wo).astype(BF16))
    grad_probs = jnp.einsum("pthd,puhd->phtu", grad_att, value, preferred_element_type=F32)
    inner_sum = jnp.sum(probs * grad_probs, axis=-1, keepdims=True)
    grad_scores = (probs * (grad_probs - inner_sum)).astype(BF16)

    def flat(per_head, factor):
        return (per_head * factor).astype(BF16).reshape(-1, feat)

    ein = lambda form, a, b: jnp.einsum(form, a, b, preferred_element_type=F32)
    grad_q = flat(ein("phtu,puhd->pthd", grad_scores, key), scale)
    grad_k = flat(ein("phtu,pthd->puhd", grad_scores, query), scale)
    grad_v = flat(ein("phtu,pthd->puhd", probs_low, grad_att), 1.0)
    grad_wq, grad_wk, grad_wv = (dot_rows(x_low, g) for g in (grad_q, grad_k, grad_v))
    grad_bq = jnp.sum(grad_q.astype(F32), axis=0)
    grad_bv = jnp.sum(grad_v.astype(F32), axis=0)
    grad_in = grad_first + dot_cols(grad_q, wq) + dot_cols(grad_k, wk) + dot_cols(grad_v, wv)
    grad_in = grad_in.astype(BF16).reshape(pages, length, feat)
    return (
        layer_slots,
        grad_in,
        (grad_wq, grad_bq, grad_wk, grad_wv, grad_bv, grad_wo, grad_bo, grad_g1, grad_s1)
        + (grad_w1, grad_b1, grad_w2, grad_b2, grad_g2, grad_s2),
    )


def to_pages(blocks):
    return lax.all_to_all(blocks, "band", split_axis=0, concat_axis=1, tiled=True)


def from_pages(blocks):
    return lax.all_to_all(blocks, "band", split_axis=1, concat_axis=0, tiled=True)


SMALL = (1, 4, 6, 7, 8, 10, 12, 13, 14)
LARGE = (0, 2, 3, 5, 9, 11)


def reduce_grads(grads, hand_made):
    if not hand_made:
        return tuple(
            lax.psum_scatter(g, BOTH, scatter_dimension=0, tiled=True) for g in grads
        )
    devices = 32
    small = jnp.concatenate([grads[i].reshape(devices, -1) for i in SMALL], axis=1)
    width = small.shape[1]
    small = jnp.pad(small, ((0, 0), (0, -width % 256)))
    small = jnp.broadcast_to(small[:, None], (devices, 8, small.shape[1]))
    parts = [grads[i].reshape(devices, -1, grads[i].shape[-1]) for i in LARGE] + [small]
    parts = [p.astype(BF16).reshape((4, 2, 2, 2) + p.shape[1:]) for p in parts]
    sums = reduce_shards(parts)
    full = [None] * len(grads)
    for i, total in zip(LARGE, sums):
        full[i] = total
    start = 0
    for i in SMALL:
        size = grads[i].shape[0] // devices
        full[i] = sums[-1][0, start : start + size]
        start += size
    return tuple(full)


def split_ref(ref, which):
    rows, width = ref.shape[-2:]
    cut = width // 6
    if cut % 128:
        return ref.at[..., pl.ds(which * (rows // 2), rows // 2), :]
    return ref.at[..., pl.ds(which * cut, (cut, width - cut)[which])]


def split_shape(shape, which):
    rows, width = shape[-2:]
    cut = width // 6
    if cut % 128:
        return shape[:-2] + (rows // 2, width)
    return shape[:-1] + ((cut, width - cut)[which],)


def in_order(*calls):
    def step():
        for method, *index in calls:
            method(*index)

    return step


class Gather:
    def __init__(self, own, buf, sems, place):
        self.own, self.buf, self.place = own, buf, place
        self.zs, self.zr, self.ss, self.sr, self.fs, self.fr, self.cs, self.cr = sems

    def z_copy(self, j):
        z, x, y, c = self.place
        there = (z ^ (j + 1), x, y, c)
        return remote(self.own, self.buf.at[z, x, y, c], self.zs.at[j], self.zr.at[j], there)

    def side_copy(self, j, axis):
        z, x, y, c = self.place
        part = self.buf.at[z ^ j, x, y, c]
        there = (z, 1 - x, y, c) if axis == 0 else (z, x, 1 - y, c)
        source = self.own if j == 0 else part
        return remote(source, part, self.ss.at[axis, j], self.sr.at[axis, j], there)

    def far_copy(self, j, axis):
        z, x, y, c = self.place
        if axis == 0:
            part, there = self.buf.at[z ^ j, 1 - x, y, c], (z, x, 1 - y, c)
        else:
            part, there = self.buf.at[z ^ j, x, 1 - y, c], (z, 1 - x, y, c)
        part = split_ref(part, axis)
        return remote(part, part, self.fs.at[axis, j], self.fr.at[axis, j], there)

    def core_copy(self, k):
        z, x, y, c = self.place
        part = self.buf.at[:, (x, 1 - x, x, 1 - x)[k], (y, y, 1 - y, 1 - y)[k], c]
        return remote(part, part, self.cs.at[k], self.cr.at[k], (z, x, y, 1 - c))

    def start(self):
        for j in range(3):
            self.z_copy(j).start()
        for axis in (0, 1):
            self.side_copy(0, axis).start()

    def side(self, j):
        self.z_copy(j - 1).wait_recv()
        for axis in (0, 1):
            self.side_copy(j, axis).start()

    def far(self, j):
        for axis in (0, 1):
            self.side_copy(j, axis).wait_recv()
            self.far_copy(j, axis).start()

    def core(self, k):
        if k == 3:
            for j in range(4):
                for axis in (0, 1):
                    self.far_copy(j, axis).wait_recv()
        self.core_copy(k).start()

    def steps(self):
        side, far, core = self.side, self.far, self.core
        return [
            in_order((side, 1)),
            in_order((far, 0)),
            in_order((side, 2)),
            in_order((far, 1)),
            in_order((side, 3), (core, 0)),
            in_order((far, 2)),
            in_order((far, 3), (core, 1), (core, 2)),
            in_order((core, 3)),
        ]

    def arrive(self):
        for k in range(4):
            self.core_copy(k).wait_recv()

    def finish(self):
        for j in range(3):
            self.z_copy(j).wait_send()
        for j in range(4):
            for axis in (0, 1):
                self.side_copy(j, axis).wait_send()
                self.far_copy(j, axis).wait_send()
            self.core_copy(j).wait_send()


def gather_sems():
    return [DMA((3,)), DMA((3,))] + [DMA((2, 4))] * 4 + [DMA((4,))] * 2


def lanes(shape):
    return lax.broadcasted_iota(jnp.int32, shape, len(shape) - 1)


def rows_of(shape):
    return lax.broadcasted_iota(jnp.int32, shape, len(shape) - 2)


def columns(buf, start, width):
    return buf[:, :, :, :, :, pl.ds(start, width)].reshape(-1, width)


def unpack_rows(block, per_shard, width):
    shards, count, _ = block.shape
    spread = (rows_of((128, width)) == lanes((128, width)) % per_shard).astype(BF16)
    wide = dot(block.reshape(-1, 128), spread).reshape(shards, count, width)
    owner = lax.broadcasted_iota(jnp.int32, wide.shape, 0) == lanes(wide.shape) // per_shard
    return jnp.sum(jnp.where(owner, wide, 0.0), axis=0)


def pack_rows(rows, per_shard, shards):
    count, width = rows.shape
    wide = jnp.broadcast_to(rows[None], (shards, count, width))
    owner = lax.broadcasted_iota(jnp.int32, wide.shape, 0) == lanes(wide.shape) // per_shard
    wide = jnp.where(owner, wide, 0.0).astype(BF16).reshape(-1, width)
    spread = (lanes((width, 128)) == rows_of((width, 128)) % per_shard).astype(BF16)
    return dot(wide, spread).astype(BF16).reshape(shards, count, 128)


def block_of(i, size):
    return pl.ds(pl.multiple_of(i * size, size), size)


def gelu_parts(v):
    cdf = 0.5 * (1.0 + lax.erf(v * (0.5**0.5)))
    return v * cdf, cdf + v * jnp.exp(-0.5 * v * v) * ((0.5 / jnp.pi) ** 0.5)


class Out:
    def __init__(self, sems):
        self.sems, self.copies = sems, []

    def send(self, src, dst):
        copy = pltpu.make_async_copy(src, dst, self.sems.at[len(self.copies)])
        copy.start()
        self.copies.append(copy)

    def wait(self):
        for copy in self.copies:
            copy.wait()


BIAS_ROWS = 8
TILE = 256


def forward_kernel(
    tokens, grads, live, slots, w_q, w_k, w_v, w_o, w_1, w_2, small_in,
    qkv_out, lse, x_out, att_out, normed1_out, low_out, act_out, slope_out, normed2_out,
    factors, bias, q_out, k_out, v_out, o_out, w1_out, w2_out, grad_pages, layer_slots,
    small, a_buf, w1_buf, w2_buf, x_buf, qkv, att, normed1, low, act, slope, second, normed2, layer, bias1,
    local, ts, tr, gs, gr, outs, *sems,
):
    place = z, x, y, c = my_place()
    me = y * 2 + c
    length, feat = low.shape
    pairs = feat // 128
    x_rows = x_buf.reshape(length, feat)
    here = (z, x, y, c)
    copies = [
        pltpu.make_async_copy(src, dst, local.at[i])
        for i, (src, dst) in enumerate(
            [(w, a_buf.at[here + (slice(None), pl.ds(i * feat, feat))]) for i, w in enumerate((w_q, w_k, w_v, w_o))]
            + [(small_in, small.at[here]), (w_1, w1_buf.at[here]), (w_2, w2_buf.at[here])]
            + [(tokens.at[me], x_buf.at[me]), (grads.at[me], grad_pages.at[me])]
        )
    ]
    for copy in copies:
        copy.start()
    meet(
        [(z ^ j, x, y, c) for j in (1, 2, 3)]
        + [(z, 1 - x, y, c), (z, x, 1 - y, c), (z, x, y, 1 - c), (z, x, 1 - y, 1 - c)]
    )

    def page_copy(src, dst, send, recv, j):
        there = me ^ (j + 1)
        return remote(src.at[there], dst.at[me], send.at[j], recv.at[j], (z, x, there // 2, there % 2))

    token_copies = [page_copy(tokens, x_buf, ts, tr, j) for j in range(3)]
    grad_copies = [page_copy(grads, grad_pages, gs, gr, j) for j in range(3)]
    gathers = [
        Gather(own, buf, sems[8 * i : 8 * i + 8], place)
        for i, (own, buf) in enumerate(
            [(small_in, small), (a_buf.at[here], a_buf), (w_1, w1_buf), (w_2, w2_buf)]
        )
    ]
    vectors, atts, inner, outer = gathers
    for copy in copies[:5]:
        copy.wait()
    atts.start()
    vectors.start()
    for copy in token_copies:
        copy.start()
    later_1, later_2 = inner.steps(), outer.steps()
    for i, (first, other) in enumerate(zip(vectors.steps(), atts.steps())):
        other()
        first()
        if i == 2:
            inner.start()
        if i == 5:
            outer.start()
        if i == 6:
            later_1[0]()
    for copy in copies[5:]:
        copy.wait()
    for copy in grad_copies:
        copy.start()
    vectors.arrive()
    shards = small[...].reshape(32, 16, 128)
    bias[...] = unpack_rows(shards[:, :8], feat // 32, feat)
    inner_width = act.shape[1]
    for i in range(4):
        part = unpack_rows(small[i].reshape(8, 16, 128)[:, 8:], inner_width // 32, inner_width // 4)
        bias1[:, i * (inner_width // 4) : (i + 1) * (inner_width // 4)] = part
    for copy in token_copies:
        copy.wait_recv()
    atts.arrive()
    out = Out(outs)
    for i, ref in enumerate((q_out, k_out, v_out, o_out)):
        out.send(a_buf.at[:, :, :, :, :, pl.ds(i * feat, feat)], ref)
    out.send(x_rows, x_out)
    for step in later_1[1:3]:
        step()

    def project(j, _):
        start = pl.multiple_of(j * TILE, TILE)
        total = dot(x_rows[...], columns(a_buf, start, TILE))
        which = j // (feat // TILE)
        inside = block_of(j % (feat // TILE), TILE)
        row = jnp.where(which == 0, bias[0:1, inside], jnp.where(which == 2, bias[1:2, inside], 0.0))
        qkv[:, pl.ds(start, TILE)] = (total + row).astype(BF16)
        return 0

    lax.fori_loop(0, 3 * feat // TILE, project, 0)
    out.send(qkv, qkv_out)
    for step in later_1[3:5]:
        step()
    under = [
        [later_1[5], later_2[0]],
        [later_1[6], later_2[1], later_2[2]],
        [later_1[7], later_2[3]],
        [later_2[4]],
        [later_2[5]],
        [later_2[6]],
    ]
    scale = HEAD_DIM**-0.5

    def pair(p, _):
        start = pl.multiple_of(p * 128, 128)
        q = qkv[:, pl.ds(start, 128)] * jnp.asarray(scale, BF16)
        k = qkv[:, pl.ds(feat + start, 128)]
        v = qkv[:, pl.ds(2 * feat + start, 128)]
        low_lane = lanes(q.shape) < HEAD_DIM
        mixed = []
        for h in (0, 1):
            part = jnp.where(low_lane if h == 0 else ~low_lane, k, jnp.zeros_like(k))
            scores = jnp.where(live[...] > 0, dot_cols(part, q), NEG_FILL)
            top = jnp.max(scores, axis=0, keepdims=True)
            shifted = jnp.exp(scores - top)
            total = jnp.sum(shifted, axis=0, keepdims=True)
            probs = (shifted * (1.0 / total)).astype(BF16)
            mixed.append(dot_rows(v, probs))
            lse[pl.ds(2 * p + h, 1), :] = top + jnp.log(total)
        both = jnp.where(rows_of(mixed[0].shape) < HEAD_DIM, mixed[0], mixed[1])
        att[:, pl.ds(start, 128)] = both.T.astype(BF16)
        for i, steps in enumerate(under):
            pl.when(p == i)(in_order(*[(step,) for step in steps]))
        return 0

    lax.fori_loop(0, pairs, pair, 0)
    out.send(att, att_out)
    rows = 128

    def norm_one(i, _):
        block = block_of(i, rows)
        total = dot(att[block, :], columns(a_buf, 3 * feat, feat))
        total = total + x_rows[block, :].astype(F32) + bias[2:3, :]
        normed, factor = norm_rows(total)
        normed1[block, :] = normed
        factors[block, 0:128] = jnp.broadcast_to(factor, (rows, 128))
        low[block, :] = (normed * bias[3:4, :] + bias[4:5, :]).astype(BF16)
        return 0

    lax.fori_loop(0, length // rows, norm_one, 0)
    out.send(normed1, normed1_out)
    out.send(low, low_out)
    inner.arrive()
    out.send(w1_buf, w1_out)
    later_2[7]()

    def ffn_in(j, _):
        block = block_of(j, TILE)
        value, grad = gelu_parts(dot(low[...], columns(w1_buf, block.start, TILE)) + bias1[0:1, block])
        act[:, block] = value.astype(BF16)
        slope[:, block] = grad.astype(BF16)
        return 0

    lax.fori_loop(0, inner_width // TILE, ffn_in, 0)
    out.send(act, act_out)
    out.send(slope, slope_out)
    outer.arrive()
    out.send(w2_buf, w2_out)

    def ffn_out(j, _):
        block = block_of(j, TILE)
        second[:, block] = dot(act[...], columns(w2_buf, block.start, TILE))
        return 0

    lax.fori_loop(0, feat // TILE, ffn_out, 0)

    def norm_two(i, _):
        block = block_of(i, rows)
        hidden = normed1[block, :] * bias[3:4, :] + bias[4:5, :]
        normed, factor = norm_rows(hidden + second[block, :] + bias[5:6, :])
        normed2[block, :] = normed
        factors[block, 128:256] = jnp.broadcast_to(factor, (rows, 128))
        layer[block, :] = (normed * bias[6:7, :] + bias[7:8, :]).astype(BF16)
        return 0

    lax.fori_loop(0, length // rows, norm_two, 0)
    out.send(normed2, normed2_out)

    def place_rows(i, _):
        cap = layer_slots.shape[1]
        here_rows = rows_of((cap, length)) + i * cap
        select = (here_rows == slots[...]).astype(BF16)
        layer_slots[i] = dot(select, layer[...]).astype(BF16)
        return 0

    lax.fori_loop(0, layer_slots.shape[0], place_rows, 0)
    for copy in grad_copies:
        copy.wait_recv()
    for copy in grad_copies + token_copies:
        copy.wait_send()
    for one in gathers:
        one.finish()
    out.wait()


def forward(tokens, grads, live, slots, w_q, w_k, w_v, w_o, w_1, w_2, small):
    length, feat, inner_width = slots.shape[1], tokens.shape[-1], w_1.shape[1]
    anywhere = pl.BlockSpec(memory_space=pl.ANY)
    vmem = pl.BlockSpec(memory_space=pltpu.VMEM)
    grid = (4, 2, 2, 2)
    heads = feat // HEAD_DIM
    results = [
        ((length, 3 * feat), BF16, anywhere),
        ((heads + -heads % 8, length), F32, vmem),
        ((length, feat), BF16, anywhere),
        ((length, feat), BF16, anywhere),
        ((length, feat), F32, anywhere),
        ((length, feat), BF16, anywhere),
        ((length, inner_width), BF16, anywhere),
        ((length, inner_width), BF16, anywhere),
        ((length, feat), F32, anywhere),
        ((length, 256), F32, vmem),
        ((BIAS_ROWS, feat), F32, vmem),
    ]
    results += [(grid + w_q.shape, BF16, anywhere)] * 4
    results += [(grid + w_1.shape, BF16, anywhere), (grid + w_2.shape, BF16, anywhere)]
    results += [(grads.shape, BF16, anywhere), (grads.shape, BF16, vmem)]
    return pl.pallas_call(
        forward_kernel,
        out_shape=[jax.ShapeDtypeStruct(shape, kind) for shape, kind, _ in results],
        in_specs=[anywhere, anywhere, vmem, vmem] + [anywhere] * 7,
        out_specs=[spec for _, _, spec in results],
        scratch_shapes=[
            pltpu.VMEM(grid + small.shape, BF16),
            pltpu.VMEM(grid + (w_q.shape[0], 4 * feat), BF16),
            pltpu.VMEM(grid + w_1.shape, BF16),
            pltpu.VMEM(grid + w_2.shape, BF16),
            pltpu.VMEM(tokens.shape, BF16),
            pltpu.VMEM((length, 3 * feat), BF16),
            pltpu.VMEM((length, feat), BF16),
            pltpu.VMEM((length, feat), F32),
            pltpu.VMEM((length, feat), BF16),
            pltpu.VMEM((length, inner_width), BF16),
            pltpu.VMEM((length, inner_width), BF16),
            pltpu.VMEM((length, feat), F32),
            pltpu.VMEM((length, feat), F32),
            pltpu.VMEM((length, feat), BF16),
            pltpu.VMEM((8, inner_width), F32),
            DMA((9,)),
            DMA((3,)),
            DMA((3,)),
            DMA((3,)),
            DMA((3,)),
            DMA((14,)),
        ]
        + gather_sems() * 4,
        compiler_params=pltpu.CompilerParams(
            collective_id=0, has_side_effects=True, vmem_limit_bytes=VMEM_LIMIT
        ),
        name="forward",
    )(tokens, grads, live, slots, w_q, w_k, w_v, w_o, w_1, w_2, small)


def add_into(dst, src, lead):
    total = 1
    for size in lead:
        total *= size

    def step(flat, _):
        index = []
        for size in reversed(lead):
            index.append(flat % size)
            flat = flat // size
        index = tuple(reversed(index))
        dst[index] = (dst[index].astype(F32) + src[index].astype(F32)).astype(BF16)
        return 0

    lax.fori_loop(0, total, step, 0)


def reduce_kernel(count, *refs):
    parts, outs = refs[:count], refs[count : 2 * count]
    bufs = refs[2 * count : 2 * count + 6 * count]
    cs, cr, ps, pr, qs, qr, zs, zr = refs[8 * count :]
    z, x, y, c = my_place()
    x_peer, y_peer, c_peer = (z, 1 - x, y, c), (z, x, 1 - y, c), (z, x, y, 1 - c)
    meet(grid_peers(z, x, y, c))
    sends, core, first, second, last = [], [], [], [], []
    for a in range(count):
        got = bufs[6 * a]
        core.append(remote(parts[a].at[:, :, :, 1 - c], got, cs.at[a], cr.at[a], c_peer))
        core[-1].start()
    for a in range(count):
        own, got = parts[a].at[:, :, :, c], bufs[6 * a]
        core[a].wait_recv()
        add_into(own, got, (4, 2, 2))
        pair = [
            remote(half(own.at[:, :, 1 - y], 0), bufs[6 * a + 1], ps.at[a, 0], pr.at[a, 0], y_peer),
            remote(half(own.at[:, 1 - x], 1), bufs[6 * a + 2], ps.at[a, 1], pr.at[a, 1], x_peer),
        ]
        for copy in pair:
            copy.start()
        first.append(pair)
    for a in range(count):
        own = parts[a].at[:, :, :, c]
        pair = []
        first[a][0].wait_recv()
        add_into(half(own.at[:, :, y], 0), bufs[6 * a + 1], (4, 2))
        pair.append(
            remote(half(own.at[:, 1 - x, y], 0), bufs[6 * a + 3], qs.at[a, 0], qr.at[a, 0], x_peer)
        )
        pair[-1].start()
        first[a][1].wait_recv()
        add_into(half(own.at[:, x], 1), bufs[6 * a + 2], (4, 2))
        pair.append(
            remote(half(own.at[:, x, 1 - y], 1), bufs[6 * a + 4], qs.at[a, 1], qr.at[a, 1], y_peer)
        )
        pair[-1].start()
        second.append(pair)
    for a in range(count):
        own = parts[a].at[:, x, y, c]
        for h in (0, 1):
            second[a][h].wait_recv()
            add_into(half(own, h), bufs[6 * a + 3 + h], (4,))
        row = []
        for j in range(3):
            there = (z + j + 1) % 4
            row.append(
                remote(
                    own.at[there],
                    bufs[6 * a + 5].at[j],
                    zs.at[a, j],
                    zr.at[a, j],
                    (there, x, y, c),
                )
            )
            row[-1].start()
        last.append(row)
    for a in range(count):
        for copy in last[a]:
            copy.wait_recv()
        total = parts[a][z, x, y, c].astype(F32)
        for j in range(3):
            total = total + bufs[6 * a + 5][j].astype(F32)
        outs[a][...] = total
    for a in range(count):
        for copy in [core[a]] + first[a] + second[a] + last[a]:
            copy.wait_send()


def reduce_shards(parts):
    count = len(parts)
    dma = pltpu.SemaphoreType.DMA
    vmem = pl.BlockSpec(memory_space=pltpu.VMEM)
    bufs = []
    for part in parts:
        rows, width = part.shape[-2:]
        bufs += [
            pltpu.VMEM((4, 2, 2, rows, width), BF16),
            pltpu.VMEM((4, 2, rows, width // 2), BF16),
            pltpu.VMEM((4, 2, rows, width // 2), BF16),
            pltpu.VMEM((4, rows, width // 2), BF16),
            pltpu.VMEM((4, rows, width // 2), BF16),
            pltpu.VMEM((3, rows, width), BF16),
        ]

    def body(*refs):
        reduce_kernel(count, *refs)

    return pl.pallas_call(
        body,
        out_shape=[jax.ShapeDtypeStruct(p.shape[-2:], F32) for p in parts],
        in_specs=[vmem] * count,
        out_specs=[vmem] * count,
        scratch_shapes=bufs
        + [dma((count,))] * 2
        + [dma((count, 2))] * 4
        + [dma((count, 3))] * 2,
        compiler_params=pltpu.CompilerParams(
            collective_id=1, has_side_effects=True, vmem_limit_bytes=VMEM_LIMIT
        ),
        name="reduce",
    )(*parts)


def backward_pages(saved, weights, grad_slots, slots, live):
    (qkv, lse, x_low, attended, normed_one, hidden_low, act_low, slope, normed_two, factors, bias) = saved
    wq, wk, wv, wo, w1, w2 = weights
    length, feat = x_low.shape
    heads = feat // HEAD_DIM
    scale = HEAD_DIM**-0.5
    g1, g2 = bias[3], bias[6]
    select = (slots == jnp.arange(grad_slots.shape[0])[:, None]).astype(BF16)
    grad_layer = dot_rows(select, grad_slots)
    grad_g2 = jnp.sum(grad_layer * normed_two, axis=0)
    grad_s2 = jnp.sum(grad_layer, axis=0)
    grad_second = norm_back(grad_layer * g2, normed_two, factors[:, 128:129])
    second_low = grad_second.astype(BF16)
    grad_w2 = dot_rows(act_low, second_low)
    grad_b2 = jnp.sum(second_low.astype(F32), axis=0)
    inner_low = (dot_cols(second_low, w2) * slope).astype(BF16)
    grad_w1 = dot_rows(hidden_low, inner_low)
    grad_b1 = jnp.sum(inner_low.astype(F32), axis=0)
    grad_hidden = grad_second + dot_cols(inner_low, w1)
    grad_g1 = jnp.sum(grad_hidden * normed_one, axis=0)
    grad_s1 = jnp.sum(grad_hidden, axis=0)
    grad_first = norm_back(grad_hidden * g1, normed_one, factors[:, 0:1])
    first_low = grad_first.astype(BF16)
    grad_wo = dot_rows(attended, first_low)
    grad_bo = jnp.sum(first_low.astype(F32), axis=0)
    split = lambda flat: flat.reshape(length, heads, HEAD_DIM)
    query, key, value = (split(qkv[:, i * feat : (i + 1) * feat]) for i in range(3))
    grad_att = split(dot_cols(first_low, wo).astype(BF16))
    ein = lambda form, a, b: jnp.einsum(form, a, b, preferred_element_type=F32)
    scores = jnp.where(live[None, None, :], ein("thd,uhd->htu", query, key) * scale, NEG_FILL)
    probs = jnp.exp(scores - lse[:heads, :, None])
    grad_probs = ein("thd,uhd->htu", grad_att, value)
    inner_sum = jnp.sum(probs * grad_probs, axis=-1, keepdims=True)
    grad_scores = (probs * (grad_probs - inner_sum)).astype(BF16)
    flat = lambda per_head, factor: (per_head * factor).astype(BF16).reshape(-1, feat)
    grad_q = flat(ein("htu,uhd->thd", grad_scores, key), scale)
    grad_k = flat(ein("htu,thd->uhd", grad_scores, query), scale)
    grad_v = flat(ein("htu,thd->uhd", probs.astype(BF16), grad_att), 1.0)
    grad_wq, grad_wk, grad_wv = (dot_rows(x_low, g) for g in (grad_q, grad_k, grad_v))
    grad_bq = jnp.sum(grad_q.astype(F32), axis=0)
    grad_bv = jnp.sum(grad_v.astype(F32), axis=0)
    grad_in = grad_first + dot_cols(grad_q, wq) + dot_cols(grad_k, wk) + dot_cols(grad_v, wv)
    return grad_in.astype(BF16), (
        (grad_wq, grad_bq, grad_wk, grad_wv, grad_bv, grad_wo, grad_bo, grad_g1, grad_s1)
        + (grad_w1, grad_b1, grad_w2, grad_b2, grad_g2, grad_s2)
    )


def small_shard(weights):
    rows = [jnp.pad(weights[i], (0, 128 - weights[i].shape[0])) for i in SMALL_ORDER]
    rows += [jnp.zeros_like(rows[0])] * (16 - len(rows))
    return jnp.stack(rows)


SMALL_ORDER = (1, 4, 6, 7, 8, 12, 13, 14, 10)


def by_kernels(tokens, band_ids, page_mask, weights, grad_output):
    bands = lax.axis_size("band")
    me = lax.axis_index("band")
    slot_cap, feat = grad_output.shape[1:]
    ids = lax.dynamic_slice_in_dim(band_ids, me, 1, 0)
    live = lax.dynamic_slice_in_dim(page_mask, me, 1, 0)
    slots = page_slots(ids, bands, slot_cap)
    large = [weights[i] for i in (0, 2, 3, 5, 9, 11)]
    got = forward(tokens, grad_output, live.reshape(-1, 1), slots, *large, small_shard(weights))
    saved, full, grad_slots, layer_slots = got[:11], got[11:17], got[17], got[18]
    full = [w.reshape(-1, w.shape[-1]) for w in full]
    grad_in, grads = backward_pages(saved, full, grad_slots.reshape(-1, feat), slots, live[0] > 0)
    return (
        from_pages(layer_slots.reshape(1, -1, feat)),
        from_pages(grad_in[None]),
    ) + reduce_grads(grads, True)


def per_device(hand_made, *args):
    tokens, band_ids, band_counts, page_mask = args[:4]
    weights, grad_output = args[4:19], args[19]
    if hand_made:
        return by_kernels(tokens, band_ids, page_mask, weights, grad_output)
    bands = lax.axis_size("band")
    slot_cap = grad_output.shape[1]
    pages = tokens.shape[0] // bands
    full = [lax.all_gather(w, BOTH, axis=0, tiled=True) for w in weights]
    first = lax.axis_index("band") * pages
    ids = lax.dynamic_slice_in_dim(band_ids, first, pages, 0)
    live = lax.dynamic_slice_in_dim(page_mask, first, pages, 0) > 0
    slots = page_slots(ids, bands, slot_cap)
    layer_slots, grad_in, grads = layer_pages(
        to_pages(tokens), slots, live, to_pages(grad_output), full
    )
    return (from_pages(layer_slots), from_pages(grad_in)) + reduce_grads(grads, False)


def solution(mesh):
    hand_made = dict(mesh.shape) == {"page": 8, "band": 4}
    shard = P(BOTH)
    rows = P(BOTH, None)
    tokens = P("page", "band", None)
    page = P("page", None)
    weights = (rows, shard, rows, rows, shard, rows, shard, shard, shard)
    weights = weights + (rows, shard, rows, shard, shard, shard)

    def step(*args):
        return per_device(hand_made, *args)

    return jax.shard_map(
        step,
        mesh=mesh,
        in_specs=(tokens, page, page, page) + weights + (tokens,),
        out_specs=(tokens, tokens) + weights,
        check_vma=False,
    )
```

```python
import jax
import jax.numpy as jnp
from jax import lax
from jax.experimental import pallas as pl
from jax.experimental.pallas import tpu as pltpu
from jax.sharding import PartitionSpec as P

HEAD_DIM = 64
LN_EPS = 1e-12
NEG_FILL = -1e30
MESH = pl.DeviceIdType.MESH
DMA = pltpu.SemaphoreType.DMA
F32 = jnp.float32
BF16 = jnp.bfloat16
BOTH = ("page", "band")
VMEM_LIMIT = 62 * 2**20


def my_place():
    page, band = lax.axis_index("page"), lax.axis_index("band")
    return page // 2, page % 2, band // 2, band % 2


def dev(z, x, y, c):
    return (z * 2 + x, y * 2 + c)


def remote(src, dst, send_sem, recv_sem, place):
    return pltpu.make_async_remote_copy(
        src_ref=src,
        dst_ref=dst,
        send_sem=send_sem,
        recv_sem=recv_sem,
        device_id=dev(*place),
        device_id_type=MESH,
    )


def meet(places):
    barrier = pltpu.get_barrier_semaphore()
    for place in places:
        pl.semaphore_signal(barrier, inc=1, device_id=dev(*place), device_id_type=MESH)
    pl.semaphore_wait(barrier, len(places))


def grid_peers(z, x, y, c):
    return [((z + j) % 4, x, y, c) for j in (1, 2, 3)] + [
        (z, 1 - x, y, c),
        (z, x, 1 - y, c),
        (z, x, y, 1 - c),
    ]


def half(ref, which):
    rows, width = ref.shape[-2] // 2, ref.shape[-1] // 2
    if width % 128:
        return ref.at[..., pl.ds(which * rows, rows), :]
    return ref.at[..., pl.ds(which * width, width)]


def norm_rows(values):
    center = values - jnp.mean(values, axis=-1, keepdims=True)
    factor = lax.rsqrt(jnp.mean(center * center, axis=-1, keepdims=True) + LN_EPS)
    return (center * factor, factor)


def norm_back(upstream, normed, factor):
    return factor * (
        upstream
        - jnp.mean(upstream, axis=-1, keepdims=True)
        - normed * jnp.mean(upstream * normed, axis=-1, keepdims=True)
    )


def dot(first, second):
    return jnp.dot(first, second, preferred_element_type=F32)


def dot_rows(first, second):
    return lax.dot_general(first, second, (((0,), (0,)), ((), ())), preferred_element_type=F32)


def dot_cols(first, second):
    return lax.dot_general(first, second, (((1,), (1,)), ((), ())), preferred_element_type=F32)


def page_slots(ids, bands, slot_cap):
    onehot = (ids[:, :, None] == jnp.arange(bands, dtype=jnp.int32)).astype(F32)
    length = ids.shape[1]
    before = (jnp.arange(length)[:, None] > jnp.arange(length)[None, :]).astype(F32)
    counts = jnp.einsum("tu,pub->ptb", before, onehot, preferred_element_type=F32)
    rank = jnp.sum(onehot * counts, axis=2).astype(jnp.int32)
    return ids * slot_cap + rank


def layer_pages(rows_in, slots, live, grad_slots, weights):
    (wq, bq, wk, wv, bv, wo, bo, g1, s1, w1, b1, w2, b2, g2, s2) = weights
    pages, length, feat = rows_in.shape
    heads = feat // HEAD_DIM
    scale = HEAD_DIM**-0.5
    x_low = rows_in.reshape(-1, feat)
    select = (slots[:, None, :] == jnp.arange(grad_slots.shape[1])[None, :, None]).astype(BF16)
    grad_layer = jnp.einsum("pst,psd->ptd", select, grad_slots, preferred_element_type=F32)
    grad_layer = grad_layer.reshape(-1, feat)

    def split(flat):
        return flat.reshape(pages, length, heads, HEAD_DIM)

    query = split((dot(x_low, wq) + bq).astype(BF16))
    key = split(dot(x_low, wk).astype(BF16))
    value = split((dot(x_low, wv) + bv).astype(BF16))
    scores = jnp.einsum("pthd,puhd->phtu", query, key, preferred_element_type=F32) * scale
    scores = jnp.where(live[:, None, None, :], scores, NEG_FILL)
    shifted = jnp.exp(scores - jnp.max(scores, axis=-1, keepdims=True))
    probs = shifted / jnp.sum(shifted, axis=-1, keepdims=True)
    probs_low = probs.astype(BF16)
    mixed = jnp.einsum("phtu,puhd->pthd", probs_low, value, preferred_element_type=F32)
    attended = mixed.astype(BF16).reshape(-1, feat)
    normed_one, factor_one = norm_rows(x_low.astype(F32) + dot(attended, wo) + bo)
    hidden = normed_one * g1 + s1
    hidden_low = hidden.astype(BF16)
    inner = dot(hidden_low, w1) + b1
    cdf = 0.5 * (1.0 + lax.erf(inner * (0.5**0.5)))
    act_low = (inner * cdf).astype(BF16)
    slope = cdf + inner * jnp.exp(-0.5 * inner * inner) * ((0.5 / jnp.pi) ** 0.5)
    normed_two, factor_two = norm_rows(hidden + dot(act_low, w2) + b2)
    layer = (normed_two * g2 + s2).astype(BF16).reshape(pages, length, feat)
    layer_slots = jnp.einsum("pst,ptd->psd", select, layer, preferred_element_type=F32).astype(BF16)

    grad_g2 = jnp.sum(grad_layer * normed_two, axis=0)
    grad_s2 = jnp.sum(grad_layer, axis=0)
    grad_second = norm_back(grad_layer * g2, normed_two, factor_two)
    second_low = grad_second.astype(BF16)
    grad_w2 = dot_rows(act_low, second_low)
    grad_b2 = jnp.sum(second_low.astype(F32), axis=0)
    inner_low = (dot_cols(second_low, w2) * slope).astype(BF16)
    grad_w1 = dot_rows(hidden_low, inner_low)
    grad_b1 = jnp.sum(inner_low.astype(F32), axis=0)
    grad_hidden = grad_second + dot_cols(inner_low, w1)
    grad_g1 = jnp.sum(grad_hidden * normed_one, axis=0)
    grad_s1 = jnp.sum(grad_hidden, axis=0)
    grad_first = norm_back(grad_hidden * g1, normed_one, factor_one)
    first_low = grad_first.astype(BF16)
    grad_wo = dot_rows(attended, first_low)
    grad_bo = jnp.sum(first_low.astype(F32), axis=0)
    grad_att = split(dot_cols(first_low, wo).astype(BF16))
    grad_probs = jnp.einsum("pthd,puhd->phtu", grad_att, value, preferred_element_type=F32)
    inner_sum = jnp.sum(probs * grad_probs, axis=-1, keepdims=True)
    grad_scores = (probs * (grad_probs - inner_sum)).astype(BF16)

    def flat(per_head, factor):
        return (per_head * factor).astype(BF16).reshape(-1, feat)

    ein = lambda form, a, b: jnp.einsum(form, a, b, preferred_element_type=F32)
    grad_q = flat(ein("phtu,puhd->pthd", grad_scores, key), scale)
    grad_k = flat(ein("phtu,pthd->puhd", grad_scores, query), scale)
    grad_v = flat(ein("phtu,pthd->puhd", probs_low, grad_att), 1.0)
    grad_wq, grad_wk, grad_wv = (dot_rows(x_low, g) for g in (grad_q, grad_k, grad_v))
    grad_bq = jnp.sum(grad_q.astype(F32), axis=0)
    grad_bv = jnp.sum(grad_v.astype(F32), axis=0)
    grad_in = grad_first + dot_cols(grad_q, wq) + dot_cols(grad_k, wk) + dot_cols(grad_v, wv)
    grad_in = grad_in.astype(BF16).reshape(pages, length, feat)
    return (
        layer_slots,
        grad_in,
        (grad_wq, grad_bq, grad_wk, grad_wv, grad_bv, grad_wo, grad_bo, grad_g1, grad_s1)
        + (grad_w1, grad_b1, grad_w2, grad_b2, grad_g2, grad_s2),
    )


def to_pages(blocks):
    return lax.all_to_all(blocks, "band", split_axis=0, concat_axis=1, tiled=True)


def from_pages(blocks):
    return lax.all_to_all(blocks, "band", split_axis=1, concat_axis=0, tiled=True)


def split_ref(ref, which):
    rows, width = ref.shape[-2:]
    cut = width // 6
    if cut % 128:
        return ref.at[..., pl.ds(which * (rows // 2), rows // 2), :]
    return ref.at[..., pl.ds(which * cut, (cut, width - cut)[which])]


def split_shape(shape, which):
    rows, width = shape[-2:]
    cut = width // 6
    if cut % 128:
        return shape[:-2] + (rows // 2, width)
    return shape[:-1] + ((cut, width - cut)[which],)


def in_order(*calls):
    def step():
        for method, *index in calls:
            method(*index)

    return step


class Gather:
    def __init__(self, own, buf, sems, place):
        self.own, self.buf, self.place = own, buf, place
        self.zs, self.zr, self.ss, self.sr, self.fs, self.fr, self.cs, self.cr = sems

    def z_copy(self, j):
        z, x, y, c = self.place
        there = (z ^ (j + 1), x, y, c)
        return remote(self.own, self.buf.at[z, x, y, c], self.zs.at[j], self.zr.at[j], there)

    def side_copy(self, j, axis):
        z, x, y, c = self.place
        part = self.buf.at[z ^ j, x, y, c]
        there = (z, 1 - x, y, c) if axis == 0 else (z, x, 1 - y, c)
        source = self.own if j == 0 else part
        return remote(source, part, self.ss.at[axis, j], self.sr.at[axis, j], there)

    def far_copy(self, j, axis):
        z, x, y, c = self.place
        if axis == 0:
            part, there = self.buf.at[z ^ j, 1 - x, y, c], (z, x, 1 - y, c)
        else:
            part, there = self.buf.at[z ^ j, x, 1 - y, c], (z, 1 - x, y, c)
        part = split_ref(part, axis)
        return remote(part, part, self.fs.at[axis, j], self.fr.at[axis, j], there)

    def core_copy(self, k):
        z, x, y, c = self.place
        part = self.buf.at[:, (x, 1 - x, x, 1 - x)[k], (y, y, 1 - y, 1 - y)[k], c]
        return remote(part, part, self.cs.at[k], self.cr.at[k], (z, x, y, 1 - c))

    def start(self):
        for j in range(3):
            self.z_copy(j).start()
        for axis in (0, 1):
            self.side_copy(0, axis).start()

    def side(self, j):
        self.z_copy(j - 1).wait_recv()
        for axis in (0, 1):
            self.side_copy(j, axis).start()

    def far(self, j):
        for axis in (0, 1):
            self.side_copy(j, axis).wait_recv()
            self.far_copy(j, axis).start()

    def core(self, k):
        if k == 3:
            for j in range(4):
                for axis in (0, 1):
                    self.far_copy(j, axis).wait_recv()
        self.core_copy(k).start()

    def steps(self):
        side, far, core = self.side, self.far, self.core
        return [
            in_order((side, 1)),
            in_order((far, 0)),
            in_order((side, 2)),
            in_order((far, 1)),
            in_order((side, 3), (core, 0)),
            in_order((far, 2)),
            in_order((far, 3), (core, 1), (core, 2)),
            in_order((core, 3)),
        ]

    def arrive(self):
        for k in range(4):
            self.core_copy(k).wait_recv()

    def finish(self):
        for j in range(3):
            self.z_copy(j).wait_send()
        for j in range(4):
            for axis in (0, 1):
                self.side_copy(j, axis).wait_send()
                self.far_copy(j, axis).wait_send()
            self.core_copy(j).wait_send()


def gather_sems():
    return [DMA((3,)), DMA((3,))] + [DMA((2, 4))] * 4 + [DMA((4,))] * 2


def lanes(shape):
    return lax.broadcasted_iota(jnp.int32, shape, len(shape) - 1)


def rows_of(shape):
    return lax.broadcasted_iota(jnp.int32, shape, len(shape) - 2)


def columns(buf, start, width):
    return buf[:, :, :, :, :, pl.ds(start, width)].reshape(-1, width)


def unpack_rows(block, per_shard, width):
    shards, count, _ = block.shape
    spread = (rows_of((128, width)) == lanes((128, width)) % per_shard).astype(BF16)
    wide = dot(block.reshape(-1, 128), spread).reshape(shards, count, width)
    owner = lax.broadcasted_iota(jnp.int32, wide.shape, 0) == lanes(wide.shape) // per_shard
    return jnp.sum(jnp.where(owner, wide, 0.0), axis=0)


def pack_rows(rows, per_shard, shards):
    count, width = rows.shape
    wide = jnp.broadcast_to(rows[None], (shards, count, width))
    owner = lax.broadcasted_iota(jnp.int32, wide.shape, 0) == lanes(wide.shape) // per_shard
    wide = jnp.where(owner, wide, 0.0).astype(BF16).reshape(-1, width)
    spread = (lanes((width, 128)) == rows_of((width, 128)) % per_shard).astype(BF16)
    return dot(wide, spread).astype(BF16).reshape(shards, count, 128)


def block_of(i, size):
    return pl.ds(pl.multiple_of(i * size, size), size)


def gelu_parts(v):
    cdf = 0.5 * (1.0 + lax.erf(v * (0.5**0.5)))
    return v * cdf, cdf + v * jnp.exp(-0.5 * v * v) * ((0.5 / jnp.pi) ** 0.5)


class Out:
    def __init__(self, sems):
        self.sems, self.copies = sems, []

    def send(self, src, dst):
        copy = pltpu.make_async_copy(src, dst, self.sems.at[len(self.copies)])
        copy.start()
        self.copies.append(copy)

    def wait(self):
        for copy in self.copies:
            copy.wait()


BIAS_ROWS = 8
TILE = 256


def forward_kernel(
    tokens, grads, live, slots, w_q, w_k, w_v, w_o, w_1, w_2, small_in,
    qkv_out, lse, x_out, att_out, normed1_out, low_out, act_out, slope_out, normed2_out,
    factors, bias, q_out, k_out, v_out, o_out, w1_out, w2_out, grad_pages, layer_slots,
    small, a_buf, w1_buf, w2_buf, x_buf, qkv, att, normed1, low, act, slope, second, normed2, layer, bias1,
    local, ts, tr, gs, gr, outs, *sems,
):
    place = z, x, y, c = my_place()
    me = y * 2 + c
    length, feat = low.shape
    pairs = feat // 128
    x_rows = x_buf.reshape(length, feat)
    here = (z, x, y, c)
    copies = [
        pltpu.make_async_copy(src, dst, local.at[i])
        for i, (src, dst) in enumerate(
            [(w, a_buf.at[here + (slice(None), pl.ds(i * feat, feat))]) for i, w in enumerate((w_q, w_k, w_v, w_o))]
            + [(small_in, small.at[here]), (w_1, w1_buf.at[here]), (w_2, w2_buf.at[here])]
            + [(tokens.at[me], x_buf.at[me]), (grads.at[me], grad_pages.at[me])]
        )
    ]
    for copy in copies:
        copy.start()
    meet(
        [(z ^ j, x, y, c) for j in (1, 2, 3)]
        + [(z, 1 - x, y, c), (z, x, 1 - y, c), (z, x, y, 1 - c), (z, x, 1 - y, 1 - c)]
    )

    def page_copy(src, dst, send, recv, j):
        there = me ^ (j + 1)
        return remote(src.at[there], dst.at[me], send.at[j], recv.at[j], (z, x, there // 2, there % 2))

    token_copies = [page_copy(tokens, x_buf, ts, tr, j) for j in range(3)]
    grad_copies = [page_copy(grads, grad_pages, gs, gr, j) for j in range(3)]
    gathers = [
        Gather(own, buf, sems[8 * i : 8 * i + 8], place)
        for i, (own, buf) in enumerate(
            [(small_in, small), (a_buf.at[here], a_buf), (w_1, w1_buf), (w_2, w2_buf)]
        )
    ]
    vectors, atts, inner, outer = gathers
    for copy in copies[:5]:
        copy.wait()
    atts.start()
    vectors.start()
    for copy in token_copies:
        copy.start()
    later_1, later_2 = inner.steps(), outer.steps()
    for i, (first, other) in enumerate(zip(vectors.steps(), atts.steps())):
        other()
        first()
        if i == 2:
            inner.start()
        if i == 5:
            outer.start()
        if i == 6:
            later_1[0]()
    for copy in copies[5:]:
        copy.wait()
    for copy in grad_copies:
        copy.start()
    vectors.arrive()
    shards = small[...].reshape(32, 16, 128)
    bias[...] = unpack_rows(shards[:, :8], feat // 32, feat)
    inner_width = act.shape[1]
    for i in range(4):
        part = unpack_rows(small[i].reshape(8, 16, 128)[:, 8:], inner_width // 32, inner_width // 4)
        bias1[:, i * (inner_width // 4) : (i + 1) * (inner_width // 4)] = part
    for copy in token_copies:
        copy.wait_recv()
    atts.arrive()
    out = Out(outs)
    for i, ref in enumerate((q_out, k_out, v_out, o_out)):
        out.send(a_buf.at[:, :, :, :, :, pl.ds(i * feat, feat)], ref)
    out.send(x_rows, x_out)
    for step in later_1[1:3]:
        step()

    def project(j, _):
        start = pl.multiple_of(j * TILE, TILE)
        total = dot(x_rows[...], columns(a_buf, start, TILE))
        which = j // (feat // TILE)
        inside = block_of(j % (feat // TILE), TILE)
        row = jnp.where(which == 0, bias[0:1, inside], jnp.where(which == 2, bias[1:2, inside], 0.0))
        qkv[:, pl.ds(start, TILE)] = (total + row).astype(BF16)
        return 0

    lax.fori_loop(0, 3 * feat // TILE, project, 0)
    out.send(qkv, qkv_out)
    for step in later_1[3:5]:
        step()
    under = [
        [later_1[5], later_2[0]],
        [later_1[6], later_2[1], later_2[2]],
        [later_1[7], later_2[3]],
        [later_2[4]],
        [later_2[5]],
        [later_2[6]],
    ]
    scale = HEAD_DIM**-0.5

    def pair(p, _):
        start = pl.multiple_of(p * 128, 128)
        q = qkv[:, pl.ds(start, 128)] * jnp.asarray(scale, BF16)
        k = qkv[:, pl.ds(feat + start, 128)]
        v = qkv[:, pl.ds(2 * feat + start, 128)]
        low_lane = lanes(q.shape) < HEAD_DIM
        mixed = []
        for h in (0, 1):
            part = jnp.where(low_lane if h == 0 else ~low_lane, k, jnp.zeros_like(k))
            scores = jnp.where(live[...] > 0, dot_cols(part, q), NEG_FILL)
            top = jnp.max(scores, axis=0, keepdims=True)
            shifted = jnp.exp(scores - top)
            total = jnp.sum(shifted, axis=0, keepdims=True)
            probs = (shifted * (1.0 / total)).astype(BF16)
            mixed.append(dot_rows(v, probs))
            lse[pl.ds(2 * p + h, 1), :] = top + jnp.log(total)
        both = jnp.where(rows_of(mixed[0].shape) < HEAD_DIM, mixed[0], mixed[1])
        att[:, pl.ds(start, 128)] = both.T.astype(BF16)
        for i, steps in enumerate(under):
            pl.when(p == i)(in_order(*[(step,) for step in steps]))
        return 0

    lax.fori_loop(0, pairs, pair, 0)
    out.send(att, att_out)
    rows = 128

    def norm_one(i, _):
        block = block_of(i, rows)
        total = dot(att[block, :], columns(a_buf, 3 * feat, feat))
        total = total + x_rows[block, :].astype(F32) + bias[2:3, :]
        normed, factor = norm_rows(total)
        normed1[block, :] = normed
        factors[block, 0:128] = jnp.broadcast_to(factor, (rows, 128))
        low[block, :] = (normed * bias[3:4, :] + bias[4:5, :]).astype(BF16)
        return 0

    lax.fori_loop(0, length // rows, norm_one, 0)
    out.send(normed1, normed1_out)
    out.send(low, low_out)
    inner.arrive()
    out.send(w1_buf, w1_out)
    later_2[7]()

    def ffn_in(j, _):
        block = block_of(j, TILE)
        value, grad = gelu_parts(dot(low[...], columns(w1_buf, block.start, TILE)) + bias1[0:1, block])
        act[:, block] = value.astype(BF16)
        slope[:, block] = grad.astype(BF16)
        return 0

    lax.fori_loop(0, inner_width // TILE, ffn_in, 0)
    out.send(act, act_out)
    out.send(slope, slope_out)
    outer.arrive()
    out.send(w2_buf, w2_out)

    def ffn_out(j, _):
        block = block_of(j, TILE)
        second[:, block] = dot(act[...], columns(w2_buf, block.start, TILE))
        return 0

    lax.fori_loop(0, feat // TILE, ffn_out, 0)

    def norm_two(i, _):
        block = block_of(i, rows)
        hidden = normed1[block, :] * bias[3:4, :] + bias[4:5, :]
        normed, factor = norm_rows(hidden + second[block, :] + bias[5:6, :])
        normed2[block, :] = normed
        factors[block, 128:256] = jnp.broadcast_to(factor, (rows, 128))
        layer[block, :] = (normed * bias[6:7, :] + bias[7:8, :]).astype(BF16)
        return 0

    lax.fori_loop(0, length // rows, norm_two, 0)
    out.send(normed2, normed2_out)

    def place_rows(i, _):
        cap = layer_slots.shape[1]
        here_rows = rows_of((cap, length)) + i * cap
        select = (here_rows == slots[...]).astype(BF16)
        layer_slots[i] = dot(select, layer[...]).astype(BF16)
        return 0

    lax.fori_loop(0, layer_slots.shape[0], place_rows, 0)
    for copy in grad_copies:
        copy.wait_recv()
    for copy in grad_copies + token_copies:
        copy.wait_send()
    for one in gathers:
        one.finish()
    out.wait()


def forward(tokens, grads, live, slots, w_q, w_k, w_v, w_o, w_1, w_2, small):
    length, feat, inner_width = slots.shape[1], tokens.shape[-1], w_1.shape[1]
    anywhere = pl.BlockSpec(memory_space=pl.ANY)
    vmem = pl.BlockSpec(memory_space=pltpu.VMEM)
    grid = (4, 2, 2, 2)
    heads = feat // HEAD_DIM
    results = [
        ((length, 3 * feat), BF16, anywhere),
        ((heads + -heads % 8, length), F32, vmem),
        ((length, feat), BF16, anywhere),
        ((length, feat), BF16, anywhere),
        ((length, feat), F32, anywhere),
        ((length, feat), BF16, anywhere),
        ((length, inner_width), BF16, anywhere),
        ((length, inner_width), BF16, anywhere),
        ((length, feat), F32, anywhere),
        ((length, 256), F32, vmem),
        ((BIAS_ROWS, feat), F32, vmem),
    ]
    results += [(grid + w_q.shape, BF16, anywhere)] * 4
    results += [(grid + w_1.shape, BF16, anywhere), (grid + w_2.shape, BF16, anywhere)]
    results += [(grads.shape, BF16, anywhere), (grads.shape, BF16, vmem)]
    return pl.pallas_call(
        forward_kernel,
        out_shape=[jax.ShapeDtypeStruct(shape, kind) for shape, kind, _ in results],
        in_specs=[anywhere, anywhere, vmem, vmem] + [anywhere] * 7,
        out_specs=[spec for _, _, spec in results],
        scratch_shapes=[
            pltpu.VMEM(grid + small.shape, BF16),
            pltpu.VMEM(grid + (w_q.shape[0], 4 * feat), BF16),
            pltpu.VMEM(grid + w_1.shape, BF16),
            pltpu.VMEM(grid + w_2.shape, BF16),
            pltpu.VMEM(tokens.shape, BF16),
            pltpu.VMEM((length, 3 * feat), BF16),
            pltpu.VMEM((length, feat), BF16),
            pltpu.VMEM((length, feat), F32),
            pltpu.VMEM((length, feat), BF16),
            pltpu.VMEM((length, inner_width), BF16),
            pltpu.VMEM((length, inner_width), BF16),
            pltpu.VMEM((length, feat), F32),
            pltpu.VMEM((length, feat), F32),
            pltpu.VMEM((length, feat), BF16),
            pltpu.VMEM((8, inner_width), F32),
            DMA((9,)),
            DMA((3,)),
            DMA((3,)),
            DMA((3,)),
            DMA((3,)),
            DMA((14,)),
        ]
        + gather_sems() * 4,
        compiler_params=pltpu.CompilerParams(
            collective_id=0, has_side_effects=True, vmem_limit_bytes=VMEM_LIMIT
        ),
        name="forward",
    )(tokens, grads, live, slots, w_q, w_k, w_v, w_o, w_1, w_2, small)


def add_into(dst, src, lead):
    def step(flat, _):
        index = []
        for size in reversed(lead):
            index.append(flat % size)
            flat = flat // size
        index = tuple(reversed(index))
        dst[index] = (dst[index].astype(F32) + src[index].astype(F32)).astype(BF16)
        return 0

    total = 1
    for size in lead:
        total *= size
    lax.fori_loop(0, total, step, 0)


class Reduce:
    def __init__(self, part, bufs, sems, place, write, by_z):
        self.part, self.place, self.write = part, place, write
        self.got_core, self.got_1, self.got_2, self.got_z = bufs[0], bufs[1:3], bufs[3:5], bufs[5]
        self.cs, self.cr, self.fs, self.fr, self.ss, self.sr, self.zs, self.zr = sems
        self.chunks = (3, 2, 1, 0) if by_z else (0,)
        self.by_z = by_z

    def at(self, j):
        return self.place[0] ^ j if self.by_z else slice(None)

    def lead(self, *rest):
        return rest if self.by_z else (4,) + rest

    def core_copy(self, j):
        z, x, y, c = self.place
        zi = self.at(j)
        there = (z, x, y, 1 - c)
        return remote(self.part.at[zi, :, :, 1 - c], self.got_core.at[zi], self.cs.at[j], self.cr.at[j], there)

    def first_copy(self, j, axis):
        z, x, y, c = self.place
        zi = self.at(j)
        if axis == 0:
            part, there = self.part.at[zi, :, 1 - y, c], (z, x, 1 - y, c)
        else:
            part, there = self.part.at[zi, 1 - x, :, c], (z, 1 - x, y, c)
        return remote(split_ref(part, axis), self.got_1[axis].at[zi], self.fs.at[axis, j], self.fr.at[axis, j], there)

    def second_copy(self, j, axis):
        z, x, y, c = self.place
        zi = self.at(j)
        if axis == 0:
            part, there = self.part.at[zi, 1 - x, y, c], (z, 1 - x, y, c)
        else:
            part, there = self.part.at[zi, x, 1 - y, c], (z, x, 1 - y, c)
        return remote(split_ref(part, axis), self.got_2[axis].at[zi], self.ss.at[axis, j], self.sr.at[axis, j], there)

    def z_copy(self, j):
        z, x, y, c = self.place
        part = self.part.at[z ^ j, x, y, c]
        return remote(part, self.got_z.at[j - 1], self.zs.at[j - 1], self.zr.at[j - 1], (z ^ j, x, y, c))

    def send(self, j):
        self.core_copy(j).start()

    def send_all(self):
        for j in self.chunks:
            self.send(j)

    def first(self, j):
        z, x, y, c = self.place
        zi = self.at(j)
        self.core_copy(j).wait_recv()
        add_into(self.part.at[zi, :, :, c], self.got_core.at[zi], self.lead(2, 2))
        for axis in (0, 1):
            self.first_copy(j, axis).start()

    def second(self, j):
        z, x, y, c = self.place
        zi = self.at(j)
        for axis in (0, 1):
            self.first_copy(j, axis).wait_recv()
            part = self.part.at[zi, :, y, c] if axis == 0 else self.part.at[zi, x, :, c]
            add_into(split_ref(part, axis), self.got_1[axis].at[zi], self.lead(2))
            self.second_copy(j, axis).start()

    def along_z(self, j):
        z, x, y, c = self.place
        zi = self.at(j)
        for axis in (0, 1):
            self.second_copy(j, axis).wait_recv()
            part = split_ref(self.part.at[zi, x, y, c], axis)
            got = self.got_2[axis].at[zi]
            if self.by_z:
                part[...] = (part[...].astype(F32) + got[...].astype(F32)).astype(BF16)
            else:
                add_into(part, got, (4,))
        for i in (1, 2, 3):
            if not self.by_z or i == j:
                self.z_copy(i).start()

    def last(self):
        z, x, y, c = self.place
        total = self.part[z, x, y, c].astype(F32)
        for i in (1, 2, 3):
            self.z_copy(i).wait_recv()
            total = total + self.got_z[i - 1].astype(F32)
        self.write(total)

    def steps(self):
        first, second, along = self.first, self.second, self.along_z
        if not self.by_z:
            return [in_order((first, 0)), in_order((second, 0)), in_order((along, 0)), in_order((self.last,))]
        return [
            in_order((first, 3)),
            in_order((first, 2), (second, 3)),
            in_order((first, 1), (second, 2), (along, 3)),
            in_order((first, 0), (second, 1), (along, 2)),
            in_order((second, 0), (along, 1)),
            in_order((along, 0)),
            in_order((self.last,)),
        ]

    def finish(self):
        for j in self.chunks:
            self.core_copy(j).wait_send()
            for axis in (0, 1):
                self.first_copy(j, axis).wait_send()
                self.second_copy(j, axis).wait_send()
        for i in (1, 2, 3):
            self.z_copy(i).wait_send()


def reduce_sems():
    return [DMA((4,))] * 2 + [DMA((2, 4))] * 4 + [DMA((3,))] * 2


def reduce_bufs(rows, width):
    shape = (rows, width)
    return [
        pltpu.VMEM((4, 2, 2) + shape, BF16),
        pltpu.VMEM(split_shape((4, 2) + shape, 0), BF16),
        pltpu.VMEM(split_shape((4, 2) + shape, 1), BF16),
        pltpu.VMEM(split_shape((4,) + shape, 0), BF16),
        pltpu.VMEM(split_shape((4,) + shape, 1), BF16),
        pltpu.VMEM((3,) + shape, BF16),
    ]


PIECES = 7
GROUPS = 3


def backward_kernel(
    qkv_in, lse, x_in, att_in, normed1_in, low_in, act_in, slope_in, normed2_in, factors, bias,
    w_q, w_k, w_v, w_o, w1_in, w2_in, grads_in, layer_in, slots, live,
    layer_out, tokens_out, q_out, k_out, v_out, o_out, w1_out, w2_out, small_out,
    qkv, x, att, normed1, low, act, slope, grad, grads, w1, wb, turned, d_qkv, g_2, g_1, g_o, g_qkv, g_small, sums, sums1,
    local, ls, lr, ts, tr, *rest,
):
    place = z, px, py, c = my_place()
    me = py * 2 + c
    length, feat = low.shape
    inner_width = act.shape[1]
    bufs, sems = rest[: 6 * PIECES], rest[6 * PIECES :]
    slots_each = grads.shape[0] // 4

    sources = [(grads_in.at[i], grads.at[pl.ds(i * slots_each, slots_each)]) for i in range(4)]
    sources += [(normed2_in, grad), (act_in, act), (w2_in, wb), (slope_in, slope), (low_in, low), (w1_in, w1)]
    sources += [(normed1_in, normed1), (att_in, att), (qkv_in, qkv), (x_in, x)]
    loads = [pltpu.make_async_copy(src, dst, local.at[i]) for i, (src, dst) in enumerate(sources)]
    for copy in loads:
        copy.start()
    meet(
        [(z ^ j, px, py, c) for j in (1, 2, 3)]
        + [(z, 1 - px, py, c), (z, px, 1 - py, c), (z, px, py, 1 - c), (z, px, 1 - py, 1 - c)]
    )

    def page_copy(src, dst, send, recv, j):
        there = me ^ (j + 1)
        return remote(src.at[there], dst.at[me], send.at[j], recv.at[j], (z, px, there // 2, there % 2))

    layer_copies = [page_copy(layer_in, layer_out, ls, lr, j) for j in range(3)]
    for copy in layer_copies:
        copy.start()
    layer_own = pltpu.make_async_copy(layer_in.at[me], layer_out.at[me], local.at[14])
    layer_own.start()

    def whole(ref):
        def write(total):
            ref[...] = total

        return write

    def thirds(group):
        def write(total):
            for i, ref in enumerate((q_out, k_out, v_out)):
                ref[:, pl.ds(group * TILE, TILE)] = total[:, i * TILE : (i + 1) * TILE]

        return write

    parts = [(g_2, whole(w2_out), True), (g_1, whole(w1_out), True), (g_o, whole(o_out), False)]
    parts += [(g_qkv.at[i], thirds(i), False) for i in range(GROUPS)]
    parts += [(g_small, whole(small_out), False)]
    sums_2, sum_1, sum_o, *sum_qkv, sum_small = reduces = [
        Reduce(part, bufs[6 * i : 6 * i + 6], sems[8 * i : 8 * i + 8], place, write, by_z)
        for i, (part, write, by_z) in enumerate(parts)
    ]
    steps_2, steps_1, steps_o, *steps_qkv, steps_small = [one.steps() for one in reduces]

    sums[...] = jnp.zeros_like(sums)
    sums1[...] = jnp.zeros_like(sums1)

    def tally(row, values):
        sums[row : row + 1, :] += jnp.sum(values, axis=0, keepdims=True)

    for copy in loads[:5]:
        copy.wait()
    rows = 128

    def norm_two(i, _):
        block = block_of(i, rows)
        select = (rows_of((grads.shape[0], rows)) == slots[:, block]).astype(BF16)
        grad_layer = dot_rows(select, grads[...])
        normed = grad[block, :]
        tally(6, grad_layer * normed)
        tally(7, grad_layer)
        back = norm_back(grad_layer * bias[6:7, :], normed, factors[block, 128:129])
        grad[block, :] = back
        second_low = back.astype(BF16)
        d_qkv[block, 0:feat] = second_low
        tally(5, second_low.astype(F32))
        return 0

    lax.fori_loop(0, length // rows, norm_two, 0)
    second = grads.at[pl.ds(0, length)]
    second[...] = d_qkv[:, 0:feat]
    loads[5].wait()

    def outer_grad(i, _):
        j = 3 - i
        zi = z ^ j
        width = inner_width // 4
        part = dot_rows(act[:, block_of(zi, width)], second[...])
        g_2[zi] = part.astype(BF16).reshape(g_2.shape[1:])
        sums_2.send(j)
        return 0

    lax.fori_loop(0, 4, outer_grad, 0)
    for copy in loads[6:9]:
        copy.wait()
    turned[...] = low[...].T
    when_2 = {2: 0, 4: 1, 6: 2, 8: 3, 10: 4}

    def inner_grad(i, _):
        block = block_of(i, TILE)
        up = dot_cols(second[...], wb[block, :])
        inner_low = (up * slope[:, block].astype(F32)).astype(BF16)
        slope[:, block] = inner_low
        sums1[0:1, block] = jnp.sum(inner_low.astype(F32), axis=0, keepdims=True)
        part = dot(turned[...], inner_low)
        g_1[:, :, :, :, :, block] = part.astype(BF16).reshape(g_1.shape[:-1] + (TILE,))
        for at, index in when_2.items():
            pl.when(i == at)(steps_2[index])
        return 0

    lax.fori_loop(0, inner_width // TILE, inner_grad, 0)
    sum_1.send_all()
    slabs = [
        pltpu.make_async_copy(src, wb.at[pl.ds(i * feat, feat)], local.at[15 + i])
        for i, src in enumerate((w_o, w_q, w_k, w_v))
    ]
    for copy in slabs:
        copy.start()
    for copy in loads[9:]:
        copy.wait()
    steps_2[5]()

    def hidden_grad(i, _):
        half_width = feat // 2
        block = block_of(i, half_width)
        weight = w1[pl.ds(2 * i, 2)].reshape(half_width, inner_width)
        grad[:, block] += dot_cols(slope[...], weight)
        return 0

    lax.fori_loop(0, 2, hidden_grad, 0)
    steps_1[0]()
    first = second

    def norm_one(i, _):
        block = block_of(i, rows)
        up, normed = grad[block, :], normed1[block, :]
        tally(3, up * normed)
        tally(4, up)
        back = norm_back(up * bias[3:4, :], normed, factors[block, 0:1])
        grad[block, :] = back
        first_low = back.astype(BF16)
        first[block, :] = first_low
        tally(2, first_low.astype(F32))
        return 0

    lax.fori_loop(0, length // rows, norm_one, 0)
    for copy in slabs:
        copy.wait()
    g_o[...] = dot_rows(att[...], first[...]).astype(BF16).reshape(g_o.shape)
    sum_o.send_all()
    grad_att = grads.at[pl.ds(length, length)]

    def att_grad(i, _):
        block = block_of(i, rows)
        grad_att[block, :] = dot_cols(first[block, :], wb[0:feat, :]).astype(BF16)
        return 0

    lax.fori_loop(0, length // rows, att_grad, 0)
    turned[...] = x[...].T
    steps_1[1]()
    scale = HEAD_DIM**-0.5

    def pair(p):
        start = pl.multiple_of(p * 128, 128)
        q = qkv[:, pl.ds(start, 128)] * jnp.asarray(scale, BF16)
        k = qkv[:, pl.ds(feat + start, 128)]
        v = qkv[:, pl.ds(2 * feat + start, 128)]
        g = grad_att[:, pl.ds(start, 128)]
        low_lane = lanes(q.shape) < HEAD_DIM
        results = []
        for h in (0, 1):
            keep = low_lane if h == 0 else ~low_lane
            zero = jnp.zeros_like(k)
            scores = jnp.where(live[...] > 0, dot_cols(jnp.where(keep, k, zero), q), NEG_FILL)
            probs = jnp.exp(scores - lse[pl.ds(2 * p + h, 1), :])
            up = dot_cols(jnp.where(keep, v, zero), g)
            inner_sum = jnp.sum(probs * up, axis=0, keepdims=True)
            grad_scores = (probs * (up - inner_sum)).astype(BF16)
            results.append((dot_rows(k, grad_scores), dot(grad_scores, q), dot(probs.astype(BF16), g)))
        (q_0, k_0, v_0), (q_1, k_1, v_1) = results
        d_q = jnp.where(rows_of(q_0.shape) < HEAD_DIM, q_0, q_1) * scale
        d_qkv[:, pl.ds(start, 128)] = d_q.T.astype(BF16)
        d_qkv[:, pl.ds(feat + start, 128)] = jnp.where(low_lane, k_0, k_1).astype(BF16)
        d_qkv[:, pl.ds(2 * feat + start, 128)] = jnp.where(low_lane, v_0, v_1).astype(BF16)

    under = [
        [steps_1[2], steps_2[6]],
        [steps_1[3], steps_o[0]],
        [steps_1[4], steps_o[1]],
        [steps_1[5], steps_qkv[0][0]],
        [steps_o[2], steps_qkv[0][1]],
        [steps_1[6], steps_qkv[1][0]],
    ]

    def group(i, _):
        def one(j, _):
            p = 2 * i + j
            pair(p)
            for at, steps in enumerate(under):
                pl.when(p == at)(in_order(*[(step,) for step in steps]))
            return 0

        lax.fori_loop(0, 2, one, 0)
        for t in range(3):
            cols = pl.ds(pl.multiple_of(t * feat + i * TILE, TILE), TILE)
            part = dot(turned[...], d_qkv[:, cols])
            g_qkv[i, :, :, :, :, :, pl.ds(t * TILE, TILE)] = part.astype(BF16).reshape(
                g_qkv.shape[1:-1] + (TILE,)
            )
        for at in range(GROUPS):
            pl.when(i == at)(sum_qkv[at].send_all)
        return 0

    lax.fori_loop(0, GROUPS, group, 0)
    tally(0, d_qkv[:, 0:feat].astype(F32))
    tally(1, d_qkv[:, 2 * feat : 3 * feat].astype(F32))
    g_small[:, :, :, :, 0:8, :] = pack_rows(sums[...], feat // 32, 32).reshape(4, 2, 2, 2, 8, 128)
    for i in range(4):
        part = sums1[:, i * (inner_width // 4) : (i + 1) * (inner_width // 4)]
        g_small[i, :, :, :, 8:16, :] = pack_rows(part, inner_width // 32, 8).reshape(2, 2, 2, 8, 128)
    sum_small.send_all()
    steps_qkv[2][0]()

    def token_grad(i, _):
        block = block_of(i, rows)
        total = grad[block, :]
        for t in range(3):
            total += dot_cols(
                d_qkv[block, t * feat : (t + 1) * feat], wb[(t + 1) * feat : (t + 2) * feat, :]
            )
        x[block, :] = total.astype(BF16)
        return 0

    lax.fori_loop(0, length // rows, token_grad, 0)
    grad_tokens = x.reshape(4, length // 4, feat)
    token_copies = [page_copy(grad_tokens, tokens_out, ts, tr, j) for j in range(3)]
    for copy in token_copies:
        copy.start()
    token_own = pltpu.make_async_copy(grad_tokens.at[me], tokens_out.at[me], local.at[19])
    token_own.start()
    steps_small[0]()
    steps_qkv[1][1]()
    steps_o[3]()
    steps_qkv[0][2]()
    steps_qkv[2][1]()
    steps_small[1]()
    steps_qkv[1][2]()
    steps_qkv[0][3]()
    steps_qkv[2][2]()
    steps_small[2]()
    steps_qkv[1][3]()
    steps_qkv[2][3]()
    steps_small[3]()
    for copy in layer_copies + token_copies:
        copy.wait()
    layer_own.wait()
    token_own.wait()
    for one in reduces:
        one.finish()


def backward(saved, weights, grad_pages, layer_slots, slots, live, tokens_shape):
    w_q, w_1, w_2 = weights[0], weights[4], weights[5]
    qkv, lse, x, att, normed1, low, act, slope, normed2, factors, bias = saved
    length, feat = low.shape
    inner_width = act.shape[1]
    anywhere = pl.BlockSpec(memory_space=pl.ANY)
    vmem = pl.BlockSpec(memory_space=pltpu.VMEM)
    grid = (4, 2, 2, 2)
    small, inner, outer = (feat // 32, feat), (feat // 32, inner_width), (inner_width // 32, feat)
    sizes = [outer, inner] + [small] * 4 + [(16, 128)]
    scratch = [
        ((length, 3 * feat), BF16),
        ((length, feat), BF16),
        ((length, feat), BF16),
        ((length, feat), F32),
        ((length, feat), BF16),
        ((length, inner_width), BF16),
        ((length, inner_width), BF16),
        ((length, feat), F32),
        ((grad_pages.shape[0] * grad_pages.shape[1], feat), BF16),
        (grid + inner, BF16),
        ((inner_width, feat), BF16),
        ((feat, length), BF16),
        ((length, 3 * feat), BF16),
        (grid + outer, BF16),
        (grid + inner, BF16),
        (grid + small, BF16),
        ((GROUPS,) + grid + small, BF16),
        (grid + (16, 128), BF16),
        ((8, feat), F32),
        ((8, inner_width), F32),
    ]
    bufs, sems = [], []
    for size in sizes:
        bufs += reduce_bufs(*size)
        sems += reduce_sems()
    outs = [(grad_pages.shape, BF16, anywhere), (tokens_shape, BF16, anywhere)]
    outs += [(small, F32, vmem)] * 4 + [(inner, F32, vmem), (outer, F32, vmem), ((16, 128), F32, vmem)]
    return pl.pallas_call(
        backward_kernel,
        out_shape=[jax.ShapeDtypeStruct(shape, kind) for shape, kind, _ in outs],
        in_specs=[anywhere, vmem] + [anywhere] * 7 + [vmem, vmem] + [anywhere] * 8 + [vmem, vmem],
        out_specs=[spec for _, _, spec in outs],
        scratch_shapes=[pltpu.VMEM(shape, kind) for shape, kind in scratch]
        + [DMA((20,)), DMA((3,)), DMA((3,)), DMA((3,)), DMA((3,))]
        + bufs
        + sems,
        compiler_params=pltpu.CompilerParams(
            collective_id=1, has_side_effects=True, vmem_limit_bytes=VMEM_LIMIT
        ),
        name="backward",
    )(*saved, *weights, grad_pages, layer_slots, slots, live)


def small_shard(weights):
    rows = [jnp.pad(weights[i], (0, 128 - weights[i].shape[0])) for i in SMALL_ORDER]
    rows += [jnp.zeros_like(rows[0])] * (16 - len(rows))
    return jnp.stack(rows)


SMALL_ORDER = (1, 4, 6, 7, 8, 12, 13, 14, 10)


def by_kernels(tokens, band_ids, page_mask, weights, grad_output):
    bands = lax.axis_size("band")
    me = lax.axis_index("band")
    slot_cap, feat = grad_output.shape[1:]
    ids = lax.dynamic_slice_in_dim(band_ids, me, 1, 0)
    live = lax.dynamic_slice_in_dim(page_mask, me, 1, 0)
    slots = page_slots(ids, bands, slot_cap)
    large = [weights[i] for i in (0, 2, 3, 5, 9, 11)]
    got = forward(tokens, grad_output, live.reshape(-1, 1), slots, *large, small_shard(weights))
    saved, full, grad_slots, layer_slots = got[:11], got[11:17], got[17], got[18]
    full = [w if i == 4 else w.reshape(-1, w.shape[-1]) for i, w in enumerate(full)]
    sums = backward(saved, full, grad_slots, layer_slots, slots, live.reshape(-1, 1), tokens.shape)
    grads = [None] * len(weights)
    for i, total in zip((0, 2, 3, 5, 9, 11), sums[2:8]):
        grads[i] = total
    for row, i in enumerate(SMALL_ORDER):
        grads[i] = sums[8][row, : weights[i].shape[0]]
    return tuple(sums[:2]) + tuple(grads)


def per_device(hand_made, *args):
    tokens, band_ids, band_counts, page_mask = args[:4]
    weights, grad_output = args[4:19], args[19]
    if hand_made:
        return by_kernels(tokens, band_ids, page_mask, weights, grad_output)
    bands = lax.axis_size("band")
    slot_cap = grad_output.shape[1]
    pages = tokens.shape[0] // bands
    full = [lax.all_gather(w, BOTH, axis=0, tiled=True) for w in weights]
    first = lax.axis_index("band") * pages
    ids = lax.dynamic_slice_in_dim(band_ids, first, pages, 0)
    live = lax.dynamic_slice_in_dim(page_mask, first, pages, 0) > 0
    slots = page_slots(ids, bands, slot_cap)
    layer_slots, grad_in, grads = layer_pages(
        to_pages(tokens), slots, live, to_pages(grad_output), full
    )
    return (from_pages(layer_slots), from_pages(grad_in)) + tuple(
        lax.psum_scatter(g, BOTH, scatter_dimension=0, tiled=True) for g in grads
    )


def solution(mesh):
    hand_made = dict(mesh.shape) == {"page": 8, "band": 4}
    shard = P(BOTH)
    rows = P(BOTH, None)
    tokens = P("page", "band", None)
    page = P("page", None)
    weights = (rows, shard, rows, rows, shard, rows, shard, shard, shard)
    weights = weights + (rows, shard, rows, shard, shard, shard)

    def step(*args):
        return per_device(hand_made, *args)

    return jax.shard_map(
        step,
        mesh=mesh,
        in_specs=(tokens, page, page, page) + weights + (tokens,),
        out_specs=(tokens, tokens) + weights,
        check_vma=False,
    )
```

```python
import jax
import jax.numpy as jnp
from jax import lax
from jax.experimental import pallas as pl
from jax.experimental.pallas import tpu as pltpu
from jax.sharding import PartitionSpec as P

HEAD_DIM = 64
LN_EPS = 1e-12
NEG_FILL = -1e30
MESH = pl.DeviceIdType.MESH
DMA = pltpu.SemaphoreType.DMA
F32 = jnp.float32
BF16 = jnp.bfloat16
BOTH = ("page", "band")
VMEM_LIMIT = 62 * 2**20


def my_place():
    page, band = lax.axis_index("page"), lax.axis_index("band")
    return page // 2, page % 2, band // 2, band % 2


def dev(z, x, y, c):
    return (z * 2 + x, y * 2 + c)


def remote(src, dst, send_sem, recv_sem, place):
    return pltpu.make_async_remote_copy(
        src_ref=src,
        dst_ref=dst,
        send_sem=send_sem,
        recv_sem=recv_sem,
        device_id=dev(*place),
        device_id_type=MESH,
    )


def meet(places):
    barrier = pltpu.get_barrier_semaphore()
    for place in places:
        pl.semaphore_signal(barrier, inc=1, device_id=dev(*place), device_id_type=MESH)
    pl.semaphore_wait(barrier, len(places))


def grid_peers(z, x, y, c):
    return [((z + j) % 4, x, y, c) for j in (1, 2, 3)] + [
        (z, 1 - x, y, c),
        (z, x, 1 - y, c),
        (z, x, y, 1 - c),
    ]


def half(ref, which):
    rows, width = ref.shape[-2] // 2, ref.shape[-1] // 2
    if width % 128:
        return ref.at[..., pl.ds(which * rows, rows), :]
    return ref.at[..., pl.ds(which * width, width)]


def norm_rows(values):
    center = values - jnp.mean(values, axis=-1, keepdims=True)
    factor = lax.rsqrt(jnp.mean(center * center, axis=-1, keepdims=True) + LN_EPS)
    return (center * factor, factor)


def norm_back(upstream, normed, factor):
    return factor * (
        upstream
        - jnp.mean(upstream, axis=-1, keepdims=True)
        - normed * jnp.mean(upstream * normed, axis=-1, keepdims=True)
    )


def dot(first, second):
    return jnp.dot(first, second, preferred_element_type=F32)


def dot_rows(first, second):
    return lax.dot_general(first, second, (((0,), (0,)), ((), ())), preferred_element_type=F32)


def dot_cols(first, second):
    return lax.dot_general(first, second, (((1,), (1,)), ((), ())), preferred_element_type=F32)


def page_slots(ids, bands, slot_cap):
    onehot = (ids[:, :, None] == jnp.arange(bands, dtype=jnp.int32)).astype(F32)
    length = ids.shape[1]
    before = (jnp.arange(length)[:, None] > jnp.arange(length)[None, :]).astype(F32)
    counts = jnp.einsum("tu,pub->ptb", before, onehot, preferred_element_type=F32)
    rank = jnp.sum(onehot * counts, axis=2).astype(jnp.int32)
    return ids * slot_cap + rank


def layer_pages(rows_in, slots, live, grad_slots, weights):
    (wq, bq, wk, wv, bv, wo, bo, g1, s1, w1, b1, w2, b2, g2, s2) = weights
    pages, length, feat = rows_in.shape
    heads = feat // HEAD_DIM
    scale = HEAD_DIM**-0.5
    x_low = rows_in.reshape(-1, feat)
    select = (slots[:, None, :] == jnp.arange(grad_slots.shape[1])[None, :, None]).astype(BF16)
    grad_layer = jnp.einsum("pst,psd->ptd", select, grad_slots, preferred_element_type=F32)
    grad_layer = grad_layer.reshape(-1, feat)

    def split(flat):
        return flat.reshape(pages, length, heads, HEAD_DIM)

    query = split((dot(x_low, wq) + bq).astype(BF16))
    key = split(dot(x_low, wk).astype(BF16))
    value = split((dot(x_low, wv) + bv).astype(BF16))
    scores = jnp.einsum("pthd,puhd->phtu", query, key, preferred_element_type=F32) * scale
    scores = jnp.where(live[:, None, None, :], scores, NEG_FILL)
    shifted = jnp.exp(scores - jnp.max(scores, axis=-1, keepdims=True))
    probs = shifted / jnp.sum(shifted, axis=-1, keepdims=True)
    probs_low = probs.astype(BF16)
    mixed = jnp.einsum("phtu,puhd->pthd", probs_low, value, preferred_element_type=F32)
    attended = mixed.astype(BF16).reshape(-1, feat)
    normed_one, factor_one = norm_rows(x_low.astype(F32) + dot(attended, wo) + bo)
    hidden = normed_one * g1 + s1
    hidden_low = hidden.astype(BF16)
    inner = dot(hidden_low, w1) + b1
    cdf = 0.5 * (1.0 + lax.erf(inner * (0.5**0.5)))
    act_low = (inner * cdf).astype(BF16)
    slope = cdf + inner * jnp.exp(-0.5 * inner * inner) * ((0.5 / jnp.pi) ** 0.5)
    normed_two, factor_two = norm_rows(hidden + dot(act_low, w2) + b2)
    layer = (normed_two * g2 + s2).astype(BF16).reshape(pages, length, feat)
    layer_slots = jnp.einsum("pst,ptd->psd", select, layer, preferred_element_type=F32).astype(BF16)

    grad_g2 = jnp.sum(grad_layer * normed_two, axis=0)
    grad_s2 = jnp.sum(grad_layer, axis=0)
    grad_second = norm_back(grad_layer * g2, normed_two, factor_two)
    second_low = grad_second.astype(BF16)
    grad_w2 = dot_rows(act_low, second_low)
    grad_b2 = jnp.sum(second_low.astype(F32), axis=0)
    inner_low = (dot_cols(second_low, w2) * slope).astype(BF16)
    grad_w1 = dot_rows(hidden_low, inner_low)
    grad_b1 = jnp.sum(inner_low.astype(F32), axis=0)
    grad_hidden = grad_second + dot_cols(inner_low, w1)
    grad_g1 = jnp.sum(grad_hidden * normed_one, axis=0)
    grad_s1 = jnp.sum(grad_hidden, axis=0)
    grad_first = norm_back(grad_hidden * g1, normed_one, factor_one)
    first_low = grad_first.astype(BF16)
    grad_wo = dot_rows(attended, first_low)
    grad_bo = jnp.sum(first_low.astype(F32), axis=0)
    grad_att = split(dot_cols(first_low, wo).astype(BF16))
    grad_probs = jnp.einsum("pthd,puhd->phtu", grad_att, value, preferred_element_type=F32)
    inner_sum = jnp.sum(probs * grad_probs, axis=-1, keepdims=True)
    grad_scores = (probs * (grad_probs - inner_sum)).astype(BF16)

    def flat(per_head, factor):
        return (per_head * factor).astype(BF16).reshape(-1, feat)

    ein = lambda form, a, b: jnp.einsum(form, a, b, preferred_element_type=F32)
    grad_q = flat(ein("phtu,puhd->pthd", grad_scores, key), scale)
    grad_k = flat(ein("phtu,pthd->puhd", grad_scores, query), scale)
    grad_v = flat(ein("phtu,pthd->puhd", probs_low, grad_att), 1.0)
    grad_wq, grad_wk, grad_wv = (dot_rows(x_low, g) for g in (grad_q, grad_k, grad_v))
    grad_bq = jnp.sum(grad_q.astype(F32), axis=0)
    grad_bv = jnp.sum(grad_v.astype(F32), axis=0)
    grad_in = grad_first + dot_cols(grad_q, wq) + dot_cols(grad_k, wk) + dot_cols(grad_v, wv)
    grad_in = grad_in.astype(BF16).reshape(pages, length, feat)
    return (
        layer_slots,
        grad_in,
        (grad_wq, grad_bq, grad_wk, grad_wv, grad_bv, grad_wo, grad_bo, grad_g1, grad_s1)
        + (grad_w1, grad_b1, grad_w2, grad_b2, grad_g2, grad_s2),
    )


def to_pages(blocks):
    return lax.all_to_all(blocks, "band", split_axis=0, concat_axis=1, tiled=True)


def from_pages(blocks):
    return lax.all_to_all(blocks, "band", split_axis=1, concat_axis=0, tiled=True)


def split_ref(ref, which):
    rows, width = ref.shape[-2:]
    cut = width // 6
    if cut % 128:
        return ref.at[..., pl.ds(which * (rows // 2), rows // 2), :]
    return ref.at[..., pl.ds(which * cut, (cut, width - cut)[which])]


def split_shape(shape, which):
    rows, width = shape[-2:]
    cut = width // 6
    if cut % 128:
        return shape[:-2] + (rows // 2, width)
    return shape[:-1] + ((cut, width - cut)[which],)


def in_order(*calls):
    def step():
        for method, *index in calls:
            method(*index)

    return step


class Gather:
    def __init__(self, own, buf, sems, place):
        self.own, self.buf, self.place = own, buf, place
        self.zs, self.zr, self.ss, self.sr, self.fs, self.fr, self.cs, self.cr = sems

    def z_copy(self, j):
        z, x, y, c = self.place
        there = (z ^ (j + 1), x, y, c)
        return remote(self.own, self.buf.at[z, x, y, c], self.zs.at[j], self.zr.at[j], there)

    def side_copy(self, j, axis):
        z, x, y, c = self.place
        part = self.buf.at[z ^ j, x, y, c]
        there = (z, 1 - x, y, c) if axis == 0 else (z, x, 1 - y, c)
        source = self.own if j == 0 else part
        return remote(source, part, self.ss.at[axis, j], self.sr.at[axis, j], there)

    def far_copy(self, j, axis):
        z, x, y, c = self.place
        if axis == 0:
            part, there = self.buf.at[z ^ j, 1 - x, y, c], (z, x, 1 - y, c)
        else:
            part, there = self.buf.at[z ^ j, x, 1 - y, c], (z, 1 - x, y, c)
        part = split_ref(part, axis)
        return remote(part, part, self.fs.at[axis, j], self.fr.at[axis, j], there)

    def core_copy(self, k):
        z, x, y, c = self.place
        part = self.buf.at[:, (x, 1 - x, x, 1 - x)[k], (y, y, 1 - y, 1 - y)[k], c]
        return remote(part, part, self.cs.at[k], self.cr.at[k], (z, x, y, 1 - c))

    def start(self):
        for j in range(3):
            self.z_copy(j).start()
        for axis in (0, 1):
            self.side_copy(0, axis).start()

    def side(self, j):
        self.z_copy(j - 1).wait_recv()
        for axis in (0, 1):
            self.side_copy(j, axis).start()

    def far(self, j):
        for axis in (0, 1):
            self.side_copy(j, axis).wait_recv()
            self.far_copy(j, axis).start()

    def core(self, k):
        if k == 3:
            for j in range(4):
                for axis in (0, 1):
                    self.far_copy(j, axis).wait_recv()
        self.core_copy(k).start()

    def steps(self):
        side, far, core = self.side, self.far, self.core
        return [
            in_order((side, 1)),
            in_order((far, 0)),
            in_order((side, 2)),
            in_order((side, 3), (core, 0)),
            in_order((far, 1)),
            in_order((far, 2)),
            in_order((far, 3), (core, 1), (core, 2)),
            in_order((core, 3)),
        ]

    def arrive(self):
        for k in range(4):
            self.core_copy(k).wait_recv()

    def finish(self):
        for j in range(3):
            self.z_copy(j).wait_send()
        for j in range(4):
            for axis in (0, 1):
                self.side_copy(j, axis).wait_send()
                self.far_copy(j, axis).wait_send()
            self.core_copy(j).wait_send()


def gather_sems():
    return [DMA((3,)), DMA((3,))] + [DMA((2, 4))] * 4 + [DMA((4,))] * 2


def split_mid(ref, which):
    width = ref.shape[-1]
    cut = width // 384 * 128
    return ref.at[..., pl.ds(which * cut, (cut, width - cut)[which])]


class GatherMid:
    def __init__(self, own, buf, sems, place):
        self.own, self.buf, self.place = own, buf, place
        self.zs, self.zr, self.ss, self.sr, self.hs, self.hr, self.fs, self.fr, self.cs, self.cr = sems

    def z_copy(self, j):
        z, x, y, c = self.place
        there = (z ^ j, x, y, c)
        return remote(self.own, self.buf.at[z, x, y, c], self.zs.at[j - 1], self.zr.at[j - 1], there)

    def side_copy(self, axis):
        z, x, y, c = self.place
        there = (z, 1 - x, y, c) if axis == 0 else (z, x, 1 - y, c)
        source = split_mid(self.own, axis)
        return remote(source, split_mid(self.buf.at[z, x, y, c], axis), self.ss.at[axis], self.sr.at[axis], there)

    def half_copy(self, j, axis):
        z, x, y, c = self.place
        part = self.buf.at[z, 1 - x, y, c] if axis == 0 else self.buf.at[z, x, 1 - y, c]
        part = split_mid(part, axis)
        return remote(part, part, self.hs.at[axis, j - 1], self.hr.at[axis, j - 1], (z ^ j, x, y, c))

    def far_copy(self, j, axis):
        z, x, y, c = self.place
        if axis == 0:
            part, there = self.buf.at[z ^ j, :, y, c], (z, x, 1 - y, c)
        else:
            part, there = self.buf.at[z ^ j, x, :, c], (z, 1 - x, y, c)
        part = split_mid(part, axis)
        return remote(part, part, self.fs.at[axis, j], self.fr.at[axis, j], there)

    def core_copy(self, k):
        z, x, y, c = self.place
        part = self.buf.at[:, (x, 1 - x, x, 1 - x)[k], (y, y, 1 - y, 1 - y)[k], c]
        return remote(part, part, self.cs.at[k], self.cr.at[k], (z, x, y, 1 - c))

    def start(self):
        for axis in (0, 1):
            self.side_copy(axis).start()
        for j in (1, 2, 3):
            self.z_copy(j).start()

    def turn(self):
        for axis in (0, 1):
            self.side_copy(axis).wait_recv()
            for j in (1, 2, 3):
                self.half_copy(j, axis).start()
        for axis in (0, 1):
            self.far_copy(0, axis).start()

    def far(self, j):
        self.z_copy(j).wait_recv()
        for axis in (0, 1):
            self.half_copy(j, axis).wait_recv()
            self.far_copy(j, axis).start()

    def core(self, k):
        if k:
            for j in range(4):
                for axis in (0, 1):
                    self.far_copy(j, axis).wait_recv()
            for k in (1, 2, 3):
                self.core_copy(k).start()
        else:
            self.core_copy(0).start()

    def steps(self):
        far, core = self.far, self.core
        return [
            in_order((self.turn,)),
            in_order((far, 1)),
            in_order((far, 2)),
            in_order((far, 3), (core, 0)),
            in_order((core, 1)),
        ]

    def arrive(self):
        for k in range(4):
            self.core_copy(k).wait_recv()

    def finish(self):
        for axis in (0, 1):
            self.side_copy(axis).wait_send()
        for j in (1, 2, 3):
            self.z_copy(j).wait_send()
            for axis in (0, 1):
                self.half_copy(j, axis).wait_send()
        for j in range(4):
            for axis in (0, 1):
                self.far_copy(j, axis).wait_send()
            self.core_copy(j).wait_send()


def mid_sems():
    return [DMA((3,))] * 2 + [DMA((2,))] * 2 + [DMA((2, 3))] * 2 + [DMA((2, 4))] * 2 + [DMA((4,))] * 2


def lanes(shape):
    return lax.broadcasted_iota(jnp.int32, shape, len(shape) - 1)


def rows_of(shape):
    return lax.broadcasted_iota(jnp.int32, shape, len(shape) - 2)


def columns(buf, start, width):
    return buf[:, :, :, :, :, pl.ds(start, width)].reshape(-1, width)


def unpack_rows(block, per_shard, width):
    shards, count, _ = block.shape
    spread = (rows_of((128, width)) == lanes((128, width)) % per_shard).astype(BF16)
    wide = dot(block.reshape(-1, 128), spread).reshape(shards, count, width)
    owner = lax.broadcasted_iota(jnp.int32, wide.shape, 0) == lanes(wide.shape) // per_shard
    return jnp.sum(jnp.where(owner, wide, 0.0), axis=0)


def pack_rows(rows, per_shard, shards):
    count, width = rows.shape
    wide = jnp.broadcast_to(rows[None], (shards, count, width))
    owner = lax.broadcasted_iota(jnp.int32, wide.shape, 0) == lanes(wide.shape) // per_shard
    wide = jnp.where(owner, wide, 0.0).astype(BF16).reshape(-1, width)
    spread = (lanes((width, 128)) == rows_of((width, 128)) % per_shard).astype(BF16)
    return dot(wide, spread).astype(BF16).reshape(shards, count, 128)


def block_of(i, size):
    return pl.ds(pl.multiple_of(i * size, size), size)


def gelu_parts(v):
    cdf = 0.5 * (1.0 + lax.erf(v * (0.5**0.5)))
    return v * cdf, cdf + v * jnp.exp(-0.5 * v * v) * ((0.5 / jnp.pi) ** 0.5)


class Out:
    def __init__(self, sems):
        self.sems, self.copies = sems, []

    def send(self, src, dst):
        copy = pltpu.make_async_copy(src, dst, self.sems.at[len(self.copies)])
        copy.start()
        self.copies.append(copy)

    def wait(self):
        for copy in self.copies:
            copy.wait()


BIAS_ROWS = 8
TILE = 256


def forward_kernel(
    tokens, grads, ids, mask, w_q, w_k, w_v, w_o, w_1, w_2, small_in,
    qkv_out, lse, x_out, att_out, normed1_out, low_out, act_out, slope_out, normed2_out,
    factors, bias, q_out, k_out, v_out, o_out, w1_out, w2_out, grad_pages, layer_slots, slots, live,
    small, a_buf, w1_buf, w2_buf, x_buf, qkv, att, normed1, low, act, slope, second, normed2, layer, bias1,
    local, ts, tr, gs, gr, outs, *sems,
):
    place = z, x, y, c = my_place()
    me = y * 2 + c
    length, feat = low.shape
    pairs = feat // 128
    x_rows = x_buf.reshape(length, feat)
    here = (z, x, y, c)
    copies = [
        pltpu.make_async_copy(src, dst, local.at[i])
        for i, (src, dst) in enumerate(
            [(w, a_buf.at[here + (slice(None), pl.ds(i * feat, feat))]) for i, w in enumerate((w_q, w_k, w_v, w_o))]
            + [(small_in, small.at[here]), (w_1, w1_buf.at[here]), (w_2, w2_buf.at[here])]
            + [(tokens.at[me], x_buf.at[me]), (grads.at[me], grad_pages.at[me])]
        )
    ]
    for copy in copies:
        copy.start()
    meet(
        [(z ^ j, x, y, c) for j in (1, 2, 3)]
        + [(z, 1 - x, y, c), (z, x, 1 - y, c), (z, x, y, 1 - c), (z, x, 1 - y, 1 - c)]
    )

    def page_copy(src, dst, send, recv, j):
        there = me ^ (j + 1)
        return remote(src.at[there], dst.at[me], send.at[j], recv.at[j], (z, x, there // 2, there % 2))

    token_copies = [page_copy(tokens, x_buf, ts, tr, j) for j in range(3)]
    grad_copies = [page_copy(grads, grad_pages, gs, gr, j) for j in range(3)]
    gathers = [
        kind(own, buf, sems[8 * i :][: 8 if kind is Gather else 10], place)
        for i, (kind, own, buf) in enumerate(
            [(Gather, small_in, small), (Gather, a_buf.at[here], a_buf)]
            + [(Gather, w_1, w1_buf), (GatherMid, w_2, w2_buf)]
        )
    ]
    vectors, atts, inner, outer = gathers
    for copy in copies[:5]:
        copy.wait()
    atts.start()
    vectors.start()
    for copy in token_copies:
        copy.start()
    inner.start()
    outer.start()
    slot_cap = grads.shape[1]
    hot = (rows_of((8, length)) == ids[pl.ds(me, 1), :]).astype(F32)
    earlier = (rows_of((length, length)) < lanes((length, length))).astype(BF16)
    rank = dot(hot.astype(BF16), earlier) + (rows_of((8, length)) * slot_cap).astype(F32)
    slots[...] = jnp.sum(hot * rank, axis=0, keepdims=True).astype(jnp.int32)
    live[...] = jnp.broadcast_to(mask[pl.ds(me, 1), :].astype(F32), (8, length)).T[:, 0:1]
    steps_0, steps_1, steps_2 = atts.steps(), inner.steps(), outer.steps()
    behind = {3: [steps_1[0]], 4: [steps_1[1]], 5: [steps_1[2], steps_2[0]], 6: [steps_1[3]]}
    for i, (main, extra) in enumerate(zip(steps_0, vectors.steps())):
        main()
        extra()
        if i == 3:
            for copy in copies[5:7]:
                copy.wait()
        for step in behind.get(i, ()):
            step()
    for copy in copies[7:]:
        copy.wait()
    for copy in grad_copies:
        copy.start()
    vectors.arrive()
    shards = small[...].reshape(32, 16, 128)
    bias[...] = unpack_rows(shards[:, :8], feat // 32, feat)
    inner_width = act.shape[1]
    for i in range(4):
        part = unpack_rows(small[i].reshape(8, 16, 128)[:, 8:], inner_width // 32, inner_width // 4)
        bias1[:, i * (inner_width // 4) : (i + 1) * (inner_width // 4)] = part
    for copy in token_copies:
        copy.wait_recv()
    atts.arrive()
    out = Out(outs)
    for i, ref in enumerate((q_out, k_out, v_out, o_out)):
        out.send(a_buf.at[:, :, :, :, :, pl.ds(i * feat, feat)], ref)
    out.send(x_rows, x_out)
    steps_1[4]()

    def project(j, _):
        start = pl.multiple_of(j * TILE, TILE)
        total = dot(x_rows[...], columns(a_buf, start, TILE))
        which = j // (feat // TILE)
        inside = block_of(j % (feat // TILE), TILE)
        row = jnp.where(which == 0, bias[0:1, inside], jnp.where(which == 2, bias[1:2, inside], 0.0))
        qkv[:, pl.ds(start, TILE)] = (total + row).astype(BF16)
        return 0

    lax.fori_loop(0, 3 * feat // TILE, project, 0)
    out.send(qkv, qkv_out)
    steps_1[5]()
    under = {0: steps_1[6], 2: steps_1[7], 3: steps_2[1], 6: steps_2[2], 9: steps_2[3]}
    scale = HEAD_DIM**-0.5

    def pair(p, _):
        start = pl.multiple_of(p * 128, 128)
        q = qkv[:, pl.ds(start, 128)] * jnp.asarray(scale, BF16)
        k = qkv[:, pl.ds(feat + start, 128)]
        v = qkv[:, pl.ds(2 * feat + start, 128)]
        low_lane = lanes(q.shape) < HEAD_DIM
        mixed = []
        for h in (0, 1):
            part = jnp.where(low_lane if h == 0 else ~low_lane, k, jnp.zeros_like(k))
            scores = jnp.where(live[...] > 0, dot_cols(part, q), NEG_FILL)
            top = jnp.max(scores, axis=0, keepdims=True)
            shifted = jnp.exp(scores - top)
            total = jnp.sum(shifted, axis=0, keepdims=True)
            probs = (shifted * (1.0 / total)).astype(BF16)
            mixed.append(dot_rows(v, probs))
            lse[pl.ds(2 * p + h, 1), :] = top + jnp.log(total)
            for at, step in under.items():
                if at % 2 == h:
                    pl.when(p == at // 2)(step)
        both = jnp.where(rows_of(mixed[0].shape) < HEAD_DIM, mixed[0], mixed[1])
        att[:, pl.ds(start, 128)] = both.T.astype(BF16)
        return 0

    lax.fori_loop(0, pairs, pair, 0)
    out.send(att, att_out)
    rows = 128

    def norm_one(i, _):
        block = block_of(i, rows)
        total = dot(att[block, :], columns(a_buf, 3 * feat, feat))
        total = total + x_rows[block, :].astype(F32) + bias[2:3, :]
        normed, factor = norm_rows(total)
        normed1[block, :] = normed
        factors[block, 0:128] = jnp.broadcast_to(factor, (rows, 128))
        low[block, :] = (normed * bias[3:4, :] + bias[4:5, :]).astype(BF16)
        return 0

    lax.fori_loop(0, length // rows, norm_one, 0)
    out.send(normed1, normed1_out)
    out.send(low, low_out)
    inner.arrive()
    out.send(w1_buf, w1_out)

    def ffn_in(j, _):
        block = block_of(j, TILE)
        value, grad = gelu_parts(dot(low[...], columns(w1_buf, block.start, TILE)) + bias1[0:1, block])
        act[:, block] = value.astype(BF16)
        slope[:, block] = grad.astype(BF16)
        return 0

    lax.fori_loop(0, inner_width // TILE, ffn_in, 0)
    out.send(act, act_out)
    out.send(slope, slope_out)
    steps_2[4]()
    outer.arrive()
    out.send(w2_buf, w2_out)

    def ffn_out(j, _):
        block = block_of(j, TILE)
        second[:, block] = dot(act[...], columns(w2_buf, block.start, TILE))
        return 0

    lax.fori_loop(0, feat // TILE, ffn_out, 0)

    def norm_two(i, _):
        block = block_of(i, rows)
        hidden = normed1[block, :] * bias[3:4, :] + bias[4:5, :]
        normed, factor = norm_rows(hidden + second[block, :] + bias[5:6, :])
        normed2[block, :] = normed
        factors[block, 128:256] = jnp.broadcast_to(factor, (rows, 128))
        layer[block, :] = (normed * bias[6:7, :] + bias[7:8, :]).astype(BF16)
        return 0

    lax.fori_loop(0, length // rows, norm_two, 0)
    out.send(normed2, normed2_out)

    def place_rows(i, _):
        cap = layer_slots.shape[1]
        here_rows = rows_of((cap, length)) + i * cap
        select = (here_rows == slots[...]).astype(BF16)
        layer_slots[i] = dot(select, layer[...]).astype(BF16)
        return 0

    lax.fori_loop(0, layer_slots.shape[0], place_rows, 0)
    for copy in grad_copies:
        copy.wait_recv()
    for copy in grad_copies + token_copies:
        copy.wait_send()
    for one in gathers:
        one.finish()
    out.wait()


def forward(tokens, grads, ids, mask, w_q, w_k, w_v, w_o, w_1, w_2, small):
    length, feat, inner_width = ids.shape[1], tokens.shape[-1], w_1.shape[1]
    anywhere = pl.BlockSpec(memory_space=pl.ANY)
    vmem = pl.BlockSpec(memory_space=pltpu.VMEM)
    grid = (4, 2, 2, 2)
    heads = feat // HEAD_DIM
    results = [
        ((length, 3 * feat), BF16, anywhere),
        ((heads + -heads % 8, length), F32, vmem),
        ((length, feat), BF16, anywhere),
        ((length, feat), BF16, anywhere),
        ((length, feat), F32, anywhere),
        ((length, feat), BF16, anywhere),
        ((length, inner_width), BF16, anywhere),
        ((length, inner_width), BF16, anywhere),
        ((length, feat), F32, anywhere),
        ((length, 256), F32, vmem),
        ((BIAS_ROWS, feat), F32, vmem),
    ]
    results += [(grid + w_q.shape, BF16, anywhere)] * 4
    results += [(grid + w_1.shape, BF16, anywhere), (grid + w_2.shape, BF16, anywhere)]
    results += [(grads.shape, BF16, anywhere), (grads.shape, BF16, vmem)]
    results += [((1, length), jnp.int32, vmem), ((length, 1), F32, vmem)]
    return pl.pallas_call(
        forward_kernel,
        out_shape=[jax.ShapeDtypeStruct(shape, kind) for shape, kind, _ in results],
        in_specs=[anywhere, anywhere, vmem, vmem] + [anywhere] * 7,
        out_specs=[spec for _, _, spec in results],
        scratch_shapes=[
            pltpu.VMEM(grid + small.shape, BF16),
            pltpu.VMEM(grid + (w_q.shape[0], 4 * feat), BF16),
            pltpu.VMEM(grid + w_1.shape, BF16),
            pltpu.VMEM(grid + w_2.shape, BF16),
            pltpu.VMEM(tokens.shape, BF16),
            pltpu.VMEM((length, 3 * feat), BF16),
            pltpu.VMEM((length, feat), BF16),
            pltpu.VMEM((length, feat), F32),
            pltpu.VMEM((length, feat), BF16),
            pltpu.VMEM((length, inner_width), BF16),
            pltpu.VMEM((length, inner_width), BF16),
            pltpu.VMEM((length, feat), F32),
            pltpu.VMEM((length, feat), F32),
            pltpu.VMEM((length, feat), BF16),
            pltpu.VMEM((8, inner_width), F32),
            DMA((9,)),
            DMA((3,)),
            DMA((3,)),
            DMA((3,)),
            DMA((3,)),
            DMA((14,)),
        ]
        + gather_sems() * 3
        + mid_sems(),
        compiler_params=pltpu.CompilerParams(
            collective_id=0, has_side_effects=True, vmem_limit_bytes=VMEM_LIMIT
        ),
        name="forward",
    )(tokens, grads, ids, mask, w_q, w_k, w_v, w_o, w_1, w_2, small)


def add_into(dst, src, lead):
    def step(flat, _):
        index = []
        for size in reversed(lead):
            index.append(flat % size)
            flat = flat // size
        index = tuple(reversed(index))
        dst[index] = (dst[index].astype(F32) + src[index].astype(F32)).astype(BF16)
        return 0

    total = 1
    for size in lead:
        total *= size
    lax.fori_loop(0, total, step, 0)


class Reduce:
    def __init__(self, part, bufs, sems, place, write):
        self.part, self.place, self.write = part, place, write
        self.got_core, self.got_1, self.got_2, self.got_z = bufs[0], bufs[1:3], bufs[3:5], bufs[5]
        self.cs, self.cr, self.fs, self.fr, self.ss, self.sr, self.zs, self.zr = sems

    def core_copy(self):
        z, x, y, c = self.place
        there = (z, x, y, 1 - c)
        return remote(self.part.at[:, :, :, 1 - c], self.got_core, self.cs.at[0], self.cr.at[0], there)

    def first_copy(self, axis):
        z, x, y, c = self.place
        if axis == 0:
            part, there = self.part.at[:, :, 1 - y, c], (z, x, 1 - y, c)
        else:
            part, there = self.part.at[:, 1 - x, :, c], (z, 1 - x, y, c)
        return remote(split_ref(part, axis), self.got_1[axis], self.fs.at[axis], self.fr.at[axis], there)

    def second_copy(self, axis):
        z, x, y, c = self.place
        if axis == 0:
            part, there = self.part.at[:, 1 - x, y, c], (z, 1 - x, y, c)
        else:
            part, there = self.part.at[:, x, 1 - y, c], (z, x, 1 - y, c)
        return remote(split_ref(part, axis), self.got_2[axis], self.ss.at[axis], self.sr.at[axis], there)

    def z_copy(self, j):
        z, x, y, c = self.place
        part = self.part.at[z ^ j, x, y, c]
        return remote(part, self.got_z.at[j - 1], self.zs.at[j - 1], self.zr.at[j - 1], (z ^ j, x, y, c))

    def send_all(self):
        self.core_copy().start()

    def first(self):
        z, x, y, c = self.place
        self.core_copy().wait_recv()
        add_into(self.part.at[:, :, :, c], self.got_core, (4, 2, 2))
        for axis in (0, 1):
            self.first_copy(axis).start()

    def second(self):
        z, x, y, c = self.place
        for axis in (0, 1):
            self.first_copy(axis).wait_recv()
            part = self.part.at[:, :, y, c] if axis == 0 else self.part.at[:, x, :, c]
            add_into(split_ref(part, axis), self.got_1[axis], (4, 2))
            self.second_copy(axis).start()

    def along_z(self):
        z, x, y, c = self.place
        for axis in (0, 1):
            self.second_copy(axis).wait_recv()
            add_into(split_ref(self.part.at[:, x, y, c], axis), self.got_2[axis], (4,))
        for j in (1, 2, 3):
            self.z_copy(j).start()

    def last(self):
        z, x, y, c = self.place
        total = self.part[z, x, y, c].astype(F32)
        for j in (1, 2, 3):
            self.z_copy(j).wait_recv()
            total = total + self.got_z[j - 1].astype(F32)
        self.write(total)

    def finish(self):
        self.core_copy().wait_send()
        for axis in (0, 1):
            self.first_copy(axis).wait_send()
            self.second_copy(axis).wait_send()
        for j in (1, 2, 3):
            self.z_copy(j).wait_send()


def reduce_sems():
    return [DMA((1,))] * 2 + [DMA((2,))] * 4 + [DMA((3,))] * 2


def reduce_bufs(rows, width):
    shape = (rows, width)
    return [
        pltpu.VMEM((4, 2, 2) + shape, BF16),
        pltpu.VMEM(split_shape((4, 2) + shape, 0), BF16),
        pltpu.VMEM(split_shape((4, 2) + shape, 1), BF16),
        pltpu.VMEM(split_shape((4,) + shape, 0), BF16),
        pltpu.VMEM(split_shape((4,) + shape, 1), BF16),
        pltpu.VMEM((3,) + shape, BF16),
    ]


class ReduceMid:
    def __init__(self, part, bufs, sems, place, write):
        self.part, self.place, self.write = part, place, write
        self.got_core, self.got_1, self.got_z, self.got_last = bufs[0], bufs[1:3], bufs[3:5], bufs[5]
        self.cs, self.cr, self.fs, self.fr, self.zs, self.zr, self.ls, self.lr = sems

    def core_copy(self, j):
        z, x, y, c = self.place
        zi = z ^ j
        there = (z, x, y, 1 - c)
        return remote(self.part.at[zi, :, :, 1 - c], self.got_core.at[zi], self.cs.at[j], self.cr.at[j], there)

    def mine(self, zi, axis, other=0):
        z, x, y, c = self.place
        part = self.part.at[zi, :, abs(other - y), c] if axis == 0 else self.part.at[zi, abs(other - x), :, c]
        return split_mid(part, axis)

    def first_copy(self, j, axis):
        z, x, y, c = self.place
        zi = z ^ j
        there = (z, x, 1 - y, c) if axis == 0 else (z, 1 - x, y, c)
        return remote(self.mine(zi, axis, 1), self.got_1[axis].at[zi], self.fs.at[axis, j], self.fr.at[axis, j], there)

    def z_copy(self, j, axis):
        z, x, y, c = self.place
        return remote(
            self.mine(z ^ j, axis), self.got_z[axis].at[j - 1], self.zs.at[axis, j - 1], self.zr.at[axis, j - 1], (z ^ j, x, y, c)
        )

    def last_copy(self, axis):
        z, x, y, c = self.place
        if axis == 0:
            part, there = self.part.at[z, 1 - x, y, c], (z, 1 - x, y, c)
        else:
            part, there = self.part.at[z, x, 1 - y, c], (z, x, 1 - y, c)
        return remote(split_mid(part, axis), split_mid(self.got_last, axis), self.ls.at[axis], self.lr.at[axis], there)

    def send(self, j):
        self.core_copy(j).start()

    def send_all(self):
        for j in (3, 2, 1, 0):
            self.send(j)

    def first(self, j):
        z, x, y, c = self.place
        zi = z ^ j
        self.core_copy(j).wait_recv()
        add_into(self.part.at[zi, :, :, c], self.got_core.at[zi], (2, 2))
        for axis in (0, 1):
            self.first_copy(j, axis).start()

    def turn(self, j):
        zi = self.place[0] ^ j
        for axis in (0, 1):
            self.first_copy(j, axis).wait_recv()
            add_into(self.mine(zi, axis), self.got_1[axis].at[zi], (2,))
            if j:
                self.z_copy(j, axis).start()

    def fold(self):
        z, x, y, c = self.place
        for axis in (0, 1):
            for j in (1, 2, 3):
                self.z_copy(j, axis).wait_recv()
            mine, got = self.mine(z, axis), self.got_z[axis]

            def add(i, _, mine=mine, got=got):
                total = mine[i].astype(F32) + got[0, i].astype(F32)
                mine[i] = (total + got[1, i].astype(F32) + got[2, i].astype(F32)).astype(BF16)
                return 0

            lax.fori_loop(0, 2, add, 0)
            self.last_copy(axis).start()

    def last(self):
        z, x, y, c = self.place
        for axis in (0, 1):
            self.last_copy(axis).wait_recv()
        self.write(self.part[z, x, y, c].astype(F32) + self.got_last[...].astype(F32))

    def finish(self):
        for j in range(4):
            self.core_copy(j).wait_send()
            for axis in (0, 1):
                self.first_copy(j, axis).wait_send()
                if j:
                    self.z_copy(j, axis).wait_send()
        for axis in (0, 1):
            self.last_copy(axis).wait_send()


def reduce_mid_sems():
    return [DMA((4,))] * 2 + [DMA((2, 4))] * 2 + [DMA((2, 3))] * 2 + [DMA((2,))] * 2


def reduce_mid_bufs(rows, width):
    cut = width // 384 * 128
    return [
        pltpu.VMEM((4, 2, 2, rows, width), BF16),
        pltpu.VMEM((4, 2, rows, cut), BF16),
        pltpu.VMEM((4, 2, rows, width - cut), BF16),
        pltpu.VMEM((3, 2, rows, cut), BF16),
        pltpu.VMEM((3, 2, rows, width - cut), BF16),
        pltpu.VMEM((rows, width), BF16),
    ]


PIECES = 7
GROUPS = 3


def backward_kernel(
    qkv_in, lse, x_in, att_in, normed1_in, low_in, act_in, slope_in, normed2_in, factors, bias,
    w_q, w_k, w_v, w_o, w1_in, w2_in, grads_in, layer_in, slots, live,
    layer_out, tokens_out, q_out, k_out, v_out, o_out, w1_out, w2_out, small_out,
    qkv, x, att, normed1, low, act, slope, grad, grads, w1, wb, turned, d_qkv, g_2, g_1, g_o, g_qkv, g_small, sums, sums1,
    local, ls, lr, ts, tr, *rest,
):
    place = z, px, py, c = my_place()
    me = py * 2 + c
    length, feat = low.shape
    inner_width = act.shape[1]
    bufs, sems = rest[: 6 * PIECES], rest[6 * PIECES :]
    slots_each = grads.shape[0] // 4

    sources = [(grads_in.at[i], grads.at[pl.ds(i * slots_each, slots_each)]) for i in range(4)]
    sources += [(normed2_in, grad), (act_in, act), (w2_in, wb), (slope_in, slope), (low_in, low), (w1_in, w1)]
    sources += [(normed1_in, normed1), (att_in, att), (qkv_in, qkv), (x_in, x)]
    loads = [pltpu.make_async_copy(src, dst, local.at[i]) for i, (src, dst) in enumerate(sources)]
    for copy in loads:
        copy.start()
    meet(
        [(z ^ j, px, py, c) for j in (1, 2, 3)]
        + [(z, 1 - px, py, c), (z, px, 1 - py, c), (z, px, py, 1 - c), (z, px, 1 - py, 1 - c)]
    )

    def page_copy(src, dst, send, recv, j):
        there = me ^ (j + 1)
        return remote(src.at[there], dst.at[me], send.at[j], recv.at[j], (z, px, there // 2, there % 2))

    layer_copies = [page_copy(layer_in, layer_out, ls, lr, j) for j in range(3)]
    for copy in layer_copies:
        copy.start()
    layer_own = pltpu.make_async_copy(layer_in.at[me], layer_out.at[me], local.at[14])
    layer_own.start()

    def whole(ref):
        def write(total):
            ref[...] = total

        return write

    def thirds(group):
        def write(total):
            for i, ref in enumerate((q_out, k_out, v_out)):
                ref[:, pl.ds(group * TILE, TILE)] = total[:, i * TILE : (i + 1) * TILE]

        return write

    parts = [(ReduceMid, g_2, whole(w2_out)), (ReduceMid, g_1, whole(w1_out)), (Reduce, g_o, whole(o_out))]
    parts += [(Reduce, g_qkv.at[i], thirds(i)) for i in range(GROUPS)]
    parts += [(Reduce, g_small, whole(small_out))]
    sums_2, sum_1, sum_o, *sum_qkv, sum_small = reduces = [
        kind(part, bufs[6 * i : 6 * i + 6], sems[8 * i : 8 * i + 8], place, write)
        for i, (kind, part, write) in enumerate(parts)
    ]

    sums[...] = jnp.zeros_like(sums)
    sums1[...] = jnp.zeros_like(sums1)

    def tally(row, values):
        sums[row : row + 1, :] += jnp.sum(values, axis=0, keepdims=True)

    for copy in loads[:5]:
        copy.wait()
    rows = 128

    def norm_two(i, _):
        block = block_of(i, rows)
        select = (rows_of((grads.shape[0], rows)) == slots[:, block]).astype(BF16)
        grad_layer = dot_rows(select, grads[...])
        normed = grad[block, :]
        tally(6, grad_layer * normed)
        tally(7, grad_layer)
        back = norm_back(grad_layer * bias[6:7, :], normed, factors[block, 128:129])
        grad[block, :] = back
        second_low = back.astype(BF16)
        d_qkv[block, 0:feat] = second_low
        tally(5, second_low.astype(F32))
        return 0

    lax.fori_loop(0, length // rows, norm_two, 0)
    second = grads.at[pl.ds(0, length)]
    second[...] = d_qkv[:, 0:feat]
    loads[5].wait()

    def outer_grad(i, _):
        j = 3 - i
        zi = z ^ j
        width = inner_width // 4
        part = dot_rows(act[:, block_of(zi, width)], second[...])
        g_2[zi] = part.astype(BF16).reshape(g_2.shape[1:])
        sums_2.send(j)
        for k in (1, 2, 3):
            pl.when(i == k)(in_order((sums_2.first, 4 - k)))
        return 0

    lax.fori_loop(0, 4, outer_grad, 0)
    sums_2.first(0)
    for copy in loads[6:9]:
        copy.wait()
    turned[...] = low[...].T
    under_inner = {5: [(sums_2.turn, 3)], 10: [(sums_2.turn, 2)]}

    def inner_grad(i, _):
        block = block_of(i, TILE)
        up = dot_cols(second[...], wb[block, :])
        inner_low = (up * slope[:, block].astype(F32)).astype(BF16)
        slope[:, block] = inner_low
        sums1[0:1, block] = jnp.sum(inner_low.astype(F32), axis=0, keepdims=True)
        part = dot(turned[...], inner_low)
        g_1[:, :, :, :, :, block] = part.astype(BF16).reshape(g_1.shape[:-1] + (TILE,))
        for at, calls in under_inner.items():
            pl.when(i == at)(in_order(*calls))
        return 0

    lax.fori_loop(0, inner_width // TILE, inner_grad, 0)
    sum_1.send_all()
    slabs = [
        pltpu.make_async_copy(src, wb.at[pl.ds(i * feat, feat)], local.at[15 + i])
        for i, src in enumerate((w_o, w_q, w_k, w_v))
    ]
    for copy in slabs:
        copy.start()
    for copy in loads[9:]:
        copy.wait()

    def hidden_grad(i, _):
        half_width = feat // 2
        block = block_of(i, half_width)
        weight = w1[pl.ds(2 * i, 2)].reshape(half_width, inner_width)
        grad[:, block] += dot_cols(slope[...], weight)
        return 0

    lax.fori_loop(0, 2, hidden_grad, 0)
    in_order((sum_1.first, 3), (sum_1.first, 2), (sums_2.turn, 1))()
    first = second

    def norm_one(i, _):
        block = block_of(i, rows)
        up, normed = grad[block, :], normed1[block, :]
        tally(3, up * normed)
        tally(4, up)
        back = norm_back(up * bias[3:4, :], normed, factors[block, 0:1])
        grad[block, :] = back
        first_low = back.astype(BF16)
        first[block, :] = first_low
        tally(2, first_low.astype(F32))
        return 0

    lax.fori_loop(0, length // rows, norm_one, 0)
    in_order((sum_1.first, 1), (sum_1.first, 0))()
    for copy in slabs:
        copy.wait()
    g_o[...] = dot_rows(att[...], first[...]).astype(BF16).reshape(g_o.shape)
    sum_o.send_all()
    grad_att = grads.at[pl.ds(length, length)]

    def att_grad(i, _):
        block = block_of(i, rows)
        grad_att[block, :] = dot_cols(first[block, :], wb[0:feat, :]).astype(BF16)
        return 0

    lax.fori_loop(0, length // rows, att_grad, 0)
    turned[...] = x[...].T
    in_order((sums_2.turn, 0), (sum_o.first,))()
    scale = HEAD_DIM**-0.5

    def pair(p):
        start = pl.multiple_of(p * 128, 128)
        q = qkv[:, pl.ds(start, 128)] * jnp.asarray(scale, BF16)
        k = qkv[:, pl.ds(feat + start, 128)]
        v = qkv[:, pl.ds(2 * feat + start, 128)]
        g = grad_att[:, pl.ds(start, 128)]
        low_lane = lanes(q.shape) < HEAD_DIM
        results = []
        for h in (0, 1):
            keep = low_lane if h == 0 else ~low_lane
            zero = jnp.zeros_like(k)
            scores = jnp.where(live[...] > 0, dot_cols(jnp.where(keep, k, zero), q), NEG_FILL)
            probs = jnp.exp(scores - lse[pl.ds(2 * p + h, 1), :])
            up = dot_cols(jnp.where(keep, v, zero), g)
            inner_sum = jnp.sum(probs * up, axis=0, keepdims=True)
            grad_scores = (probs * (up - inner_sum)).astype(BF16)
            for at, calls in under.items():
                if at % 2 == h:
                    pl.when(p == at // 2)(in_order(*calls))
            results.append((dot_rows(k, grad_scores), dot(grad_scores, q), dot(probs.astype(BF16), g)))
        (q_0, k_0, v_0), (q_1, k_1, v_1) = results
        d_q = jnp.where(rows_of(q_0.shape) < HEAD_DIM, q_0, q_1) * scale
        d_qkv[:, pl.ds(start, 128)] = d_q.T.astype(BF16)
        d_qkv[:, pl.ds(feat + start, 128)] = jnp.where(low_lane, k_0, k_1).astype(BF16)
        d_qkv[:, pl.ds(2 * feat + start, 128)] = jnp.where(low_lane, v_0, v_1).astype(BF16)

    under = {
        2: [(sum_1.turn, 3)],
        4: [(sum_1.turn, 2)],
        5: [(sum_qkv[0].first,)],
        7: [(sum_1.turn, 1)],
        9: [(sums_2.fold,), (sum_qkv[1].first,)],
        10: [(sum_1.turn, 0)],
        11: [(sums_2.last,)],
    }

    def group(i, _):
        def one(j, _):
            pair(2 * i + j)
            return 0

        lax.fori_loop(0, 2, one, 0)
        for t in range(3):
            cols = pl.ds(pl.multiple_of(t * feat + i * TILE, TILE), TILE)
            part = dot(turned[...], d_qkv[:, cols])
            g_qkv[i, :, :, :, :, :, pl.ds(t * TILE, TILE)] = part.astype(BF16).reshape(
                g_qkv.shape[1:-1] + (TILE,)
            )
        for at in range(GROUPS):
            pl.when(i == at)(sum_qkv[at].send_all)
        return 0

    lax.fori_loop(0, GROUPS, group, 0)
    tally(0, d_qkv[:, 0:feat].astype(F32))
    tally(1, d_qkv[:, 2 * feat : 3 * feat].astype(F32))
    g_small[:, :, :, :, 0:8, :] = pack_rows(sums[...], feat // 32, 32).reshape(4, 2, 2, 2, 8, 128)
    for i in range(4):
        part = sums1[:, i * (inner_width // 4) : (i + 1) * (inner_width // 4)]
        g_small[i, :, :, :, 8:16, :] = pack_rows(part, inner_width // 32, 8).reshape(2, 2, 2, 8, 128)
    sum_small.send_all()
    sum_qkv[2].first()

    def token_grad(i, _):
        block = block_of(i, rows)
        total = grad[block, :]
        for t in range(3):
            total += dot_cols(
                d_qkv[block, t * feat : (t + 1) * feat], wb[(t + 1) * feat : (t + 2) * feat, :]
            )
        x[block, :] = total.astype(BF16)
        return 0

    lax.fori_loop(0, length // rows, token_grad, 0)
    grad_tokens = x.reshape(4, length // 4, feat)
    token_copies = [page_copy(grad_tokens, tokens_out, ts, tr, j) for j in range(3)]
    for copy in token_copies:
        copy.start()
    token_own = pltpu.make_async_copy(grad_tokens.at[me], tokens_out.at[me], local.at[19])
    token_own.start()
    thirds_0, thirds_1, thirds_2 = sum_qkv
    in_order(
        (sum_small.first,),
        (sum_o.second,),
        (thirds_0.second,),
        (sum_o.along_z,),
        (thirds_1.second,),
        (thirds_0.along_z,),
        (sum_small.second,),
        (sum_1.fold,),
        (thirds_2.second,),
        (thirds_1.along_z,),
        (sum_small.along_z,),
        (sum_o.last,),
        (thirds_2.along_z,),
        (sum_1.last,),
        (thirds_0.last,),
        (thirds_1.last,),
        (sum_small.last,),
        (thirds_2.last,),
    )()
    for copy in layer_copies + token_copies:
        copy.wait()
    layer_own.wait()
    token_own.wait()
    for one in reduces:
        one.finish()


def backward(saved, weights, grad_pages, layer_slots, slots, live, tokens_shape):
    w_q, w_1, w_2 = weights[0], weights[4], weights[5]
    qkv, lse, x, att, normed1, low, act, slope, normed2, factors, bias = saved
    length, feat = low.shape
    inner_width = act.shape[1]
    anywhere = pl.BlockSpec(memory_space=pl.ANY)
    vmem = pl.BlockSpec(memory_space=pltpu.VMEM)
    grid = (4, 2, 2, 2)
    small, inner, outer = (feat // 32, feat), (feat // 32, inner_width), (inner_width // 32, feat)
    sizes = [outer, inner] + [small] * 4 + [(16, 128)]
    scratch = [
        ((length, 3 * feat), BF16),
        ((length, feat), BF16),
        ((length, feat), BF16),
        ((length, feat), F32),
        ((length, feat), BF16),
        ((length, inner_width), BF16),
        ((length, inner_width), BF16),
        ((length, feat), F32),
        ((grad_pages.shape[0] * grad_pages.shape[1], feat), BF16),
        (grid + inner, BF16),
        ((inner_width, feat), BF16),
        ((feat, length), BF16),
        ((length, 3 * feat), BF16),
        (grid + outer, BF16),
        (grid + inner, BF16),
        (grid + small, BF16),
        ((GROUPS,) + grid + small, BF16),
        (grid + (16, 128), BF16),
        ((8, feat), F32),
        ((8, inner_width), F32),
    ]
    bufs, sems = [], []
    for i, size in enumerate(sizes):
        bufs += reduce_mid_bufs(*size) if i < 2 else reduce_bufs(*size)
        sems += reduce_mid_sems() if i < 2 else reduce_sems()
    outs = [(grad_pages.shape, BF16, anywhere), (tokens_shape, BF16, anywhere)]
    outs += [(small, F32, vmem)] * 4 + [(inner, F32, vmem), (outer, F32, vmem), ((16, 128), F32, vmem)]
    return pl.pallas_call(
        backward_kernel,
        out_shape=[jax.ShapeDtypeStruct(shape, kind) for shape, kind, _ in outs],
        in_specs=[anywhere, vmem] + [anywhere] * 7 + [vmem, vmem] + [anywhere] * 8 + [vmem, vmem],
        out_specs=[spec for _, _, spec in outs],
        scratch_shapes=[pltpu.VMEM(shape, kind) for shape, kind in scratch]
        + [DMA((20,)), DMA((3,)), DMA((3,)), DMA((3,)), DMA((3,))]
        + bufs
        + sems,
        compiler_params=pltpu.CompilerParams(
            collective_id=1, has_side_effects=True, vmem_limit_bytes=VMEM_LIMIT
        ),
        name="backward",
    )(*saved, *weights, grad_pages, layer_slots, slots, live)


def small_shard(weights):
    rows = []
    for i in SMALL_ORDER:
        rows += [weights[i], jnp.zeros((128 - weights[i].shape[0],), BF16)]
    rows.append(jnp.zeros((128 * (16 - len(SMALL_ORDER)),), BF16))
    return jnp.concatenate(rows).reshape(16, 128)


SMALL_ORDER = (1, 4, 6, 7, 8, 12, 13, 14, 10)


def finish_kernel(count, *refs):
    ins, outs, stages, sems = refs[:count], refs[count : 2 * count], refs[2 * count : 3 * count], refs[3 * count]
    inward = [pltpu.make_async_copy(i, s, sems.at[0, n]) for n, (i, s) in enumerate(zip(ins, stages))]
    outward = [pltpu.make_async_copy(s, o, sems.at[1, n]) for n, (s, o) in enumerate(zip(stages, outs))]
    for copy in inward:
        copy.start()
    for first, second in zip(inward, outward):
        first.wait()
        second.start()
    for copy in outward:
        copy.wait()


def finish(arrays):
    count = len(arrays)
    anywhere = pl.BlockSpec(memory_space=pl.ANY)

    def body(*refs):
        finish_kernel(count, *refs)

    return pl.pallas_call(
        body,
        out_shape=[jax.ShapeDtypeStruct(a.shape, a.dtype) for a in arrays],
        in_specs=[anywhere] * count,
        out_specs=[anywhere] * count,
        scratch_shapes=[pltpu.VMEM(a.shape, a.dtype) for a in arrays] + [DMA((2, count))],
        compiler_params=pltpu.CompilerParams(vmem_limit_bytes=VMEM_LIMIT),
        name="finish",
    )(*arrays)


def by_kernels(tokens, band_ids, page_mask, weights, grad_output):
    large = [weights[i] for i in (0, 2, 3, 5, 9, 11)]
    got = forward(tokens, grad_output, band_ids, page_mask, *large, small_shard(weights))
    saved, full, (grad_slots, layer_slots, slots, live) = got[:11], got[11:17], got[17:]
    full = [w if i == 4 else w.reshape(-1, w.shape[-1]) for i, w in enumerate(full)]
    sums = backward(saved, full, grad_slots, layer_slots, slots, live, tokens.shape)
    grads = [None] * len(weights)
    for row, i in enumerate(SMALL_ORDER):
        grads[i] = sums[8][row, : weights[i].shape[0]]
    sums = finish(sums[:8])
    for i, total in zip((0, 2, 3, 5, 9, 11), sums[2:]):
        grads[i] = total
    return tuple(sums[:2]) + tuple(grads)


def per_device(hand_made, *args):
    tokens, band_ids, band_counts, page_mask = args[:4]
    weights, grad_output = args[4:19], args[19]
    if hand_made:
        return by_kernels(tokens, band_ids, page_mask, weights, grad_output)
    bands = lax.axis_size("band")
    slot_cap = grad_output.shape[1]
    pages = tokens.shape[0] // bands
    full = [lax.all_gather(w, BOTH, axis=0, tiled=True) for w in weights]
    first = lax.axis_index("band") * pages
    ids = lax.dynamic_slice_in_dim(band_ids, first, pages, 0)
    live = lax.dynamic_slice_in_dim(page_mask, first, pages, 0) > 0
    slots = page_slots(ids, bands, slot_cap)
    layer_slots, grad_in, grads = layer_pages(
        to_pages(tokens), slots, live, to_pages(grad_output), full
    )
    return (from_pages(layer_slots), from_pages(grad_in)) + tuple(
        lax.psum_scatter(g, BOTH, scatter_dimension=0, tiled=True) for g in grads
    )


def solution(mesh):
    hand_made = dict(mesh.shape) == {"page": 8, "band": 4}
    shard = P(BOTH)
    rows = P(BOTH, None)
    tokens = P("page", "band", None)
    page = P("page", None)
    weights = (rows, shard, rows, rows, shard, rows, shard, shard, shard)
    weights = weights + (rows, shard, rows, shard, shard, shard)

    def step(*args):
        return per_device(hand_made, *args)

    return jax.shard_map(
        step,
        mesh=mesh,
        in_specs=(tokens, page, page, page) + weights + (tokens,),
        out_specs=(tokens, tokens) + weights,
        check_vma=False,
    )
```

```python
import jax
import jax.numpy as jnp
from jax import lax
from jax.experimental import pallas as pl
from jax.experimental.pallas import tpu as pltpu
from jax.sharding import PartitionSpec as P

HEAD_DIM = 64
LN_EPS = 1e-12
NEG_FILL = -1e30
MESH = pl.DeviceIdType.MESH
DMA = pltpu.SemaphoreType.DMA
F32 = jnp.float32
BF16 = jnp.bfloat16
BOTH = ("page", "band")
VMEM_LIMIT = 62 * 2**20


def my_place():
    page, band = lax.axis_index("page"), lax.axis_index("band")
    return page // 2, page % 2, band // 2, band % 2


def dev(z, x, y, c):
    return (z * 2 + x, y * 2 + c)


def remote(src, dst, send_sem, recv_sem, place):
    return pltpu.make_async_remote_copy(
        src_ref=src,
        dst_ref=dst,
        send_sem=send_sem,
        recv_sem=recv_sem,
        device_id=dev(*place),
        device_id_type=MESH,
    )


def meet(places):
    barrier = pltpu.get_barrier_semaphore()
    for place in places:
        pl.semaphore_signal(barrier, inc=1, device_id=dev(*place), device_id_type=MESH)
    pl.semaphore_wait(barrier, len(places))


def grid_peers(z, x, y, c):
    return [((z + j) % 4, x, y, c) for j in (1, 2, 3)] + [
        (z, 1 - x, y, c),
        (z, x, 1 - y, c),
        (z, x, y, 1 - c),
    ]


def half(ref, which):
    rows, width = ref.shape[-2] // 2, ref.shape[-1] // 2
    if width % 128:
        return ref.at[..., pl.ds(which * rows, rows), :]
    return ref.at[..., pl.ds(which * width, width)]


def norm_rows(values):
    center = values - jnp.mean(values, axis=-1, keepdims=True)
    factor = lax.rsqrt(jnp.mean(center * center, axis=-1, keepdims=True) + LN_EPS)
    return (center * factor, factor)


def norm_back(upstream, normed, factor):
    return factor * (
        upstream
        - jnp.mean(upstream, axis=-1, keepdims=True)
        - normed * jnp.mean(upstream * normed, axis=-1, keepdims=True)
    )


def dot(first, second):
    return jnp.dot(first, second, preferred_element_type=F32)


def dot_rows(first, second):
    return lax.dot_general(first, second, (((0,), (0,)), ((), ())), preferred_element_type=F32)


def dot_cols(first, second):
    return lax.dot_general(first, second, (((1,), (1,)), ((), ())), preferred_element_type=F32)


def page_slots(ids, bands, slot_cap):
    onehot = (ids[:, :, None] == jnp.arange(bands, dtype=jnp.int32)).astype(F32)
    length = ids.shape[1]
    before = (jnp.arange(length)[:, None] > jnp.arange(length)[None, :]).astype(F32)
    counts = jnp.einsum("tu,pub->ptb", before, onehot, preferred_element_type=F32)
    rank = jnp.sum(onehot * counts, axis=2).astype(jnp.int32)
    return ids * slot_cap + rank


def layer_pages(rows_in, slots, live, grad_slots, weights):
    (wq, bq, wk, wv, bv, wo, bo, g1, s1, w1, b1, w2, b2, g2, s2) = weights
    pages, length, feat = rows_in.shape
    heads = feat // HEAD_DIM
    scale = HEAD_DIM**-0.5
    x_low = rows_in.reshape(-1, feat)
    select = (slots[:, None, :] == jnp.arange(grad_slots.shape[1])[None, :, None]).astype(BF16)
    grad_layer = jnp.einsum("pst,psd->ptd", select, grad_slots, preferred_element_type=F32)
    grad_layer = grad_layer.reshape(-1, feat)

    def split(flat):
        return flat.reshape(pages, length, heads, HEAD_DIM)

    query = split((dot(x_low, wq) + bq).astype(BF16))
    key = split(dot(x_low, wk).astype(BF16))
    value = split((dot(x_low, wv) + bv).astype(BF16))
    scores = jnp.einsum("pthd,puhd->phtu", query, key, preferred_element_type=F32) * scale
    scores = jnp.where(live[:, None, None, :], scores, NEG_FILL)
    shifted = jnp.exp(scores - jnp.max(scores, axis=-1, keepdims=True))
    probs = shifted / jnp.sum(shifted, axis=-1, keepdims=True)
    probs_low = probs.astype(BF16)
    mixed = jnp.einsum("phtu,puhd->pthd", probs_low, value, preferred_element_type=F32)
    attended = mixed.astype(BF16).reshape(-1, feat)
    normed_one, factor_one = norm_rows(x_low.astype(F32) + dot(attended, wo) + bo)
    hidden = normed_one * g1 + s1
    hidden_low = hidden.astype(BF16)
    inner = dot(hidden_low, w1) + b1
    cdf = 0.5 * (1.0 + lax.erf(inner * (0.5**0.5)))
    act_low = (inner * cdf).astype(BF16)
    slope = cdf + inner * jnp.exp(-0.5 * inner * inner) * ((0.5 / jnp.pi) ** 0.5)
    normed_two, factor_two = norm_rows(hidden + dot(act_low, w2) + b2)
    layer = (normed_two * g2 + s2).astype(BF16).reshape(pages, length, feat)
    layer_slots = jnp.einsum("pst,ptd->psd", select, layer, preferred_element_type=F32).astype(BF16)

    grad_g2 = jnp.sum(grad_layer * normed_two, axis=0)
    grad_s2 = jnp.sum(grad_layer, axis=0)
    grad_second = norm_back(grad_layer * g2, normed_two, factor_two)
    second_low = grad_second.astype(BF16)
    grad_w2 = dot_rows(act_low, second_low)
    grad_b2 = jnp.sum(second_low.astype(F32), axis=0)
    inner_low = (dot_cols(second_low, w2) * slope).astype(BF16)
    grad_w1 = dot_rows(hidden_low, inner_low)
    grad_b1 = jnp.sum(inner_low.astype(F32), axis=0)
    grad_hidden = grad_second + dot_cols(inner_low, w1)
    grad_g1 = jnp.sum(grad_hidden * normed_one, axis=0)
    grad_s1 = jnp.sum(grad_hidden, axis=0)
    grad_first = norm_back(grad_hidden * g1, normed_one, factor_one)
    first_low = grad_first.astype(BF16)
    grad_wo = dot_rows(attended, first_low)
    grad_bo = jnp.sum(first_low.astype(F32), axis=0)
    grad_att = split(dot_cols(first_low, wo).astype(BF16))
    grad_probs = jnp.einsum("pthd,puhd->phtu", grad_att, value, preferred_element_type=F32)
    inner_sum = jnp.sum(probs * grad_probs, axis=-1, keepdims=True)
    grad_scores = (probs * (grad_probs - inner_sum)).astype(BF16)

    def flat(per_head, factor):
        return (per_head * factor).astype(BF16).reshape(-1, feat)

    ein = lambda form, a, b: jnp.einsum(form, a, b, preferred_element_type=F32)
    grad_q = flat(ein("phtu,puhd->pthd", grad_scores, key), scale)
    grad_k = flat(ein("phtu,pthd->puhd", grad_scores, query), scale)
    grad_v = flat(ein("phtu,pthd->puhd", probs_low, grad_att), 1.0)
    grad_wq, grad_wk, grad_wv = (dot_rows(x_low, g) for g in (grad_q, grad_k, grad_v))
    grad_bq = jnp.sum(grad_q.astype(F32), axis=0)
    grad_bv = jnp.sum(grad_v.astype(F32), axis=0)
    grad_in = grad_first + dot_cols(grad_q, wq) + dot_cols(grad_k, wk) + dot_cols(grad_v, wv)
    grad_in = grad_in.astype(BF16).reshape(pages, length, feat)
    return (
        layer_slots,
        grad_in,
        (grad_wq, grad_bq, grad_wk, grad_wv, grad_bv, grad_wo, grad_bo, grad_g1, grad_s1)
        + (grad_w1, grad_b1, grad_w2, grad_b2, grad_g2, grad_s2),
    )


def to_pages(blocks):
    return lax.all_to_all(blocks, "band", split_axis=0, concat_axis=1, tiled=True)


def from_pages(blocks):
    return lax.all_to_all(blocks, "band", split_axis=1, concat_axis=0, tiled=True)


def split_ref(ref, which):
    rows, width = ref.shape[-2:]
    cut = width // 6
    if cut % 128:
        return ref.at[..., pl.ds(which * (rows // 2), rows // 2), :]
    return ref.at[..., pl.ds(which * cut, (cut, width - cut)[which])]


def split_shape(shape, which):
    rows, width = shape[-2:]
    cut = width // 6
    if cut % 128:
        return shape[:-2] + (rows // 2, width)
    return shape[:-1] + ((cut, width - cut)[which],)


def in_order(*calls):
    def step():
        for method, *index in calls:
            method(*index)

    return step


class Gather:
    def __init__(self, own, buf, sems, place):
        self.own, self.buf, self.place = own, buf, place
        self.zs, self.zr, self.ss, self.sr, self.fs, self.fr, self.cs, self.cr = sems

    def z_copy(self, j):
        z, x, y, c = self.place
        there = (z ^ (j + 1), x, y, c)
        return remote(self.own, self.buf.at[z, x, y, c], self.zs.at[j], self.zr.at[j], there)

    def side_copy(self, j, axis):
        z, x, y, c = self.place
        part = self.buf.at[z ^ j, x, y, c]
        there = (z, 1 - x, y, c) if axis == 0 else (z, x, 1 - y, c)
        source = self.own if j == 0 else part
        return remote(source, part, self.ss.at[axis, j], self.sr.at[axis, j], there)

    def far_copy(self, j, axis):
        z, x, y, c = self.place
        if axis == 0:
            part, there = self.buf.at[z ^ j, 1 - x, y, c], (z, x, 1 - y, c)
        else:
            part, there = self.buf.at[z ^ j, x, 1 - y, c], (z, 1 - x, y, c)
        part = split_ref(part, axis)
        return remote(part, part, self.fs.at[axis, j], self.fr.at[axis, j], there)

    def core_copy(self, k):
        z, x, y, c = self.place
        part = self.buf.at[:, (x, 1 - x, x, 1 - x)[k], (y, y, 1 - y, 1 - y)[k], c]
        return remote(part, part, self.cs.at[k], self.cr.at[k], (z, x, y, 1 - c))

    def start(self):
        for j in range(3):
            self.z_copy(j).start()
        for axis in (0, 1):
            self.side_copy(0, axis).start()

    def side(self, j):
        self.z_copy(j - 1).wait_recv()
        for axis in (0, 1):
            self.side_copy(j, axis).start()

    def far(self, j):
        for axis in (0, 1):
            self.side_copy(j, axis).wait_recv()
            self.far_copy(j, axis).start()

    def core(self, k):
        if k == 3:
            for j in range(4):
                for axis in (0, 1):
                    self.far_copy(j, axis).wait_recv()
        self.core_copy(k).start()

    def steps(self):
        side, far, core = self.side, self.far, self.core
        return [
            in_order((side, 1)),
            in_order((far, 0)),
            in_order((side, 2)),
            in_order((side, 3), (core, 0)),
            in_order((far, 1)),
            in_order((far, 2)),
            in_order((far, 3), (core, 1), (core, 2)),
            in_order((core, 3)),
        ]

    def arrive(self):
        for k in range(4):
            self.core_copy(k).wait_recv()

    def finish(self):
        for j in range(3):
            self.z_copy(j).wait_send()
        for j in range(4):
            for axis in (0, 1):
                self.side_copy(j, axis).wait_send()
                self.far_copy(j, axis).wait_send()
            self.core_copy(j).wait_send()


def gather_sems():
    return [DMA((3,)), DMA((3,))] + [DMA((2, 4))] * 4 + [DMA((4,))] * 2


def split_mid(ref, which):
    width = ref.shape[-1]
    cut = width // 384 * 128
    return ref.at[..., pl.ds(which * cut, (cut, width - cut)[which])]


class GatherMid:
    def __init__(self, own, buf, sems, place):
        self.own, self.buf, self.place = own, buf, place
        self.zs, self.zr, self.ss, self.sr, self.hs, self.hr, self.fs, self.fr, self.cs, self.cr = sems

    def z_copy(self, j):
        z, x, y, c = self.place
        there = (z ^ j, x, y, c)
        return remote(self.own, self.buf.at[z, x, y, c], self.zs.at[j - 1], self.zr.at[j - 1], there)

    def side_copy(self, axis):
        z, x, y, c = self.place
        there = (z, 1 - x, y, c) if axis == 0 else (z, x, 1 - y, c)
        source = split_mid(self.own, axis)
        return remote(source, split_mid(self.buf.at[z, x, y, c], axis), self.ss.at[axis], self.sr.at[axis], there)

    def half_copy(self, j, axis):
        z, x, y, c = self.place
        part = self.buf.at[z, 1 - x, y, c] if axis == 0 else self.buf.at[z, x, 1 - y, c]
        part = split_mid(part, axis)
        return remote(part, part, self.hs.at[axis, j - 1], self.hr.at[axis, j - 1], (z ^ j, x, y, c))

    def far_copy(self, j, axis):
        z, x, y, c = self.place
        if axis == 0:
            part, there = self.buf.at[z ^ j, :, y, c], (z, x, 1 - y, c)
        else:
            part, there = self.buf.at[z ^ j, x, :, c], (z, 1 - x, y, c)
        part = split_mid(part, axis)
        return remote(part, part, self.fs.at[axis, j], self.fr.at[axis, j], there)

    def core_copy(self, k):
        z, x, y, c = self.place
        part = self.buf.at[:, (x, 1 - x, x, 1 - x)[k], (y, y, 1 - y, 1 - y)[k], c]
        return remote(part, part, self.cs.at[k], self.cr.at[k], (z, x, y, 1 - c))

    def start(self):
        for axis in (0, 1):
            self.side_copy(axis).start()
        for j in (1, 2, 3):
            self.z_copy(j).start()

    def turn(self):
        for axis in (0, 1):
            self.side_copy(axis).wait_recv()
            for j in (1, 2, 3):
                self.half_copy(j, axis).start()
        for axis in (0, 1):
            self.far_copy(0, axis).start()

    def far(self, j):
        self.z_copy(j).wait_recv()
        for axis in (0, 1):
            self.half_copy(j, axis).wait_recv()
            self.far_copy(j, axis).start()

    def core(self, k):
        if k:
            for j in range(4):
                for axis in (0, 1):
                    self.far_copy(j, axis).wait_recv()
            for k in (1, 2, 3):
                self.core_copy(k).start()
        else:
            self.core_copy(0).start()

    def steps(self):
        far, core = self.far, self.core
        return [
            in_order((self.turn,)),
            in_order((far, 1)),
            in_order((far, 2)),
            in_order((far, 3), (core, 0)),
            in_order((core, 1)),
        ]

    def arrive(self):
        for k in range(4):
            self.core_copy(k).wait_recv()

    def finish(self):
        for axis in (0, 1):
            self.side_copy(axis).wait_send()
        for j in (1, 2, 3):
            self.z_copy(j).wait_send()
            for axis in (0, 1):
                self.half_copy(j, axis).wait_send()
        for j in range(4):
            for axis in (0, 1):
                self.far_copy(j, axis).wait_send()
            self.core_copy(j).wait_send()


def mid_sems():
    return [DMA((3,))] * 2 + [DMA((2,))] * 2 + [DMA((2, 3))] * 2 + [DMA((2, 4))] * 2 + [DMA((4,))] * 2


def lanes(shape):
    return lax.broadcasted_iota(jnp.int32, shape, len(shape) - 1)


def rows_of(shape):
    return lax.broadcasted_iota(jnp.int32, shape, len(shape) - 2)


def columns(buf, start, width):
    return buf[:, :, :, :, :, pl.ds(start, width)].reshape(-1, width)


def unpack_rows(block, per_shard, width):
    shards, count, _ = block.shape
    spread = (rows_of((128, width)) == lanes((128, width)) % per_shard).astype(BF16)
    wide = dot(block.reshape(-1, 128), spread).reshape(shards, count, width)
    owner = lax.broadcasted_iota(jnp.int32, wide.shape, 0) == lanes(wide.shape) // per_shard
    return jnp.sum(jnp.where(owner, wide, 0.0), axis=0)


def pack_rows(rows, per_shard, shards):
    count, width = rows.shape
    wide = jnp.broadcast_to(rows[None], (shards, count, width))
    owner = lax.broadcasted_iota(jnp.int32, wide.shape, 0) == lanes(wide.shape) // per_shard
    wide = jnp.where(owner, wide, 0.0).astype(BF16).reshape(-1, width)
    spread = (lanes((width, 128)) == rows_of((width, 128)) % per_shard).astype(BF16)
    return dot(wide, spread).astype(BF16).reshape(shards, count, 128)


def block_of(i, size):
    return pl.ds(pl.multiple_of(i * size, size), size)


def gelu_parts(v):
    cdf = 0.5 * (1.0 + lax.erf(v * (0.5**0.5)))
    return v * cdf, cdf + v * jnp.exp(-0.5 * v * v) * ((0.5 / jnp.pi) ** 0.5)


class Out:
    def __init__(self, sems):
        self.sems, self.copies = sems, []

    def send(self, src, dst):
        copy = pltpu.make_async_copy(src, dst, self.sems.at[len(self.copies)])
        copy.start()
        self.copies.append(copy)

    def wait(self):
        for copy in self.copies:
            copy.wait()


BIAS_ROWS = 8
TILE = 256


def forward_kernel(*refs):
    vector_refs, refs = refs[: BIAS_ROWS + 1], refs[BIAS_ROWS + 1 :]
    tokens, grads, ids, mask, w_q, w_k, w_v, w_o, w_1, w_2 = refs[:10]
    qkv_out, lse, x_out, att_out, normed1_out, low_out, act_out, slope_out, normed2_out = refs[10:19]
    factors, bias, q_out, k_out, v_out, o_out, w1_out, w2_out, grad_pages, layer_slots, slots, live = refs[19:31]
    small, small_own, a_buf, w1_buf, w2_buf, x_buf, qkv, att, normed1, low, act, slope = refs[31:43]
    second, normed2, layer, bias1, local, ts, tr, gs, gr, outs, *sems = refs[43:]
    place = z, x, y, c = my_place()
    me = y * 2 + c
    length, feat = low.shape
    pairs = feat // 128
    x_rows = x_buf.reshape(length, feat)
    here = (z, x, y, c)
    copies = [
        pltpu.make_async_copy(src, dst, local.at[i])
        for i, (src, dst) in enumerate(
            [(w, a_buf.at[here + (slice(None), pl.ds(i * feat, feat))]) for i, w in enumerate((w_q, w_k, w_v, w_o))]
            + [(w_1, w1_buf.at[here]), (w_2, w2_buf.at[here])]
            + [(tokens.at[me], x_buf.at[me]), (grads.at[me], grad_pages.at[me])]
        )
    ]
    for copy in copies:
        copy.start()
    small_own[...] = jnp.zeros_like(small_own)
    for row, ref in enumerate(vector_refs):
        size = ref.shape[0]
        small_own[row : row + 1, 0:size] = ref[...].astype(F32).reshape(1, size)
    small[here] = small_own[...].astype(BF16)
    meet(
        [(z ^ j, x, y, c) for j in (1, 2, 3)]
        + [(z, 1 - x, y, c), (z, x, 1 - y, c), (z, x, y, 1 - c), (z, x, 1 - y, 1 - c)]
    )

    def page_copy(src, dst, send, recv, j):
        there = me ^ (j + 1)
        return remote(src.at[there], dst.at[me], send.at[j], recv.at[j], (z, x, there // 2, there % 2))

    token_copies = [page_copy(tokens, x_buf, ts, tr, j) for j in range(3)]
    grad_copies = [page_copy(grads, grad_pages, gs, gr, j) for j in range(3)]
    gathers = [
        kind(own, buf, sems[8 * i :][: 8 if kind is Gather else 10], place)
        for i, (kind, own, buf) in enumerate(
            [(Gather, small.at[here], small), (Gather, a_buf.at[here], a_buf)]
            + [(Gather, w_1, w1_buf), (GatherMid, w_2, w2_buf)]
        )
    ]
    vectors, atts, inner, outer = gathers
    for copy in copies[:4]:
        copy.wait()
    atts.start()
    vectors.start()
    for copy in token_copies:
        copy.start()
    inner.start()
    outer.start()
    slot_cap = grads.shape[1]
    hot = (rows_of((8, length)) == ids[pl.ds(me, 1), :]).astype(F32)
    earlier = (rows_of((length, length)) < lanes((length, length))).astype(BF16)
    rank = dot(hot.astype(BF16), earlier) + (rows_of((8, length)) * slot_cap).astype(F32)
    slots[...] = jnp.sum(hot * rank, axis=0, keepdims=True).astype(jnp.int32)
    live[...] = jnp.broadcast_to(mask[pl.ds(me, 1), :].astype(F32), (8, length)).T[:, 0:1]
    steps_0, steps_1, steps_2 = atts.steps(), inner.steps(), outer.steps()
    behind = {3: [steps_1[0]], 4: [steps_1[1]], 5: [steps_1[2], steps_2[0]], 6: [steps_1[3]]}
    for i, (main, extra) in enumerate(zip(steps_0, vectors.steps())):
        main()
        extra()
        if i == 3:
            for copy in copies[4:6]:
                copy.wait()
        for step in behind.get(i, ()):
            step()
    for copy in copies[6:]:
        copy.wait()
    for copy in grad_copies:
        copy.start()
    vectors.arrive()
    shards = small[...].reshape(32, 16, 128)
    bias[...] = unpack_rows(shards[:, :8], feat // 32, feat)
    inner_width = act.shape[1]
    for i in range(4):
        part = unpack_rows(small[i].reshape(8, 16, 128)[:, 8:], inner_width // 32, inner_width // 4)
        bias1[:, i * (inner_width // 4) : (i + 1) * (inner_width // 4)] = part
    for copy in token_copies:
        copy.wait_recv()
    atts.arrive()
    out = Out(outs)
    for i, ref in enumerate((q_out, k_out, v_out, o_out)):
        out.send(a_buf.at[:, :, :, :, :, pl.ds(i * feat, feat)], ref)
    out.send(x_rows, x_out)
    steps_1[4]()

    def project(j, _):
        start = pl.multiple_of(j * TILE, TILE)
        total = dot(x_rows[...], columns(a_buf, start, TILE))
        which = j // (feat // TILE)
        inside = block_of(j % (feat // TILE), TILE)
        row = jnp.where(which == 0, bias[0:1, inside], jnp.where(which == 2, bias[1:2, inside], 0.0))
        qkv[:, pl.ds(start, TILE)] = (total + row).astype(BF16)
        return 0

    lax.fori_loop(0, 3 * feat // TILE, project, 0)
    out.send(qkv, qkv_out)
    steps_1[5]()
    under = {0: steps_1[6], 2: steps_1[7], 3: steps_2[1], 6: steps_2[2], 9: steps_2[3]}
    scale = HEAD_DIM**-0.5

    def pair(p, _):
        start = pl.multiple_of(p * 128, 128)
        q = qkv[:, pl.ds(start, 128)] * jnp.asarray(scale, BF16)
        k = qkv[:, pl.ds(feat + start, 128)]
        v = qkv[:, pl.ds(2 * feat + start, 128)]
        low_lane = lanes(q.shape) < HEAD_DIM
        mixed = []
        for h in (0, 1):
            part = jnp.where(low_lane if h == 0 else ~low_lane, k, jnp.zeros_like(k))
            scores = jnp.where(live[...] > 0, dot_cols(part, q), NEG_FILL)
            top = jnp.max(scores, axis=0, keepdims=True)
            shifted = jnp.exp(scores - top)
            total = jnp.sum(shifted, axis=0, keepdims=True)
            probs = (shifted * (1.0 / total)).astype(BF16)
            mixed.append(dot_rows(v, probs))
            lse[pl.ds(2 * p + h, 1), :] = top + jnp.log(total)
            for at, step in under.items():
                if at % 2 == h:
                    pl.when(p == at // 2)(step)
        both = jnp.where(rows_of(mixed[0].shape) < HEAD_DIM, mixed[0], mixed[1])
        att[:, pl.ds(start, 128)] = both.T.astype(BF16)
        return 0

    lax.fori_loop(0, pairs, pair, 0)
    out.send(att, att_out)
    rows = 128

    def norm_one(i, _):
        block = block_of(i, rows)
        total = dot(att[block, :], columns(a_buf, 3 * feat, feat))
        total = total + x_rows[block, :].astype(F32) + bias[2:3, :]
        normed, factor = norm_rows(total)
        normed1[block, :] = normed
        factors[block, 0:128] = jnp.broadcast_to(factor, (rows, 128))
        low[block, :] = (normed * bias[3:4, :] + bias[4:5, :]).astype(BF16)
        return 0

    lax.fori_loop(0, length // rows, norm_one, 0)
    out.send(normed1, normed1_out)
    out.send(low, low_out)
    inner.arrive()
    out.send(w1_buf, w1_out)

    def ffn_in(j, _):
        block = block_of(j, TILE)
        value, grad = gelu_parts(dot(low[...], columns(w1_buf, block.start, TILE)) + bias1[0:1, block])
        act[:, block] = value.astype(BF16)
        slope[:, block] = grad.astype(BF16)
        return 0

    lax.fori_loop(0, inner_width // TILE, ffn_in, 0)
    out.send(act, act_out)
    out.send(slope, slope_out)
    steps_2[4]()
    outer.arrive()
    out.send(w2_buf, w2_out)

    def ffn_out(j, _):
        block = block_of(j, TILE)
        second[:, block] = dot(act[...], columns(w2_buf, block.start, TILE))
        return 0

    lax.fori_loop(0, feat // TILE, ffn_out, 0)

    def norm_two(i, _):
        block = block_of(i, rows)
        hidden = normed1[block, :] * bias[3:4, :] + bias[4:5, :]
        normed, factor = norm_rows(hidden + second[block, :] + bias[5:6, :])
        normed2[block, :] = normed
        factors[block, 128:256] = jnp.broadcast_to(factor, (rows, 128))
        layer[block, :] = (normed * bias[6:7, :] + bias[7:8, :]).astype(BF16)
        return 0

    lax.fori_loop(0, length // rows, norm_two, 0)
    out.send(normed2, normed2_out)

    def place_rows(i, _):
        cap = layer_slots.shape[1]
        here_rows = rows_of((cap, length)) + i * cap
        select = (here_rows == slots[...]).astype(BF16)
        layer_slots[i] = dot(select, layer[...]).astype(BF16)
        return 0

    lax.fori_loop(0, layer_slots.shape[0], place_rows, 0)
    for copy in grad_copies:
        copy.wait_recv()
    for copy in grad_copies + token_copies:
        copy.wait_send()
    for one in gathers:
        one.finish()
    out.wait()


def forward(vectors, tokens, grads, ids, mask, w_q, w_k, w_v, w_o, w_1, w_2):
    length, feat, inner_width = ids.shape[1], tokens.shape[-1], w_1.shape[1]
    anywhere = pl.BlockSpec(memory_space=pl.ANY)
    vmem = pl.BlockSpec(memory_space=pltpu.VMEM)
    grid = (4, 2, 2, 2)
    heads = feat // HEAD_DIM
    results = [
        ((length, 3 * feat), BF16, anywhere),
        ((heads + -heads % 8, length), F32, vmem),
        ((length, feat), BF16, anywhere),
        ((length, feat), BF16, anywhere),
        ((length, feat), F32, anywhere),
        ((length, feat), BF16, anywhere),
        ((length, inner_width), BF16, anywhere),
        ((length, inner_width), BF16, anywhere),
        ((length, feat), F32, anywhere),
        ((length, 256), F32, vmem),
        ((BIAS_ROWS, feat), F32, vmem),
    ]
    small = (16, 128)
    results += [(grid + w_q.shape, BF16, anywhere)] * 4
    results += [(grid + w_1.shape, BF16, anywhere), (grid + w_2.shape, BF16, anywhere)]
    results += [(grads.shape, BF16, anywhere), (grads.shape, BF16, vmem)]
    results += [((1, length), jnp.int32, vmem), ((length, 1), F32, vmem)]
    return pl.pallas_call(
        forward_kernel,
        out_shape=[jax.ShapeDtypeStruct(shape, kind) for shape, kind, _ in results],
        in_specs=[vmem] * len(vectors) + [anywhere, anywhere, vmem, vmem] + [anywhere] * 6,
        out_specs=[spec for _, _, spec in results],
        scratch_shapes=[
            pltpu.VMEM(grid + small, BF16),
            pltpu.VMEM(small, F32),
            pltpu.VMEM(grid + (w_q.shape[0], 4 * feat), BF16),
            pltpu.VMEM(grid + w_1.shape, BF16),
            pltpu.VMEM(grid + w_2.shape, BF16),
            pltpu.VMEM(tokens.shape, BF16),
            pltpu.VMEM((length, 3 * feat), BF16),
            pltpu.VMEM((length, feat), BF16),
            pltpu.VMEM((length, feat), F32),
            pltpu.VMEM((length, feat), BF16),
            pltpu.VMEM((length, inner_width), BF16),
            pltpu.VMEM((length, inner_width), BF16),
            pltpu.VMEM((length, feat), F32),
            pltpu.VMEM((length, feat), F32),
            pltpu.VMEM((length, feat), BF16),
            pltpu.VMEM((8, inner_width), F32),
            DMA((8,)),
            DMA((3,)),
            DMA((3,)),
            DMA((3,)),
            DMA((3,)),
            DMA((14,)),
        ]
        + gather_sems() * 3
        + mid_sems(),
        compiler_params=pltpu.CompilerParams(
            collective_id=0, has_side_effects=True, vmem_limit_bytes=VMEM_LIMIT
        ),
        name="forward",
    )(*vectors, tokens, grads, ids, mask, w_q, w_k, w_v, w_o, w_1, w_2)


def add_into(dst, src, lead):
    def step(flat, _):
        index = []
        for size in reversed(lead):
            index.append(flat % size)
            flat = flat // size
        index = tuple(reversed(index))
        dst[index] = (dst[index].astype(F32) + src[index].astype(F32)).astype(BF16)
        return 0

    total = 1
    for size in lead:
        total *= size
    lax.fori_loop(0, total, step, 0)


class Reduce:
    def __init__(self, part, bufs, sems, place, write):
        self.part, self.place, self.write = part, place, write
        self.got_core, self.got_plane, self.got_z = bufs
        self.cs, self.cr, self.ps, self.pr, self.zs, self.zr = sems

    def core_copy(self):
        z, x, y, c = self.place
        there = (z, x, y, 1 - c)
        return remote(self.part.at[:, :, :, 1 - c], self.got_core, self.cs.at[0], self.cr.at[0], there)

    def plane_copy(self, j):
        z, x, y, c = self.place
        px, py = x ^ (j // 2), y ^ (j % 2)
        there = (z, px, py, c)
        return remote(self.part.at[:, px, py, c], self.got_plane.at[j - 1], self.ps.at[j - 1], self.pr.at[j - 1], there)

    def z_copy(self, j):
        z, x, y, c = self.place
        part = self.part.at[z ^ j, x, y, c]
        return remote(part, self.got_z.at[j - 1], self.zs.at[j - 1], self.zr.at[j - 1], (z ^ j, x, y, c))

    def send_all(self):
        self.core_copy().start()

    def first(self):
        z, x, y, c = self.place
        self.core_copy().wait_recv()
        add_into(self.part.at[:, :, :, c], self.got_core, (4, 2, 2))
        for j in (3, 2, 1):
            self.plane_copy(j).start()

    def along_z(self):
        z, x, y, c = self.place
        for j in (1, 2, 3):
            self.plane_copy(j).wait_recv()
        mine, got = self.part.at[:, x, y, c], self.got_plane

        def add(i, _):
            total = mine[i].astype(F32) + got[0, i].astype(F32)
            mine[i] = (total + got[1, i].astype(F32) + got[2, i].astype(F32)).astype(BF16)
            return 0

        lax.fori_loop(0, 4, add, 0)
        for j in (3, 2, 1):
            self.z_copy(j).start()

    def last(self):
        z, x, y, c = self.place
        total = self.part[z, x, y, c].astype(F32)
        for j in (1, 2, 3):
            self.z_copy(j).wait_recv()
            total = total + self.got_z[j - 1].astype(F32)
        self.write(total)

    def finish(self):
        self.core_copy().wait_send()
        for j in (1, 2, 3):
            self.plane_copy(j).wait_send()
            self.z_copy(j).wait_send()


def reduce_sems():
    return [DMA((1,))] * 2 + [DMA((3,))] * 4


def reduce_bufs(rows, width):
    shape = (rows, width)
    return [pltpu.VMEM(lead + shape, BF16) for lead in ((4, 2, 2), (3, 4), (3,))]


MID_PARTS = 2


def split_sum(ref, which):
    width = ref.shape[-1]
    cut = width // (MID_PARTS * 128) * 128
    return ref.at[..., pl.ds(which * cut, (cut, width - cut)[which])]


ORDER = (3, 1, 2, 0)


class ReduceMid:
    def __init__(self, part, bufs, sems, place, write):
        self.part, self.place, self.write = part, place, write
        self.got_core, self.got_1, self.got_z, self.got_last = bufs[0], bufs[1:3], bufs[3:5], bufs[5]
        self.cs, self.cr, self.fs, self.fr, self.zs, self.zr, self.ls, self.lr = sems

    def core_copy(self, j):
        z, x, y, c = self.place
        zi = z ^ j
        there = (z, x, y, 1 - c)
        return remote(self.part.at[zi, :, :, 1 - c], self.got_core.at[zi], self.cs.at[j], self.cr.at[j], there)

    def mine(self, zi, axis, other=0):
        z, x, y, c = self.place
        part = self.part.at[zi, :, abs(other - y), c] if axis == 0 else self.part.at[zi, abs(other - x), :, c]
        return split_sum(part, axis)

    def first_copy(self, j, axis):
        z, x, y, c = self.place
        zi = z ^ j
        there = (z, x, 1 - y, c) if axis == 0 else (z, 1 - x, y, c)
        return remote(self.mine(zi, axis, 1), self.got_1[axis].at[zi], self.fs.at[axis, j], self.fr.at[axis, j], there)

    def z_copy(self, j, axis):
        z, x, y, c = self.place
        there = (z ^ (2 if j == 2 else 1), x, y, c)
        slot = {3: 0, 1: 1, 2: 2}[j]
        return remote(
            self.mine(z ^ j, axis), self.got_z[axis].at[slot], self.zs.at[axis, slot], self.zr.at[axis, slot], there
        )

    def last_copy(self, axis):
        z, x, y, c = self.place
        if axis == 0:
            part, there = self.part.at[z, 1 - x, y, c], (z, 1 - x, y, c)
        else:
            part, there = self.part.at[z, x, 1 - y, c], (z, x, 1 - y, c)
        return remote(split_sum(part, axis), split_sum(self.got_last, axis), self.ls.at[axis], self.lr.at[axis], there)

    def send(self, j):
        self.core_copy(j).start()

    def send_all(self):
        for j in ORDER:
            self.send(j)

    def first(self, j):
        z, x, y, c = self.place
        zi = z ^ j
        self.core_copy(j).wait_recv()
        add_into(self.part.at[zi, :, :, c], self.got_core.at[zi], (2, 2))
        for axis in (0, 1):
            self.first_copy(j, axis).start()

    def turn(self, j):
        zi = self.place[0] ^ j
        for axis in (0, 1):
            self.first_copy(j, axis).wait_recv()
            add_into(self.mine(zi, axis), self.got_1[axis].at[zi], (2,))
            if j % 2:
                self.z_copy(j, axis).start()

    def cross(self):
        for axis in (0, 1):
            self.z_copy(3, axis).wait_recv()
            add_into(self.mine(self.place[0] ^ 2, axis), self.got_z[axis].at[0], (2,))
            self.z_copy(2, axis).start()

    def fold(self):
        z, x, y, c = self.place
        for axis in (0, 1):
            for j in (1, 2):
                self.z_copy(j, axis).wait_recv()
            mine, got = self.mine(z, axis), self.got_z[axis]

            def add(i, _, mine=mine, got=got):
                total = mine[i].astype(F32) + got[1, i].astype(F32)
                mine[i] = (total + got[2, i].astype(F32)).astype(BF16)
                return 0

            lax.fori_loop(0, 2, add, 0)
            self.last_copy(axis).start()

    def last(self):
        z, x, y, c = self.place
        for axis in (0, 1):
            self.last_copy(axis).wait_recv()
        self.write(self.part[z, x, y, c].astype(F32) + self.got_last[...].astype(F32))

    def finish(self):
        for j in range(4):
            self.core_copy(j).wait_send()
            for axis in (0, 1):
                self.first_copy(j, axis).wait_send()
                if j:
                    self.z_copy(j, axis).wait_send()
        for axis in (0, 1):
            self.last_copy(axis).wait_send()


def reduce_mid_sems():
    return [DMA((4,))] * 2 + [DMA((2, 4))] * 2 + [DMA((2, 3))] * 2 + [DMA((2,))] * 2


def reduce_mid_bufs(rows, width):
    cut = width // (MID_PARTS * 128) * 128
    return [
        pltpu.VMEM((4, 2, 2, rows, width), BF16),
        pltpu.VMEM((4, 2, rows, cut), BF16),
        pltpu.VMEM((4, 2, rows, width - cut), BF16),
        pltpu.VMEM((3, 2, rows, cut), BF16),
        pltpu.VMEM((3, 2, rows, width - cut), BF16),
        pltpu.VMEM((rows, width), BF16),
    ]


PIECES = 7
GROUPS = 3


def split_scratch(i, rest):
    buf_count = [6, 6] + [3] * (PIECES - 2)
    sem_count = [8, 8] + [6] * (PIECES - 2)
    bufs, sems = rest[: sum(buf_count)], rest[sum(buf_count) :]
    buf_at, sem_at = sum(buf_count[:i]), sum(sem_count[:i])
    return bufs[buf_at : buf_at + buf_count[i]], sems[sem_at : sem_at + sem_count[i]]


def backward_kernel(
    qkv_in, lse, x_in, att_in, normed1_in, low_in, act_in, slope_in, normed2_in, factors, bias,
    w_q, w_k, w_v, w_o, w1_in, w2_in, grads_in, layer_in, slots, live,
    layer_out, tokens_out, q_out, k_out, v_out, o_out, w1_out, w2_out, small_out,
    qkv, x, att, normed1, low, act, slope, grad, grads, w1, wb, turned, d_qkv, g_2, g_1, g_o, g_qkv, g_small, sums, sums1,
    local, ls, lr, ts, tr, *rest,
):
    place = z, px, py, c = my_place()
    me = py * 2 + c
    length, feat = low.shape
    inner_width = act.shape[1]
    slots_each = grads.shape[0] // 4

    sources = [(grads_in.at[i], grads.at[pl.ds(i * slots_each, slots_each)]) for i in range(4)]
    sources += [(normed2_in, grad), (act_in, act), (w2_in, wb), (slope_in, slope), (low_in, low), (w1_in, w1)]
    sources += [(normed1_in, normed1), (att_in, att), (qkv_in, qkv), (x_in, x)]
    loads = [pltpu.make_async_copy(src, dst, local.at[i]) for i, (src, dst) in enumerate(sources)]
    for copy in loads:
        copy.start()
    meet(
        [(z ^ j, px, py, c) for j in (1, 2, 3)]
        + [(z, 1 - px, py, c), (z, px, 1 - py, c), (z, px, py, 1 - c), (z, px, 1 - py, 1 - c)]
    )

    def page_copy(src, dst, send, recv, j):
        there = me ^ (j + 1)
        return remote(src.at[there], dst.at[me], send.at[j], recv.at[j], (z, px, there // 2, there % 2))

    layer_copies = [page_copy(layer_in, layer_out, ls, lr, j) for j in range(3)]
    for copy in layer_copies:
        copy.start()
    layer_own = pltpu.make_async_copy(layer_in.at[me], layer_out.at[me], local.at[14])
    layer_own.start()

    def whole(ref):
        def write(total):
            ref[...] = total

        return write

    def thirds(group):
        def write(total):
            for i, ref in enumerate((q_out, k_out, v_out)):
                ref[:, pl.ds(group * TILE, TILE)] = total[:, i * TILE : (i + 1) * TILE]

        return write

    parts = [(ReduceMid, g_2, whole(w2_out)), (ReduceMid, g_1, whole(w1_out)), (Reduce, g_o, whole(o_out))]
    parts += [(Reduce, g_qkv.at[i], thirds(i)) for i in range(GROUPS)]
    parts += [(Reduce, g_small, whole(small_out))]
    sums_2, sum_1, sum_o, *sum_qkv, sum_small = reduces = [
        kind(part, *split_scratch(i, rest), place, write) for i, (kind, part, write) in enumerate(parts)
    ]

    sums[...] = jnp.zeros_like(sums)
    sums1[...] = jnp.zeros_like(sums1)

    def tally(row, values):
        sums[row : row + 1, :] += jnp.sum(values, axis=0, keepdims=True)

    for copy in loads[:5]:
        copy.wait()
    rows = 128

    def norm_two(i, _):
        block = block_of(i, rows)
        select = (rows_of((grads.shape[0], rows)) == slots[:, block]).astype(BF16)
        grad_layer = dot_rows(select, grads[...])
        normed = grad[block, :]
        tally(6, grad_layer * normed)
        tally(7, grad_layer)
        back = norm_back(grad_layer * bias[6:7, :], normed, factors[block, 128:129])
        grad[block, :] = back
        second_low = back.astype(BF16)
        d_qkv[block, 0:feat] = second_low
        tally(5, second_low.astype(F32))
        return 0

    lax.fori_loop(0, length // rows, norm_two, 0)
    second = grads.at[pl.ds(0, length)]
    second[...] = d_qkv[:, 0:feat]
    loads[5].wait()

    def outer_grad(i, _):
        j = jnp.where(i == 1, 1, jnp.where(i == 2, 2, 3 - i))
        zi = z ^ j
        width = inner_width // 4
        part = dot_rows(act[:, block_of(zi, width)], second[...])
        g_2[zi] = part.astype(BF16).reshape(g_2.shape[1:])
        sums_2.send(j)
        for k in (1, 2, 3):
            pl.when(i == k)(in_order((sums_2.first, ORDER[k - 1])))
        return 0

    lax.fori_loop(0, 4, outer_grad, 0)
    sums_2.first(0)
    for copy in loads[6:9]:
        copy.wait()
    turned[...] = low[...].T
    under_inner = {8: [(sums_2.turn, 3)]}

    def inner_grad(i, _):
        block = block_of(i, TILE)
        up = dot_cols(second[...], wb[block, :])
        inner_low = (up * slope[:, block].astype(F32)).astype(BF16)
        slope[:, block] = inner_low
        sums1[0:1, block] = jnp.sum(inner_low.astype(F32), axis=0, keepdims=True)
        part = dot(turned[...], inner_low)
        g_1[:, :, :, :, :, block] = part.astype(BF16).reshape(g_1.shape[:-1] + (TILE,))
        for at, calls in under_inner.items():
            pl.when(i == at)(in_order(*calls))
        return 0

    lax.fori_loop(0, inner_width // TILE, inner_grad, 0)
    sum_1.send_all()
    slabs = [
        pltpu.make_async_copy(src, wb.at[pl.ds(i * feat, feat)], local.at[15 + i])
        for i, src in enumerate((w_o, w_q, w_k, w_v))
    ]
    for copy in slabs:
        copy.start()
    for copy in loads[9:]:
        copy.wait()

    def hidden_grad(i, _):
        half_width = feat // 2
        block = block_of(i, half_width)
        weight = w1[pl.ds(2 * i, 2)].reshape(half_width, inner_width)
        grad[:, block] += dot_cols(slope[...], weight)
        return 0

    lax.fori_loop(0, 2, hidden_grad, 0)
    in_order((sum_1.first, 3), (sum_1.first, 1), (sums_2.turn, 1))()
    first = second

    def norm_one(i, _):
        block = block_of(i, rows)
        up, normed = grad[block, :], normed1[block, :]
        tally(3, up * normed)
        tally(4, up)
        back = norm_back(up * bias[3:4, :], normed, factors[block, 0:1])
        grad[block, :] = back
        first_low = back.astype(BF16)
        first[block, :] = first_low
        tally(2, first_low.astype(F32))
        return 0

    lax.fori_loop(0, length // rows, norm_one, 0)
    in_order((sum_1.first, 2), (sum_1.first, 0), (sums_2.turn, 2), (sums_2.cross,))()
    for copy in slabs:
        copy.wait()
    g_o[...] = dot_rows(att[...], first[...]).astype(BF16).reshape(g_o.shape)
    sum_o.send_all()
    grad_att = grads.at[pl.ds(length, length)]

    def att_grad(i, _):
        block = block_of(i, rows)
        grad_att[block, :] = dot_cols(first[block, :], wb[0:feat, :]).astype(BF16)
        return 0

    lax.fori_loop(0, length // rows, att_grad, 0)
    turned[...] = x[...].T
    in_order((sums_2.turn, 0), (sum_o.first,))()
    scale = HEAD_DIM**-0.5

    def pair(p):
        start = pl.multiple_of(p * 128, 128)
        q = qkv[:, pl.ds(start, 128)] * jnp.asarray(scale, BF16)
        k = qkv[:, pl.ds(feat + start, 128)]
        v = qkv[:, pl.ds(2 * feat + start, 128)]
        g = grad_att[:, pl.ds(start, 128)]
        low_lane = lanes(q.shape) < HEAD_DIM
        results = []
        for h in (0, 1):
            keep = low_lane if h == 0 else ~low_lane
            zero = jnp.zeros_like(k)
            scores = jnp.where(live[...] > 0, dot_cols(jnp.where(keep, k, zero), q), NEG_FILL)
            probs = jnp.exp(scores - lse[pl.ds(2 * p + h, 1), :])
            up = dot_cols(jnp.where(keep, v, zero), g)
            inner_sum = jnp.sum(probs * up, axis=0, keepdims=True)
            grad_scores = (probs * (up - inner_sum)).astype(BF16)
            for at, calls in under.items():
                if at % 2 == h:
                    pl.when(p == at // 2)(in_order(*calls))
            results.append((dot_rows(k, grad_scores), dot(grad_scores, q), dot(probs.astype(BF16), g)))
        (q_0, k_0, v_0), (q_1, k_1, v_1) = results
        d_q = jnp.where(rows_of(q_0.shape) < HEAD_DIM, q_0, q_1) * scale
        d_qkv[:, pl.ds(start, 128)] = d_q.T.astype(BF16)
        d_qkv[:, pl.ds(feat + start, 128)] = jnp.where(low_lane, k_0, k_1).astype(BF16)
        d_qkv[:, pl.ds(2 * feat + start, 128)] = jnp.where(low_lane, v_0, v_1).astype(BF16)

    under = {
        4: [(sums_2.fold,)],
        5: [(sum_1.turn, 3), (sum_qkv[0].first,)],
        8: [(sums_2.last,), (sum_1.turn, 1)],
        9: [(sum_qkv[1].first,)],
        10: [(sum_1.turn, 2), (sum_1.cross,)],
    }

    def group(i, _):
        def one(j, _):
            pair(2 * i + j)
            return 0

        lax.fori_loop(0, 2, one, 0)
        for t in range(3):
            cols = pl.ds(pl.multiple_of(t * feat + i * TILE, TILE), TILE)
            part = dot(turned[...], d_qkv[:, cols])
            g_qkv[i, :, :, :, :, :, pl.ds(t * TILE, TILE)] = part.astype(BF16).reshape(
                g_qkv.shape[1:-1] + (TILE,)
            )
        for at in range(GROUPS):
            pl.when(i == at)(sum_qkv[at].send_all)
        return 0

    lax.fori_loop(0, GROUPS, group, 0)
    thirds_0, thirds_1, thirds_2 = sum_qkv
    in_order((sum_1.turn, 0), (sum_1.fold,), (sum_o.along_z,))()
    tally(0, d_qkv[:, 0:feat].astype(F32))
    tally(1, d_qkv[:, 2 * feat : 3 * feat].astype(F32))
    thirds_2.first()
    g_small[:, :, :, :, 0:8, :] = pack_rows(sums[...], feat // 32, 32).reshape(4, 2, 2, 2, 8, 128)
    for i in range(4):
        part = sums1[:, i * (inner_width // 4) : (i + 1) * (inner_width // 4)]
        g_small[i, :, :, :, 8:16, :] = pack_rows(part, inner_width // 32, 8).reshape(2, 2, 2, 8, 128)
    sum_small.send_all()
    grad_tokens = x.reshape(4, length // 4, feat)
    token_copies = [page_copy(grad_tokens, tokens_out, ts, tr, j) for j in range(3)]
    token_own = pltpu.make_async_copy(grad_tokens.at[me], tokens_out.at[me], local.at[19])

    def token_grad(i, _):
        block = block_of(me ^ (3 - i), length // 4)
        total = grad[block, :]
        for t in range(3):
            total += dot_cols(
                d_qkv[block, t * feat : (t + 1) * feat], wb[(t + 1) * feat : (t + 2) * feat, :]
            )
        x[block, :] = total.astype(BF16)
        for j in range(3):
            pl.when(i == 2 - j)(in_order((token_copies[j].start,)))
        return 0

    lax.fori_loop(0, 4, token_grad, 0)
    token_own.start()
    in_order(
        (sum_small.first,),
        (thirds_0.along_z,),
        (thirds_1.along_z,),
        (sum_1.last,),
        (sum_o.last,),
        (sum_small.along_z,),
        (thirds_2.along_z,),
        (thirds_0.last,),
        (thirds_1.last,),
        (sum_small.last,),
        (thirds_2.last,),
    )()
    for copy in layer_copies + token_copies:
        copy.wait()
    layer_own.wait()
    token_own.wait()
    for one in reduces:
        one.finish()


def backward(saved, weights, grad_pages, layer_slots, slots, live, tokens_shape):
    w_q, w_1, w_2 = weights[0], weights[4], weights[5]
    qkv, lse, x, att, normed1, low, act, slope, normed2, factors, bias = saved
    length, feat = low.shape
    inner_width = act.shape[1]
    anywhere = pl.BlockSpec(memory_space=pl.ANY)
    vmem = pl.BlockSpec(memory_space=pltpu.VMEM)
    grid = (4, 2, 2, 2)
    small, inner, outer = (feat // 32, feat), (feat // 32, inner_width), (inner_width // 32, feat)
    sizes = [outer, inner] + [small] * 4 + [(16, 128)]
    scratch = [
        ((length, 3 * feat), BF16),
        ((length, feat), BF16),
        ((length, feat), BF16),
        ((length, feat), F32),
        ((length, feat), BF16),
        ((length, inner_width), BF16),
        ((length, inner_width), BF16),
        ((length, feat), F32),
        ((grad_pages.shape[0] * grad_pages.shape[1], feat), BF16),
        (grid + inner, BF16),
        ((inner_width, feat), BF16),
        ((feat, length), BF16),
        ((length, 3 * feat), BF16),
        (grid + outer, BF16),
        (grid + inner, BF16),
        (grid + small, BF16),
        ((GROUPS,) + grid + small, BF16),
        (grid + (16, 128), BF16),
        ((8, feat), F32),
        ((8, inner_width), F32),
    ]
    bufs, sems = [], []
    for i, size in enumerate(sizes):
        bufs += reduce_mid_bufs(*size) if i < 2 else reduce_bufs(*size)
        sems += reduce_mid_sems() if i < 2 else reduce_sems()
    outs = [(grad_pages.shape, BF16, anywhere), (tokens_shape, BF16, anywhere)]
    outs += [(small, F32, vmem)] * 4 + [(inner, F32, vmem), (outer, F32, vmem), ((16, 128), F32, vmem)]
    return pl.pallas_call(
        backward_kernel,
        out_shape=[jax.ShapeDtypeStruct(shape, kind) for shape, kind, _ in outs],
        in_specs=[anywhere, vmem] + [anywhere] * 7 + [vmem, vmem] + [anywhere] * 8 + [vmem, vmem],
        out_specs=[spec for _, _, spec in outs],
        scratch_shapes=[pltpu.VMEM(shape, kind) for shape, kind in scratch]
        + [DMA((20,)), DMA((3,)), DMA((3,)), DMA((3,)), DMA((3,))]
        + bufs
        + sems,
        compiler_params=pltpu.CompilerParams(
            collective_id=1, has_side_effects=True, vmem_limit_bytes=VMEM_LIMIT
        ),
        name="backward",
    )(*saved, *weights, grad_pages, layer_slots, slots, live)


LARGE = (0, 2, 3, 5, 9, 11)
SMALL_ORDER = (1, 4, 6, 7, 8, 12, 13, 14, 10)


def finish_kernel(count, sizes, *refs):
    ins, small, outs = refs[:count], refs[count], refs[count + 1 : 2 * count + 1]
    vectors, stages, sems = refs[2 * count + 1 :][: len(sizes)], refs[-count - 1 : -1], refs[-1]
    inward = [pltpu.make_async_copy(i, s, sems.at[0, n]) for n, (i, s) in enumerate(zip(ins, stages))]
    outward = [pltpu.make_async_copy(s, o, sems.at[1, n]) for n, (s, o) in enumerate(zip(stages, outs))]
    for copy in inward:
        copy.start()
    for row, (size, ref) in enumerate(zip(sizes, vectors)):
        ref[...] = small[row : row + 1, 0:size].reshape(size)
    for first, second in zip(inward, outward):
        first.wait()
        second.start()
    for copy in outward:
        copy.wait()


def finish(arrays, small, sizes):
    count = len(arrays)
    anywhere = pl.BlockSpec(memory_space=pl.ANY)
    vmem = pl.BlockSpec(memory_space=pltpu.VMEM)

    def body(*refs):
        finish_kernel(count, sizes, *refs)

    return pl.pallas_call(
        body,
        out_shape=[jax.ShapeDtypeStruct(a.shape, a.dtype) for a in arrays]
        + [jax.ShapeDtypeStruct((size,), F32) for size in sizes],
        in_specs=[anywhere] * count + [vmem],
        out_specs=[anywhere] * count + [vmem] * len(sizes),
        scratch_shapes=[pltpu.VMEM(a.shape, a.dtype) for a in arrays] + [DMA((2, count))],
        compiler_params=pltpu.CompilerParams(vmem_limit_bytes=VMEM_LIMIT),
        name="finish",
    )(*arrays, small)


def by_kernels(tokens, band_ids, page_mask, weights, grad_output):
    large = [weights[i] for i in LARGE]
    vectors = [weights[i] for i in SMALL_ORDER]
    got = forward(vectors, tokens, grad_output, band_ids, page_mask, *large)
    saved, full, (grad_slots, layer_slots, slots, live) = got[:11], got[11:17], got[17:]
    full = [w if i == 4 else w.reshape(-1, w.shape[-1]) for i, w in enumerate(full)]
    sums = backward(saved, full, grad_slots, layer_slots, slots, live, tokens.shape)
    results = finish(sums[:8], sums[8], [v.shape[0] for v in vectors])
    grads = dict(zip(LARGE + SMALL_ORDER, results[2:]))
    return tuple(results[:2]) + tuple(grads[i] for i in range(len(weights)))


def per_device(hand_made, *args):
    tokens, band_ids, band_counts, page_mask = args[:4]
    weights, grad_output = args[4:19], args[19]
    if hand_made:
        return by_kernels(tokens, band_ids, page_mask, weights, grad_output)
    bands = lax.axis_size("band")
    slot_cap = grad_output.shape[1]
    pages = tokens.shape[0] // bands
    full = [lax.all_gather(w, BOTH, axis=0, tiled=True) for w in weights]
    first = lax.axis_index("band") * pages
    ids = lax.dynamic_slice_in_dim(band_ids, first, pages, 0)
    live = lax.dynamic_slice_in_dim(page_mask, first, pages, 0) > 0
    slots = page_slots(ids, bands, slot_cap)
    layer_slots, grad_in, grads = layer_pages(
        to_pages(tokens), slots, live, to_pages(grad_output), full
    )
    return (from_pages(layer_slots), from_pages(grad_in)) + tuple(
        lax.psum_scatter(g, BOTH, scatter_dimension=0, tiled=True) for g in grads
    )


def solution(mesh):
    hand_made = dict(mesh.shape) == {"page": 8, "band": 4}
    shard = P(BOTH)
    rows = P(BOTH, None)
    tokens = P("page", "band", None)
    page = P("page", None)
    weights = (rows, shard, rows, rows, shard, rows, shard, shard, shard)
    weights = weights + (rows, shard, rows, shard, shard, shard)

    def step(*args):
        return per_device(hand_made, *args)

    return jax.shard_map(
        step,
        mesh=mesh,
        in_specs=(tokens, page, page, page) + weights + (tokens,),
        out_specs=(tokens, tokens) + weights,
        check_vma=False,
    )
```

```python
import jax
import jax.numpy as jnp
from jax import lax
from jax.experimental import pallas as pl
from jax.experimental.pallas import tpu as pltpu
from jax.sharding import PartitionSpec as P

HEAD_DIM = 64
LN_EPS = 1e-12
NEG_FILL = -1e30
MESH = pl.DeviceIdType.MESH
DMA = pltpu.SemaphoreType.DMA
F32 = jnp.float32
BF16 = jnp.bfloat16
BOTH = ("page", "band")
VMEM_LIMIT = 62 * 2**20


def my_place():
    page, band = lax.axis_index("page"), lax.axis_index("band")
    return page // 2, page % 2, band // 2, band % 2


def dev(z, x, y, c):
    return (z * 2 + x, y * 2 + c)


def remote(src, dst, send_sem, recv_sem, place):
    return pltpu.make_async_remote_copy(
        src_ref=src,
        dst_ref=dst,
        send_sem=send_sem,
        recv_sem=recv_sem,
        device_id=dev(*place),
        device_id_type=MESH,
    )


def meet(places):
    barrier = pltpu.get_barrier_semaphore()
    for place in places:
        pl.semaphore_signal(barrier, inc=1, device_id=dev(*place), device_id_type=MESH)
    pl.semaphore_wait(barrier, len(places))


def grid_peers(z, x, y, c):
    return [((z + j) % 4, x, y, c) for j in (1, 2, 3)] + [
        (z, 1 - x, y, c),
        (z, x, 1 - y, c),
        (z, x, y, 1 - c),
    ]


def half(ref, which):
    rows, width = ref.shape[-2] // 2, ref.shape[-1] // 2
    if width % 128:
        return ref.at[..., pl.ds(which * rows, rows), :]
    return ref.at[..., pl.ds(which * width, width)]


def norm_rows(values):
    center = values - jnp.mean(values, axis=-1, keepdims=True)
    factor = lax.rsqrt(jnp.mean(center * center, axis=-1, keepdims=True) + LN_EPS)
    return (center * factor, factor)


def norm_back(upstream, normed, factor):
    return factor * (
        upstream
        - jnp.mean(upstream, axis=-1, keepdims=True)
        - normed * jnp.mean(upstream * normed, axis=-1, keepdims=True)
    )


def dot(first, second):
    return jnp.dot(first, second, preferred_element_type=F32)


def dot_rows(first, second):
    return lax.dot_general(first, second, (((0,), (0,)), ((), ())), preferred_element_type=F32)


def dot_cols(first, second):
    return lax.dot_general(first, second, (((1,), (1,)), ((), ())), preferred_element_type=F32)


def page_slots(ids, bands, slot_cap):
    onehot = (ids[:, :, None] == jnp.arange(bands, dtype=jnp.int32)).astype(F32)
    length = ids.shape[1]
    before = (jnp.arange(length)[:, None] > jnp.arange(length)[None, :]).astype(F32)
    counts = jnp.einsum("tu,pub->ptb", before, onehot, preferred_element_type=F32)
    rank = jnp.sum(onehot * counts, axis=2).astype(jnp.int32)
    return ids * slot_cap + rank


def layer_pages(rows_in, slots, live, grad_slots, weights):
    (wq, bq, wk, wv, bv, wo, bo, g1, s1, w1, b1, w2, b2, g2, s2) = weights
    pages, length, feat = rows_in.shape
    heads = feat // HEAD_DIM
    scale = HEAD_DIM**-0.5
    x_low = rows_in.reshape(-1, feat)
    select = (slots[:, None, :] == jnp.arange(grad_slots.shape[1])[None, :, None]).astype(BF16)
    grad_layer = jnp.einsum("pst,psd->ptd", select, grad_slots, preferred_element_type=F32)
    grad_layer = grad_layer.reshape(-1, feat)

    def split(flat):
        return flat.reshape(pages, length, heads, HEAD_DIM)

    query = split((dot(x_low, wq) + bq).astype(BF16))
    key = split(dot(x_low, wk).astype(BF16))
    value = split((dot(x_low, wv) + bv).astype(BF16))
    scores = jnp.einsum("pthd,puhd->phtu", query, key, preferred_element_type=F32) * scale
    scores = jnp.where(live[:, None, None, :], scores, NEG_FILL)
    shifted = jnp.exp(scores - jnp.max(scores, axis=-1, keepdims=True))
    probs = shifted / jnp.sum(shifted, axis=-1, keepdims=True)
    probs_low = probs.astype(BF16)
    mixed = jnp.einsum("phtu,puhd->pthd", probs_low, value, preferred_element_type=F32)
    attended = mixed.astype(BF16).reshape(-1, feat)
    normed_one, factor_one = norm_rows(x_low.astype(F32) + dot(attended, wo) + bo)
    hidden = normed_one * g1 + s1
    hidden_low = hidden.astype(BF16)
    inner = dot(hidden_low, w1) + b1
    cdf = 0.5 * (1.0 + lax.erf(inner * (0.5**0.5)))
    act_low = (inner * cdf).astype(BF16)
    slope = cdf + inner * jnp.exp(-0.5 * inner * inner) * ((0.5 / jnp.pi) ** 0.5)
    normed_two, factor_two = norm_rows(hidden + dot(act_low, w2) + b2)
    layer = (normed_two * g2 + s2).astype(BF16).reshape(pages, length, feat)
    layer_slots = jnp.einsum("pst,ptd->psd", select, layer, preferred_element_type=F32).astype(BF16)

    grad_g2 = jnp.sum(grad_layer * normed_two, axis=0)
    grad_s2 = jnp.sum(grad_layer, axis=0)
    grad_second = norm_back(grad_layer * g2, normed_two, factor_two)
    second_low = grad_second.astype(BF16)
    grad_w2 = dot_rows(act_low, second_low)
    grad_b2 = jnp.sum(second_low.astype(F32), axis=0)
    inner_low = (dot_cols(second_low, w2) * slope).astype(BF16)
    grad_w1 = dot_rows(hidden_low, inner_low)
    grad_b1 = jnp.sum(inner_low.astype(F32), axis=0)
    grad_hidden = grad_second + dot_cols(inner_low, w1)
    grad_g1 = jnp.sum(grad_hidden * normed_one, axis=0)
    grad_s1 = jnp.sum(grad_hidden, axis=0)
    grad_first = norm_back(grad_hidden * g1, normed_one, factor_one)
    first_low = grad_first.astype(BF16)
    grad_wo = dot_rows(attended, first_low)
    grad_bo = jnp.sum(first_low.astype(F32), axis=0)
    grad_att = split(dot_cols(first_low, wo).astype(BF16))
    grad_probs = jnp.einsum("pthd,puhd->phtu", grad_att, value, preferred_element_type=F32)
    inner_sum = jnp.sum(probs * grad_probs, axis=-1, keepdims=True)
    grad_scores = (probs * (grad_probs - inner_sum)).astype(BF16)

    def flat(per_head, factor):
        return (per_head * factor).astype(BF16).reshape(-1, feat)

    ein = lambda form, a, b: jnp.einsum(form, a, b, preferred_element_type=F32)
    grad_q = flat(ein("phtu,puhd->pthd", grad_scores, key), scale)
    grad_k = flat(ein("phtu,pthd->puhd", grad_scores, query), scale)
    grad_v = flat(ein("phtu,pthd->puhd", probs_low, grad_att), 1.0)
    grad_wq, grad_wk, grad_wv = (dot_rows(x_low, g) for g in (grad_q, grad_k, grad_v))
    grad_bq = jnp.sum(grad_q.astype(F32), axis=0)
    grad_bv = jnp.sum(grad_v.astype(F32), axis=0)
    grad_in = grad_first + dot_cols(grad_q, wq) + dot_cols(grad_k, wk) + dot_cols(grad_v, wv)
    grad_in = grad_in.astype(BF16).reshape(pages, length, feat)
    return (
        layer_slots,
        grad_in,
        (grad_wq, grad_bq, grad_wk, grad_wv, grad_bv, grad_wo, grad_bo, grad_g1, grad_s1)
        + (grad_w1, grad_b1, grad_w2, grad_b2, grad_g2, grad_s2),
    )


def to_pages(blocks):
    return lax.all_to_all(blocks, "band", split_axis=0, concat_axis=1, tiled=True)


def from_pages(blocks):
    return lax.all_to_all(blocks, "band", split_axis=1, concat_axis=0, tiled=True)


def split_ref(ref, which):
    rows, width = ref.shape[-2:]
    cut = width // 6
    if cut % 128:
        return ref.at[..., pl.ds(which * (rows // 2), rows // 2), :]
    return ref.at[..., pl.ds(which * cut, (cut, width - cut)[which])]


def split_shape(shape, which):
    rows, width = shape[-2:]
    cut = width // 6
    if cut % 128:
        return shape[:-2] + (rows // 2, width)
    return shape[:-1] + ((cut, width - cut)[which],)


def in_order(*calls):
    def step():
        for method, *index in calls:
            method(*index)

    return step


class Gather:
    def __init__(self, own, buf, sems, place):
        self.own, self.buf, self.place = own, buf, place
        self.zs, self.zr, self.ss, self.sr, self.fs, self.fr, self.cs, self.cr = sems

    def z_copy(self, j):
        z, x, y, c = self.place
        there = (z ^ (j + 1), x, y, c)
        return remote(self.own, self.buf.at[z, x, y, c], self.zs.at[j], self.zr.at[j], there)

    def side_copy(self, j, axis):
        z, x, y, c = self.place
        part = self.buf.at[z ^ j, x, y, c]
        there = (z, 1 - x, y, c) if axis == 0 else (z, x, 1 - y, c)
        source = self.own if j == 0 else part
        return remote(source, part, self.ss.at[axis, j], self.sr.at[axis, j], there)

    def far_copy(self, j, axis):
        z, x, y, c = self.place
        if axis == 0:
            part, there = self.buf.at[z ^ j, 1 - x, y, c], (z, x, 1 - y, c)
        else:
            part, there = self.buf.at[z ^ j, x, 1 - y, c], (z, 1 - x, y, c)
        part = split_ref(part, axis)
        return remote(part, part, self.fs.at[axis, j], self.fr.at[axis, j], there)

    def core_copy(self, k):
        z, x, y, c = self.place
        part = self.buf.at[:, (x, 1 - x, x, 1 - x)[k], (y, y, 1 - y, 1 - y)[k], c]
        return remote(part, part, self.cs.at[k], self.cr.at[k], (z, x, y, 1 - c))

    def start(self):
        for j in range(3):
            self.z_copy(j).start()
        for axis in (0, 1):
            self.side_copy(0, axis).start()

    def side(self, j):
        self.z_copy(j - 1).wait_recv()
        for axis in (0, 1):
            self.side_copy(j, axis).start()

    def far(self, j):
        for axis in (0, 1):
            self.side_copy(j, axis).wait_recv()
            self.far_copy(j, axis).start()

    def core(self, k):
        if k == 3:
            for j in range(4):
                for axis in (0, 1):
                    self.far_copy(j, axis).wait_recv()
        self.core_copy(k).start()

    def steps(self):
        side, far, core = self.side, self.far, self.core
        return [
            in_order((side, 1)),
            in_order((far, 0)),
            in_order((side, 2)),
            in_order((side, 3), (core, 0)),
            in_order((far, 1)),
            in_order((far, 2)),
            in_order((far, 3), (core, 1), (core, 2)),
            in_order((core, 3)),
        ]

    def arrive(self):
        for k in range(4):
            self.core_copy(k).wait_recv()

    def finish(self):
        for j in range(3):
            self.z_copy(j).wait_send()
        for j in range(4):
            for axis in (0, 1):
                self.side_copy(j, axis).wait_send()
                self.far_copy(j, axis).wait_send()
            self.core_copy(j).wait_send()


def gather_sems():
    return [DMA((3,)), DMA((3,))] + [DMA((2, 4))] * 4 + [DMA((4,))] * 2


def split_mid(ref, which):
    width = ref.shape[-1]
    cut = width // 384 * 128
    return ref.at[..., pl.ds(which * cut, (cut, width - cut)[which])]


class GatherMid:
    def __init__(self, own, buf, sems, place):
        self.own, self.buf, self.place = own, buf, place
        self.zs, self.zr, self.ss, self.sr, self.hs, self.hr, self.fs, self.fr, self.cs, self.cr = sems

    def z_copy(self, j):
        z, x, y, c = self.place
        zi = z ^ (2 if j == 3 else 0)
        source = self.buf.at[zi, x, y, c] if j == 3 else self.own
        there = (z ^ (2 if j == 2 else 1), x, y, c)
        return remote(source, self.buf.at[zi, x, y, c], self.zs.at[j - 1], self.zr.at[j - 1], there)

    def side_copy(self, axis):
        z, x, y, c = self.place
        there = (z, 1 - x, y, c) if axis == 0 else (z, x, 1 - y, c)
        source = split_mid(self.own, axis)
        return remote(source, split_mid(self.buf.at[z, x, y, c], axis), self.ss.at[axis], self.sr.at[axis], there)

    def half_copy(self, j, axis):
        z, x, y, c = self.place
        zi = z ^ (2 if j == 3 else 0)
        part = self.buf.at[zi, 1 - x, y, c] if axis == 0 else self.buf.at[zi, x, 1 - y, c]
        part = split_mid(part, axis)
        there = (z ^ (2 if j == 2 else 1), x, y, c)
        return remote(part, part, self.hs.at[axis, j - 1], self.hr.at[axis, j - 1], there)

    def far_copy(self, j, axis):
        z, x, y, c = self.place
        if axis == 0:
            part, there = self.buf.at[z ^ j, :, y, c], (z, x, 1 - y, c)
        else:
            part, there = self.buf.at[z ^ j, x, :, c], (z, 1 - x, y, c)
        part = split_mid(part, axis)
        return remote(part, part, self.fs.at[axis, j], self.fr.at[axis, j], there)

    def core_copy(self, j):
        z, x, y, c = self.place
        part = self.buf.at[z ^ j, :, :, c]
        return remote(part, part, self.cs.at[j], self.cr.at[j], (z, x, y, 1 - c))

    def start(self):
        for axis in (0, 1):
            self.side_copy(axis).start()
        for j in (2, 1):
            self.z_copy(j).start()

    def turn(self):
        for axis in (0, 1):
            self.side_copy(axis).wait_recv()
            for j in (2, 1):
                self.half_copy(j, axis).start()
        for axis in (0, 1):
            self.far_copy(0, axis).start()

    def far(self, j):
        self.z_copy(j).wait_recv()
        if j == 2:
            self.z_copy(3).start()
        for axis in (0, 1):
            self.half_copy(j, axis).wait_recv()
            if j == 2:
                self.half_copy(3, axis).start()
            self.far_copy(j, axis).start()

    def core(self, j):
        for axis in (0, 1):
            self.far_copy(j, axis).wait_recv()
        self.core_copy(j).start()

    def steps(self):
        far, core = self.far, self.core
        return [
            in_order((self.turn,)),
            in_order((far, 2)),
            in_order((far, 1)),
            in_order((far, 3)),
            in_order((core, 0)),
            in_order((core, 2)),
            in_order((core, 1)),
            in_order((core, 3)),
        ]

    def arrive(self):
        for k in range(4):
            self.core_copy(k).wait_recv()

    def finish(self):
        for axis in (0, 1):
            self.side_copy(axis).wait_send()
        for j in (1, 2, 3):
            self.z_copy(j).wait_send()
            for axis in (0, 1):
                self.half_copy(j, axis).wait_send()
        for j in range(4):
            for axis in (0, 1):
                self.far_copy(j, axis).wait_send()
            self.core_copy(j).wait_send()


def mid_sems():
    return [DMA((3,))] * 2 + [DMA((2,))] * 2 + [DMA((2, 3))] * 2 + [DMA((2, 4))] * 2 + [DMA((4,))] * 2


def lanes(shape):
    return lax.broadcasted_iota(jnp.int32, shape, len(shape) - 1)


def rows_of(shape):
    return lax.broadcasted_iota(jnp.int32, shape, len(shape) - 2)


def columns(buf, start, width):
    return buf[:, :, :, :, :, pl.ds(start, width)].reshape(-1, width)


def unpack_rows(block, per_shard, width):
    shards, count, _ = block.shape
    spread = (rows_of((128, width)) == lanes((128, width)) % per_shard).astype(BF16)
    wide = dot(block.reshape(-1, 128), spread).reshape(shards, count, width)
    owner = lax.broadcasted_iota(jnp.int32, wide.shape, 0) == lanes(wide.shape) // per_shard
    return jnp.sum(jnp.where(owner, wide, 0.0), axis=0)


def pack_rows(rows, per_shard, shards):
    count, width = rows.shape
    wide = jnp.broadcast_to(rows[None], (shards, count, width))
    owner = lax.broadcasted_iota(jnp.int32, wide.shape, 0) == lanes(wide.shape) // per_shard
    wide = jnp.where(owner, wide, 0.0).astype(BF16).reshape(-1, width)
    spread = (lanes((width, 128)) == rows_of((width, 128)) % per_shard).astype(BF16)
    return dot(wide, spread).astype(BF16).reshape(shards, count, 128)


def block_of(i, size):
    return pl.ds(pl.multiple_of(i * size, size), size)


def gelu_parts(v):
    cdf = 0.5 * (1.0 + lax.erf(v * (0.5**0.5)))
    return v * cdf, cdf + v * jnp.exp(-0.5 * v * v) * ((0.5 / jnp.pi) ** 0.5)


class Out:
    def __init__(self, sems):
        self.sems, self.copies = sems, []

    def send(self, src, dst):
        copy = pltpu.make_async_copy(src, dst, self.sems.at[len(self.copies)])
        copy.start()
        self.copies.append(copy)

    def wait(self):
        for copy in self.copies:
            copy.wait()


BIAS_ROWS = 8
TILE = 256


def forward_kernel(*refs):
    vector_refs, refs = refs[: BIAS_ROWS + 1], refs[BIAS_ROWS + 1 :]
    tokens, grads, ids, mask, w_q, w_k, w_v, w_o, w_1, w_2 = refs[:10]
    qkv_out, lse, x_out, att_out, normed1_out, low_out, act_out, slope_out, normed2_out = refs[10:19]
    factors, bias, q_out, k_out, v_out, o_out, w1_out, w2_out, grad_pages, layer_slots, slots, live = refs[19:31]
    small, small_own, a_buf, w1_buf, w2_buf, x_buf, qkv, att, normed1, low, act, slope = refs[31:43]
    second, normed2, layer, bias1, local, ts, tr, gs, gr, outs, *sems = refs[43:]
    place = z, x, y, c = my_place()
    me = y * 2 + c
    length, feat = low.shape
    pairs = feat // 128
    x_rows = x_buf.reshape(length, feat)
    here = (z, x, y, c)
    copies = [
        pltpu.make_async_copy(src, dst, local.at[i])
        for i, (src, dst) in enumerate(
            [(w, a_buf.at[here + (slice(None), pl.ds(i * feat, feat))]) for i, w in enumerate((w_q, w_k, w_v, w_o))]
            + [(w_1, w1_buf.at[here]), (w_2, w2_buf.at[here])]
            + [(tokens.at[me], x_buf.at[me]), (grads.at[me], grad_pages.at[me])]
        )
    ]
    for copy in copies:
        copy.start()
    small_own[...] = jnp.zeros_like(small_own)
    for row, ref in enumerate(vector_refs):
        size = ref.shape[0]
        small_own[row : row + 1, 0:size] = ref[...].astype(F32).reshape(1, size)
    small[here] = small_own[...].astype(BF16)
    meet(
        [(z ^ j, x, y, c) for j in (1, 2, 3)]
        + [(z, 1 - x, y, c), (z, x, 1 - y, c), (z, x, y, 1 - c), (z, x, 1 - y, 1 - c)]
    )

    def page_copy(src, dst, send, recv, j):
        there = me ^ (j + 1)
        return remote(src.at[there], dst.at[me], send.at[j], recv.at[j], (z, x, there // 2, there % 2))

    token_copies = [page_copy(tokens, x_buf, ts, tr, j) for j in range(3)]
    grad_copies = [page_copy(grads, grad_pages, gs, gr, j) for j in range(3)]
    gathers = [
        kind(own, buf, sems[(0, 8, 16, 26)[i] :][: 8 if kind is Gather else 10], place)
        for i, (kind, own, buf) in enumerate(
            [(Gather, small.at[here], small), (Gather, a_buf.at[here], a_buf)]
            + [(GatherMid, w_1, w1_buf), (GatherMid, w_2, w2_buf)]
        )
    ]
    vectors, atts, inner, outer = gathers
    for copy in copies[:4]:
        copy.wait()
    atts.start()
    vectors.start()
    for copy in token_copies:
        copy.start()
    slot_cap = grads.shape[1]
    hot = (rows_of((8, length)) == ids[pl.ds(me, 1), :]).astype(F32)
    earlier = (rows_of((length, length)) < lanes((length, length))).astype(BF16)
    rank = dot(hot.astype(BF16), earlier) + (rows_of((8, length)) * slot_cap).astype(F32)
    slots[...] = jnp.sum(hot * rank, axis=0, keepdims=True).astype(jnp.int32)
    live[...] = jnp.broadcast_to(mask[pl.ds(me, 1), :].astype(F32), (8, length)).T[:, 0:1]
    steps_0, steps_1, steps_2 = atts.steps(), inner.steps(), outer.steps()
    own = in_order(*[(copy.wait,) for copy in copies[4:6]])
    behind = {1: [inner.start], 3: [own, steps_1[0]], 4: [outer.start], 6: [steps_1[1]]}
    for i, (main, extra) in enumerate(zip(steps_0, vectors.steps())):
        main()
        extra()
        for step in behind.get(i, ()):
            step()
    for copy in copies[6:]:
        copy.wait()
    for copy in grad_copies:
        copy.start()
    vectors.arrive()
    shards = small[...].reshape(32, 16, 128)
    bias[...] = unpack_rows(shards[:, :8], feat // 32, feat)
    inner_width = act.shape[1]
    for i in range(4):
        part = unpack_rows(small[i].reshape(8, 16, 128)[:, 8:], inner_width // 32, inner_width // 4)
        bias1[:, i * (inner_width // 4) : (i + 1) * (inner_width // 4)] = part
    for copy in token_copies:
        copy.wait_recv()
    atts.arrive()
    out = Out(outs)
    for i, ref in enumerate((q_out, k_out, v_out, o_out)):
        out.send(a_buf.at[:, :, :, :, :, pl.ds(i * feat, feat)], ref)
    out.send(x_rows, x_out)
    steps_1[2]()

    def project(j, _):
        start = pl.multiple_of(j * TILE, TILE)
        total = dot(x_rows[...], columns(a_buf, start, TILE))
        which = j // (feat // TILE)
        inside = block_of(j % (feat // TILE), TILE)
        row = jnp.where(which == 0, bias[0:1, inside], jnp.where(which == 2, bias[1:2, inside], 0.0))
        qkv[:, pl.ds(start, TILE)] = (total + row).astype(BF16)
        return 0

    lax.fori_loop(0, 3 * feat // TILE, project, 0)
    out.send(qkv, qkv_out)
    steps_2[0]()
    under = {2: steps_1[3], 4: steps_2[1], 6: steps_1[4], 7: steps_2[2], 8: steps_1[5]}
    under |= {9: steps_1[6], 10: steps_1[7], 11: steps_2[3]}
    scale = HEAD_DIM**-0.5

    def pair(p, _):
        start = pl.multiple_of(p * 128, 128)
        q = qkv[:, pl.ds(start, 128)] * jnp.asarray(scale, BF16)
        k = qkv[:, pl.ds(feat + start, 128)]
        v = qkv[:, pl.ds(2 * feat + start, 128)]
        low_lane = lanes(q.shape) < HEAD_DIM
        mixed = []
        for h in (0, 1):
            part = jnp.where(low_lane if h == 0 else ~low_lane, k, jnp.zeros_like(k))
            scores = jnp.where(live[...] > 0, dot_cols(part, q), NEG_FILL)
            top = jnp.max(scores, axis=0, keepdims=True)
            shifted = jnp.exp(scores - top)
            total = jnp.sum(shifted, axis=0, keepdims=True)
            probs = (shifted * (1.0 / total)).astype(BF16)
            mixed.append(dot_rows(v, probs))
            lse[pl.ds(2 * p + h, 1), :] = top + jnp.log(total)
            for at, step in under.items():
                if at % 2 == h:
                    pl.when(p == at // 2)(step)
        both = jnp.where(rows_of(mixed[0].shape) < HEAD_DIM, mixed[0], mixed[1])
        att[:, pl.ds(start, 128)] = both.T.astype(BF16)
        return 0

    lax.fori_loop(0, pairs, pair, 0)
    out.send(att, att_out)
    rows = 128

    def norm_one(i, _):
        block = block_of(i, rows)
        total = dot(att[block, :], columns(a_buf, 3 * feat, feat))
        total = total + x_rows[block, :].astype(F32) + bias[2:3, :]
        normed, factor = norm_rows(total)
        normed1[block, :] = normed
        factors[block, 0:128] = jnp.broadcast_to(factor, (rows, 128))
        low[block, :] = (normed * bias[3:4, :] + bias[4:5, :]).astype(BF16)
        return 0

    lax.fori_loop(0, length // rows, norm_one, 0)
    out.send(normed1, normed1_out)
    out.send(low, low_out)
    inner.arrive()
    out.send(w1_buf, w1_out)

    def ffn_in(j, _):
        block = block_of(j, TILE)
        value, grad = gelu_parts(dot(low[...], columns(w1_buf, block.start, TILE)) + bias1[0:1, block])
        act[:, block] = value.astype(BF16)
        slope[:, block] = grad.astype(BF16)
        return 0

    lax.fori_loop(0, inner_width // TILE, ffn_in, 0)
    out.send(act, act_out)
    out.send(slope, slope_out)
    chunk = inner_width // 4

    def add_chunk(j):
        outer.core_copy(j).wait_recv()
        zi = z ^ j

        def part(i, _):
            block = block_of(i, TILE)
            more = dot(act[:, block_of(zi, chunk)], w2_buf[zi, :, :, :, :, block].reshape(chunk, TILE))
            second[:, block] = more if j == 0 else second[:, block] + more
            return 0

        lax.fori_loop(0, feat // TILE, part, 0)

    steps_2[4]()
    steps_2[5]()
    add_chunk(0)
    steps_2[6]()
    add_chunk(2)
    steps_2[7]()
    add_chunk(1)
    add_chunk(3)
    out.send(w2_buf, w2_out)

    def norm_two(i, _):
        block = block_of(i, rows)
        hidden = normed1[block, :] * bias[3:4, :] + bias[4:5, :]
        normed, factor = norm_rows(hidden + second[block, :] + bias[5:6, :])
        normed2[block, :] = normed
        factors[block, 128:256] = jnp.broadcast_to(factor, (rows, 128))
        layer[block, :] = (normed * bias[6:7, :] + bias[7:8, :]).astype(BF16)
        return 0

    lax.fori_loop(0, length // rows, norm_two, 0)
    out.send(normed2, normed2_out)

    def place_rows(i, _):
        cap = layer_slots.shape[1]
        here_rows = rows_of((cap, length)) + i * cap
        select = (here_rows == slots[...]).astype(BF16)
        layer_slots[i] = dot(select, layer[...]).astype(BF16)
        return 0

    lax.fori_loop(0, layer_slots.shape[0], place_rows, 0)
    for copy in grad_copies:
        copy.wait_recv()
    for copy in grad_copies + token_copies:
        copy.wait_send()
    for one in gathers:
        one.finish()
    out.wait()


def forward(vectors, tokens, grads, ids, mask, w_q, w_k, w_v, w_o, w_1, w_2):
    length, feat, inner_width = ids.shape[1], tokens.shape[-1], w_1.shape[1]
    anywhere = pl.BlockSpec(memory_space=pl.ANY)
    vmem = pl.BlockSpec(memory_space=pltpu.VMEM)
    grid = (4, 2, 2, 2)
    heads = feat // HEAD_DIM
    results = [
        ((length, 3 * feat), BF16, anywhere),
        ((heads + -heads % 8, length), F32, vmem),
        ((length, feat), BF16, anywhere),
        ((length, feat), BF16, anywhere),
        ((length, feat), F32, anywhere),
        ((length, feat), BF16, anywhere),
        ((length, inner_width), BF16, anywhere),
        ((length, inner_width), BF16, anywhere),
        ((length, feat), F32, anywhere),
        ((length, 256), F32, vmem),
        ((BIAS_ROWS, feat), F32, vmem),
    ]
    small = (16, 128)
    results += [(grid + w_q.shape, BF16, anywhere)] * 4
    results += [(grid + w_1.shape, BF16, anywhere), (grid + w_2.shape, BF16, anywhere)]
    results += [(grads.shape, BF16, anywhere), (grads.shape, BF16, vmem)]
    results += [((1, length), jnp.int32, vmem), ((length, 1), F32, vmem)]
    return pl.pallas_call(
        forward_kernel,
        out_shape=[jax.ShapeDtypeStruct(shape, kind) for shape, kind, _ in results],
        in_specs=[vmem] * len(vectors) + [anywhere, anywhere, vmem, vmem] + [anywhere] * 6,
        out_specs=[spec for _, _, spec in results],
        scratch_shapes=[
            pltpu.VMEM(grid + small, BF16),
            pltpu.VMEM(small, F32),
            pltpu.VMEM(grid + (w_q.shape[0], 4 * feat), BF16),
            pltpu.VMEM(grid + w_1.shape, BF16),
            pltpu.VMEM(grid + w_2.shape, BF16),
            pltpu.VMEM(tokens.shape, BF16),
            pltpu.VMEM((length, 3 * feat), BF16),
            pltpu.VMEM((length, feat), BF16),
            pltpu.VMEM((length, feat), F32),
            pltpu.VMEM((length, feat), BF16),
            pltpu.VMEM((length, inner_width), BF16),
            pltpu.VMEM((length, inner_width), BF16),
            pltpu.VMEM((length, feat), F32),
            pltpu.VMEM((length, feat), F32),
            pltpu.VMEM((length, feat), BF16),
            pltpu.VMEM((8, inner_width), F32),
            DMA((8,)),
            DMA((3,)),
            DMA((3,)),
            DMA((3,)),
            DMA((3,)),
            DMA((14,)),
        ]
        + gather_sems() * 2
        + mid_sems() * 2,
        compiler_params=pltpu.CompilerParams(
            collective_id=0, has_side_effects=True, vmem_limit_bytes=VMEM_LIMIT
        ),
        name="forward",
    )(*vectors, tokens, grads, ids, mask, w_q, w_k, w_v, w_o, w_1, w_2)


def add_into(dst, src, lead):
    def step(flat, _):
        index = []
        for size in reversed(lead):
            index.append(flat % size)
            flat = flat // size
        index = tuple(reversed(index))
        dst[index] = (dst[index].astype(F32) + src[index].astype(F32)).astype(BF16)
        return 0

    total = 1
    for size in lead:
        total *= size
    lax.fori_loop(0, total, step, 0)


class Reduce:
    def __init__(self, part, bufs, sems, place, write):
        self.part, self.place, self.write = part, place, write
        self.got_core, self.got_plane, self.got_z = bufs
        self.cs, self.cr, self.ps, self.pr, self.zs, self.zr = sems

    def core_copy(self):
        z, x, y, c = self.place
        there = (z, x, y, 1 - c)
        return remote(self.part.at[:, :, :, 1 - c], self.got_core, self.cs.at[0], self.cr.at[0], there)

    def plane_copy(self, j):
        z, x, y, c = self.place
        px, py = x ^ (j // 2), y ^ (j % 2)
        there = (z, px, py, c)
        return remote(self.part.at[:, px, py, c], self.got_plane.at[j - 1], self.ps.at[j - 1], self.pr.at[j - 1], there)

    def z_copy(self, j):
        z, x, y, c = self.place
        part = self.part.at[z ^ j, x, y, c]
        return remote(part, self.got_z.at[j - 1], self.zs.at[j - 1], self.zr.at[j - 1], (z ^ j, x, y, c))

    def send_all(self):
        self.core_copy().start()

    def first(self):
        z, x, y, c = self.place
        self.core_copy().wait_recv()
        add_into(self.part.at[:, :, :, c], self.got_core, (4, 2, 2))
        for j in (3, 2, 1):
            self.plane_copy(j).start()

    def along_z(self):
        z, x, y, c = self.place
        for j in (1, 2, 3):
            self.plane_copy(j).wait_recv()
        mine, got = self.part.at[:, x, y, c], self.got_plane

        def add(i, _):
            total = mine[i].astype(F32) + got[0, i].astype(F32)
            mine[i] = (total + got[1, i].astype(F32) + got[2, i].astype(F32)).astype(BF16)
            return 0

        lax.fori_loop(0, 4, add, 0)
        for j in (3, 2, 1):
            self.z_copy(j).start()

    def last(self):
        z, x, y, c = self.place
        total = self.part[z, x, y, c].astype(F32)
        for j in (1, 2, 3):
            self.z_copy(j).wait_recv()
            total = total + self.got_z[j - 1].astype(F32)
        self.write(total)

    def finish(self):
        self.core_copy().wait_send()
        for j in (1, 2, 3):
            self.plane_copy(j).wait_send()
            self.z_copy(j).wait_send()


def reduce_sems():
    return [DMA((1,))] * 2 + [DMA((3,))] * 4


def reduce_bufs(rows, width):
    shape = (rows, width)
    return [pltpu.VMEM(lead + shape, BF16) for lead in ((4, 2, 2), (3, 4), (3,))]


MID_PARTS = 2


def split_sum(ref, which):
    width = ref.shape[-1]
    cut = width // (MID_PARTS * 128) * 128
    return ref.at[..., pl.ds(which * cut, (cut, width - cut)[which])]


ORDER = (3, 1, 2, 0)


class ReduceMid:
    def __init__(self, part, bufs, sems, place, write):
        self.part, self.place, self.write = part, place, write
        self.got_core, self.got_1, self.got_z, self.got_last = bufs[0], bufs[1:3], bufs[3:5], bufs[5]
        self.cs, self.cr, self.fs, self.fr, self.zs, self.zr, self.ls, self.lr = sems

    def core_copy(self, j):
        z, x, y, c = self.place
        zi = z ^ j
        there = (z, x, y, 1 - c)
        return remote(self.part.at[zi, :, :, 1 - c], self.got_core.at[zi], self.cs.at[j], self.cr.at[j], there)

    def mine(self, zi, axis, other=0):
        z, x, y, c = self.place
        part = self.part.at[zi, :, abs(other - y), c] if axis == 0 else self.part.at[zi, abs(other - x), :, c]
        return split_sum(part, axis)

    def first_copy(self, j, axis):
        z, x, y, c = self.place
        zi = z ^ j
        there = (z, x, 1 - y, c) if axis == 0 else (z, 1 - x, y, c)
        return remote(self.mine(zi, axis, 1), self.got_1[axis].at[zi], self.fs.at[axis, j], self.fr.at[axis, j], there)

    def z_copy(self, j, axis):
        z, x, y, c = self.place
        there = (z ^ (2 if j == 2 else 1), x, y, c)
        slot = {3: 0, 1: 1, 2: 2}[j]
        return remote(
            self.mine(z ^ j, axis), self.got_z[axis].at[slot], self.zs.at[axis, slot], self.zr.at[axis, slot], there
        )

    def last_copy(self, axis):
        z, x, y, c = self.place
        if axis == 0:
            part, there = self.part.at[z, 1 - x, y, c], (z, 1 - x, y, c)
        else:
            part, there = self.part.at[z, x, 1 - y, c], (z, x, 1 - y, c)
        return remote(split_sum(part, axis), split_sum(self.got_last, axis), self.ls.at[axis], self.lr.at[axis], there)

    def send(self, j):
        self.core_copy(j).start()

    def send_all(self):
        for j in ORDER:
            self.send(j)

    def first(self, j):
        z, x, y, c = self.place
        zi = z ^ j
        self.core_copy(j).wait_recv()
        add_into(self.part.at[zi, :, :, c], self.got_core.at[zi], (2, 2))
        for axis in (0, 1):
            self.first_copy(j, axis).start()

    def turn(self, j):
        zi = self.place[0] ^ j
        for axis in (0, 1):
            self.first_copy(j, axis).wait_recv()
            add_into(self.mine(zi, axis), self.got_1[axis].at[zi], (2,))
            if j % 2:
                self.z_copy(j, axis).start()

    def cross(self):
        for axis in (0, 1):
            self.z_copy(3, axis).wait_recv()
            add_into(self.mine(self.place[0] ^ 2, axis), self.got_z[axis].at[0], (2,))
            self.z_copy(2, axis).start()

    def fold(self):
        z, x, y, c = self.place
        for axis in (0, 1):
            for j in (1, 2):
                self.z_copy(j, axis).wait_recv()
            mine, got = self.mine(z, axis), self.got_z[axis]

            def add(i, _, mine=mine, got=got):
                total = mine[i].astype(F32) + got[1, i].astype(F32)
                mine[i] = (total + got[2, i].astype(F32)).astype(BF16)
                return 0

            lax.fori_loop(0, 2, add, 0)
            self.last_copy(axis).start()

    def last(self):
        z, x, y, c = self.place
        for axis in (0, 1):
            self.last_copy(axis).wait_recv()
        self.write(self.part[z, x, y, c].astype(F32) + self.got_last[...].astype(F32))

    def finish(self):
        for j in range(4):
            self.core_copy(j).wait_send()
            for axis in (0, 1):
                self.first_copy(j, axis).wait_send()
                if j:
                    self.z_copy(j, axis).wait_send()
        for axis in (0, 1):
            self.last_copy(axis).wait_send()


def reduce_mid_sems():
    return [DMA((4,))] * 2 + [DMA((2, 4))] * 2 + [DMA((2, 3))] * 2 + [DMA((2,))] * 2


def reduce_mid_bufs(rows, width):
    cut = width // (MID_PARTS * 128) * 128
    return [
        pltpu.VMEM((4, 2, 2, rows, width), BF16),
        pltpu.VMEM((4, 2, rows, cut), BF16),
        pltpu.VMEM((4, 2, rows, width - cut), BF16),
        pltpu.VMEM((3, 2, rows, cut), BF16),
        pltpu.VMEM((3, 2, rows, width - cut), BF16),
        pltpu.VMEM((rows, width), BF16),
    ]


PIECES = 7
GROUPS = 3


def split_scratch(i, rest):
    buf_count = [6, 6] + [3] * (PIECES - 2)
    sem_count = [8, 8] + [6] * (PIECES - 2)
    bufs, sems = rest[: sum(buf_count)], rest[sum(buf_count) :]
    buf_at, sem_at = sum(buf_count[:i]), sum(sem_count[:i])
    return bufs[buf_at : buf_at + buf_count[i]], sems[sem_at : sem_at + sem_count[i]]


def backward_kernel(
    qkv_in, lse, x_in, att_in, normed1_in, low_in, act_in, slope_in, normed2_in, factors, bias,
    w_q, w_k, w_v, w_o, w1_in, w2_in, grads_in, layer_in, slots, live,
    layer_out, tokens_out, q_out, k_out, v_out, o_out, w1_out, w2_out, small_out,
    qkv, x, att, normed1, low, act, slope, grad, grads, w1, wb, turned, d_qkv, g_2, g_1, g_o, g_qkv, g_small, sums, sums1,
    local, ls, lr, ts, tr, *rest,
):
    place = z, px, py, c = my_place()
    me = py * 2 + c
    length, feat = low.shape
    inner_width = act.shape[1]
    slots_each = grads.shape[0] // 4

    sources = [(grads_in.at[i], grads.at[pl.ds(i * slots_each, slots_each)]) for i in range(4)]
    sources += [(normed2_in, grad), (act_in, act), (w2_in, wb), (slope_in, slope), (low_in, low), (w1_in, w1)]
    sources += [(normed1_in, normed1), (att_in, att), (qkv_in, qkv), (x_in, x)]
    loads = [pltpu.make_async_copy(src, dst, local.at[i]) for i, (src, dst) in enumerate(sources)]
    for copy in loads:
        copy.start()
    meet(
        [(z ^ j, px, py, c) for j in (1, 2, 3)]
        + [(z, 1 - px, py, c), (z, px, 1 - py, c), (z, px, py, 1 - c), (z, px, 1 - py, 1 - c)]
    )

    def page_copy(src, dst, send, recv, j):
        there = me ^ (j + 1)
        return remote(src.at[there], dst.at[me], send.at[j], recv.at[j], (z, px, there // 2, there % 2))

    layer_copies = [page_copy(layer_in, layer_out, ls, lr, j) for j in range(3)]
    for copy in layer_copies:
        copy.start()
    layer_own = pltpu.make_async_copy(layer_in.at[me], layer_out.at[me], local.at[14])
    layer_own.start()

    def whole(ref):
        def write(total):
            ref[...] = total

        return write

    def thirds(group):
        def write(total):
            for i, ref in enumerate((q_out, k_out, v_out)):
                ref[:, pl.ds(group * TILE, TILE)] = total[:, i * TILE : (i + 1) * TILE]

        return write

    parts = [(ReduceMid, g_2, whole(w2_out)), (ReduceMid, g_1, whole(w1_out)), (Reduce, g_o, whole(o_out))]
    parts += [(Reduce, g_qkv.at[i], thirds(i)) for i in range(GROUPS)]
    parts += [(Reduce, g_small, whole(small_out))]
    sums_2, sum_1, sum_o, *sum_qkv, sum_small = reduces = [
        kind(part, *split_scratch(i, rest), place, write) for i, (kind, part, write) in enumerate(parts)
    ]

    sums[...] = jnp.zeros_like(sums)
    sums1[...] = jnp.zeros_like(sums1)

    def tally(row, values):
        sums[row : row + 1, :] += jnp.sum(values, axis=0, keepdims=True)

    for copy in loads[:5]:
        copy.wait()
    rows = 128

    def norm_two(i, _):
        block = block_of(i, rows)
        select = (rows_of((grads.shape[0], rows)) == slots[:, block]).astype(BF16)
        grad_layer = dot_rows(select, grads[...])
        normed = grad[block, :]
        tally(6, grad_layer * normed)
        tally(7, grad_layer)
        back = norm_back(grad_layer * bias[6:7, :], normed, factors[block, 128:129])
        grad[block, :] = back
        second_low = back.astype(BF16)
        d_qkv[block, 0:feat] = second_low
        tally(5, second_low.astype(F32))
        return 0

    lax.fori_loop(0, length // rows, norm_two, 0)
    second = grads.at[pl.ds(0, length)]
    second[...] = d_qkv[:, 0:feat]
    loads[5].wait()

    def outer_grad(i, _):
        j = jnp.where(i == 1, 1, jnp.where(i == 2, 2, 3 - i))
        zi = z ^ j
        width = inner_width // 4
        part = dot_rows(act[:, block_of(zi, width)], second[...])
        g_2[zi] = part.astype(BF16).reshape(g_2.shape[1:])
        sums_2.send(j)
        for k in (1, 2, 3):
            pl.when(i == k)(in_order((sums_2.first, ORDER[k - 1])))
        return 0

    lax.fori_loop(0, 4, outer_grad, 0)
    sums_2.first(0)
    for copy in loads[6:9]:
        copy.wait()
    turned[...] = low[...].T
    under_inner = {8: [(sums_2.turn, 3)]}

    def inner_grad(i, _):
        block = block_of(i, TILE)
        up = dot_cols(second[...], wb[block, :])
        inner_low = (up * slope[:, block].astype(F32)).astype(BF16)
        slope[:, block] = inner_low
        sums1[0:1, block] = jnp.sum(inner_low.astype(F32), axis=0, keepdims=True)
        part = dot(turned[...], inner_low)
        g_1[:, :, :, :, :, block] = part.astype(BF16).reshape(g_1.shape[:-1] + (TILE,))
        for at, calls in under_inner.items():
            pl.when(i == at)(in_order(*calls))
        return 0

    lax.fori_loop(0, inner_width // TILE, inner_grad, 0)
    sum_1.send_all()
    slabs = [
        pltpu.make_async_copy(src, wb.at[pl.ds(i * feat, feat)], local.at[15 + i])
        for i, src in enumerate((w_o, w_q, w_k, w_v))
    ]
    for copy in slabs:
        copy.start()
    for copy in loads[9:]:
        copy.wait()

    def hidden_grad(i, _):
        half_width = feat // 2
        block = block_of(i, half_width)
        weight = w1[pl.ds(2 * i, 2)].reshape(half_width, inner_width)
        grad[:, block] += dot_cols(slope[...], weight)
        return 0

    lax.fori_loop(0, 2, hidden_grad, 0)
    in_order((sum_1.first, 3), (sum_1.first, 1), (sums_2.turn, 1))()
    first = second

    def norm_one(i, _):
        block = block_of(i, rows)
        up, normed = grad[block, :], normed1[block, :]
        tally(3, up * normed)
        tally(4, up)
        back = norm_back(up * bias[3:4, :], normed, factors[block, 0:1])
        grad[block, :] = back
        first_low = back.astype(BF16)
        first[block, :] = first_low
        tally(2, first_low.astype(F32))
        return 0

    lax.fori_loop(0, length // rows, norm_one, 0)
    in_order((sum_1.first, 2), (sum_1.first, 0), (sums_2.turn, 2), (sums_2.cross,))()
    for copy in slabs:
        copy.wait()
    g_o[...] = dot_rows(att[...], first[...]).astype(BF16).reshape(g_o.shape)
    sum_o.send_all()
    grad_att = grads.at[pl.ds(length, length)]

    def att_grad(i, _):
        block = block_of(i, rows)
        grad_att[block, :] = dot_cols(first[block, :], wb[0:feat, :]).astype(BF16)
        return 0

    lax.fori_loop(0, length // rows, att_grad, 0)
    turned[...] = x[...].T
    in_order((sums_2.turn, 0), (sum_o.first,))()
    scale = HEAD_DIM**-0.5

    def pair(p):
        start = pl.multiple_of(p * 128, 128)
        q = qkv[:, pl.ds(start, 128)] * jnp.asarray(scale, BF16)
        k = qkv[:, pl.ds(feat + start, 128)]
        v = qkv[:, pl.ds(2 * feat + start, 128)]
        g = grad_att[:, pl.ds(start, 128)]
        low_lane = lanes(q.shape) < HEAD_DIM
        results = []
        for h in (0, 1):
            keep = low_lane if h == 0 else ~low_lane
            zero = jnp.zeros_like(k)
            scores = jnp.where(live[...] > 0, dot_cols(jnp.where(keep, k, zero), q), NEG_FILL)
            probs = jnp.exp(scores - lse[pl.ds(2 * p + h, 1), :])
            up = dot_cols(jnp.where(keep, v, zero), g)
            inner_sum = jnp.sum(probs * up, axis=0, keepdims=True)
            grad_scores = (probs * (up - inner_sum)).astype(BF16)
            for at, calls in under.items():
                if at % 2 == h:
                    pl.when(p == at // 2)(in_order(*calls))
            results.append((dot_rows(k, grad_scores), dot(grad_scores, q), dot(probs.astype(BF16), g)))
        (q_0, k_0, v_0), (q_1, k_1, v_1) = results
        d_q = jnp.where(rows_of(q_0.shape) < HEAD_DIM, q_0, q_1) * scale
        d_qkv[:, pl.ds(start, 128)] = d_q.T.astype(BF16)
        d_qkv[:, pl.ds(feat + start, 128)] = jnp.where(low_lane, k_0, k_1).astype(BF16)
        d_qkv[:, pl.ds(2 * feat + start, 128)] = jnp.where(low_lane, v_0, v_1).astype(BF16)

    under = {
        4: [(sums_2.fold,)],
        5: [(sum_1.turn, 3), (sum_qkv[0].first,)],
        8: [(sums_2.last,), (sum_1.turn, 1)],
        9: [(sum_qkv[1].first,)],
        10: [(sum_1.turn, 2), (sum_1.cross,)],
    }

    def group(i, _):
        def one(j, _):
            pair(2 * i + j)
            return 0

        lax.fori_loop(0, 2, one, 0)
        for t in range(3):
            cols = pl.ds(pl.multiple_of(t * feat + i * TILE, TILE), TILE)
            part = dot(turned[...], d_qkv[:, cols])
            g_qkv[i, :, :, :, :, :, pl.ds(t * TILE, TILE)] = part.astype(BF16).reshape(
                g_qkv.shape[1:-1] + (TILE,)
            )
        for at in range(GROUPS):
            pl.when(i == at)(sum_qkv[at].send_all)
        return 0

    lax.fori_loop(0, GROUPS, group, 0)
    thirds_0, thirds_1, thirds_2 = sum_qkv
    in_order((sum_1.turn, 0), (sum_1.fold,), (sum_o.along_z,))()
    tally(0, d_qkv[:, 0:feat].astype(F32))
    tally(1, d_qkv[:, 2 * feat : 3 * feat].astype(F32))
    thirds_2.first()
    g_small[:, :, :, :, 0:8, :] = pack_rows(sums[...], feat // 32, 32).reshape(4, 2, 2, 2, 8, 128)
    for i in range(4):
        part = sums1[:, i * (inner_width // 4) : (i + 1) * (inner_width // 4)]
        g_small[i, :, :, :, 8:16, :] = pack_rows(part, inner_width // 32, 8).reshape(2, 2, 2, 8, 128)
    sum_small.send_all()
    grad_tokens = x.reshape(4, length // 4, feat)
    token_copies = [page_copy(grad_tokens, tokens_out, ts, tr, j) for j in range(3)]
    token_own = pltpu.make_async_copy(grad_tokens.at[me], tokens_out.at[me], local.at[19])

    def token_grad(i, _):
        block = block_of(me ^ (3 - i), length // 4)
        total = grad[block, :]
        for t in range(3):
            total += dot_cols(
                d_qkv[block, t * feat : (t + 1) * feat], wb[(t + 1) * feat : (t + 2) * feat, :]
            )
        x[block, :] = total.astype(BF16)
        for j in range(3):
            pl.when(i == 2 - j)(in_order((token_copies[j].start,)))
        return 0

    lax.fori_loop(0, 4, token_grad, 0)
    token_own.start()
    in_order(
        (sum_small.first,),
        (thirds_0.along_z,),
        (thirds_1.along_z,),
        (sum_1.last,),
        (sum_o.last,),
        (sum_small.along_z,),
        (thirds_2.along_z,),
        (thirds_0.last,),
        (thirds_1.last,),
        (sum_small.last,),
        (thirds_2.last,),
    )()
    for copy in layer_copies + token_copies:
        copy.wait()
    layer_own.wait()
    token_own.wait()
    for one in reduces:
        one.finish()


def backward(saved, weights, grad_pages, layer_slots, slots, live, tokens_shape):
    w_q, w_1, w_2 = weights[0], weights[4], weights[5]
    qkv, lse, x, att, normed1, low, act, slope, normed2, factors, bias = saved
    length, feat = low.shape
    inner_width = act.shape[1]
    anywhere = pl.BlockSpec(memory_space=pl.ANY)
    vmem = pl.BlockSpec(memory_space=pltpu.VMEM)
    grid = (4, 2, 2, 2)
    small, inner, outer = (feat // 32, feat), (feat // 32, inner_width), (inner_width // 32, feat)
    sizes = [outer, inner] + [small] * 4 + [(16, 128)]
    scratch = [
        ((length, 3 * feat), BF16),
        ((length, feat), BF16),
        ((length, feat), BF16),
        ((length, feat), F32),
        ((length, feat), BF16),
        ((length, inner_width), BF16),
        ((length, inner_width), BF16),
        ((length, feat), F32),
        ((grad_pages.shape[0] * grad_pages.shape[1], feat), BF16),
        (grid + inner, BF16),
        ((inner_width, feat), BF16),
        ((feat, length), BF16),
        ((length, 3 * feat), BF16),
        (grid + outer, BF16),
        (grid + inner, BF16),
        (grid + small, BF16),
        ((GROUPS,) + grid + small, BF16),
        (grid + (16, 128), BF16),
        ((8, feat), F32),
        ((8, inner_width), F32),
    ]
    bufs, sems = [], []
    for i, size in enumerate(sizes):
        bufs += reduce_mid_bufs(*size) if i < 2 else reduce_bufs(*size)
        sems += reduce_mid_sems() if i < 2 else reduce_sems()
    outs = [(grad_pages.shape, BF16, anywhere), (tokens_shape, BF16, anywhere)]
    outs += [(small, F32, vmem)] * 4 + [(inner, F32, vmem), (outer, F32, vmem), ((16, 128), F32, vmem)]
    return pl.pallas_call(
        backward_kernel,
        out_shape=[jax.ShapeDtypeStruct(shape, kind) for shape, kind, _ in outs],
        in_specs=[anywhere, vmem] + [anywhere] * 7 + [vmem, vmem] + [anywhere] * 8 + [vmem, vmem],
        out_specs=[spec for _, _, spec in outs],
        scratch_shapes=[pltpu.VMEM(shape, kind) for shape, kind in scratch]
        + [DMA((20,)), DMA((3,)), DMA((3,)), DMA((3,)), DMA((3,))]
        + bufs
        + sems,
        compiler_params=pltpu.CompilerParams(
            collective_id=1, has_side_effects=True, vmem_limit_bytes=VMEM_LIMIT
        ),
        name="backward",
    )(*saved, *weights, grad_pages, layer_slots, slots, live)


LARGE = (0, 2, 3, 5, 9, 11)
SMALL_ORDER = (1, 4, 6, 7, 8, 12, 13, 14, 10)


def finish_kernel(count, sizes, *refs):
    ins, small, outs = refs[:count], refs[count], refs[count + 1 : 2 * count + 1]
    vectors, stages, sems = refs[2 * count + 1 :][: len(sizes)], refs[-count - 1 : -1], refs[-1]
    inward = [pltpu.make_async_copy(i, s, sems.at[0, n]) for n, (i, s) in enumerate(zip(ins, stages))]
    outward = [pltpu.make_async_copy(s, o, sems.at[1, n]) for n, (s, o) in enumerate(zip(stages, outs))]
    for copy in inward:
        copy.start()
    for row, (size, ref) in enumerate(zip(sizes, vectors)):
        ref[...] = small[row : row + 1, 0:size].reshape(size)
    for first, second in zip(inward, outward):
        first.wait()
        second.start()
    for copy in outward:
        copy.wait()


def finish(arrays, small, sizes):
    count = len(arrays)
    anywhere = pl.BlockSpec(memory_space=pl.ANY)
    vmem = pl.BlockSpec(memory_space=pltpu.VMEM)

    def body(*refs):
        finish_kernel(count, sizes, *refs)

    return pl.pallas_call(
        body,
        out_shape=[jax.ShapeDtypeStruct(a.shape, a.dtype) for a in arrays]
        + [jax.ShapeDtypeStruct((size,), F32) for size in sizes],
        in_specs=[anywhere] * count + [vmem],
        out_specs=[anywhere] * count + [vmem] * len(sizes),
        scratch_shapes=[pltpu.VMEM(a.shape, a.dtype) for a in arrays] + [DMA((2, count))],
        compiler_params=pltpu.CompilerParams(vmem_limit_bytes=VMEM_LIMIT),
        name="finish",
    )(*arrays, small)


def by_kernels(tokens, band_ids, page_mask, weights, grad_output):
    large = [weights[i] for i in LARGE]
    vectors = [weights[i] for i in SMALL_ORDER]
    got = forward(vectors, tokens, grad_output, band_ids, page_mask, *large)
    saved, full, (grad_slots, layer_slots, slots, live) = got[:11], got[11:17], got[17:]
    full = [w if i == 4 else w.reshape(-1, w.shape[-1]) for i, w in enumerate(full)]
    sums = backward(saved, full, grad_slots, layer_slots, slots, live, tokens.shape)
    results = finish(sums[:8], sums[8], [v.shape[0] for v in vectors])
    grads = dict(zip(LARGE + SMALL_ORDER, results[2:]))
    return tuple(results[:2]) + tuple(grads[i] for i in range(len(weights)))


def per_device(hand_made, *args):
    tokens, band_ids, band_counts, page_mask = args[:4]
    weights, grad_output = args[4:19], args[19]
    if hand_made:
        return by_kernels(tokens, band_ids, page_mask, weights, grad_output)
    bands = lax.axis_size("band")
    slot_cap = grad_output.shape[1]
    pages = tokens.shape[0] // bands
    full = [lax.all_gather(w, BOTH, axis=0, tiled=True) for w in weights]
    first = lax.axis_index("band") * pages
    ids = lax.dynamic_slice_in_dim(band_ids, first, pages, 0)
    live = lax.dynamic_slice_in_dim(page_mask, first, pages, 0) > 0
    slots = page_slots(ids, bands, slot_cap)
    layer_slots, grad_in, grads = layer_pages(
        to_pages(tokens), slots, live, to_pages(grad_output), full
    )
    return (from_pages(layer_slots), from_pages(grad_in)) + tuple(
        lax.psum_scatter(g, BOTH, scatter_dimension=0, tiled=True) for g in grads
    )


def solution(mesh):
    hand_made = dict(mesh.shape) == {"page": 8, "band": 4}
    shard = P(BOTH)
    rows = P(BOTH, None)
    tokens = P("page", "band", None)
    page = P("page", None)
    weights = (rows, shard, rows, rows, shard, rows, shard, shard, shard)
    weights = weights + (rows, shard, rows, shard, shard, shard)

    def step(*args):
        return per_device(hand_made, *args)

    return jax.shard_map(
        step,
        mesh=mesh,
        in_specs=(tokens, page, page, page) + weights + (tokens,),
        out_specs=(tokens, tokens) + weights,
        check_vma=False,
    )
```

```python
import jax
import jax.numpy as jnp
from jax import lax
from jax.experimental import pallas as pl
from jax.experimental.pallas import tpu as pltpu
from jax.sharding import PartitionSpec as P

HEAD_DIM = 64
LN_EPS = 1e-12
NEG_FILL = -1e30
MESH = pl.DeviceIdType.MESH
DMA = pltpu.SemaphoreType.DMA
F32 = jnp.float32
BF16 = jnp.bfloat16
BOTH = ("page", "band")
VMEM_LIMIT = 62 * 2**20


def my_place():
    page, band = lax.axis_index("page"), lax.axis_index("band")
    return page // 2, page % 2, band // 2, band % 2


def dev(z, x, y, c):
    return (z * 2 + x, y * 2 + c)


def remote(src, dst, send_sem, recv_sem, place):
    return pltpu.make_async_remote_copy(
        src_ref=src,
        dst_ref=dst,
        send_sem=send_sem,
        recv_sem=recv_sem,
        device_id=dev(*place),
        device_id_type=MESH,
    )


def meet(places):
    barrier = pltpu.get_barrier_semaphore()
    for place in places:
        pl.semaphore_signal(barrier, inc=1, device_id=dev(*place), device_id_type=MESH)
    pl.semaphore_wait(barrier, len(places))


def grid_peers(z, x, y, c):
    return [((z + j) % 4, x, y, c) for j in (1, 2, 3)] + [
        (z, 1 - x, y, c),
        (z, x, 1 - y, c),
        (z, x, y, 1 - c),
    ]


def half(ref, which):
    rows, width = ref.shape[-2] // 2, ref.shape[-1] // 2
    if width % 128:
        return ref.at[..., pl.ds(which * rows, rows), :]
    return ref.at[..., pl.ds(which * width, width)]


def norm_rows(values):
    center = values - jnp.mean(values, axis=-1, keepdims=True)
    factor = lax.rsqrt(jnp.mean(center * center, axis=-1, keepdims=True) + LN_EPS)
    return (center * factor, factor)


def norm_back(upstream, normed, factor):
    return factor * (
        upstream
        - jnp.mean(upstream, axis=-1, keepdims=True)
        - normed * jnp.mean(upstream * normed, axis=-1, keepdims=True)
    )


def dot(first, second):
    return jnp.dot(first, second, preferred_element_type=F32)


def dot_rows(first, second):
    return lax.dot_general(first, second, (((0,), (0,)), ((), ())), preferred_element_type=F32)


def dot_cols(first, second):
    return lax.dot_general(first, second, (((1,), (1,)), ((), ())), preferred_element_type=F32)


def page_slots(ids, bands, slot_cap):
    onehot = (ids[:, :, None] == jnp.arange(bands, dtype=jnp.int32)).astype(F32)
    length = ids.shape[1]
    before = (jnp.arange(length)[:, None] > jnp.arange(length)[None, :]).astype(F32)
    counts = jnp.einsum("tu,pub->ptb", before, onehot, preferred_element_type=F32)
    rank = jnp.sum(onehot * counts, axis=2).astype(jnp.int32)
    return ids * slot_cap + rank


def layer_pages(rows_in, slots, live, grad_slots, weights):
    (wq, bq, wk, wv, bv, wo, bo, g1, s1, w1, b1, w2, b2, g2, s2) = weights
    pages, length, feat = rows_in.shape
    heads = feat // HEAD_DIM
    scale = HEAD_DIM**-0.5
    x_low = rows_in.reshape(-1, feat)
    select = (slots[:, None, :] == jnp.arange(grad_slots.shape[1])[None, :, None]).astype(BF16)
    grad_layer = jnp.einsum("pst,psd->ptd", select, grad_slots, preferred_element_type=F32)
    grad_layer = grad_layer.reshape(-1, feat)

    def split(flat):
        return flat.reshape(pages, length, heads, HEAD_DIM)

    query = split((dot(x_low, wq) + bq).astype(BF16))
    key = split(dot(x_low, wk).astype(BF16))
    value = split((dot(x_low, wv) + bv).astype(BF16))
    scores = jnp.einsum("pthd,puhd->phtu", query, key, preferred_element_type=F32) * scale
    scores = jnp.where(live[:, None, None, :], scores, NEG_FILL)
    shifted = jnp.exp(scores - jnp.max(scores, axis=-1, keepdims=True))
    probs = shifted / jnp.sum(shifted, axis=-1, keepdims=True)
    probs_low = probs.astype(BF16)
    mixed = jnp.einsum("phtu,puhd->pthd", probs_low, value, preferred_element_type=F32)
    attended = mixed.astype(BF16).reshape(-1, feat)
    normed_one, factor_one = norm_rows(x_low.astype(F32) + dot(attended, wo) + bo)
    hidden = normed_one * g1 + s1
    hidden_low = hidden.astype(BF16)
    inner = dot(hidden_low, w1) + b1
    cdf = 0.5 * (1.0 + lax.erf(inner * (0.5**0.5)))
    act_low = (inner * cdf).astype(BF16)
    slope = cdf + inner * jnp.exp(-0.5 * inner * inner) * ((0.5 / jnp.pi) ** 0.5)
    normed_two, factor_two = norm_rows(hidden + dot(act_low, w2) + b2)
    layer = (normed_two * g2 + s2).astype(BF16).reshape(pages, length, feat)
    layer_slots = jnp.einsum("pst,ptd->psd", select, layer, preferred_element_type=F32).astype(BF16)

    grad_g2 = jnp.sum(grad_layer * normed_two, axis=0)
    grad_s2 = jnp.sum(grad_layer, axis=0)
    grad_second = norm_back(grad_layer * g2, normed_two, factor_two)
    second_low = grad_second.astype(BF16)
    grad_w2 = dot_rows(act_low, second_low)
    grad_b2 = jnp.sum(second_low.astype(F32), axis=0)
    inner_low = (dot_cols(second_low, w2) * slope).astype(BF16)
    grad_w1 = dot_rows(hidden_low, inner_low)
    grad_b1 = jnp.sum(inner_low.astype(F32), axis=0)
    grad_hidden = grad_second + dot_cols(inner_low, w1)
    grad_g1 = jnp.sum(grad_hidden * normed_one, axis=0)
    grad_s1 = jnp.sum(grad_hidden, axis=0)
    grad_first = norm_back(grad_hidden * g1, normed_one, factor_one)
    first_low = grad_first.astype(BF16)
    grad_wo = dot_rows(attended, first_low)
    grad_bo = jnp.sum(first_low.astype(F32), axis=0)
    grad_att = split(dot_cols(first_low, wo).astype(BF16))
    grad_probs = jnp.einsum("pthd,puhd->phtu", grad_att, value, preferred_element_type=F32)
    inner_sum = jnp.sum(probs * grad_probs, axis=-1, keepdims=True)
    grad_scores = (probs * (grad_probs - inner_sum)).astype(BF16)

    def flat(per_head, factor):
        return (per_head * factor).astype(BF16).reshape(-1, feat)

    ein = lambda form, a, b: jnp.einsum(form, a, b, preferred_element_type=F32)
    grad_q = flat(ein("phtu,puhd->pthd", grad_scores, key), scale)
    grad_k = flat(ein("phtu,pthd->puhd", grad_scores, query), scale)
    grad_v = flat(ein("phtu,pthd->puhd", probs_low, grad_att), 1.0)
    grad_wq, grad_wk, grad_wv = (dot_rows(x_low, g) for g in (grad_q, grad_k, grad_v))
    grad_bq = jnp.sum(grad_q.astype(F32), axis=0)
    grad_bv = jnp.sum(grad_v.astype(F32), axis=0)
    grad_in = grad_first + dot_cols(grad_q, wq) + dot_cols(grad_k, wk) + dot_cols(grad_v, wv)
    grad_in = grad_in.astype(BF16).reshape(pages, length, feat)
    return (
        layer_slots,
        grad_in,
        (grad_wq, grad_bq, grad_wk, grad_wv, grad_bv, grad_wo, grad_bo, grad_g1, grad_s1)
        + (grad_w1, grad_b1, grad_w2, grad_b2, grad_g2, grad_s2),
    )


def to_pages(blocks):
    return lax.all_to_all(blocks, "band", split_axis=0, concat_axis=1, tiled=True)


def from_pages(blocks):
    return lax.all_to_all(blocks, "band", split_axis=1, concat_axis=0, tiled=True)


def split_ref(ref, which):
    rows, width = ref.shape[-2:]
    cut = width // 6
    if cut % 128:
        return ref.at[..., pl.ds(which * (rows // 2), rows // 2), :]
    return ref.at[..., pl.ds(which * cut, (cut, width - cut)[which])]


def split_shape(shape, which):
    rows, width = shape[-2:]
    cut = width // 6
    if cut % 128:
        return shape[:-2] + (rows // 2, width)
    return shape[:-1] + ((cut, width - cut)[which],)


def in_order(*calls):
    def step():
        for method, *index in calls:
            method(*index)

    return step


class Gather:
    def __init__(self, own, buf, sems, place):
        self.own, self.buf, self.place = own, buf, place
        self.zs, self.zr, self.ss, self.sr, self.fs, self.fr, self.cs, self.cr = sems

    def z_copy(self, j):
        z, x, y, c = self.place
        there = (z ^ (j + 1), x, y, c)
        return remote(self.own, self.buf.at[z, x, y, c], self.zs.at[j], self.zr.at[j], there)

    def side_copy(self, j, axis):
        z, x, y, c = self.place
        part = self.buf.at[z ^ j, x, y, c]
        there = (z, 1 - x, y, c) if axis == 0 else (z, x, 1 - y, c)
        source = self.own if j == 0 else part
        return remote(source, part, self.ss.at[axis, j], self.sr.at[axis, j], there)

    def far_copy(self, j, axis):
        z, x, y, c = self.place
        if axis == 0:
            part, there = self.buf.at[z ^ j, 1 - x, y, c], (z, x, 1 - y, c)
        else:
            part, there = self.buf.at[z ^ j, x, 1 - y, c], (z, 1 - x, y, c)
        part = split_ref(part, axis)
        return remote(part, part, self.fs.at[axis, j], self.fr.at[axis, j], there)

    def core_copy(self, k):
        z, x, y, c = self.place
        part = self.buf.at[:, (x, 1 - x, x, 1 - x)[k], (y, y, 1 - y, 1 - y)[k], c]
        return remote(part, part, self.cs.at[k], self.cr.at[k], (z, x, y, 1 - c))

    def start(self):
        for j in range(3):
            self.z_copy(j).start()
        for axis in (0, 1):
            self.side_copy(0, axis).start()

    def side(self, j):
        self.z_copy(j - 1).wait_recv()
        for axis in (0, 1):
            self.side_copy(j, axis).start()

    def far(self, j):
        for axis in (0, 1):
            self.side_copy(j, axis).wait_recv()
            self.far_copy(j, axis).start()

    def core(self, k):
        if k == 3:
            for j in range(4):
                for axis in (0, 1):
                    self.far_copy(j, axis).wait_recv()
        self.core_copy(k).start()

    def steps(self):
        side, far, core = self.side, self.far, self.core
        return [
            in_order((side, 1)),
            in_order((far, 0)),
            in_order((side, 2)),
            in_order((side, 3), (core, 0)),
            in_order((far, 1)),
            in_order((far, 2)),
            in_order((far, 3), (core, 1), (core, 2)),
            in_order((core, 3)),
        ]

    def arrive(self):
        for k in range(4):
            self.core_copy(k).wait_recv()

    def finish(self):
        for j in range(3):
            self.z_copy(j).wait_send()
        for j in range(4):
            for axis in (0, 1):
                self.side_copy(j, axis).wait_send()
                self.far_copy(j, axis).wait_send()
            self.core_copy(j).wait_send()


def gather_sems():
    return [DMA((3,)), DMA((3,))] + [DMA((2, 4))] * 4 + [DMA((4,))] * 2


def split_mid(ref, which):
    width = ref.shape[-1]
    cut = width // 384 * 128
    return ref.at[..., pl.ds(which * cut, (cut, width - cut)[which])]


class GatherMid:
    def __init__(self, own, buf, sems, place):
        self.own, self.buf, self.place = own, buf, place
        self.zs, self.zr, self.ss, self.sr, self.hs, self.hr, self.fs, self.fr, self.cs, self.cr = sems

    def z_copy(self, j):
        z, x, y, c = self.place
        zi = z ^ (2 if j == 3 else 0)
        source = self.buf.at[zi, x, y, c] if j == 3 else self.own
        there = (z ^ (2 if j == 2 else 1), x, y, c)
        return remote(source, self.buf.at[zi, x, y, c], self.zs.at[j - 1], self.zr.at[j - 1], there)

    def side_copy(self, axis):
        z, x, y, c = self.place
        there = (z, 1 - x, y, c) if axis == 0 else (z, x, 1 - y, c)
        source = split_mid(self.own, axis)
        return remote(source, split_mid(self.buf.at[z, x, y, c], axis), self.ss.at[axis], self.sr.at[axis], there)

    def half_copy(self, j, axis):
        z, x, y, c = self.place
        zi = z ^ (2 if j == 3 else 0)
        part = self.buf.at[zi, 1 - x, y, c] if axis == 0 else self.buf.at[zi, x, 1 - y, c]
        part = split_mid(part, axis)
        there = (z ^ (2 if j == 2 else 1), x, y, c)
        return remote(part, part, self.hs.at[axis, j - 1], self.hr.at[axis, j - 1], there)

    def far_copy(self, j, axis):
        z, x, y, c = self.place
        if axis == 0:
            part, there = self.buf.at[z ^ j, :, y, c], (z, x, 1 - y, c)
        else:
            part, there = self.buf.at[z ^ j, x, :, c], (z, 1 - x, y, c)
        part = split_mid(part, axis)
        return remote(part, part, self.fs.at[axis, j], self.fr.at[axis, j], there)

    def core_copy(self, j):
        z, x, y, c = self.place
        part = self.buf.at[z ^ j, :, :, c]
        return remote(part, part, self.cs.at[j], self.cr.at[j], (z, x, y, 1 - c))

    def start(self):
        for axis in (0, 1):
            self.side_copy(axis).start()
        for j in (2, 1):
            self.z_copy(j).start()

    def turn(self):
        for axis in (0, 1):
            self.side_copy(axis).wait_recv()
            for j in (2, 1):
                self.half_copy(j, axis).start()
        for axis in (0, 1):
            self.far_copy(0, axis).start()

    def far(self, j):
        self.z_copy(j).wait_recv()
        if j == 2:
            self.z_copy(3).start()
        for axis in (0, 1):
            self.half_copy(j, axis).wait_recv()
            if j == 2:
                self.half_copy(3, axis).start()
            self.far_copy(j, axis).start()

    def core(self, j):
        for axis in (0, 1):
            self.far_copy(j, axis).wait_recv()
        self.core_copy(j).start()

    def steps(self):
        far, core = self.far, self.core
        return [
            in_order((self.turn,)),
            in_order((far, 2)),
            in_order((far, 1)),
            in_order((far, 3)),
            in_order((core, 0)),
            in_order((core, 2)),
            in_order((core, 1)),
            in_order((core, 3)),
        ]

    def arrive(self):
        for k in range(4):
            self.core_copy(k).wait_recv()

    def finish(self):
        for axis in (0, 1):
            self.side_copy(axis).wait_send()
        for j in (1, 2, 3):
            self.z_copy(j).wait_send()
            for axis in (0, 1):
                self.half_copy(j, axis).wait_send()
        for j in range(4):
            for axis in (0, 1):
                self.far_copy(j, axis).wait_send()
            self.core_copy(j).wait_send()


def mid_sems():
    return [DMA((3,))] * 2 + [DMA((2,))] * 2 + [DMA((2, 3))] * 2 + [DMA((2, 4))] * 2 + [DMA((4,))] * 2


def lanes(shape):
    return lax.broadcasted_iota(jnp.int32, shape, len(shape) - 1)


def rows_of(shape):
    return lax.broadcasted_iota(jnp.int32, shape, len(shape) - 2)


def columns(buf, start, width):
    return buf[:, :, :, :, :, pl.ds(start, width)].reshape(-1, width)


def unpack_rows(block, per_shard, width):
    shards, count, _ = block.shape
    spread = (rows_of((128, width)) == lanes((128, width)) % per_shard).astype(BF16)
    wide = dot(block.reshape(-1, 128), spread).reshape(shards, count, width)
    owner = lax.broadcasted_iota(jnp.int32, wide.shape, 0) == lanes(wide.shape) // per_shard
    return jnp.sum(jnp.where(owner, wide, 0.0), axis=0)


def pack_rows(rows, per_shard, shards):
    count, width = rows.shape
    wide = jnp.broadcast_to(rows[None], (shards, count, width))
    owner = lax.broadcasted_iota(jnp.int32, wide.shape, 0) == lanes(wide.shape) // per_shard
    wide = jnp.where(owner, wide, 0.0).astype(BF16).reshape(-1, width)
    spread = (lanes((width, 128)) == rows_of((width, 128)) % per_shard).astype(BF16)
    return dot(wide, spread).astype(BF16).reshape(shards, count, 128)


def block_of(i, size):
    return pl.ds(pl.multiple_of(i * size, size), size)


def gelu_parts(v):
    cdf = 0.5 * (1.0 + lax.erf(v * (0.5**0.5)))
    return v * cdf, cdf + v * jnp.exp(-0.5 * v * v) * ((0.5 / jnp.pi) ** 0.5)


class Out:
    def __init__(self, sems):
        self.sems, self.copies = sems, []

    def send(self, src, dst):
        copy = pltpu.make_async_copy(src, dst, self.sems.at[len(self.copies)])
        copy.start()
        self.copies.append(copy)

    def wait(self):
        for copy in self.copies:
            copy.wait()


BIAS_ROWS = 8
TILE = 256


def forward_kernel(*refs):
    vector_refs, refs = refs[: BIAS_ROWS + 1], refs[BIAS_ROWS + 1 :]
    tokens, grads, ids, mask, w_q, w_k, w_v, w_o, w_1, w_2 = refs[:10]
    qkv_out, lse, x_out, att_out, normed1_out, low_out, act_out, slope_out, normed2_out = refs[10:19]
    factors, bias, q_out, k_out, v_out, o_out, w1_out, w2_out, grad_pages, layer_slots, slots, live = refs[19:31]
    small, small_own, a_buf, w1_buf, w2_buf, x_buf, qkv, att, normed1, low, act, slope = refs[31:43]
    second, normed2, layer, bias1, local, ts, tr, gs, gr, outs, *sems = refs[43:]
    place = z, x, y, c = my_place()
    me = y * 2 + c
    length, feat = low.shape
    pairs = feat // 128
    x_rows = x_buf.reshape(length, feat)
    here = (z, x, y, c)
    copies = [
        pltpu.make_async_copy(src, dst, local.at[i])
        for i, (src, dst) in enumerate(
            [(w, a_buf.at[here + (slice(None), pl.ds(i * feat, feat))]) for i, w in enumerate((w_q, w_k, w_v, w_o))]
            + [(w_1, w1_buf.at[here]), (w_2, w2_buf.at[here])]
            + [(tokens.at[me], x_buf.at[me]), (grads.at[me], grad_pages.at[me])]
        )
    ]
    for copy in copies:
        copy.start()
    small_own[...] = jnp.zeros_like(small_own)
    for row, ref in enumerate(vector_refs):
        size = ref.shape[0]
        small_own[row : row + 1, 0:size] = ref[...].astype(F32).reshape(1, size)
    small[here] = small_own[...].astype(BF16)
    meet(
        [(z ^ j, x, y, c) for j in (1, 2, 3)]
        + [(z, 1 - x, y, c), (z, x, 1 - y, c), (z, x, y, 1 - c), (z, x, 1 - y, 1 - c)]
    )

    def page_copy(src, dst, send, recv, j):
        there = me ^ (j + 1)
        return remote(src.at[there], dst.at[me], send.at[j], recv.at[j], (z, x, there // 2, there % 2))

    token_copies = [page_copy(tokens, x_buf, ts, tr, j) for j in range(3)]
    grad_copies = [page_copy(grads, grad_pages, gs, gr, j) for j in range(3)]
    gathers = [
        kind(own, buf, sems[(0, 8, 16, 26)[i] :][: 8 if kind is Gather else 10], place)
        for i, (kind, own, buf) in enumerate(
            [(Gather, small.at[here], small), (Gather, a_buf.at[here], a_buf)]
            + [(GatherMid, w_1, w1_buf), (GatherMid, w_2, w2_buf)]
        )
    ]
    vectors, atts, inner, outer = gathers
    for copy in copies[:4]:
        copy.wait()
    atts.start()
    vectors.start()
    for copy in token_copies:
        copy.start()
    slot_cap = grads.shape[1]
    hot = (rows_of((8, length)) == ids[pl.ds(me, 1), :]).astype(F32)
    earlier = (rows_of((length, length)) < lanes((length, length))).astype(BF16)
    rank = dot(hot.astype(BF16), earlier) + (rows_of((8, length)) * slot_cap).astype(F32)
    slots[...] = jnp.sum(hot * rank, axis=0, keepdims=True).astype(jnp.int32)
    live[...] = jnp.broadcast_to(mask[pl.ds(me, 1), :].astype(F32), (8, length)).T[:, 0:1]
    steps_0, steps_1, steps_2 = atts.steps(), inner.steps(), outer.steps()
    own = in_order(*[(copy.wait,) for copy in copies[4:6]])
    behind = {1: [inner.start], 3: [own, steps_1[0]], 4: [outer.start], 6: [steps_1[1]]}
    for i, (main, extra) in enumerate(zip(steps_0, vectors.steps())):
        main()
        extra()
        for step in behind.get(i, ()):
            step()
    for copy in copies[6:]:
        copy.wait()
    for copy in grad_copies:
        copy.start()
    vectors.arrive()
    shards = small[...].reshape(32, 16, 128)
    bias[...] = unpack_rows(shards[:, :8], feat // 32, feat)
    inner_width = act.shape[1]
    for i in range(4):
        part = unpack_rows(small[i].reshape(8, 16, 128)[:, 8:], inner_width // 32, inner_width // 4)
        bias1[:, i * (inner_width // 4) : (i + 1) * (inner_width // 4)] = part
    for copy in token_copies:
        copy.wait_recv()
    atts.arrive()
    out = Out(outs)
    for i, ref in enumerate((q_out, k_out, v_out, o_out)):
        out.send(a_buf.at[:, :, :, :, :, pl.ds(i * feat, feat)], ref)
    out.send(x_rows, x_out)
    steps_1[2]()

    def project(j, _):
        start = pl.multiple_of(j * TILE, TILE)
        total = dot(x_rows[...], columns(a_buf, start, TILE))
        which = j // (feat // TILE)
        inside = block_of(j % (feat // TILE), TILE)
        row = jnp.where(which == 0, bias[0:1, inside], jnp.where(which == 2, bias[1:2, inside], 0.0))
        qkv[:, pl.ds(start, TILE)] = (total + row).astype(BF16)
        return 0

    lax.fori_loop(0, 3 * feat // TILE, project, 0)
    out.send(qkv, qkv_out)
    steps_2[0]()
    under = {3: steps_1[3], 5: steps_2[1], 8: steps_1[4], 9: steps_2[2], 10: steps_1[5], 11: steps_1[6]}
    scale = HEAD_DIM**-0.5

    def pair(p, _):
        start = pl.multiple_of(p * 128, 128)
        q = qkv[:, pl.ds(start, 128)] * jnp.asarray(scale, BF16)
        k = qkv[:, pl.ds(feat + start, 128)]
        v = qkv[:, pl.ds(2 * feat + start, 128)]
        low_lane = lanes(q.shape) < HEAD_DIM
        mixed = []
        for h in (0, 1):
            part = jnp.where(low_lane if h == 0 else ~low_lane, k, jnp.zeros_like(k))
            scores = jnp.where(live[...] > 0, dot_cols(part, q), NEG_FILL)
            top = jnp.max(scores, axis=0, keepdims=True)
            shifted = jnp.exp(scores - top)
            total = jnp.sum(shifted, axis=0, keepdims=True)
            probs = (shifted * (1.0 / total)).astype(BF16)
            mixed.append(dot_rows(v, probs))
            lse[pl.ds(2 * p + h, 1), :] = top + jnp.log(total)
            for at, step in under.items():
                if at % 2 == h:
                    pl.when(p == at // 2)(step)
        both = jnp.where(rows_of(mixed[0].shape) < HEAD_DIM, mixed[0], mixed[1])
        att[:, pl.ds(start, 128)] = both.T.astype(BF16)
        return 0

    lax.fori_loop(0, pairs, pair, 0)
    out.send(att, att_out)
    steps_1[7]()
    steps_2[3]()
    rows = 128

    def norm_one(i, _):
        block = block_of(i, rows)
        total = dot(att[block, :], columns(a_buf, 3 * feat, feat))
        total = total + x_rows[block, :].astype(F32) + bias[2:3, :]
        normed, factor = norm_rows(total)
        normed1[block, :] = normed
        factors[block, 0:128] = jnp.broadcast_to(factor, (rows, 128))
        low[block, :] = (normed * bias[3:4, :] + bias[4:5, :]).astype(BF16)
        return 0

    lax.fori_loop(0, length // rows, norm_one, 0)
    out.send(normed1, normed1_out)
    out.send(low, low_out)
    inner.arrive()
    out.send(w1_buf, w1_out)

    def ffn_in(j, _):
        block = block_of(j, TILE)
        value, grad = gelu_parts(dot(low[...], columns(w1_buf, block.start, TILE)) + bias1[0:1, block])
        act[:, block] = value.astype(BF16)
        slope[:, block] = grad.astype(BF16)
        return 0

    lax.fori_loop(0, inner_width // TILE, ffn_in, 0)
    out.send(act, act_out)
    out.send(slope, slope_out)
    chunk = inner_width // 4

    def add_chunk(j):
        outer.core_copy(j).wait_recv()
        zi = z ^ j

        def part(i, _):
            block = block_of(i, TILE)
            more = dot(act[:, block_of(zi, chunk)], w2_buf[zi, :, :, :, :, block].reshape(chunk, TILE))
            second[:, block] = more if j == 0 else second[:, block] + more
            return 0

        lax.fori_loop(0, feat // TILE, part, 0)

    steps_2[4]()
    steps_2[5]()
    add_chunk(0)
    steps_2[6]()
    add_chunk(2)
    steps_2[7]()
    add_chunk(1)
    add_chunk(3)
    out.send(w2_buf, w2_out)

    def norm_two(i, _):
        block = block_of(i, rows)
        hidden = normed1[block, :] * bias[3:4, :] + bias[4:5, :]
        normed, factor = norm_rows(hidden + second[block, :] + bias[5:6, :])
        normed2[block, :] = normed
        factors[block, 128:256] = jnp.broadcast_to(factor, (rows, 128))
        layer[block, :] = (normed * bias[6:7, :] + bias[7:8, :]).astype(BF16)
        return 0

    lax.fori_loop(0, length // rows, norm_two, 0)
    out.send(normed2, normed2_out)

    def place_rows(i, _):
        cap = layer_slots.shape[1]
        here_rows = rows_of((cap, length)) + i * cap
        select = (here_rows == slots[...]).astype(BF16)
        layer_slots[i] = dot(select, layer[...]).astype(BF16)
        return 0

    lax.fori_loop(0, layer_slots.shape[0], place_rows, 0)
    for copy in grad_copies:
        copy.wait_recv()
    for copy in grad_copies + token_copies:
        copy.wait_send()
    for one in gathers:
        one.finish()
    out.wait()


def forward(vectors, tokens, grads, ids, mask, w_q, w_k, w_v, w_o, w_1, w_2):
    length, feat, inner_width = ids.shape[1], tokens.shape[-1], w_1.shape[1]
    anywhere = pl.BlockSpec(memory_space=pl.ANY)
    vmem = pl.BlockSpec(memory_space=pltpu.VMEM)
    grid = (4, 2, 2, 2)
    heads = feat // HEAD_DIM
    results = [
        ((length, 3 * feat), BF16, anywhere),
        ((heads + -heads % 8, length), F32, vmem),
        ((length, feat), BF16, anywhere),
        ((length, feat), BF16, anywhere),
        ((length, feat), F32, anywhere),
        ((length, feat), BF16, anywhere),
        ((length, inner_width), BF16, anywhere),
        ((length, inner_width), BF16, anywhere),
        ((length, feat), F32, anywhere),
        ((length, 256), F32, vmem),
        ((BIAS_ROWS, feat), F32, vmem),
    ]
    small = (16, 128)
    results += [(grid + w_q.shape, BF16, anywhere)] * 4
    results += [(grid + w_1.shape, BF16, anywhere), (grid + w_2.shape, BF16, anywhere)]
    results += [(grads.shape, BF16, anywhere), (grads.shape, BF16, vmem)]
    results += [((1, length), jnp.int32, vmem), ((length, 1), F32, vmem)]
    return pl.pallas_call(
        forward_kernel,
        out_shape=[jax.ShapeDtypeStruct(shape, kind) for shape, kind, _ in results],
        in_specs=[vmem] * len(vectors) + [anywhere, anywhere, vmem, vmem] + [anywhere] * 6,
        out_specs=[spec for _, _, spec in results],
        scratch_shapes=[
            pltpu.VMEM(grid + small, BF16),
            pltpu.VMEM(small, F32),
            pltpu.VMEM(grid + (w_q.shape[0], 4 * feat), BF16),
            pltpu.VMEM(grid + w_1.shape, BF16),
            pltpu.VMEM(grid + w_2.shape, BF16),
            pltpu.VMEM(tokens.shape, BF16),
            pltpu.VMEM((length, 3 * feat), BF16),
            pltpu.VMEM((length, feat), BF16),
            pltpu.VMEM((length, feat), F32),
            pltpu.VMEM((length, feat), BF16),
            pltpu.VMEM((length, inner_width), BF16),
            pltpu.VMEM((length, inner_width), BF16),
            pltpu.VMEM((length, feat), F32),
            pltpu.VMEM((length, feat), F32),
            pltpu.VMEM((length, feat), BF16),
            pltpu.VMEM((8, inner_width), F32),
            DMA((8,)),
            DMA((3,)),
            DMA((3,)),
            DMA((3,)),
            DMA((3,)),
            DMA((14,)),
        ]
        + gather_sems() * 2
        + mid_sems() * 2,
        compiler_params=pltpu.CompilerParams(
            collective_id=0, has_side_effects=True, vmem_limit_bytes=VMEM_LIMIT
        ),
        name="forward",
    )(*vectors, tokens, grads, ids, mask, w_q, w_k, w_v, w_o, w_1, w_2)


def add_into(dst, src, lead):
    def step(flat, _):
        index = []
        for size in reversed(lead):
            index.append(flat % size)
            flat = flat // size
        index = tuple(reversed(index))
        dst[index] = (dst[index].astype(F32) + src[index].astype(F32)).astype(BF16)
        return 0

    total = 1
    for size in lead:
        total *= size
    lax.fori_loop(0, total, step, 0)


class Reduce:
    def __init__(self, part, bufs, sems, place, write):
        self.part, self.place, self.write = part, place, write
        self.got_core, self.got_plane, self.got_z = bufs
        self.cs, self.cr, self.ps, self.pr, self.zs, self.zr = sems

    def core_copy(self):
        z, x, y, c = self.place
        there = (z, x, y, 1 - c)
        return remote(self.part.at[:, :, :, 1 - c], self.got_core, self.cs.at[0], self.cr.at[0], there)

    def plane_copy(self, j):
        z, x, y, c = self.place
        px, py = x ^ (j // 2), y ^ (j % 2)
        there = (z, px, py, c)
        return remote(self.part.at[:, px, py, c], self.got_plane.at[j - 1], self.ps.at[j - 1], self.pr.at[j - 1], there)

    def z_copy(self, j):
        z, x, y, c = self.place
        part = self.part.at[z ^ j, x, y, c]
        return remote(part, self.got_z.at[j - 1], self.zs.at[j - 1], self.zr.at[j - 1], (z ^ j, x, y, c))

    def send_all(self):
        self.core_copy().start()

    def first(self):
        z, x, y, c = self.place
        self.core_copy().wait_recv()
        add_into(self.part.at[:, :, :, c], self.got_core, (4, 2, 2))
        for j in (3, 2, 1):
            self.plane_copy(j).start()

    def along_z(self):
        z, x, y, c = self.place
        for j in (1, 2, 3):
            self.plane_copy(j).wait_recv()
        mine, got = self.part.at[:, x, y, c], self.got_plane

        def add(i, _):
            total = mine[i].astype(F32) + got[0, i].astype(F32)
            mine[i] = (total + got[1, i].astype(F32) + got[2, i].astype(F32)).astype(BF16)
            return 0

        lax.fori_loop(0, 4, add, 0)
        for j in (3, 2, 1):
            self.z_copy(j).start()

    def last(self):
        z, x, y, c = self.place
        total = self.part[z, x, y, c].astype(F32)
        for j in (1, 2, 3):
            self.z_copy(j).wait_recv()
            total = total + self.got_z[j - 1].astype(F32)
        self.write(total)

    def finish(self):
        self.core_copy().wait_send()
        for j in (1, 2, 3):
            self.plane_copy(j).wait_send()
            self.z_copy(j).wait_send()


def reduce_sems():
    return [DMA((1,))] * 2 + [DMA((3,))] * 4


def reduce_bufs(rows, width):
    shape = (rows, width)
    return [pltpu.VMEM(lead + shape, BF16) for lead in ((4, 2, 2), (3, 4), (3,))]


MID_PARTS = 3


def split_sum(ref, which):
    width = ref.shape[-1]
    cut = width // (MID_PARTS * 128) * 128
    return ref.at[..., pl.ds(which * cut, (cut, width - cut)[which])]


ORDER = (3, 1, 2, 0)


class ReduceMid:
    def __init__(self, part, bufs, sems, place, write):
        self.part, self.place, self.write = part, place, write
        self.got_core, self.got_1, self.got_z, self.got_last = bufs[0], bufs[1:3], bufs[3:5], bufs[5]
        self.cs, self.cr, self.fs, self.fr, self.zs, self.zr, self.ls, self.lr = sems

    def core_copy(self, j):
        z, x, y, c = self.place
        zi = z ^ j
        there = (z, x, y, 1 - c)
        return remote(self.part.at[zi, :, :, 1 - c], self.got_core.at[zi], self.cs.at[j], self.cr.at[j], there)

    def mine(self, zi, axis, other=0):
        z, x, y, c = self.place
        part = self.part.at[zi, :, abs(other - y), c] if axis == 0 else self.part.at[zi, abs(other - x), :, c]
        return split_sum(part, axis)

    def first_copy(self, j, axis):
        z, x, y, c = self.place
        zi = z ^ j
        there = (z, x, 1 - y, c) if axis == 0 else (z, 1 - x, y, c)
        return remote(self.mine(zi, axis, 1), self.got_1[axis].at[zi], self.fs.at[axis, j], self.fr.at[axis, j], there)

    def z_copy(self, j, axis):
        z, x, y, c = self.place
        there = (z ^ (2 if j == 2 else 1), x, y, c)
        slot = {3: 0, 1: 1, 2: 2}[j]
        return remote(
            self.mine(z ^ j, axis), self.got_z[axis].at[slot], self.zs.at[axis, slot], self.zr.at[axis, slot], there
        )

    def last_copy(self, axis):
        z, x, y, c = self.place
        if axis == 0:
            part, there = self.part.at[z, 1 - x, y, c], (z, 1 - x, y, c)
        else:
            part, there = self.part.at[z, x, 1 - y, c], (z, x, 1 - y, c)
        return remote(split_sum(part, axis), split_sum(self.got_last, axis), self.ls.at[axis], self.lr.at[axis], there)

    def send(self, j):
        self.core_copy(j).start()

    def send_all(self):
        for j in ORDER:
            self.send(j)

    def first(self, j):
        z, x, y, c = self.place
        zi = z ^ j
        self.core_copy(j).wait_recv()
        add_into(self.part.at[zi, :, :, c], self.got_core.at[zi], (2, 2))
        for axis in (0, 1):
            self.first_copy(j, axis).start()

    def turn(self, j):
        zi = self.place[0] ^ j
        for axis in (0, 1):
            self.first_copy(j, axis).wait_recv()
            add_into(self.mine(zi, axis), self.got_1[axis].at[zi], (2,))
            if j % 2:
                self.z_copy(j, axis).start()

    def cross(self):
        for axis in (0, 1):
            self.z_copy(3, axis).wait_recv()
            add_into(self.mine(self.place[0] ^ 2, axis), self.got_z[axis].at[0], (2,))
            self.z_copy(2, axis).start()

    def fold(self):
        z, x, y, c = self.place
        for axis in (0, 1):
            for j in (1, 2):
                self.z_copy(j, axis).wait_recv()
            mine, got = self.mine(z, axis), self.got_z[axis]

            def add(i, _, mine=mine, got=got):
                total = mine[i].astype(F32) + got[1, i].astype(F32)
                mine[i] = (total + got[2, i].astype(F32)).astype(BF16)
                return 0

            lax.fori_loop(0, 2, add, 0)
            self.last_copy(axis).start()

    def last(self):
        z, x, y, c = self.place
        for axis in (0, 1):
            self.last_copy(axis).wait_recv()
        self.write(self.part[z, x, y, c].astype(F32) + self.got_last[...].astype(F32))

    def finish(self):
        for j in range(4):
            self.core_copy(j).wait_send()
            for axis in (0, 1):
                self.first_copy(j, axis).wait_send()
                if j:
                    self.z_copy(j, axis).wait_send()
        for axis in (0, 1):
            self.last_copy(axis).wait_send()


def reduce_mid_sems():
    return [DMA((4,))] * 2 + [DMA((2, 4))] * 2 + [DMA((2, 3))] * 2 + [DMA((2,))] * 2


def reduce_mid_bufs(rows, width):
    cut = width // (MID_PARTS * 128) * 128
    return [
        pltpu.VMEM((4, 2, 2, rows, width), BF16),
        pltpu.VMEM((4, 2, rows, cut), BF16),
        pltpu.VMEM((4, 2, rows, width - cut), BF16),
        pltpu.VMEM((3, 2, rows, cut), BF16),
        pltpu.VMEM((3, 2, rows, width - cut), BF16),
        pltpu.VMEM((rows, width), BF16),
    ]


PIECES = 7
GROUPS = 3


def split_scratch(i, rest):
    buf_count = [6, 6] + [3] * (PIECES - 2)
    sem_count = [8, 8] + [6] * (PIECES - 2)
    bufs, sems = rest[: sum(buf_count)], rest[sum(buf_count) :]
    buf_at, sem_at = sum(buf_count[:i]), sum(sem_count[:i])
    return bufs[buf_at : buf_at + buf_count[i]], sems[sem_at : sem_at + sem_count[i]]


def backward_kernel(
    qkv_in, lse, x_in, att_in, normed1_in, low_in, act_in, slope_in, normed2_in, factors, bias,
    w_q, w_k, w_v, w_o, w1_in, w2_in, grads_in, layer_in, slots, live,
    layer_out, tokens_out, q_out, k_out, v_out, o_out, w1_out, w2_out, small_out,
    qkv, x, att, normed1, low, act, slope, grad, grads, w1, wb, turned, d_qkv, g_2, g_1, g_o, g_qkv, g_small, sums, sums1,
    local, ls, lr, ts, tr, *rest,
):
    place = z, px, py, c = my_place()
    me = py * 2 + c
    length, feat = low.shape
    inner_width = act.shape[1]
    slots_each = grads.shape[0] // 4

    sources = [(grads_in.at[i], grads.at[pl.ds(i * slots_each, slots_each)]) for i in range(4)]
    sources += [(normed2_in, grad), (act_in, act), (w2_in, wb), (slope_in, slope), (low_in, low), (w1_in, w1)]
    sources += [(normed1_in, normed1), (att_in, att), (qkv_in, qkv), (x_in, x)]
    loads = [pltpu.make_async_copy(src, dst, local.at[i]) for i, (src, dst) in enumerate(sources)]
    for copy in loads:
        copy.start()
    meet(
        [(z ^ j, px, py, c) for j in (1, 2, 3)]
        + [(z, 1 - px, py, c), (z, px, 1 - py, c), (z, px, py, 1 - c), (z, px, 1 - py, 1 - c)]
    )

    def page_copy(src, dst, send, recv, j):
        there = me ^ (j + 1)
        return remote(src.at[there], dst.at[me], send.at[j], recv.at[j], (z, px, there // 2, there % 2))

    layer_copies = [page_copy(layer_in, layer_out, ls, lr, j) for j in range(3)]
    for copy in layer_copies:
        copy.start()
    layer_own = pltpu.make_async_copy(layer_in.at[me], layer_out.at[me], local.at[14])
    layer_own.start()

    def whole(ref):
        def write(total):
            ref[...] = total

        return write

    def thirds(group):
        def write(total):
            for i, ref in enumerate((q_out, k_out, v_out)):
                ref[:, pl.ds(group * TILE, TILE)] = total[:, i * TILE : (i + 1) * TILE]

        return write

    parts = [(ReduceMid, g_2, whole(w2_out)), (ReduceMid, g_1, whole(w1_out)), (Reduce, g_o, whole(o_out))]
    parts += [(Reduce, g_qkv.at[i], thirds(i)) for i in range(GROUPS)]
    parts += [(Reduce, g_small, whole(small_out))]
    sums_2, sum_1, sum_o, *sum_qkv, sum_small = reduces = [
        kind(part, *split_scratch(i, rest), place, write) for i, (kind, part, write) in enumerate(parts)
    ]

    sums[...] = jnp.zeros_like(sums)
    sums1[...] = jnp.zeros_like(sums1)

    def tally(row, values):
        sums[row : row + 1, :] += jnp.sum(values, axis=0, keepdims=True)

    for copy in loads[:5]:
        copy.wait()
    rows = 128

    def norm_two(i, _):
        block = block_of(i, rows)
        select = (rows_of((grads.shape[0], rows)) == slots[:, block]).astype(BF16)
        grad_layer = dot_rows(select, grads[...])
        normed = grad[block, :]
        tally(6, grad_layer * normed)
        tally(7, grad_layer)
        back = norm_back(grad_layer * bias[6:7, :], normed, factors[block, 128:129])
        grad[block, :] = back
        second_low = back.astype(BF16)
        d_qkv[block, 0:feat] = second_low
        tally(5, second_low.astype(F32))
        return 0

    lax.fori_loop(0, length // rows, norm_two, 0)
    second = grads.at[pl.ds(0, length)]
    second[...] = d_qkv[:, 0:feat]
    loads[5].wait()

    def outer_grad(i, _):
        j = jnp.where(i == 1, 1, jnp.where(i == 2, 2, 3 - i))
        zi = z ^ j
        width = inner_width // 4
        part = dot_rows(act[:, block_of(zi, width)], second[...])
        g_2[zi] = part.astype(BF16).reshape(g_2.shape[1:])
        sums_2.send(j)
        for k in (1, 2, 3):
            pl.when(i == k)(in_order((sums_2.first, ORDER[k - 1])))
        return 0

    lax.fori_loop(0, 4, outer_grad, 0)
    sums_2.first(0)
    for copy in loads[6:9]:
        copy.wait()
    turned[...] = low[...].T
    under_inner = {8: [(sums_2.turn, 3)]}

    def inner_grad(i, _):
        block = block_of(i, TILE)
        up = dot_cols(second[...], wb[block, :])
        inner_low = (up * slope[:, block].astype(F32)).astype(BF16)
        slope[:, block] = inner_low
        sums1[0:1, block] = jnp.sum(inner_low.astype(F32), axis=0, keepdims=True)
        part = dot(turned[...], inner_low)
        g_1[:, :, :, :, :, block] = part.astype(BF16).reshape(g_1.shape[:-1] + (TILE,))
        for at, calls in under_inner.items():
            pl.when(i == at)(in_order(*calls))
        return 0

    lax.fori_loop(0, inner_width // TILE, inner_grad, 0)
    sum_1.send_all()
    slabs = [
        pltpu.make_async_copy(src, wb.at[pl.ds(i * feat, feat)], local.at[15 + i])
        for i, src in enumerate((w_o, w_q, w_k, w_v))
    ]
    for copy in slabs:
        copy.start()
    for copy in loads[9:]:
        copy.wait()

    def hidden_grad(i, _):
        half_width = feat // 2
        block = block_of(i, half_width)
        weight = w1[pl.ds(2 * i, 2)].reshape(half_width, inner_width)
        grad[:, block] += dot_cols(slope[...], weight)
        return 0

    lax.fori_loop(0, 2, hidden_grad, 0)
    in_order((sum_1.first, 3), (sum_1.first, 1), (sums_2.turn, 1))()
    first = second

    def norm_one(i, _):
        block = block_of(i, rows)
        up, normed = grad[block, :], normed1[block, :]
        tally(3, up * normed)
        tally(4, up)
        back = norm_back(up * bias[3:4, :], normed, factors[block, 0:1])
        grad[block, :] = back
        first_low = back.astype(BF16)
        first[block, :] = first_low
        tally(2, first_low.astype(F32))
        return 0

    lax.fori_loop(0, length // rows, norm_one, 0)
    in_order((sum_1.first, 2), (sum_1.first, 0), (sums_2.turn, 2), (sums_2.cross,))()
    for copy in slabs:
        copy.wait()
    g_o[...] = dot_rows(att[...], first[...]).astype(BF16).reshape(g_o.shape)
    sum_o.send_all()
    grad_att = grads.at[pl.ds(length, length)]

    def att_grad(i, _):
        block = block_of(i, rows)
        grad_att[block, :] = dot_cols(first[block, :], wb[0:feat, :]).astype(BF16)
        return 0

    lax.fori_loop(0, length // rows, att_grad, 0)
    turned[...] = x[...].T
    in_order((sums_2.turn, 0), (sum_o.first,))()
    scale = HEAD_DIM**-0.5

    def pair(p):
        start = pl.multiple_of(p * 128, 128)
        q = qkv[:, pl.ds(start, 128)] * jnp.asarray(scale, BF16)
        k = qkv[:, pl.ds(feat + start, 128)]
        v = qkv[:, pl.ds(2 * feat + start, 128)]
        g = grad_att[:, pl.ds(start, 128)]
        low_lane = lanes(q.shape) < HEAD_DIM
        results = []
        for h in (0, 1):
            keep = low_lane if h == 0 else ~low_lane
            zero = jnp.zeros_like(k)
            scores = jnp.where(live[...] > 0, dot_cols(jnp.where(keep, k, zero), q), NEG_FILL)
            probs = jnp.exp(scores - lse[pl.ds(2 * p + h, 1), :])
            up = dot_cols(jnp.where(keep, v, zero), g)
            inner_sum = jnp.sum(probs * up, axis=0, keepdims=True)
            grad_scores = (probs * (up - inner_sum)).astype(BF16)
            for at, calls in under.items():
                if at % 2 == h:
                    pl.when(p == at // 2)(in_order(*calls))
            results.append((dot_rows(k, grad_scores), dot(grad_scores, q), dot(probs.astype(BF16), g)))
        (q_0, k_0, v_0), (q_1, k_1, v_1) = results
        d_q = jnp.where(rows_of(q_0.shape) < HEAD_DIM, q_0, q_1) * scale
        d_qkv[:, pl.ds(start, 128)] = d_q.T.astype(BF16)
        d_qkv[:, pl.ds(feat + start, 128)] = jnp.where(low_lane, k_0, k_1).astype(BF16)
        d_qkv[:, pl.ds(2 * feat + start, 128)] = jnp.where(low_lane, v_0, v_1).astype(BF16)

    under = {
        4: [(sums_2.fold,)],
        5: [(sum_1.turn, 3), (sum_qkv[0].first,)],
        8: [(sums_2.last,), (sum_1.turn, 1)],
        9: [(sum_qkv[1].first,)],
        10: [(sum_1.turn, 2), (sum_1.cross,)],
    }

    def group(i, _):
        def one(j, _):
            pair(2 * i + j)
            return 0

        lax.fori_loop(0, 2, one, 0)
        for t in range(3):
            cols = pl.ds(pl.multiple_of(t * feat + i * TILE, TILE), TILE)
            part = dot(turned[...], d_qkv[:, cols])
            g_qkv[i, :, :, :, :, :, pl.ds(t * TILE, TILE)] = part.astype(BF16).reshape(
                g_qkv.shape[1:-1] + (TILE,)
            )
        for at in range(GROUPS):
            pl.when(i == at)(sum_qkv[at].send_all)
        return 0

    lax.fori_loop(0, GROUPS, group, 0)
    thirds_0, thirds_1, thirds_2 = sum_qkv
    sum_1.turn(0)
    tally(0, d_qkv[:, 0:feat].astype(F32))
    tally(1, d_qkv[:, 2 * feat : 3 * feat].astype(F32))
    thirds_2.first()
    in_order((sum_1.fold,), (sum_o.along_z,))()
    grad_tokens = x.reshape(4, length // 4, feat)
    token_copies = [page_copy(grad_tokens, tokens_out, ts, tr, j) for j in range(3)]
    token_own = pltpu.make_async_copy(grad_tokens.at[me], tokens_out.at[me], local.at[19])

    def token_grad(i, _):
        block = block_of(me ^ (3 - i), length // 4)
        total = grad[block, :]
        for t in range(3):
            total += dot_cols(
                d_qkv[block, t * feat : (t + 1) * feat], wb[(t + 1) * feat : (t + 2) * feat, :]
            )
        x[block, :] = total.astype(BF16)
        for j in range(3):
            pl.when(i == 2 - j)(in_order((token_copies[j].start,)))
        return 0

    lax.fori_loop(0, 4, token_grad, 0)
    g_small[:, :, :, :, 0:8, :] = pack_rows(sums[...], feat // 32, 32).reshape(4, 2, 2, 2, 8, 128)
    for i in range(4):
        part = sums1[:, i * (inner_width // 4) : (i + 1) * (inner_width // 4)]
        g_small[i, :, :, :, 8:16, :] = pack_rows(part, inner_width // 32, 8).reshape(2, 2, 2, 8, 128)
    sum_small.send_all()
    token_own.start()
    in_order(
        (sum_small.first,),
        (thirds_0.along_z,),
        (thirds_1.along_z,),
        (sum_1.last,),
        (sum_o.last,),
        (sum_small.along_z,),
        (thirds_2.along_z,),
        (thirds_0.last,),
        (thirds_1.last,),
        (sum_small.last,),
        (thirds_2.last,),
    )()
    for copy in layer_copies + token_copies:
        copy.wait()
    layer_own.wait()
    token_own.wait()
    for one in reduces:
        one.finish()


def backward(saved, weights, grad_pages, layer_slots, slots, live, tokens_shape):
    w_q, w_1, w_2 = weights[0], weights[4], weights[5]
    qkv, lse, x, att, normed1, low, act, slope, normed2, factors, bias = saved
    length, feat = low.shape
    inner_width = act.shape[1]
    anywhere = pl.BlockSpec(memory_space=pl.ANY)
    vmem = pl.BlockSpec(memory_space=pltpu.VMEM)
    grid = (4, 2, 2, 2)
    small, inner, outer = (feat // 32, feat), (feat // 32, inner_width), (inner_width // 32, feat)
    sizes = [outer, inner] + [small] * 4 + [(16, 128)]
    scratch = [
        ((length, 3 * feat), BF16),
        ((length, feat), BF16),
        ((length, feat), BF16),
        ((length, feat), F32),
        ((length, feat), BF16),
        ((length, inner_width), BF16),
        ((length, inner_width), BF16),
        ((length, feat), F32),
        ((grad_pages.shape[0] * grad_pages.shape[1], feat), BF16),
        (grid + inner, BF16),
        ((inner_width, feat), BF16),
        ((feat, length), BF16),
        ((length, 3 * feat), BF16),
        (grid + outer, BF16),
        (grid + inner, BF16),
        (grid + small, BF16),
        ((GROUPS,) + grid + small, BF16),
        (grid + (16, 128), BF16),
        ((8, feat), F32),
        ((8, inner_width), F32),
    ]
    bufs, sems = [], []
    for i, size in enumerate(sizes):
        bufs += reduce_mid_bufs(*size) if i < 2 else reduce_bufs(*size)
        sems += reduce_mid_sems() if i < 2 else reduce_sems()
    outs = [(grad_pages.shape, BF16, anywhere), (tokens_shape, BF16, anywhere)]
    outs += [(small, F32, vmem)] * 4 + [(inner, F32, vmem), (outer, F32, vmem), ((16, 128), F32, vmem)]
    return pl.pallas_call(
        backward_kernel,
        out_shape=[jax.ShapeDtypeStruct(shape, kind) for shape, kind, _ in outs],
        in_specs=[anywhere, vmem] + [anywhere] * 7 + [vmem, vmem] + [anywhere] * 8 + [vmem, vmem],
        out_specs=[spec for _, _, spec in outs],
        scratch_shapes=[pltpu.VMEM(shape, kind) for shape, kind in scratch]
        + [DMA((20,)), DMA((3,)), DMA((3,)), DMA((3,)), DMA((3,))]
        + bufs
        + sems,
        compiler_params=pltpu.CompilerParams(
            collective_id=1, has_side_effects=True, vmem_limit_bytes=VMEM_LIMIT
        ),
        name="backward",
    )(*saved, *weights, grad_pages, layer_slots, slots, live)


LARGE = (0, 2, 3, 5, 9, 11)
SMALL_ORDER = (1, 4, 6, 7, 8, 12, 13, 14, 10)


def finish_kernel(count, sizes, *refs):
    ins, small, outs = refs[:count], refs[count], refs[count + 1 : 2 * count + 1]
    vectors, stages, sems = refs[2 * count + 1 :][: len(sizes)], refs[-count - 1 : -1], refs[-1]
    inward = [pltpu.make_async_copy(i, s, sems.at[0, n]) for n, (i, s) in enumerate(zip(ins, stages))]
    outward = [pltpu.make_async_copy(s, o, sems.at[1, n]) for n, (s, o) in enumerate(zip(stages, outs))]
    for copy in inward:
        copy.start()
    for row, (size, ref) in enumerate(zip(sizes, vectors)):
        ref[...] = small[row : row + 1, 0:size].reshape(size)
    for first, second in zip(inward, outward):
        first.wait()
        second.start()
    for copy in outward:
        copy.wait()


def finish(arrays, small, sizes):
    count = len(arrays)
    anywhere = pl.BlockSpec(memory_space=pl.ANY)
    vmem = pl.BlockSpec(memory_space=pltpu.VMEM)

    def body(*refs):
        finish_kernel(count, sizes, *refs)

    return pl.pallas_call(
        body,
        out_shape=[jax.ShapeDtypeStruct(a.shape, a.dtype) for a in arrays]
        + [jax.ShapeDtypeStruct((size,), F32) for size in sizes],
        in_specs=[anywhere] * count + [vmem],
        out_specs=[anywhere] * count + [vmem] * len(sizes),
        scratch_shapes=[pltpu.VMEM(a.shape, a.dtype) for a in arrays] + [DMA((2, count))],
        compiler_params=pltpu.CompilerParams(vmem_limit_bytes=VMEM_LIMIT),
        name="finish",
    )(*arrays, small)


def by_kernels(tokens, band_ids, page_mask, weights, grad_output):
    large = [weights[i] for i in LARGE]
    vectors = [weights[i] for i in SMALL_ORDER]
    got = forward(vectors, tokens, grad_output, band_ids, page_mask, *large)
    saved, full, (grad_slots, layer_slots, slots, live) = got[:11], got[11:17], got[17:]
    full = [w if i == 4 else w.reshape(-1, w.shape[-1]) for i, w in enumerate(full)]
    sums = backward(saved, full, grad_slots, layer_slots, slots, live, tokens.shape)
    results = finish(sums[:8], sums[8], [v.shape[0] for v in vectors])
    grads = dict(zip(LARGE + SMALL_ORDER, results[2:]))
    return tuple(results[:2]) + tuple(grads[i] for i in range(len(weights)))


def per_device(hand_made, *args):
    tokens, band_ids, band_counts, page_mask = args[:4]
    weights, grad_output = args[4:19], args[19]
    if hand_made:
        return by_kernels(tokens, band_ids, page_mask, weights, grad_output)
    bands = lax.axis_size("band")
    slot_cap = grad_output.shape[1]
    pages = tokens.shape[0] // bands
    full = [lax.all_gather(w, BOTH, axis=0, tiled=True) for w in weights]
    first = lax.axis_index("band") * pages
    ids = lax.dynamic_slice_in_dim(band_ids, first, pages, 0)
    live = lax.dynamic_slice_in_dim(page_mask, first, pages, 0) > 0
    slots = page_slots(ids, bands, slot_cap)
    layer_slots, grad_in, grads = layer_pages(
        to_pages(tokens), slots, live, to_pages(grad_output), full
    )
    return (from_pages(layer_slots), from_pages(grad_in)) + tuple(
        lax.psum_scatter(g, BOTH, scatter_dimension=0, tiled=True) for g in grads
    )


def solution(mesh):
    hand_made = dict(mesh.shape) == {"page": 8, "band": 4}
    shard = P(BOTH)
    rows = P(BOTH, None)
    tokens = P("page", "band", None)
    page = P("page", None)
    weights = (rows, shard, rows, rows, shard, rows, shard, shard, shard)
    weights = weights + (rows, shard, rows, shard, shard, shard)

    def step(*args):
        return per_device(hand_made, *args)

    return jax.shard_map(
        step,
        mesh=mesh,
        in_specs=(tokens, page, page, page) + weights + (tokens,),
        out_specs=(tokens, tokens) + weights,
        check_vma=False,
    )
```

```python
import jax
import jax.numpy as jnp
from jax import lax
from jax.experimental import pallas as pl
from jax.experimental.pallas import tpu as pltpu
from jax.sharding import PartitionSpec as P

HEAD_DIM = 64
LN_EPS = 1e-12
NEG_FILL = -1e30
MESH = pl.DeviceIdType.MESH
DMA = pltpu.SemaphoreType.DMA
F32 = jnp.float32
BF16 = jnp.bfloat16
BOTH = ("page", "band")
VMEM_LIMIT = 62 * 2**20


def my_place():
    page, band = lax.axis_index("page"), lax.axis_index("band")
    return page // 2, page % 2, band // 2, band % 2


def dev(z, x, y, c):
    return (z * 2 + x, y * 2 + c)


def remote(src, dst, send_sem, recv_sem, place):
    return pltpu.make_async_remote_copy(
        src_ref=src,
        dst_ref=dst,
        send_sem=send_sem,
        recv_sem=recv_sem,
        device_id=dev(*place),
        device_id_type=MESH,
    )


def meet(places):
    barrier = pltpu.get_barrier_semaphore()
    for place in places:
        pl.semaphore_signal(barrier, inc=1, device_id=dev(*place), device_id_type=MESH)
    pl.semaphore_wait(barrier, len(places))


def grid_peers(z, x, y, c):
    return [((z + j) % 4, x, y, c) for j in (1, 2, 3)] + [
        (z, 1 - x, y, c),
        (z, x, 1 - y, c),
        (z, x, y, 1 - c),
    ]


def half(ref, which):
    rows, width = ref.shape[-2] // 2, ref.shape[-1] // 2
    if width % 128:
        return ref.at[..., pl.ds(which * rows, rows), :]
    return ref.at[..., pl.ds(which * width, width)]


def norm_rows(values):
    center = values - jnp.mean(values, axis=-1, keepdims=True)
    factor = lax.rsqrt(jnp.mean(center * center, axis=-1, keepdims=True) + LN_EPS)
    return (center * factor, factor)


def norm_back(upstream, normed, factor):
    return factor * (
        upstream
        - jnp.mean(upstream, axis=-1, keepdims=True)
        - normed * jnp.mean(upstream * normed, axis=-1, keepdims=True)
    )


def dot(first, second):
    return jnp.dot(first, second, preferred_element_type=F32)


def dot_rows(first, second):
    return lax.dot_general(first, second, (((0,), (0,)), ((), ())), preferred_element_type=F32)


def dot_cols(first, second):
    return lax.dot_general(first, second, (((1,), (1,)), ((), ())), preferred_element_type=F32)


def page_slots(ids, bands, slot_cap):
    onehot = (ids[:, :, None] == jnp.arange(bands, dtype=jnp.int32)).astype(F32)
    length = ids.shape[1]
    before = (jnp.arange(length)[:, None] > jnp.arange(length)[None, :]).astype(F32)
    counts = jnp.einsum("tu,pub->ptb", before, onehot, preferred_element_type=F32)
    rank = jnp.sum(onehot * counts, axis=2).astype(jnp.int32)
    return ids * slot_cap + rank


def layer_pages(rows_in, slots, live, grad_slots, weights):
    (wq, bq, wk, wv, bv, wo, bo, g1, s1, w1, b1, w2, b2, g2, s2) = weights
    pages, length, feat = rows_in.shape
    heads = feat // HEAD_DIM
    scale = HEAD_DIM**-0.5
    x_low = rows_in.reshape(-1, feat)
    select = (slots[:, None, :] == jnp.arange(grad_slots.shape[1])[None, :, None]).astype(BF16)
    grad_layer = jnp.einsum("pst,psd->ptd", select, grad_slots, preferred_element_type=F32)
    grad_layer = grad_layer.reshape(-1, feat)

    def split(flat):
        return flat.reshape(pages, length, heads, HEAD_DIM)

    query = split((dot(x_low, wq) + bq).astype(BF16))
    key = split(dot(x_low, wk).astype(BF16))
    value = split((dot(x_low, wv) + bv).astype(BF16))
    scores = jnp.einsum("pthd,puhd->phtu", query, key, preferred_element_type=F32) * scale
    scores = jnp.where(live[:, None, None, :], scores, NEG_FILL)
    shifted = jnp.exp(scores - jnp.max(scores, axis=-1, keepdims=True))
    probs = shifted / jnp.sum(shifted, axis=-1, keepdims=True)
    probs_low = probs.astype(BF16)
    mixed = jnp.einsum("phtu,puhd->pthd", probs_low, value, preferred_element_type=F32)
    attended = mixed.astype(BF16).reshape(-1, feat)
    normed_one, factor_one = norm_rows(x_low.astype(F32) + dot(attended, wo) + bo)
    hidden = normed_one * g1 + s1
    hidden_low = hidden.astype(BF16)
    inner = dot(hidden_low, w1) + b1
    cdf = 0.5 * (1.0 + lax.erf(inner * (0.5**0.5)))
    act_low = (inner * cdf).astype(BF16)
    slope = cdf + inner * jnp.exp(-0.5 * inner * inner) * ((0.5 / jnp.pi) ** 0.5)
    normed_two, factor_two = norm_rows(hidden + dot(act_low, w2) + b2)
    layer = (normed_two * g2 + s2).astype(BF16).reshape(pages, length, feat)
    layer_slots = jnp.einsum("pst,ptd->psd", select, layer, preferred_element_type=F32).astype(BF16)

    grad_g2 = jnp.sum(grad_layer * normed_two, axis=0)
    grad_s2 = jnp.sum(grad_layer, axis=0)
    grad_second = norm_back(grad_layer * g2, normed_two, factor_two)
    second_low = grad_second.astype(BF16)
    grad_w2 = dot_rows(act_low, second_low)
    grad_b2 = jnp.sum(second_low.astype(F32), axis=0)
    inner_low = (dot_cols(second_low, w2) * slope).astype(BF16)
    grad_w1 = dot_rows(hidden_low, inner_low)
    grad_b1 = jnp.sum(inner_low.astype(F32), axis=0)
    grad_hidden = grad_second + dot_cols(inner_low, w1)
    grad_g1 = jnp.sum(grad_hidden * normed_one, axis=0)
    grad_s1 = jnp.sum(grad_hidden, axis=0)
    grad_first = norm_back(grad_hidden * g1, normed_one, factor_one)
    first_low = grad_first.astype(BF16)
    grad_wo = dot_rows(attended, first_low)
    grad_bo = jnp.sum(first_low.astype(F32), axis=0)
    grad_att = split(dot_cols(first_low, wo).astype(BF16))
    grad_probs = jnp.einsum("pthd,puhd->phtu", grad_att, value, preferred_element_type=F32)
    inner_sum = jnp.sum(probs * grad_probs, axis=-1, keepdims=True)
    grad_scores = (probs * (grad_probs - inner_sum)).astype(BF16)

    def flat(per_head, factor):
        return (per_head * factor).astype(BF16).reshape(-1, feat)

    ein = lambda form, a, b: jnp.einsum(form, a, b, preferred_element_type=F32)
    grad_q = flat(ein("phtu,puhd->pthd", grad_scores, key), scale)
    grad_k = flat(ein("phtu,pthd->puhd", grad_scores, query), scale)
    grad_v = flat(ein("phtu,pthd->puhd", probs_low, grad_att), 1.0)
    grad_wq, grad_wk, grad_wv = (dot_rows(x_low, g) for g in (grad_q, grad_k, grad_v))
    grad_bq = jnp.sum(grad_q.astype(F32), axis=0)
    grad_bv = jnp.sum(grad_v.astype(F32), axis=0)
    grad_in = grad_first + dot_cols(grad_q, wq) + dot_cols(grad_k, wk) + dot_cols(grad_v, wv)
    grad_in = grad_in.astype(BF16).reshape(pages, length, feat)
    return (
        layer_slots,
        grad_in,
        (grad_wq, grad_bq, grad_wk, grad_wv, grad_bv, grad_wo, grad_bo, grad_g1, grad_s1)
        + (grad_w1, grad_b1, grad_w2, grad_b2, grad_g2, grad_s2),
    )


def to_pages(blocks):
    return lax.all_to_all(blocks, "band", split_axis=0, concat_axis=1, tiled=True)


def from_pages(blocks):
    return lax.all_to_all(blocks, "band", split_axis=1, concat_axis=0, tiled=True)


def split_ref(ref, which):
    rows, width = ref.shape[-2:]
    cut = width // 3
    if cut % 128:
        return ref.at[..., pl.ds(which * (rows // 2), rows // 2), :]
    return ref.at[..., pl.ds(which * cut, (cut, width - cut)[which])]


def in_order(*calls):
    def step():
        for method, *index in calls:
            method(*index)

    return step


class Gather:
    def __init__(self, own, buf, sems, place):
        self.own, self.buf, self.place = own, buf, place
        self.zs, self.zr, self.ss, self.sr, self.fs, self.fr, self.cs, self.cr = sems

    def z_copy(self, j):
        z, x, y, c = self.place
        there = (z ^ (j + 1), x, y, c)
        return remote(self.own, self.buf.at[z, x, y, c], self.zs.at[j], self.zr.at[j], there)

    def side_copy(self, j, axis):
        z, x, y, c = self.place
        part = self.buf.at[z ^ j, x, y, c]
        there = (z, 1 - x, y, c) if axis == 0 else (z, x, 1 - y, c)
        source = self.own if j == 0 else part
        return remote(source, part, self.ss.at[axis, j], self.sr.at[axis, j], there)

    def far_copy(self, j, axis):
        z, x, y, c = self.place
        if axis == 0:
            part, there = self.buf.at[z ^ j, 1 - x, y, c], (z, x, 1 - y, c)
        else:
            part, there = self.buf.at[z ^ j, x, 1 - y, c], (z, 1 - x, y, c)
        part = split_ref(part, axis)
        return remote(part, part, self.fs.at[axis, j], self.fr.at[axis, j], there)

    def core_copy(self, k):
        z, x, y, c = self.place
        part = self.buf.at[:, (x, 1 - x, x, 1 - x)[k], (y, y, 1 - y, 1 - y)[k], c]
        return remote(part, part, self.cs.at[k], self.cr.at[k], (z, x, y, 1 - c))

    def start(self):
        for j in range(3):
            self.z_copy(j).start()
        for axis in (0, 1):
            self.side_copy(0, axis).start()

    def side(self, j):
        self.z_copy(j - 1).wait_recv()
        for axis in (0, 1):
            self.side_copy(j, axis).start()

    def far(self, j):
        for axis in (0, 1):
            self.side_copy(j, axis).wait_recv()
            self.far_copy(j, axis).start()

    def core(self, k):
        if k == 3:
            for j in range(4):
                for axis in (0, 1):
                    self.far_copy(j, axis).wait_recv()
        self.core_copy(k).start()

    def steps(self):
        side, far, core = self.side, self.far, self.core
        return [
            in_order((side, 1)),
            in_order((far, 0)),
            in_order((side, 2)),
            in_order((side, 3), (core, 0)),
            in_order((far, 1)),
            in_order((far, 2)),
            in_order((far, 3), (core, 1), (core, 2)),
            in_order((core, 3)),
        ]

    def arrive(self):
        for k in range(4):
            self.core_copy(k).wait_recv()

    def finish(self):
        for j in range(3):
            self.z_copy(j).wait_send()
        for j in range(4):
            for axis in (0, 1):
                self.side_copy(j, axis).wait_send()
                self.far_copy(j, axis).wait_send()
            self.core_copy(j).wait_send()


def gather_sems():
    return [DMA((3,)), DMA((3,))] + [DMA((2, 4))] * 4 + [DMA((4,))] * 2


def split_mid(ref, which):
    width = ref.shape[-1]
    cut = width // 640 * 128
    return ref.at[..., pl.ds(which * cut, (cut, width - cut)[which])]


class GatherMid:
    def __init__(self, own, buf, sems, place):
        self.own, self.buf, self.place = own, buf, place
        self.zs, self.zr, self.ss, self.sr, self.hs, self.hr, self.fs, self.fr, self.cs, self.cr = sems

    def z_copy(self, j):
        z, x, y, c = self.place
        zi = z ^ (2 if j == 3 else 0)
        source = self.buf.at[zi, x, y, c] if j == 3 else self.own
        there = (z ^ (2 if j == 2 else 1), x, y, c)
        return remote(source, self.buf.at[zi, x, y, c], self.zs.at[j - 1], self.zr.at[j - 1], there)

    def side_copy(self, axis):
        z, x, y, c = self.place
        there = (z, 1 - x, y, c) if axis == 0 else (z, x, 1 - y, c)
        source = split_mid(self.own, axis)
        return remote(source, split_mid(self.buf.at[z, x, y, c], axis), self.ss.at[axis], self.sr.at[axis], there)

    def half_copy(self, j, axis):
        z, x, y, c = self.place
        zi = z ^ (2 if j == 3 else 0)
        part = self.buf.at[zi, 1 - x, y, c] if axis == 0 else self.buf.at[zi, x, 1 - y, c]
        part = split_mid(part, axis)
        there = (z ^ (2 if j == 2 else 1), x, y, c)
        return remote(part, part, self.hs.at[axis, j - 1], self.hr.at[axis, j - 1], there)

    def far_copy(self, j, axis):
        z, x, y, c = self.place
        if axis == 0:
            part, there = self.buf.at[z ^ j, :, y, c], (z, x, 1 - y, c)
        else:
            part, there = self.buf.at[z ^ j, x, :, c], (z, 1 - x, y, c)
        part = split_mid(part, axis)
        return remote(part, part, self.fs.at[axis, j], self.fr.at[axis, j], there)

    def core_copy(self, j):
        z, x, y, c = self.place
        part = self.buf.at[z ^ j, :, :, c]
        return remote(part, part, self.cs.at[j], self.cr.at[j], (z, x, y, 1 - c))

    def start(self):
        for axis in (0, 1):
            self.side_copy(axis).start()
        for j in (2, 1):
            self.z_copy(j).start()

    def turn(self):
        for axis in (0, 1):
            self.side_copy(axis).wait_recv()
            for j in (2, 1):
                self.half_copy(j, axis).start()
        for axis in (0, 1):
            self.far_copy(0, axis).start()

    def far(self, j):
        self.z_copy(j).wait_recv()
        if j == 2:
            self.z_copy(3).start()
        for axis in (0, 1):
            self.half_copy(j, axis).wait_recv()
            if j == 2:
                self.half_copy(3, axis).start()
            self.far_copy(j, axis).start()

    def core(self, j):
        for axis in (0, 1):
            self.far_copy(j, axis).wait_recv()
        self.core_copy(j).start()

    def steps(self):
        far, core = self.far, self.core
        return [
            in_order((self.turn,)),
            in_order((far, 2)),
            in_order((far, 1)),
            in_order((far, 3)),
            in_order((core, 0)),
            in_order((core, 2)),
            in_order((core, 1)),
            in_order((core, 3)),
        ]

    def arrive(self):
        for k in range(4):
            self.core_copy(k).wait_recv()

    def finish(self):
        for axis in (0, 1):
            self.side_copy(axis).wait_send()
        for j in (1, 2, 3):
            self.z_copy(j).wait_send()
            for axis in (0, 1):
                self.half_copy(j, axis).wait_send()
        for j in range(4):
            for axis in (0, 1):
                self.far_copy(j, axis).wait_send()
            self.core_copy(j).wait_send()


def mid_sems():
    return [DMA((3,))] * 2 + [DMA((2,))] * 2 + [DMA((2, 3))] * 2 + [DMA((2, 4))] * 2 + [DMA((4,))] * 2


def lanes(shape):
    return lax.broadcasted_iota(jnp.int32, shape, len(shape) - 1)


def rows_of(shape):
    return lax.broadcasted_iota(jnp.int32, shape, len(shape) - 2)


def columns(buf, start, width):
    return buf[:, :, :, :, :, pl.ds(start, width)].reshape(-1, width)


def unpack_rows(block, per_shard, width):
    shards, count, _ = block.shape
    spread = (rows_of((128, width)) == lanes((128, width)) % per_shard).astype(BF16)
    wide = dot(block.reshape(-1, 128), spread).reshape(shards, count, width)
    owner = lax.broadcasted_iota(jnp.int32, wide.shape, 0) == lanes(wide.shape) // per_shard
    return jnp.sum(jnp.where(owner, wide, 0.0), axis=0)


def pack_rows(rows, per_shard, shards):
    count, width = rows.shape
    wide = jnp.broadcast_to(rows[None], (shards, count, width))
    owner = lax.broadcasted_iota(jnp.int32, wide.shape, 0) == lanes(wide.shape) // per_shard
    wide = jnp.where(owner, wide, 0.0).astype(BF16).reshape(-1, width)
    spread = (lanes((width, 128)) == rows_of((width, 128)) % per_shard).astype(BF16)
    return dot(wide, spread).astype(BF16).reshape(shards, count, 128)


def block_of(i, size):
    return pl.ds(pl.multiple_of(i * size, size), size)


def gelu_parts(v):
    cdf = 0.5 * (1.0 + lax.erf(v * (0.5**0.5)))
    return v * cdf, cdf + v * jnp.exp(-0.5 * v * v) * ((0.5 / jnp.pi) ** 0.5)


class Out:
    def __init__(self, sems):
        self.sems, self.copies = sems, []

    def send(self, src, dst):
        copy = pltpu.make_async_copy(src, dst, self.sems.at[len(self.copies)])
        copy.start()
        self.copies.append(copy)

    def wait(self):
        for copy in self.copies:
            copy.wait()


BIAS_ROWS = 8
TILE = 256


def forward_kernel(*refs):
    vector_refs, refs = refs[: BIAS_ROWS + 1], refs[BIAS_ROWS + 1 :]
    tokens, grads, ids, mask, w_q, w_k, w_v, w_o, w_1, w_2 = refs[:10]
    qkv_out, lse, x_out, att_out, normed1_out, low_out, act_out, slope_out, normed2_out = refs[10:19]
    factors, bias, q_out, k_out, v_out, o_out, w1_out, w2_out, grad_pages, layer_slots, slots, live = refs[19:31]
    small, small_own, a_buf, w1_buf, w2_buf, x_buf, qkv, att, normed1, low, act, slope = refs[31:43]
    second, normed2, layer, bias1, local, ts, tr, gs, gr, outs, *sems = refs[43:]
    place = z, x, y, c = my_place()
    me = y * 2 + c
    length, feat = low.shape
    pairs = feat // 128
    x_rows = x_buf.reshape(length, feat)
    here = (z, x, y, c)
    copies = [
        pltpu.make_async_copy(src, dst, local.at[i])
        for i, (src, dst) in enumerate(
            [(w, a_buf.at[here + (slice(None), pl.ds(i * feat, feat))]) for i, w in enumerate((w_q, w_k, w_v, w_o))]
            + [(w_1, w1_buf.at[here]), (w_2, w2_buf.at[here])]
            + [(tokens.at[me], x_buf.at[me]), (grads.at[me], grad_pages.at[me])]
        )
    ]
    for copy in copies:
        copy.start()
    small_own[...] = jnp.zeros_like(small_own)
    for row, ref in enumerate(vector_refs):
        size = ref.shape[0]
        small_own[row : row + 1, 0:size] = ref[...].astype(F32).reshape(1, size)
    small[here] = small_own[...].astype(BF16)
    meet(
        [(z ^ j, x, y, c) for j in (1, 2, 3)]
        + [(z, 1 - x, y, c), (z, x, 1 - y, c), (z, x, y, 1 - c), (z, x, 1 - y, 1 - c)]
    )

    def page_copy(src, dst, send, recv, j):
        there = me ^ (j + 1)
        return remote(src.at[there], dst.at[me], send.at[j], recv.at[j], (z, x, there // 2, there % 2))

    token_copies = [page_copy(tokens, x_buf, ts, tr, j) for j in range(3)]
    grad_copies = [page_copy(grads, grad_pages, gs, gr, j) for j in range(3)]
    gathers = [
        kind(own, buf, sems[(0, 8, 16, 26)[i] :][: 8 if kind is Gather else 10], place)
        for i, (kind, own, buf) in enumerate(
            [(Gather, small.at[here], small), (Gather, a_buf.at[here], a_buf)]
            + [(GatherMid, w_1, w1_buf), (GatherMid, w_2, w2_buf)]
        )
    ]
    vectors, atts, inner, outer = gathers
    for copy in copies[:4]:
        copy.wait()
    atts.start()
    vectors.start()
    for copy in token_copies:
        copy.start()
    slot_cap = grads.shape[1]
    hot = (rows_of((8, length)) == ids[pl.ds(me, 1), :]).astype(F32)
    earlier = (rows_of((length, length)) < lanes((length, length))).astype(BF16)
    rank = dot(hot.astype(BF16), earlier) + (rows_of((8, length)) * slot_cap).astype(F32)
    slots[...] = jnp.sum(hot * rank, axis=0, keepdims=True).astype(jnp.int32)
    live[...] = jnp.broadcast_to(mask[pl.ds(me, 1), :].astype(F32), (8, length)).T[:, 0:1]
    steps_0, steps_1, steps_2 = atts.steps(), inner.steps(), outer.steps()
    own = in_order(*[(copy.wait,) for copy in copies[4:6]])
    behind = {1: [inner.start], 3: [own, steps_1[0]], 4: [outer.start], 6: [steps_1[1]]}
    for i, (main, extra) in enumerate(zip(steps_0, vectors.steps())):
        main()
        extra()
        for step in behind.get(i, ()):
            step()
    for copy in copies[6:]:
        copy.wait()
    for copy in grad_copies:
        copy.start()
    vectors.arrive()
    shards = small[...].reshape(32, 16, 128)
    bias[...] = unpack_rows(shards[:, :8], feat // 32, feat)
    inner_width = act.shape[1]
    for i in range(4):
        part = unpack_rows(small[i].reshape(8, 16, 128)[:, 8:], inner_width // 32, inner_width // 4)
        bias1[:, i * (inner_width // 4) : (i + 1) * (inner_width // 4)] = part
    for copy in token_copies:
        copy.wait_recv()
    atts.arrive()
    out = Out(outs)
    for i, ref in enumerate((q_out, k_out, v_out, o_out)):
        out.send(a_buf.at[:, :, :, :, :, pl.ds(i * feat, feat)], ref)
    out.send(x_rows, x_out)
    steps_1[2]()

    def project(j, _):
        start = pl.multiple_of(j * TILE, TILE)
        total = dot(x_rows[...], columns(a_buf, start, TILE))
        which = j // (feat // TILE)
        inside = block_of(j % (feat // TILE), TILE)
        row = jnp.where(which == 0, bias[0:1, inside], jnp.where(which == 2, bias[1:2, inside], 0.0))
        qkv[:, pl.ds(start, TILE)] = (total + row).astype(BF16)
        return 0

    lax.fori_loop(0, 3 * feat // TILE, project, 0)
    out.send(qkv, qkv_out)
    steps_2[0]()
    under = {3: steps_1[3], 5: steps_2[1], 8: steps_1[4], 9: steps_2[2], 10: steps_1[5], 11: steps_1[6]}
    scale = HEAD_DIM**-0.5

    def pair(p, _):
        start = pl.multiple_of(p * 128, 128)
        q = qkv[:, pl.ds(start, 128)] * jnp.asarray(scale, BF16)
        k = qkv[:, pl.ds(feat + start, 128)]
        v = qkv[:, pl.ds(2 * feat + start, 128)]
        low_lane = lanes(q.shape) < HEAD_DIM
        mixed = []
        for h in (0, 1):
            part = jnp.where(low_lane if h == 0 else ~low_lane, k, jnp.zeros_like(k))
            scores = jnp.where(live[...] > 0, dot_cols(part, q), NEG_FILL)
            top = jnp.max(scores, axis=0, keepdims=True)
            shifted = jnp.exp(scores - top)
            total = jnp.sum(shifted, axis=0, keepdims=True)
            probs = (shifted * (1.0 / total)).astype(BF16)
            mixed.append(dot_rows(v, probs))
            lse[pl.ds(2 * p + h, 1), :] = top + jnp.log(total)
            for at, step in under.items():
                if at % 2 == h:
                    pl.when(p == at // 2)(step)
        both = jnp.where(rows_of(mixed[0].shape) < HEAD_DIM, mixed[0], mixed[1])
        att[:, pl.ds(start, 128)] = both.T.astype(BF16)
        return 0

    lax.fori_loop(0, pairs, pair, 0)
    out.send(att, att_out)
    steps_1[7]()
    steps_2[3]()
    rows = 128

    def norm_one(i, _):
        block = block_of(i, rows)
        total = dot(att[block, :], columns(a_buf, 3 * feat, feat))
        total = total + x_rows[block, :].astype(F32) + bias[2:3, :]
        normed, factor = norm_rows(total)
        normed1[block, :] = normed
        factors[block, 0:128] = jnp.broadcast_to(factor, (rows, 128))
        low[block, :] = (normed * bias[3:4, :] + bias[4:5, :]).astype(BF16)
        return 0

    lax.fori_loop(0, length // rows, norm_one, 0)
    out.send(normed1, normed1_out)
    out.send(low, low_out)
    inner.arrive()
    out.send(w1_buf, w1_out)

    def ffn_in(j, _):
        block = block_of(j, TILE)
        value, grad = gelu_parts(dot(low[...], columns(w1_buf, block.start, TILE)) + bias1[0:1, block])
        act[:, block] = value.astype(BF16)
        slope[:, block] = grad.astype(BF16)
        return 0

    lax.fori_loop(0, inner_width // TILE, ffn_in, 0)
    out.send(act, act_out)
    out.send(slope, slope_out)
    chunk = inner_width // 4

    def add_chunk(j):
        outer.core_copy(j).wait_recv()
        zi = z ^ j

        def part(i, _):
            block = block_of(i, TILE)
            more = dot(act[:, block_of(zi, chunk)], w2_buf[zi, :, :, :, :, block].reshape(chunk, TILE))
            second[:, block] = more if j == 0 else second[:, block] + more
            return 0

        lax.fori_loop(0, feat // TILE, part, 0)

    steps_2[4]()
    steps_2[5]()
    add_chunk(0)
    steps_2[6]()
    add_chunk(2)
    steps_2[7]()
    add_chunk(1)
    add_chunk(3)
    out.send(w2_buf, w2_out)

    def norm_two(i, _):
        block = block_of(i, rows)
        hidden = normed1[block, :] * bias[3:4, :] + bias[4:5, :]
        normed, factor = norm_rows(hidden + second[block, :] + bias[5:6, :])
        normed2[block, :] = normed
        factors[block, 128:256] = jnp.broadcast_to(factor, (rows, 128))
        layer[block, :] = (normed * bias[6:7, :] + bias[7:8, :]).astype(BF16)
        return 0

    lax.fori_loop(0, length // rows, norm_two, 0)
    out.send(normed2, normed2_out)

    def place_rows(i, _):
        cap = layer_slots.shape[1]
        here_rows = rows_of((cap, length)) + i * cap
        select = (here_rows == slots[...]).astype(BF16)
        layer_slots[i] = dot(select, layer[...]).astype(BF16)
        return 0

    lax.fori_loop(0, layer_slots.shape[0], place_rows, 0)
    for copy in grad_copies:
        copy.wait_recv()
    for copy in grad_copies + token_copies:
        copy.wait_send()
    for one in gathers:
        one.finish()
    out.wait()


def forward(vectors, tokens, grads, ids, mask, w_q, w_k, w_v, w_o, w_1, w_2):
    length, feat, inner_width = ids.shape[1], tokens.shape[-1], w_1.shape[1]
    anywhere = pl.BlockSpec(memory_space=pl.ANY)
    vmem = pl.BlockSpec(memory_space=pltpu.VMEM)
    grid = (4, 2, 2, 2)
    heads = feat // HEAD_DIM
    results = [
        ((length, 3 * feat), BF16, anywhere),
        ((heads + -heads % 8, length), F32, vmem),
        ((length, feat), BF16, anywhere),
        ((length, feat), BF16, anywhere),
        ((length, feat), F32, anywhere),
        ((length, feat), BF16, anywhere),
        ((length, inner_width), BF16, anywhere),
        ((length, inner_width), BF16, anywhere),
        ((length, feat), F32, anywhere),
        ((length, 256), F32, vmem),
        ((BIAS_ROWS, feat), F32, vmem),
    ]
    small = (16, 128)
    results += [(grid + w_q.shape, BF16, anywhere)] * 4
    results += [(grid + w_1.shape, BF16, anywhere), (grid + w_2.shape, BF16, anywhere)]
    results += [(grads.shape, BF16, anywhere), (grads.shape, BF16, vmem)]
    results += [((1, length), jnp.int32, vmem), ((length, 1), F32, vmem)]
    return pl.pallas_call(
        forward_kernel,
        out_shape=[jax.ShapeDtypeStruct(shape, kind) for shape, kind, _ in results],
        in_specs=[vmem] * len(vectors) + [anywhere, anywhere, vmem, vmem] + [anywhere] * 6,
        out_specs=[spec for _, _, spec in results],
        scratch_shapes=[
            pltpu.VMEM(grid + small, BF16),
            pltpu.VMEM(small, F32),
            pltpu.VMEM(grid + (w_q.shape[0], 4 * feat), BF16),
            pltpu.VMEM(grid + w_1.shape, BF16),
            pltpu.VMEM(grid + w_2.shape, BF16),
            pltpu.VMEM(tokens.shape, BF16),
            pltpu.VMEM((length, 3 * feat), BF16),
            pltpu.VMEM((length, feat), BF16),
            pltpu.VMEM((length, feat), F32),
            pltpu.VMEM((length, feat), BF16),
            pltpu.VMEM((length, inner_width), BF16),
            pltpu.VMEM((length, inner_width), BF16),
            pltpu.VMEM((length, feat), F32),
            pltpu.VMEM((length, feat), F32),
            pltpu.VMEM((length, feat), BF16),
            pltpu.VMEM((8, inner_width), F32),
            DMA((8,)),
            DMA((3,)),
            DMA((3,)),
            DMA((3,)),
            DMA((3,)),
            DMA((14,)),
        ]
        + gather_sems() * 2
        + mid_sems() * 2,
        compiler_params=pltpu.CompilerParams(
            collective_id=0, has_side_effects=True, vmem_limit_bytes=VMEM_LIMIT
        ),
        name="forward",
    )(*vectors, tokens, grads, ids, mask, w_q, w_k, w_v, w_o, w_1, w_2)


def add_into(dst, src, lead):
    def step(flat, _):
        index = []
        for size in reversed(lead):
            index.append(flat % size)
            flat = flat // size
        index = tuple(reversed(index))
        dst[index] = (dst[index].astype(F32) + src[index].astype(F32)).astype(BF16)
        return 0

    total = 1
    for size in lead:
        total *= size
    lax.fori_loop(0, total, step, 0)


class Reduce:
    def __init__(self, part, bufs, sems, place, write):
        self.part, self.place, self.write = part, place, write
        self.got_core, self.got_plane, self.got_z = bufs
        self.cs, self.cr, self.ps, self.pr, self.zs, self.zr = sems

    def core_copy(self):
        z, x, y, c = self.place
        there = (z, x, y, 1 - c)
        return remote(self.part.at[:, :, :, 1 - c], self.got_core, self.cs.at[0], self.cr.at[0], there)

    def plane_copy(self, j):
        z, x, y, c = self.place
        px, py = x ^ (j // 2), y ^ (j % 2)
        there = (z, px, py, c)
        return remote(self.part.at[:, px, py, c], self.got_plane.at[j - 1], self.ps.at[j - 1], self.pr.at[j - 1], there)

    def z_copy(self, j):
        z, x, y, c = self.place
        part = self.part.at[z ^ j, x, y, c]
        return remote(part, self.got_z.at[j - 1], self.zs.at[j - 1], self.zr.at[j - 1], (z ^ j, x, y, c))

    def send_all(self):
        self.core_copy().start()

    def first(self):
        z, x, y, c = self.place
        self.core_copy().wait_recv()
        add_into(self.part.at[:, :, :, c], self.got_core, (4, 2, 2))
        for j in (3, 2, 1):
            self.plane_copy(j).start()

    def along_z(self):
        z, x, y, c = self.place
        for j in (1, 2, 3):
            self.plane_copy(j).wait_recv()
        mine, got = self.part.at[:, x, y, c], self.got_plane

        def add(i, _):
            total = mine[i].astype(F32) + got[0, i].astype(F32)
            mine[i] = (total + got[1, i].astype(F32) + got[2, i].astype(F32)).astype(BF16)
            return 0

        lax.fori_loop(0, 4, add, 0)
        for j in (3, 2, 1):
            self.z_copy(j).start()

    def last(self):
        z, x, y, c = self.place
        total = self.part[z, x, y, c].astype(F32)
        for j in (1, 2, 3):
            self.z_copy(j).wait_recv()
            total = total + self.got_z[j - 1].astype(F32)
        self.write(total)

    def finish(self):
        self.core_copy().wait_send()
        for j in (1, 2, 3):
            self.plane_copy(j).wait_send()
            self.z_copy(j).wait_send()


def reduce_sems():
    return [DMA((1,))] * 2 + [DMA((3,))] * 4


def reduce_bufs(rows, width):
    shape = (rows, width)
    return [pltpu.VMEM(lead + shape, BF16) for lead in ((4, 2, 2), (3, 4), (3,))]


MID_PARTS = 3


def split_sum(ref, which):
    width = ref.shape[-1]
    cut = width // (MID_PARTS * 128) * 128
    return ref.at[..., pl.ds(which * cut, (cut, width - cut)[which])]


ORDER = (3, 1, 2, 0)


class ReduceMid:
    def __init__(self, part, bufs, sems, place, write):
        self.part, self.place, self.write = part, place, write
        self.got_core, self.got_1, self.got_z, self.got_last = bufs[0], bufs[1:3], bufs[3:5], bufs[5]
        self.cs, self.cr, self.fs, self.fr, self.zs, self.zr, self.ls, self.lr = sems

    def core_copy(self, j):
        z, x, y, c = self.place
        zi = z ^ j
        there = (z, x, y, 1 - c)
        return remote(self.part.at[zi, :, :, 1 - c], self.got_core.at[zi], self.cs.at[j], self.cr.at[j], there)

    def mine(self, zi, axis, other=0):
        z, x, y, c = self.place
        part = self.part.at[zi, :, abs(other - y), c] if axis == 0 else self.part.at[zi, abs(other - x), :, c]
        return split_sum(part, axis)

    def first_copy(self, j, axis):
        z, x, y, c = self.place
        zi = z ^ j
        there = (z, x, 1 - y, c) if axis == 0 else (z, 1 - x, y, c)
        return remote(self.mine(zi, axis, 1), self.got_1[axis].at[zi], self.fs.at[axis, j], self.fr.at[axis, j], there)

    def z_copy(self, j, axis):
        z, x, y, c = self.place
        there = (z ^ (2 if j == 2 else 1), x, y, c)
        slot = {3: 0, 1: 1, 2: 2}[j]
        return remote(
            self.mine(z ^ j, axis), self.got_z[axis].at[slot], self.zs.at[axis, slot], self.zr.at[axis, slot], there
        )

    def last_copy(self, axis):
        z, x, y, c = self.place
        if axis == 0:
            part, there = self.part.at[z, 1 - x, y, c], (z, 1 - x, y, c)
        else:
            part, there = self.part.at[z, x, 1 - y, c], (z, x, 1 - y, c)
        return remote(split_sum(part, axis), split_sum(self.got_last, axis), self.ls.at[axis], self.lr.at[axis], there)

    def send(self, j):
        self.core_copy(j).start()

    def send_all(self):
        for j in ORDER:
            self.send(j)

    def first(self, j):
        z, x, y, c = self.place
        zi = z ^ j
        self.core_copy(j).wait_recv()
        add_into(self.part.at[zi, :, :, c], self.got_core.at[zi], (2, 2))
        for axis in (0, 1):
            self.first_copy(j, axis).start()

    def turn(self, j):
        zi = self.place[0] ^ j
        for axis in (0, 1):
            self.first_copy(j, axis).wait_recv()
            add_into(self.mine(zi, axis), self.got_1[axis].at[zi], (2,))
            if j % 2:
                self.z_copy(j, axis).start()

    def cross(self):
        for axis in (0, 1):
            self.z_copy(3, axis).wait_recv()
            add_into(self.mine(self.place[0] ^ 2, axis), self.got_z[axis].at[0], (2,))
            self.z_copy(2, axis).start()

    def fold(self):
        z, x, y, c = self.place
        for axis in (0, 1):
            for j in (1, 2):
                self.z_copy(j, axis).wait_recv()
            mine, got = self.mine(z, axis), self.got_z[axis]

            def add(i, _, mine=mine, got=got):
                total = mine[i].astype(F32) + got[1, i].astype(F32)
                mine[i] = (total + got[2, i].astype(F32)).astype(BF16)
                return 0

            lax.fori_loop(0, 2, add, 0)
            self.last_copy(axis).start()

    def last(self):
        z, x, y, c = self.place
        for axis in (0, 1):
            self.last_copy(axis).wait_recv()
        self.write(self.part[z, x, y, c].astype(F32) + self.got_last[...].astype(F32))

    def finish(self):
        for j in range(4):
            self.core_copy(j).wait_send()
            for axis in (0, 1):
                self.first_copy(j, axis).wait_send()
                if j:
                    self.z_copy(j, axis).wait_send()
        for axis in (0, 1):
            self.last_copy(axis).wait_send()


def reduce_mid_sems():
    return [DMA((4,))] * 2 + [DMA((2, 4))] * 2 + [DMA((2, 3))] * 2 + [DMA((2,))] * 2


def reduce_mid_bufs(rows, width):
    cut = width // (MID_PARTS * 128) * 128
    return [
        pltpu.VMEM((4, 2, 2, rows, width), BF16),
        pltpu.VMEM((4, 2, rows, cut), BF16),
        pltpu.VMEM((4, 2, rows, width - cut), BF16),
        pltpu.VMEM((3, 2, rows, cut), BF16),
        pltpu.VMEM((3, 2, rows, width - cut), BF16),
        pltpu.VMEM((rows, width), BF16),
    ]


PIECES = 7
GROUPS = 3


def split_scratch(i, rest):
    buf_count = [6, 6] + [3] * (PIECES - 2)
    sem_count = [8, 8] + [6] * (PIECES - 2)
    bufs, sems = rest[: sum(buf_count)], rest[sum(buf_count) :]
    buf_at, sem_at = sum(buf_count[:i]), sum(sem_count[:i])
    return bufs[buf_at : buf_at + buf_count[i]], sems[sem_at : sem_at + sem_count[i]]


def backward_kernel(
    qkv_in, lse, x_in, att_in, normed1_in, low_in, act_in, slope_in, normed2_in, factors, bias,
    w_q, w_k, w_v, w_o, w1_in, w2_in, grads_in, layer_in, slots, live,
    layer_out, tokens_out, q_out, k_out, v_out, o_out, w1_out, w2_out, small_out,
    qkv, x, att, normed1, low, act, slope, grad, grads, w1, wb, turned, d_qkv, g_2, g_1, g_o, g_qkv, g_small, sums, sums1,
    local, ls, lr, ts, tr, *rest,
):
    place = z, px, py, c = my_place()
    me = py * 2 + c
    length, feat = low.shape
    inner_width = act.shape[1]
    slots_each = grads.shape[0] // 4

    sources = [(grads_in.at[i], grads.at[pl.ds(i * slots_each, slots_each)]) for i in range(4)]
    sources += [(normed2_in, grad), (act_in, act), (w2_in, wb), (slope_in, slope), (low_in, low), (w1_in, w1)]
    sources += [(normed1_in, normed1), (att_in, att), (qkv_in, qkv), (x_in, x)]
    loads = [pltpu.make_async_copy(src, dst, local.at[i]) for i, (src, dst) in enumerate(sources)]
    for copy in loads:
        copy.start()
    meet(
        [(z ^ j, px, py, c) for j in (1, 2, 3)]
        + [(z, 1 - px, py, c), (z, px, 1 - py, c), (z, px, py, 1 - c), (z, px, 1 - py, 1 - c)]
    )

    def page_copy(src, dst, send, recv, j):
        there = me ^ (j + 1)
        return remote(src.at[there], dst.at[me], send.at[j], recv.at[j], (z, px, there // 2, there % 2))

    layer_copies = [page_copy(layer_in, layer_out, ls, lr, j) for j in range(3)]
    for copy in layer_copies:
        copy.start()
    layer_own = pltpu.make_async_copy(layer_in.at[me], layer_out.at[me], local.at[14])
    layer_own.start()

    def whole(ref):
        def write(total):
            ref[...] = total

        return write

    def thirds(group):
        def write(total):
            for i, ref in enumerate((q_out, k_out, v_out)):
                ref[:, pl.ds(group * TILE, TILE)] = total[:, i * TILE : (i + 1) * TILE]

        return write

    parts = [(ReduceMid, g_2, whole(w2_out)), (ReduceMid, g_1, whole(w1_out)), (Reduce, g_o, whole(o_out))]
    parts += [(Reduce, g_qkv.at[i], thirds(i)) for i in range(GROUPS)]
    parts += [(Reduce, g_small, whole(small_out))]
    sums_2, sum_1, sum_o, *sum_qkv, sum_small = reduces = [
        kind(part, *split_scratch(i, rest), place, write) for i, (kind, part, write) in enumerate(parts)
    ]

    sums[...] = jnp.zeros_like(sums)
    sums1[...] = jnp.zeros_like(sums1)

    def tally(row, values):
        sums[row : row + 1, :] += jnp.sum(values, axis=0, keepdims=True)

    for copy in loads[:5]:
        copy.wait()
    rows = 128

    def norm_two(i, _):
        block = block_of(i, rows)
        select = (rows_of((grads.shape[0], rows)) == slots[:, block]).astype(BF16)
        grad_layer = dot_rows(select, grads[...])
        normed = grad[block, :]
        tally(6, grad_layer * normed)
        tally(7, grad_layer)
        back = norm_back(grad_layer * bias[6:7, :], normed, factors[block, 128:129])
        grad[block, :] = back
        second_low = back.astype(BF16)
        d_qkv[block, 0:feat] = second_low
        tally(5, second_low.astype(F32))
        return 0

    lax.fori_loop(0, length // rows, norm_two, 0)
    second = grads.at[pl.ds(0, length)]
    second[...] = d_qkv[:, 0:feat]
    loads[5].wait()

    def outer_grad(i, _):
        j = jnp.where(i == 1, 1, jnp.where(i == 2, 2, 3 - i))
        zi = z ^ j
        width = inner_width // 4
        part = dot_rows(act[:, block_of(zi, width)], second[...])
        g_2[zi] = part.astype(BF16).reshape(g_2.shape[1:])
        sums_2.send(j)
        for k in (1, 2, 3):
            pl.when(i == k)(in_order((sums_2.first, ORDER[k - 1])))
        return 0

    lax.fori_loop(0, 4, outer_grad, 0)
    sums_2.first(0)
    for copy in loads[6:9]:
        copy.wait()
    turned[...] = low[...].T
    under_inner = {8: [(sums_2.turn, 3)]}

    def inner_grad(i, _):
        block = block_of(i, TILE)
        up = dot_cols(second[...], wb[block, :])
        inner_low = (up * slope[:, block].astype(F32)).astype(BF16)
        slope[:, block] = inner_low
        sums1[0:1, block] = jnp.sum(inner_low.astype(F32), axis=0, keepdims=True)
        part = dot(turned[...], inner_low)
        g_1[:, :, :, :, :, block] = part.astype(BF16).reshape(g_1.shape[:-1] + (TILE,))
        for at, calls in under_inner.items():
            pl.when(i == at)(in_order(*calls))
        return 0

    lax.fori_loop(0, inner_width // TILE, inner_grad, 0)
    sum_1.send_all()
    slabs = [
        pltpu.make_async_copy(src, wb.at[pl.ds(i * feat, feat)], local.at[15 + i])
        for i, src in enumerate((w_o, w_q, w_k, w_v))
    ]
    for copy in slabs:
        copy.start()
    for copy in loads[9:]:
        copy.wait()

    def hidden_grad(i, _):
        half_width = feat // 2
        block = block_of(i, half_width)
        weight = w1[pl.ds(2 * i, 2)].reshape(half_width, inner_width)
        grad[:, block] += dot_cols(slope[...], weight)
        return 0

    lax.fori_loop(0, 2, hidden_grad, 0)
    in_order((sum_1.first, 3), (sum_1.first, 1), (sums_2.turn, 1))()
    first = second

    def norm_one(i, _):
        block = block_of(i, rows)
        up, normed = grad[block, :], normed1[block, :]
        tally(3, up * normed)
        tally(4, up)
        back = norm_back(up * bias[3:4, :], normed, factors[block, 0:1])
        grad[block, :] = back
        first_low = back.astype(BF16)
        first[block, :] = first_low
        tally(2, first_low.astype(F32))
        return 0

    lax.fori_loop(0, length // rows, norm_one, 0)
    in_order((sum_1.first, 2), (sum_1.first, 0), (sums_2.turn, 2), (sums_2.cross,))()
    for copy in slabs:
        copy.wait()
    g_o[...] = dot_rows(att[...], first[...]).astype(BF16).reshape(g_o.shape)
    sum_o.send_all()
    grad_att = grads.at[pl.ds(length, length)]

    def att_grad(i, _):
        block = block_of(i, rows)
        grad_att[block, :] = dot_cols(first[block, :], wb[0:feat, :]).astype(BF16)
        return 0

    lax.fori_loop(0, length // rows, att_grad, 0)
    turned[...] = x[...].T
    in_order((sums_2.turn, 0), (sum_o.first,))()
    scale = HEAD_DIM**-0.5

    def pair(p):
        start = pl.multiple_of(p * 128, 128)
        q = qkv[:, pl.ds(start, 128)] * jnp.asarray(scale, BF16)
        k = qkv[:, pl.ds(feat + start, 128)]
        v = qkv[:, pl.ds(2 * feat + start, 128)]
        g = grad_att[:, pl.ds(start, 128)]
        low_lane = lanes(q.shape) < HEAD_DIM
        results = []
        for h in (0, 1):
            keep = low_lane if h == 0 else ~low_lane
            zero = jnp.zeros_like(k)
            scores = jnp.where(live[...] > 0, dot_cols(jnp.where(keep, k, zero), q), NEG_FILL)
            probs = jnp.exp(scores - lse[pl.ds(2 * p + h, 1), :])
            up = dot_cols(jnp.where(keep, v, zero), g)
            inner_sum = jnp.sum(probs * up, axis=0, keepdims=True)
            grad_scores = (probs * (up - inner_sum)).astype(BF16)
            for at, calls in under.items():
                if at % 2 == h:
                    pl.when(p == at // 2)(in_order(*calls))
            results.append((dot_rows(k, grad_scores), dot(grad_scores, q), dot(probs.astype(BF16), g)))
        (q_0, k_0, v_0), (q_1, k_1, v_1) = results
        d_q = jnp.where(rows_of(q_0.shape) < HEAD_DIM, q_0, q_1) * scale
        d_qkv[:, pl.ds(start, 128)] = d_q.T.astype(BF16)
        d_qkv[:, pl.ds(feat + start, 128)] = jnp.where(low_lane, k_0, k_1).astype(BF16)
        d_qkv[:, pl.ds(2 * feat + start, 128)] = jnp.where(low_lane, v_0, v_1).astype(BF16)

    under = {
        4: [(sums_2.fold,)],
        5: [(sum_1.turn, 3), (sum_qkv[0].first,)],
        8: [(sums_2.last,), (sum_1.turn, 1)],
        9: [(sum_qkv[1].first,)],
        10: [(sum_1.turn, 2), (sum_1.cross,)],
    }

    def group(i, _):
        def one(j, _):
            pair(2 * i + j)
            return 0

        lax.fori_loop(0, 2, one, 0)
        for t in range(3):
            cols = pl.ds(pl.multiple_of(t * feat + i * TILE, TILE), TILE)
            part = dot(turned[...], d_qkv[:, cols])
            g_qkv[i, :, :, :, :, :, pl.ds(t * TILE, TILE)] = part.astype(BF16).reshape(
                g_qkv.shape[1:-1] + (TILE,)
            )
        for at in range(GROUPS):
            pl.when(i == at)(sum_qkv[at].send_all)
        return 0

    lax.fori_loop(0, GROUPS, group, 0)
    thirds_0, thirds_1, thirds_2 = sum_qkv
    sum_1.turn(0)
    tally(0, d_qkv[:, 0:feat].astype(F32))
    tally(1, d_qkv[:, 2 * feat : 3 * feat].astype(F32))
    thirds_2.first()
    in_order((sum_1.fold,), (sum_o.along_z,))()
    grad_tokens = x.reshape(4, length // 4, feat)
    token_copies = [page_copy(grad_tokens, tokens_out, ts, tr, j) for j in range(3)]
    token_own = pltpu.make_async_copy(grad_tokens.at[me], tokens_out.at[me], local.at[19])

    def token_grad(i, _):
        block = block_of(me ^ (3 - i), length // 4)
        total = grad[block, :]
        for t in range(3):
            total += dot_cols(
                d_qkv[block, t * feat : (t + 1) * feat], wb[(t + 1) * feat : (t + 2) * feat, :]
            )
        x[block, :] = total.astype(BF16)
        for j in range(3):
            pl.when(i == 2 - j)(in_order((token_copies[j].start,)))
        return 0

    lax.fori_loop(0, 4, token_grad, 0)
    g_small[:, :, :, :, 0:8, :] = pack_rows(sums[...], feat // 32, 32).reshape(4, 2, 2, 2, 8, 128)
    for i in range(4):
        part = sums1[:, i * (inner_width // 4) : (i + 1) * (inner_width // 4)]
        g_small[i, :, :, :, 8:16, :] = pack_rows(part, inner_width // 32, 8).reshape(2, 2, 2, 8, 128)
    sum_small.send_all()
    token_own.start()
    in_order(
        (sum_small.first,),
        (thirds_0.along_z,),
        (thirds_1.along_z,),
        (sum_1.last,),
        (sum_o.last,),
        (sum_small.along_z,),
        (thirds_2.along_z,),
        (thirds_0.last,),
        (thirds_1.last,),
        (sum_small.last,),
        (thirds_2.last,),
    )()
    for copy in layer_copies + token_copies:
        copy.wait()
    layer_own.wait()
    token_own.wait()
    for one in reduces:
        one.finish()


def backward(saved, weights, grad_pages, layer_slots, slots, live, tokens_shape):
    w_q, w_1, w_2 = weights[0], weights[4], weights[5]
    qkv, lse, x, att, normed1, low, act, slope, normed2, factors, bias = saved
    length, feat = low.shape
    inner_width = act.shape[1]
    anywhere = pl.BlockSpec(memory_space=pl.ANY)
    vmem = pl.BlockSpec(memory_space=pltpu.VMEM)
    grid = (4, 2, 2, 2)
    small, inner, outer = (feat // 32, feat), (feat // 32, inner_width), (inner_width // 32, feat)
    sizes = [outer, inner] + [small] * 4 + [(16, 128)]
    scratch = [
        ((length, 3 * feat), BF16),
        ((length, feat), BF16),
        ((length, feat), BF16),
        ((length, feat), F32),
        ((length, feat), BF16),
        ((length, inner_width), BF16),
        ((length, inner_width), BF16),
        ((length, feat), F32),
        ((grad_pages.shape[0] * grad_pages.shape[1], feat), BF16),
        (grid + inner, BF16),
        ((inner_width, feat), BF16),
        ((feat, length), BF16),
        ((length, 3 * feat), BF16),
        (grid + outer, BF16),
        (grid + inner, BF16),
        (grid + small, BF16),
        ((GROUPS,) + grid + small, BF16),
        (grid + (16, 128), BF16),
        ((8, feat), F32),
        ((8, inner_width), F32),
    ]
    bufs, sems = [], []
    for i, size in enumerate(sizes):
        bufs += reduce_mid_bufs(*size) if i < 2 else reduce_bufs(*size)
        sems += reduce_mid_sems() if i < 2 else reduce_sems()
    outs = [(grad_pages.shape, BF16, anywhere), (tokens_shape, BF16, anywhere)]
    outs += [(small, F32, vmem)] * 4 + [(inner, F32, vmem), (outer, F32, vmem), ((16, 128), F32, vmem)]
    return pl.pallas_call(
        backward_kernel,
        out_shape=[jax.ShapeDtypeStruct(shape, kind) for shape, kind, _ in outs],
        in_specs=[anywhere, vmem] + [anywhere] * 7 + [vmem, vmem] + [anywhere] * 8 + [vmem, vmem],
        out_specs=[spec for _, _, spec in outs],
        scratch_shapes=[pltpu.VMEM(shape, kind) for shape, kind in scratch]
        + [DMA((20,)), DMA((3,)), DMA((3,)), DMA((3,)), DMA((3,))]
        + bufs
        + sems,
        compiler_params=pltpu.CompilerParams(
            collective_id=1, has_side_effects=True, vmem_limit_bytes=VMEM_LIMIT
        ),
        name="backward",
    )(*saved, *weights, grad_pages, layer_slots, slots, live)


LARGE = (0, 2, 3, 5, 9, 11)
SMALL_ORDER = (1, 4, 6, 7, 8, 12, 13, 14, 10)


def finish_kernel(count, sizes, *refs):
    ins, small, outs = refs[:count], refs[count], refs[count + 1 : 2 * count + 1]
    vectors, stages, sems = refs[2 * count + 1 :][: len(sizes)], refs[-count - 1 : -1], refs[-1]
    inward = [pltpu.make_async_copy(i, s, sems.at[0, n]) for n, (i, s) in enumerate(zip(ins, stages))]
    outward = [pltpu.make_async_copy(s, o, sems.at[1, n]) for n, (s, o) in enumerate(zip(stages, outs))]
    for copy in inward:
        copy.start()
    for row, (size, ref) in enumerate(zip(sizes, vectors)):
        ref[...] = small[row : row + 1, 0:size].reshape(size)
    for first, second in zip(inward, outward):
        first.wait()
        second.start()
    for copy in outward:
        copy.wait()


def finish(arrays, small, sizes):
    count = len(arrays)
    anywhere = pl.BlockSpec(memory_space=pl.ANY)
    vmem = pl.BlockSpec(memory_space=pltpu.VMEM)

    def body(*refs):
        finish_kernel(count, sizes, *refs)

    return pl.pallas_call(
        body,
        out_shape=[jax.ShapeDtypeStruct(a.shape, a.dtype) for a in arrays]
        + [jax.ShapeDtypeStruct((size,), F32) for size in sizes],
        in_specs=[anywhere] * count + [vmem],
        out_specs=[anywhere] * count + [vmem] * len(sizes),
        scratch_shapes=[pltpu.VMEM(a.shape, a.dtype) for a in arrays] + [DMA((2, count))],
        compiler_params=pltpu.CompilerParams(vmem_limit_bytes=VMEM_LIMIT),
        name="finish",
    )(*arrays, small)


def by_kernels(tokens, band_ids, page_mask, weights, grad_output):
    large = [weights[i] for i in LARGE]
    vectors = [weights[i] for i in SMALL_ORDER]
    got = forward(vectors, tokens, grad_output, band_ids, page_mask, *large)
    saved, full, (grad_slots, layer_slots, slots, live) = got[:11], got[11:17], got[17:]
    full = [w if i == 4 else w.reshape(-1, w.shape[-1]) for i, w in enumerate(full)]
    sums = backward(saved, full, grad_slots, layer_slots, slots, live, tokens.shape)
    results = finish(sums[:8], sums[8], [v.shape[0] for v in vectors])
    grads = dict(zip(LARGE + SMALL_ORDER, results[2:]))
    return tuple(results[:2]) + tuple(grads[i] for i in range(len(weights)))


def per_device(hand_made, *args):
    tokens, band_ids, band_counts, page_mask = args[:4]
    weights, grad_output = args[4:19], args[19]
    if hand_made:
        return by_kernels(tokens, band_ids, page_mask, weights, grad_output)
    bands = lax.axis_size("band")
    slot_cap = grad_output.shape[1]
    pages = tokens.shape[0] // bands
    full = [lax.all_gather(w, BOTH, axis=0, tiled=True) for w in weights]
    first = lax.axis_index("band") * pages
    ids = lax.dynamic_slice_in_dim(band_ids, first, pages, 0)
    live = lax.dynamic_slice_in_dim(page_mask, first, pages, 0) > 0
    slots = page_slots(ids, bands, slot_cap)
    layer_slots, grad_in, grads = layer_pages(
        to_pages(tokens), slots, live, to_pages(grad_output), full
    )
    return (from_pages(layer_slots), from_pages(grad_in)) + tuple(
        lax.psum_scatter(g, BOTH, scatter_dimension=0, tiled=True) for g in grads
    )


def solution(mesh):
    hand_made = dict(mesh.shape) == {"page": 8, "band": 4}
    shard = P(BOTH)
    rows = P(BOTH, None)
    tokens = P("page", "band", None)
    page = P("page", None)
    weights = (rows, shard, rows, rows, shard, rows, shard, shard, shard)
    weights = weights + (rows, shard, rows, shard, shard, shard)

    def step(*args):
        return per_device(hand_made, *args)

    return jax.shard_map(
        step,
        mesh=mesh,
        in_specs=(tokens, page, page, page) + weights + (tokens,),
        out_specs=(tokens, tokens) + weights,
        check_vma=False,
    )
```

```python
import jax
import jax.numpy as jnp
from jax import lax
from jax.experimental import pallas as pl
from jax.experimental.pallas import tpu as pltpu
from jax.sharding import PartitionSpec as P

HEAD_DIM = 64
LN_EPS = 1e-12
NEG_FILL = -1e30
MESH = pl.DeviceIdType.MESH
DMA = pltpu.SemaphoreType.DMA
F32 = jnp.float32
BF16 = jnp.bfloat16
BOTH = ("page", "band")
VMEM_LIMIT = 62 * 2**20


def my_place():
    page, band = lax.axis_index("page"), lax.axis_index("band")
    return page // 2, page % 2, band // 2, band % 2


def dev(z, x, y, c):
    return (z * 2 + x, y * 2 + c)


def remote(src, dst, send_sem, recv_sem, place):
    return pltpu.make_async_remote_copy(
        src_ref=src,
        dst_ref=dst,
        send_sem=send_sem,
        recv_sem=recv_sem,
        device_id=dev(*place),
        device_id_type=MESH,
    )


def meet(places):
    barrier = pltpu.get_barrier_semaphore()
    for place in places:
        pl.semaphore_signal(barrier, inc=1, device_id=dev(*place), device_id_type=MESH)
    pl.semaphore_wait(barrier, len(places))


def grid_peers(z, x, y, c):
    return [((z + j) % 4, x, y, c) for j in (1, 2, 3)] + [
        (z, 1 - x, y, c),
        (z, x, 1 - y, c),
        (z, x, y, 1 - c),
    ]


def half(ref, which):
    rows, width = ref.shape[-2] // 2, ref.shape[-1] // 2
    if width % 128:
        return ref.at[..., pl.ds(which * rows, rows), :]
    return ref.at[..., pl.ds(which * width, width)]


def norm_rows(values):
    center = values - jnp.mean(values, axis=-1, keepdims=True)
    factor = lax.rsqrt(jnp.mean(center * center, axis=-1, keepdims=True) + LN_EPS)
    return (center * factor, factor)


def norm_back(upstream, normed, factor):
    return factor * (
        upstream
        - jnp.mean(upstream, axis=-1, keepdims=True)
        - normed * jnp.mean(upstream * normed, axis=-1, keepdims=True)
    )


def dot(first, second):
    return jnp.dot(first, second, preferred_element_type=F32)


def dot_rows(first, second):
    return lax.dot_general(first, second, (((0,), (0,)), ((), ())), preferred_element_type=F32)


def dot_cols(first, second):
    return lax.dot_general(first, second, (((1,), (1,)), ((), ())), preferred_element_type=F32)


def page_slots(ids, bands, slot_cap):
    onehot = (ids[:, :, None] == jnp.arange(bands, dtype=jnp.int32)).astype(F32)
    length = ids.shape[1]
    before = (jnp.arange(length)[:, None] > jnp.arange(length)[None, :]).astype(F32)
    counts = jnp.einsum("tu,pub->ptb", before, onehot, preferred_element_type=F32)
    rank = jnp.sum(onehot * counts, axis=2).astype(jnp.int32)
    return ids * slot_cap + rank


def layer_pages(rows_in, slots, live, grad_slots, weights):
    (wq, bq, wk, wv, bv, wo, bo, g1, s1, w1, b1, w2, b2, g2, s2) = weights
    pages, length, feat = rows_in.shape
    heads = feat // HEAD_DIM
    scale = HEAD_DIM**-0.5
    x_low = rows_in.reshape(-1, feat)
    select = (slots[:, None, :] == jnp.arange(grad_slots.shape[1])[None, :, None]).astype(BF16)
    grad_layer = jnp.einsum("pst,psd->ptd", select, grad_slots, preferred_element_type=F32)
    grad_layer = grad_layer.reshape(-1, feat)

    def split(flat):
        return flat.reshape(pages, length, heads, HEAD_DIM)

    query = split((dot(x_low, wq) + bq).astype(BF16))
    key = split(dot(x_low, wk).astype(BF16))
    value = split((dot(x_low, wv) + bv).astype(BF16))
    scores = jnp.einsum("pthd,puhd->phtu", query, key, preferred_element_type=F32) * scale
    scores = jnp.where(live[:, None, None, :], scores, NEG_FILL)
    shifted = jnp.exp(scores - jnp.max(scores, axis=-1, keepdims=True))
    probs = shifted / jnp.sum(shifted, axis=-1, keepdims=True)
    probs_low = probs.astype(BF16)
    mixed = jnp.einsum("phtu,puhd->pthd", probs_low, value, preferred_element_type=F32)
    attended = mixed.astype(BF16).reshape(-1, feat)
    normed_one, factor_one = norm_rows(x_low.astype(F32) + dot(attended, wo) + bo)
    hidden = normed_one * g1 + s1
    hidden_low = hidden.astype(BF16)
    inner = dot(hidden_low, w1) + b1
    cdf = 0.5 * (1.0 + lax.erf(inner * (0.5**0.5)))
    act_low = (inner * cdf).astype(BF16)
    slope = cdf + inner * jnp.exp(-0.5 * inner * inner) * ((0.5 / jnp.pi) ** 0.5)
    normed_two, factor_two = norm_rows(hidden + dot(act_low, w2) + b2)
    layer = (normed_two * g2 + s2).astype(BF16).reshape(pages, length, feat)
    layer_slots = jnp.einsum("pst,ptd->psd", select, layer, preferred_element_type=F32).astype(BF16)

    grad_g2 = jnp.sum(grad_layer * normed_two, axis=0)
    grad_s2 = jnp.sum(grad_layer, axis=0)
    grad_second = norm_back(grad_layer * g2, normed_two, factor_two)
    second_low = grad_second.astype(BF16)
    grad_w2 = dot_rows(act_low, second_low)
    grad_b2 = jnp.sum(second_low.astype(F32), axis=0)
    inner_low = (dot_cols(second_low, w2) * slope).astype(BF16)
    grad_w1 = dot_rows(hidden_low, inner_low)
    grad_b1 = jnp.sum(inner_low.astype(F32), axis=0)
    grad_hidden = grad_second + dot_cols(inner_low, w1)
    grad_g1 = jnp.sum(grad_hidden * normed_one, axis=0)
    grad_s1 = jnp.sum(grad_hidden, axis=0)
    grad_first = norm_back(grad_hidden * g1, normed_one, factor_one)
    first_low = grad_first.astype(BF16)
    grad_wo = dot_rows(attended, first_low)
    grad_bo = jnp.sum(first_low.astype(F32), axis=0)
    grad_att = split(dot_cols(first_low, wo).astype(BF16))
    grad_probs = jnp.einsum("pthd,puhd->phtu", grad_att, value, preferred_element_type=F32)
    inner_sum = jnp.sum(probs * grad_probs, axis=-1, keepdims=True)
    grad_scores = (probs * (grad_probs - inner_sum)).astype(BF16)

    def flat(per_head, factor):
        return (per_head * factor).astype(BF16).reshape(-1, feat)

    ein = lambda form, a, b: jnp.einsum(form, a, b, preferred_element_type=F32)
    grad_q = flat(ein("phtu,puhd->pthd", grad_scores, key), scale)
    grad_k = flat(ein("phtu,pthd->puhd", grad_scores, query), scale)
    grad_v = flat(ein("phtu,pthd->puhd", probs_low, grad_att), 1.0)
    grad_wq, grad_wk, grad_wv = (dot_rows(x_low, g) for g in (grad_q, grad_k, grad_v))
    grad_bq = jnp.sum(grad_q.astype(F32), axis=0)
    grad_bv = jnp.sum(grad_v.astype(F32), axis=0)
    grad_in = grad_first + dot_cols(grad_q, wq) + dot_cols(grad_k, wk) + dot_cols(grad_v, wv)
    grad_in = grad_in.astype(BF16).reshape(pages, length, feat)
    return (
        layer_slots,
        grad_in,
        (grad_wq, grad_bq, grad_wk, grad_wv, grad_bv, grad_wo, grad_bo, grad_g1, grad_s1)
        + (grad_w1, grad_b1, grad_w2, grad_b2, grad_g2, grad_s2),
    )


def to_pages(blocks):
    return lax.all_to_all(blocks, "band", split_axis=0, concat_axis=1, tiled=True)


def from_pages(blocks):
    return lax.all_to_all(blocks, "band", split_axis=1, concat_axis=0, tiled=True)


def split_ref(ref, which):
    rows, width = ref.shape[-2:]
    cut = width // 3
    if cut % 128:
        return ref.at[..., pl.ds(which * (rows // 2), rows // 2), :]
    return ref.at[..., pl.ds(which * cut, (cut, width - cut)[which])]


def in_order(*calls):
    def step():
        for method, *index in calls:
            method(*index)

    return step


class Gather:
    def __init__(self, own, buf, sems, place):
        self.own, self.buf, self.place = own, buf, place
        self.zs, self.zr, self.ss, self.sr, self.fs, self.fr, self.cs, self.cr = sems

    def z_copy(self, j):
        z, x, y, c = self.place
        there = (z ^ (j + 1), x, y, c)
        return remote(self.own, self.buf.at[z, x, y, c], self.zs.at[j], self.zr.at[j], there)

    def side_copy(self, j, axis):
        z, x, y, c = self.place
        part = self.buf.at[z ^ j, x, y, c]
        there = (z, 1 - x, y, c) if axis == 0 else (z, x, 1 - y, c)
        source = self.own if j == 0 else part
        return remote(source, part, self.ss.at[axis, j], self.sr.at[axis, j], there)

    def far_copy(self, j, axis):
        z, x, y, c = self.place
        if axis == 0:
            part, there = self.buf.at[z ^ j, 1 - x, y, c], (z, x, 1 - y, c)
        else:
            part, there = self.buf.at[z ^ j, x, 1 - y, c], (z, 1 - x, y, c)
        part = split_ref(part, axis)
        return remote(part, part, self.fs.at[axis, j], self.fr.at[axis, j], there)

    def core_copy(self, k):
        z, x, y, c = self.place
        part = self.buf.at[:, (x, 1 - x, x, 1 - x)[k], (y, y, 1 - y, 1 - y)[k], c]
        return remote(part, part, self.cs.at[k], self.cr.at[k], (z, x, y, 1 - c))

    def start(self):
        for j in range(3):
            self.z_copy(j).start()
        for axis in (0, 1):
            self.side_copy(0, axis).start()

    def side(self, j):
        self.z_copy(j - 1).wait_recv()
        for axis in (0, 1):
            self.side_copy(j, axis).start()

    def far(self, j):
        for axis in (0, 1):
            self.side_copy(j, axis).wait_recv()
            self.far_copy(j, axis).start()

    def core(self, k):
        if k == 3:
            for j in range(4):
                for axis in (0, 1):
                    self.far_copy(j, axis).wait_recv()
        self.core_copy(k).start()

    def steps(self):
        side, far, core = self.side, self.far, self.core
        return [
            in_order((side, 1)),
            in_order((far, 0)),
            in_order((side, 2)),
            in_order((side, 3), (core, 0)),
            in_order((far, 1)),
            in_order((far, 2)),
            in_order((far, 3), (core, 1), (core, 2)),
            in_order((core, 3)),
        ]

    def arrive(self):
        for k in range(4):
            self.core_copy(k).wait_recv()

    def finish(self):
        for j in range(3):
            self.z_copy(j).wait_send()
        for j in range(4):
            for axis in (0, 1):
                self.side_copy(j, axis).wait_send()
                self.far_copy(j, axis).wait_send()
            self.core_copy(j).wait_send()


def gather_sems():
    return [DMA((3,)), DMA((3,))] + [DMA((2, 4))] * 4 + [DMA((4,))] * 2


def split_mid(ref, which):
    width = ref.shape[-1]
    cut = width // 640 * 128
    return ref.at[..., pl.ds(which * cut, (cut, width - cut)[which])]


class GatherMid:
    def __init__(self, own, buf, sems, place):
        self.own, self.buf, self.place = own, buf, place
        self.zs, self.zr, self.ss, self.sr, self.hs, self.hr, self.fs, self.fr, self.cs, self.cr = sems

    def z_copy(self, j):
        z, x, y, c = self.place
        zi = z ^ (2 if j == 3 else 0)
        source = self.buf.at[zi, x, y, c] if j == 3 else self.own
        there = (z ^ (2 if j == 2 else 1), x, y, c)
        return remote(source, self.buf.at[zi, x, y, c], self.zs.at[j - 1], self.zr.at[j - 1], there)

    def side_copy(self, axis):
        z, x, y, c = self.place
        there = (z, 1 - x, y, c) if axis == 0 else (z, x, 1 - y, c)
        source = split_mid(self.own, axis)
        return remote(source, split_mid(self.buf.at[z, x, y, c], axis), self.ss.at[axis], self.sr.at[axis], there)

    def half_copy(self, j, axis):
        z, x, y, c = self.place
        zi = z ^ (2 if j == 3 else 0)
        part = self.buf.at[zi, 1 - x, y, c] if axis == 0 else self.buf.at[zi, x, 1 - y, c]
        part = split_mid(part, axis)
        there = (z ^ (2 if j == 2 else 1), x, y, c)
        return remote(part, part, self.hs.at[axis, j - 1], self.hr.at[axis, j - 1], there)

    def far_copy(self, j, axis):
        z, x, y, c = self.place
        if axis == 0:
            part, there = self.buf.at[z ^ j, :, y, c], (z, x, 1 - y, c)
        else:
            part, there = self.buf.at[z ^ j, x, :, c], (z, 1 - x, y, c)
        part = split_mid(part, axis)
        return remote(part, part, self.fs.at[axis, j], self.fr.at[axis, j], there)

    def core_copy(self, j):
        z, x, y, c = self.place
        part = self.buf.at[z ^ j, :, :, c]
        return remote(part, part, self.cs.at[j], self.cr.at[j], (z, x, y, 1 - c))

    def start(self):
        for axis in (0, 1):
            self.side_copy(axis).start()
        for j in (2, 1):
            self.z_copy(j).start()

    def turn(self):
        for axis in (0, 1):
            self.side_copy(axis).wait_recv()
            for j in (2, 1):
                self.half_copy(j, axis).start()
        for axis in (0, 1):
            self.far_copy(0, axis).start()

    def far(self, j):
        self.z_copy(j).wait_recv()
        if j == 2:
            self.z_copy(3).start()
        for axis in (0, 1):
            self.half_copy(j, axis).wait_recv()
            if j == 2:
                self.half_copy(3, axis).start()
            self.far_copy(j, axis).start()

    def core(self, j):
        for axis in (0, 1):
            self.far_copy(j, axis).wait_recv()
        self.core_copy(j).start()

    def steps(self):
        far, core = self.far, self.core
        return [
            in_order((self.turn,)),
            in_order((far, 2)),
            in_order((far, 1)),
            in_order((far, 3)),
            in_order((core, 0)),
            in_order((core, 2)),
            in_order((core, 1)),
            in_order((core, 3)),
        ]

    def arrive(self):
        for k in range(4):
            self.core_copy(k).wait_recv()

    def finish(self):
        for axis in (0, 1):
            self.side_copy(axis).wait_send()
        for j in (1, 2, 3):
            self.z_copy(j).wait_send()
            for axis in (0, 1):
                self.half_copy(j, axis).wait_send()
        for j in range(4):
            for axis in (0, 1):
                self.far_copy(j, axis).wait_send()
            self.core_copy(j).wait_send()


def mid_sems():
    return [DMA((3,))] * 2 + [DMA((2,))] * 2 + [DMA((2, 3))] * 2 + [DMA((2, 4))] * 2 + [DMA((4,))] * 2


def lanes(shape):
    return lax.broadcasted_iota(jnp.int32, shape, len(shape) - 1)


def rows_of(shape):
    return lax.broadcasted_iota(jnp.int32, shape, len(shape) - 2)


def columns(buf, start, width):
    return buf[:, :, :, :, :, pl.ds(start, width)].reshape(-1, width)


def unpack_rows(block, per_shard, width):
    shards, count, _ = block.shape
    spread = (rows_of((128, width)) == lanes((128, width)) % per_shard).astype(BF16)
    wide = dot(block.reshape(-1, 128), spread).reshape(shards, count, width)
    owner = lax.broadcasted_iota(jnp.int32, wide.shape, 0) == lanes(wide.shape) // per_shard
    return jnp.sum(jnp.where(owner, wide, 0.0), axis=0)


def pack_rows(rows, per_shard, shards):
    count, width = rows.shape
    wide = jnp.broadcast_to(rows[None], (shards, count, width))
    owner = lax.broadcasted_iota(jnp.int32, wide.shape, 0) == lanes(wide.shape) // per_shard
    wide = jnp.where(owner, wide, 0.0).astype(BF16).reshape(-1, width)
    spread = (lanes((width, 128)) == rows_of((width, 128)) % per_shard).astype(BF16)
    return dot(wide, spread).astype(BF16).reshape(shards, count, 128)


def block_of(i, size):
    return pl.ds(pl.multiple_of(i * size, size), size)


def gelu_parts(v):
    cdf = 0.5 * (1.0 + lax.erf(v * (0.5**0.5)))
    return v * cdf, cdf + v * jnp.exp(-0.5 * v * v) * ((0.5 / jnp.pi) ** 0.5)


class Out:
    def __init__(self, sems):
        self.sems, self.copies = sems, []

    def send(self, src, dst):
        copy = pltpu.make_async_copy(src, dst, self.sems.at[len(self.copies)])
        copy.start()
        self.copies.append(copy)

    def wait(self):
        for copy in self.copies:
            copy.wait()


BIAS_ROWS = 8
TILE = 256


def forward_kernel(*refs):
    vector_refs, refs = refs[: BIAS_ROWS + 1], refs[BIAS_ROWS + 1 :]
    tokens, grads, ids, mask, w_q, w_k, w_v, w_o, w_1, w_2 = refs[:10]
    qkv_out, lse, x_out, att_out, normed1_out, low_out, act_out, slope_out, normed2_out = refs[10:19]
    factors, bias, q_out, k_out, v_out, o_out, w1_out, w2_out, grad_pages, layer_slots, slots, live = refs[19:31]
    small, small_own, a_buf, w1_buf, w2_buf, x_buf, qkv, att, normed1, low, act, slope = refs[31:43]
    second, normed2, layer, bias1, local, ts, tr, gs, gr, outs, *sems = refs[43:]
    place = z, x, y, c = my_place()
    me = y * 2 + c
    length, feat = low.shape
    pairs = feat // 128
    x_rows = x_buf.reshape(length, feat)
    here = (z, x, y, c)
    copies = [
        pltpu.make_async_copy(src, dst, local.at[i])
        for i, (src, dst) in enumerate(
            [(w, a_buf.at[here + (slice(None), pl.ds(i * feat, feat))]) for i, w in enumerate((w_q, w_k, w_v, w_o))]
            + [(w_1, w1_buf.at[here]), (w_2, w2_buf.at[here])]
            + [(tokens.at[me], x_buf.at[me]), (grads.at[me], grad_pages.at[me])]
        )
    ]
    for copy in copies:
        copy.start()
    small_own[...] = jnp.zeros_like(small_own)
    for row, ref in enumerate(vector_refs):
        size = ref.shape[0]
        small_own[row : row + 1, 0:size] = ref[...].astype(F32).reshape(1, size)
    small[here] = small_own[...].astype(BF16)
    meet(
        [(z ^ j, x, y, c) for j in (1, 2, 3)]
        + [(z, 1 - x, y, c), (z, x, 1 - y, c), (z, x, y, 1 - c), (z, x, 1 - y, 1 - c)]
    )

    def page_copy(src, dst, send, recv, j):
        there = me ^ (j + 1)
        return remote(src.at[there], dst.at[me], send.at[j], recv.at[j], (z, x, there // 2, there % 2))

    token_copies = [page_copy(tokens, x_buf, ts, tr, j) for j in range(3)]
    grad_copies = [page_copy(grads, grad_pages, gs, gr, j) for j in range(3)]
    gathers = [
        kind(own, buf, sems[(0, 8, 16, 26)[i] :][: 8 if kind is Gather else 10], place)
        for i, (kind, own, buf) in enumerate(
            [(Gather, small.at[here], small), (Gather, a_buf.at[here], a_buf)]
            + [(GatherMid, w_1, w1_buf), (GatherMid, w_2, w2_buf)]
        )
    ]
    vectors, atts, inner, outer = gathers
    for copy in copies[:4]:
        copy.wait()
    atts.start()
    vectors.start()
    for copy in token_copies:
        copy.start()
    slot_cap = grads.shape[1]
    hot = (rows_of((8, length)) == ids[pl.ds(me, 1), :]).astype(F32)
    earlier = (rows_of((length, length)) < lanes((length, length))).astype(BF16)
    rank = dot(hot.astype(BF16), earlier) + (rows_of((8, length)) * slot_cap).astype(F32)
    slots[...] = jnp.sum(hot * rank, axis=0, keepdims=True).astype(jnp.int32)
    live[...] = jnp.broadcast_to(mask[pl.ds(me, 1), :].astype(F32), (8, length)).T[:, 0:1]
    steps_0, steps_1, steps_2 = atts.steps(), inner.steps(), outer.steps()
    own = in_order(*[(copy.wait,) for copy in copies[4:6]])
    behind = {1: [inner.start], 3: [own, steps_1[0]], 4: [outer.start], 6: [steps_1[1]]}
    for i, (main, extra) in enumerate(zip(steps_0, vectors.steps())):
        main()
        extra()
        for step in behind.get(i, ()):
            step()
    for copy in copies[6:]:
        copy.wait()
    for copy in grad_copies:
        copy.start()
    vectors.arrive()
    shards = small[...].reshape(32, 16, 128)
    bias[...] = unpack_rows(shards[:, :8], feat // 32, feat)
    inner_width = act.shape[1]
    for i in range(4):
        part = unpack_rows(small[i].reshape(8, 16, 128)[:, 8:], inner_width // 32, inner_width // 4)
        bias1[:, i * (inner_width // 4) : (i + 1) * (inner_width // 4)] = part
    for copy in token_copies:
        copy.wait_recv()
    atts.arrive()
    out = Out(outs)
    for i, ref in enumerate((q_out, k_out, v_out, o_out)):
        out.send(a_buf.at[:, :, :, :, :, pl.ds(i * feat, feat)], ref)
    out.send(x_rows, x_out)
    steps_1[2]()

    def project(j, _):
        start = pl.multiple_of(j * TILE, TILE)
        total = dot(x_rows[...], columns(a_buf, start, TILE))
        which = j // (feat // TILE)
        inside = block_of(j % (feat // TILE), TILE)
        row = jnp.where(which == 0, bias[0:1, inside], jnp.where(which == 2, bias[1:2, inside], 0.0))
        qkv[:, pl.ds(start, TILE)] = (total + row).astype(BF16)
        return 0

    lax.fori_loop(0, 3 * feat // TILE, project, 0)
    out.send(qkv, qkv_out)
    steps_2[0]()
    under = {3: steps_1[3], 5: steps_2[1], 8: steps_1[4], 9: steps_2[2], 10: steps_1[5], 11: steps_1[6]}
    scale = HEAD_DIM**-0.5

    def pair(p, _):
        start = pl.multiple_of(p * 128, 128)
        q = qkv[:, pl.ds(start, 128)] * jnp.asarray(scale, BF16)
        k = qkv[:, pl.ds(feat + start, 128)]
        v = qkv[:, pl.ds(2 * feat + start, 128)]
        low_lane = lanes(q.shape) < HEAD_DIM
        mixed = []
        for h in (0, 1):
            part = jnp.where(low_lane if h == 0 else ~low_lane, k, jnp.zeros_like(k))
            scores = jnp.where(live[...] > 0, dot_cols(part, q), NEG_FILL)
            top = jnp.max(scores, axis=0, keepdims=True)
            shifted = jnp.exp(scores - top)
            total = jnp.sum(shifted, axis=0, keepdims=True)
            probs = (shifted * (1.0 / total)).astype(BF16)
            mixed.append(dot_rows(v, probs))
            lse[pl.ds(2 * p + h, 1), :] = top + jnp.log(total)
            for at, step in under.items():
                if at % 2 == h:
                    pl.when(p == at // 2)(step)
        both = jnp.where(rows_of(mixed[0].shape) < HEAD_DIM, mixed[0], mixed[1])
        att[:, pl.ds(start, 128)] = both.T.astype(BF16)
        return 0

    lax.fori_loop(0, pairs, pair, 0)
    out.send(att, att_out)
    steps_1[7]()
    steps_2[3]()
    rows = 256

    def norm_one(i, _):
        block = block_of(i, rows)
        total = dot(att[block, :], columns(a_buf, 3 * feat, feat))
        total = total + x_rows[block, :].astype(F32) + bias[2:3, :]
        normed, factor = norm_rows(total)
        normed1[block, :] = normed
        factors[block, 0:128] = jnp.broadcast_to(factor, (rows, 128))
        low[block, :] = (normed * bias[3:4, :] + bias[4:5, :]).astype(BF16)
        return 0

    lax.fori_loop(0, length // rows, norm_one, 0)
    out.send(normed1, normed1_out)
    out.send(low, low_out)
    inner.arrive()
    out.send(w1_buf, w1_out)

    def ffn_in(j, _):
        block = block_of(j, TILE)
        value, grad = gelu_parts(dot(low[...], columns(w1_buf, block.start, TILE)) + bias1[0:1, block])
        act[:, block] = value.astype(BF16)
        slope[:, block] = grad.astype(BF16)
        return 0

    lax.fori_loop(0, inner_width // TILE, ffn_in, 0)
    out.send(act, act_out)
    out.send(slope, slope_out)
    chunk = inner_width // 4

    def add_chunk(j):
        outer.core_copy(j).wait_recv()
        zi = z ^ j

        def part(i, _):
            block = block_of(i, TILE)
            more = dot(act[:, block_of(zi, chunk)], w2_buf[zi, :, :, :, :, block].reshape(chunk, TILE))
            second[:, block] = more if j == 0 else second[:, block] + more
            return 0

        lax.fori_loop(0, feat // TILE, part, 0)

    steps_2[4]()
    steps_2[5]()
    add_chunk(0)
    steps_2[6]()
    add_chunk(2)
    steps_2[7]()
    add_chunk(1)
    add_chunk(3)
    out.send(w2_buf, w2_out)

    def norm_two(i, _):
        block = block_of(i, rows)
        hidden = normed1[block, :] * bias[3:4, :] + bias[4:5, :]
        normed, factor = norm_rows(hidden + second[block, :] + bias[5:6, :])
        normed2[block, :] = normed
        factors[block, 128:256] = jnp.broadcast_to(factor, (rows, 128))
        layer[block, :] = (normed * bias[6:7, :] + bias[7:8, :]).astype(BF16)
        return 0

    lax.fori_loop(0, length // rows, norm_two, 0)
    out.send(normed2, normed2_out)

    def place_rows(i, _):
        cap = layer_slots.shape[1]
        here_rows = rows_of((cap, length)) + i * cap
        select = (here_rows == slots[...]).astype(BF16)
        layer_slots[i] = dot(select, layer[...]).astype(BF16)
        return 0

    lax.fori_loop(0, layer_slots.shape[0], place_rows, 0)
    for copy in grad_copies:
        copy.wait_recv()
    for copy in grad_copies + token_copies:
        copy.wait_send()
    for one in gathers:
        one.finish()
    out.wait()


def forward(vectors, tokens, grads, ids, mask, w_q, w_k, w_v, w_o, w_1, w_2):
    length, feat, inner_width = ids.shape[1], tokens.shape[-1], w_1.shape[1]
    anywhere = pl.BlockSpec(memory_space=pl.ANY)
    vmem = pl.BlockSpec(memory_space=pltpu.VMEM)
    grid = (4, 2, 2, 2)
    heads = feat // HEAD_DIM
    results = [
        ((length, 3 * feat), BF16, anywhere),
        ((heads + -heads % 8, length), F32, vmem),
        ((length, feat), BF16, anywhere),
        ((length, feat), BF16, anywhere),
        ((length, feat), F32, anywhere),
        ((length, feat), BF16, anywhere),
        ((length, inner_width), BF16, anywhere),
        ((length, inner_width), BF16, anywhere),
        ((length, feat), F32, anywhere),
        ((length, 256), F32, vmem),
        ((BIAS_ROWS, feat), F32, vmem),
    ]
    small = (16, 128)
    results += [(grid + w_q.shape, BF16, anywhere)] * 4
    results += [(grid + w_1.shape, BF16, anywhere), (grid + w_2.shape, BF16, anywhere)]
    results += [(grads.shape, BF16, anywhere), (grads.shape, BF16, vmem)]
    results += [((1, length), jnp.int32, vmem), ((length, 1), F32, vmem)]
    return pl.pallas_call(
        forward_kernel,
        out_shape=[jax.ShapeDtypeStruct(shape, kind) for shape, kind, _ in results],
        in_specs=[vmem] * len(vectors) + [anywhere, anywhere, vmem, vmem] + [anywhere] * 6,
        out_specs=[spec for _, _, spec in results],
        scratch_shapes=[
            pltpu.VMEM(grid + small, BF16),
            pltpu.VMEM(small, F32),
            pltpu.VMEM(grid + (w_q.shape[0], 4 * feat), BF16),
            pltpu.VMEM(grid + w_1.shape, BF16),
            pltpu.VMEM(grid + w_2.shape, BF16),
            pltpu.VMEM(tokens.shape, BF16),
            pltpu.VMEM((length, 3 * feat), BF16),
            pltpu.VMEM((length, feat), BF16),
            pltpu.VMEM((length, feat), F32),
            pltpu.VMEM((length, feat), BF16),
            pltpu.VMEM((length, inner_width), BF16),
            pltpu.VMEM((length, inner_width), BF16),
            pltpu.VMEM((length, feat), F32),
            pltpu.VMEM((length, feat), F32),
            pltpu.VMEM((length, feat), BF16),
            pltpu.VMEM((8, inner_width), F32),
            DMA((8,)),
            DMA((3,)),
            DMA((3,)),
            DMA((3,)),
            DMA((3,)),
            DMA((14,)),
        ]
        + gather_sems() * 2
        + mid_sems() * 2,
        compiler_params=pltpu.CompilerParams(
            collective_id=0, has_side_effects=True, vmem_limit_bytes=VMEM_LIMIT
        ),
        name="forward",
    )(*vectors, tokens, grads, ids, mask, w_q, w_k, w_v, w_o, w_1, w_2)


def add_into(dst, src, lead):
    def step(flat, _):
        index = []
        for size in reversed(lead):
            index.append(flat % size)
            flat = flat // size
        index = tuple(reversed(index))
        dst[index] = (dst[index].astype(F32) + src[index].astype(F32)).astype(BF16)
        return 0

    total = 1
    for size in lead:
        total *= size
    lax.fori_loop(0, total, step, 0)


class Reduce:
    def __init__(self, part, bufs, sems, place, write):
        self.part, self.place, self.write = part, place, write
        self.got_core, self.got_plane, self.got_z = bufs
        self.cs, self.cr, self.ps, self.pr, self.zs, self.zr = sems

    def core_copy(self):
        z, x, y, c = self.place
        there = (z, x, y, 1 - c)
        return remote(self.part.at[:, :, :, 1 - c], self.got_core, self.cs.at[0], self.cr.at[0], there)

    def plane_copy(self, j):
        z, x, y, c = self.place
        px, py = x ^ (j // 2), y ^ (j % 2)
        there = (z, px, py, c)
        return remote(self.part.at[:, px, py, c], self.got_plane.at[j - 1], self.ps.at[j - 1], self.pr.at[j - 1], there)

    def z_copy(self, j):
        z, x, y, c = self.place
        part = self.part.at[z ^ j, x, y, c]
        return remote(part, self.got_z.at[j - 1], self.zs.at[j - 1], self.zr.at[j - 1], (z ^ j, x, y, c))

    def send_all(self):
        self.core_copy().start()

    def first(self):
        z, x, y, c = self.place
        self.core_copy().wait_recv()
        add_into(self.part.at[:, :, :, c], self.got_core, (4, 2, 2))
        for j in (3, 2, 1):
            self.plane_copy(j).start()

    def along_z(self):
        z, x, y, c = self.place
        for j in (1, 2, 3):
            self.plane_copy(j).wait_recv()
        mine, got = self.part.at[:, x, y, c], self.got_plane

        def add(i, _):
            total = mine[i].astype(F32) + got[0, i].astype(F32)
            mine[i] = (total + got[1, i].astype(F32) + got[2, i].astype(F32)).astype(BF16)
            return 0

        lax.fori_loop(0, 4, add, 0)
        for j in (3, 2, 1):
            self.z_copy(j).start()

    def last(self):
        z, x, y, c = self.place
        total = self.part[z, x, y, c].astype(F32)
        for j in (1, 2, 3):
            self.z_copy(j).wait_recv()
            total = total + self.got_z[j - 1].astype(F32)
        self.write(total)

    def finish(self):
        self.core_copy().wait_send()
        for j in (1, 2, 3):
            self.plane_copy(j).wait_send()
            self.z_copy(j).wait_send()


def reduce_sems():
    return [DMA((1,))] * 2 + [DMA((3,))] * 4


def reduce_bufs(rows, width):
    shape = (rows, width)
    return [pltpu.VMEM(lead + shape, BF16) for lead in ((4, 2, 2), (3, 4), (3,))]


MID_PARTS = 3


def split_sum(ref, which):
    width = ref.shape[-1]
    cut = width // (MID_PARTS * 128) * 128
    return ref.at[..., pl.ds(which * cut, (cut, width - cut)[which])]


ORDER = (3, 1, 2, 0)


class ReduceMid:
    def __init__(self, part, bufs, sems, place, write):
        self.part, self.place, self.write = part, place, write
        self.got_core, self.got_1, self.got_z, self.got_last = bufs[0], bufs[1:3], bufs[3:5], bufs[5]
        self.cs, self.cr, self.fs, self.fr, self.zs, self.zr, self.ls, self.lr = sems

    def core_copy(self, j):
        z, x, y, c = self.place
        zi = z ^ j
        there = (z, x, y, 1 - c)
        return remote(self.part.at[zi, :, :, 1 - c], self.got_core.at[zi], self.cs.at[j], self.cr.at[j], there)

    def mine(self, zi, axis, other=0):
        z, x, y, c = self.place
        part = self.part.at[zi, :, abs(other - y), c] if axis == 0 else self.part.at[zi, abs(other - x), :, c]
        return split_sum(part, axis)

    def first_copy(self, j, axis):
        z, x, y, c = self.place
        zi = z ^ j
        there = (z, x, 1 - y, c) if axis == 0 else (z, 1 - x, y, c)
        return remote(self.mine(zi, axis, 1), self.got_1[axis].at[zi], self.fs.at[axis, j], self.fr.at[axis, j], there)

    def z_copy(self, j, axis):
        z, x, y, c = self.place
        there = (z ^ (2 if j == 2 else 1), x, y, c)
        slot = {3: 0, 1: 1, 2: 2}[j]
        return remote(
            self.mine(z ^ j, axis), self.got_z[axis].at[slot], self.zs.at[axis, slot], self.zr.at[axis, slot], there
        )

    def last_copy(self, axis):
        z, x, y, c = self.place
        if axis == 0:
            part, there = self.part.at[z, 1 - x, y, c], (z, 1 - x, y, c)
        else:
            part, there = self.part.at[z, x, 1 - y, c], (z, x, 1 - y, c)
        return remote(split_sum(part, axis), split_sum(self.got_last, axis), self.ls.at[axis], self.lr.at[axis], there)

    def send(self, j):
        self.core_copy(j).start()

    def send_all(self):
        for j in ORDER:
            self.send(j)

    def first(self, j):
        z, x, y, c = self.place
        zi = z ^ j
        self.core_copy(j).wait_recv()
        add_into(self.part.at[zi, :, :, c], self.got_core.at[zi], (2, 2))
        for axis in (0, 1):
            self.first_copy(j, axis).start()

    def turn(self, j):
        zi = self.place[0] ^ j
        for axis in (0, 1):
            self.first_copy(j, axis).wait_recv()
            add_into(self.mine(zi, axis), self.got_1[axis].at[zi], (2,))
            if j % 2:
                self.z_copy(j, axis).start()

    def cross(self):
        for axis in (0, 1):
            self.z_copy(3, axis).wait_recv()
            add_into(self.mine(self.place[0] ^ 2, axis), self.got_z[axis].at[0], (2,))
            self.z_copy(2, axis).start()

    def fold(self):
        z, x, y, c = self.place
        for axis in (0, 1):
            for j in (1, 2):
                self.z_copy(j, axis).wait_recv()
            mine, got = self.mine(z, axis), self.got_z[axis]

            def add(i, _, mine=mine, got=got):
                total = mine[i].astype(F32) + got[1, i].astype(F32)
                mine[i] = (total + got[2, i].astype(F32)).astype(BF16)
                return 0

            lax.fori_loop(0, 2, add, 0)
            self.last_copy(axis).start()

    def last(self):
        z, x, y, c = self.place
        for axis in (0, 1):
            self.last_copy(axis).wait_recv()
        self.write(self.part[z, x, y, c].astype(F32) + self.got_last[...].astype(F32))

    def finish(self):
        for j in range(4):
            self.core_copy(j).wait_send()
            for axis in (0, 1):
                self.first_copy(j, axis).wait_send()
                if j:
                    self.z_copy(j, axis).wait_send()
        for axis in (0, 1):
            self.last_copy(axis).wait_send()


def reduce_mid_sems():
    return [DMA((4,))] * 2 + [DMA((2, 4))] * 2 + [DMA((2, 3))] * 2 + [DMA((2,))] * 2


def reduce_mid_bufs(rows, width):
    cut = width // (MID_PARTS * 128) * 128
    return [
        pltpu.VMEM((4, 2, 2, rows, width), BF16),
        pltpu.VMEM((4, 2, rows, cut), BF16),
        pltpu.VMEM((4, 2, rows, width - cut), BF16),
        pltpu.VMEM((3, 2, rows, cut), BF16),
        pltpu.VMEM((3, 2, rows, width - cut), BF16),
        pltpu.VMEM((rows, width), BF16),
    ]


PIECES = 7
GROUPS = 3


def split_scratch(i, rest):
    buf_count = [6, 6] + [3] * (PIECES - 2)
    sem_count = [8, 8] + [6] * (PIECES - 2)
    bufs, sems = rest[: sum(buf_count)], rest[sum(buf_count) :]
    buf_at, sem_at = sum(buf_count[:i]), sum(sem_count[:i])
    return bufs[buf_at : buf_at + buf_count[i]], sems[sem_at : sem_at + sem_count[i]]


def backward_kernel(
    qkv_in, lse, x_in, att_in, normed1_in, low_in, act_in, slope_in, normed2_in, factors, bias,
    w_q, w_k, w_v, w_o, w1_in, w2_in, grads_in, layer_in, slots, live,
    layer_out, tokens_out, q_out, k_out, v_out, o_out, w1_out, w2_out, small_out,
    qkv, x, att, normed1, low, act, slope, grad, grads, w1, wb, turned, d_qkv, g_2, g_1, g_o, g_qkv, g_small, sums, sums1,
    local, ls, lr, ts, tr, *rest,
):
    place = z, px, py, c = my_place()
    me = py * 2 + c
    length, feat = low.shape
    inner_width = act.shape[1]
    slots_each = grads.shape[0] // 4

    sources = [(grads_in.at[i], grads.at[pl.ds(i * slots_each, slots_each)]) for i in range(4)]
    sources += [(normed2_in, grad), (act_in, act), (w2_in, wb), (slope_in, slope), (low_in, low), (w1_in, w1)]
    sources += [(normed1_in, normed1), (att_in, att), (qkv_in, qkv), (x_in, x)]
    loads = [pltpu.make_async_copy(src, dst, local.at[i]) for i, (src, dst) in enumerate(sources)]
    for copy in loads:
        copy.start()
    meet(
        [(z ^ j, px, py, c) for j in (1, 2, 3)]
        + [(z, 1 - px, py, c), (z, px, 1 - py, c), (z, px, py, 1 - c), (z, px, 1 - py, 1 - c)]
    )

    def page_copy(src, dst, send, recv, j):
        there = me ^ (j + 1)
        return remote(src.at[there], dst.at[me], send.at[j], recv.at[j], (z, px, there // 2, there % 2))

    layer_copies = [page_copy(layer_in, layer_out, ls, lr, j) for j in range(3)]
    for copy in layer_copies:
        copy.start()
    layer_own = pltpu.make_async_copy(layer_in.at[me], layer_out.at[me], local.at[14])
    layer_own.start()

    def whole(ref):
        def write(total):
            ref[...] = total

        return write

    def thirds(group):
        def write(total):
            for i, ref in enumerate((q_out, k_out, v_out)):
                ref[:, pl.ds(group * TILE, TILE)] = total[:, i * TILE : (i + 1) * TILE]

        return write

    parts = [(ReduceMid, g_2, whole(w2_out)), (ReduceMid, g_1, whole(w1_out)), (Reduce, g_o, whole(o_out))]
    parts += [(Reduce, g_qkv.at[i], thirds(i)) for i in range(GROUPS)]
    parts += [(Reduce, g_small, whole(small_out))]
    sums_2, sum_1, sum_o, *sum_qkv, sum_small = reduces = [
        kind(part, *split_scratch(i, rest), place, write) for i, (kind, part, write) in enumerate(parts)
    ]

    sums[...] = jnp.zeros_like(sums)
    sums1[...] = jnp.zeros_like(sums1)

    def tally(row, values):
        sums[row : row + 1, :] += jnp.sum(values, axis=0, keepdims=True)

    for copy in loads[:5]:
        copy.wait()
    rows = 256

    def norm_two(i, _):
        block = block_of(i, rows)
        select = (rows_of((grads.shape[0], rows)) == slots[:, block]).astype(BF16)
        grad_layer = dot_rows(select, grads[...])
        normed = grad[block, :]
        tally(6, grad_layer * normed)
        tally(7, grad_layer)
        back = norm_back(grad_layer * bias[6:7, :], normed, factors[block, 128:129])
        grad[block, :] = back
        second_low = back.astype(BF16)
        d_qkv[block, 0:feat] = second_low
        tally(5, second_low.astype(F32))
        return 0

    lax.fori_loop(0, length // rows, norm_two, 0)
    second = grads.at[pl.ds(0, length)]
    second[...] = d_qkv[:, 0:feat]
    loads[5].wait()

    def outer_grad(i, _):
        j = jnp.where(i == 1, 1, jnp.where(i == 2, 2, 3 - i))
        zi = z ^ j
        width = inner_width // 4
        part = dot_rows(act[:, block_of(zi, width)], second[...])
        g_2[zi] = part.astype(BF16).reshape(g_2.shape[1:])
        sums_2.send(j)
        for k in (1, 2, 3):
            pl.when(i == k)(in_order((sums_2.first, ORDER[k - 1])))
        return 0

    lax.fori_loop(0, 4, outer_grad, 0)
    sums_2.first(0)
    for copy in loads[6:9]:
        copy.wait()
    turned[...] = low[...].T
    under_inner = {8: [(sums_2.turn, 3)]}

    def inner_grad(i, _):
        block = block_of(i, TILE)
        up = dot_cols(second[...], wb[block, :])
        inner_low = (up * slope[:, block].astype(F32)).astype(BF16)
        slope[:, block] = inner_low
        sums1[0:1, block] = jnp.sum(inner_low.astype(F32), axis=0, keepdims=True)
        part = dot(turned[...], inner_low)
        g_1[:, :, :, :, :, block] = part.astype(BF16).reshape(g_1.shape[:-1] + (TILE,))
        for at, calls in under_inner.items():
            pl.when(i == at)(in_order(*calls))
        return 0

    lax.fori_loop(0, inner_width // TILE, inner_grad, 0)
    sum_1.send_all()
    slabs = [
        pltpu.make_async_copy(src, wb.at[pl.ds(i * feat, feat)], local.at[15 + i])
        for i, src in enumerate((w_o, w_q, w_k, w_v))
    ]
    for copy in slabs:
        copy.start()
    for copy in loads[9:]:
        copy.wait()

    def hidden_grad(i, _):
        half_width = feat // 2
        block = block_of(i, half_width)
        weight = w1[pl.ds(2 * i, 2)].reshape(half_width, inner_width)
        grad[:, block] += dot_cols(slope[...], weight)
        return 0

    lax.fori_loop(0, 2, hidden_grad, 0)
    in_order((sum_1.first, 3), (sum_1.first, 1), (sums_2.turn, 1))()
    first = second

    def norm_one(i, _):
        block = block_of(i, rows)
        up, normed = grad[block, :], normed1[block, :]
        tally(3, up * normed)
        tally(4, up)
        back = norm_back(up * bias[3:4, :], normed, factors[block, 0:1])
        grad[block, :] = back
        first_low = back.astype(BF16)
        first[block, :] = first_low
        tally(2, first_low.astype(F32))
        return 0

    lax.fori_loop(0, length // rows, norm_one, 0)
    in_order((sum_1.first, 2), (sum_1.first, 0), (sums_2.turn, 2), (sums_2.cross,))()
    for copy in slabs:
        copy.wait()
    g_o[...] = dot_rows(att[...], first[...]).astype(BF16).reshape(g_o.shape)
    sum_o.send_all()
    grad_att = grads.at[pl.ds(length, length)]

    def att_grad(i, _):
        block = block_of(i, rows)
        grad_att[block, :] = dot_cols(first[block, :], wb[0:feat, :]).astype(BF16)
        return 0

    lax.fori_loop(0, length // rows, att_grad, 0)
    turned[...] = x[...].T
    in_order((sums_2.turn, 0), (sum_o.first,))()
    scale = HEAD_DIM**-0.5

    def pair(p):
        start = pl.multiple_of(p * 128, 128)
        q = qkv[:, pl.ds(start, 128)] * jnp.asarray(scale, BF16)
        k = qkv[:, pl.ds(feat + start, 128)]
        v = qkv[:, pl.ds(2 * feat + start, 128)]
        g = grad_att[:, pl.ds(start, 128)]
        low_lane = lanes(q.shape) < HEAD_DIM
        results = []
        for h in (0, 1):
            keep = low_lane if h == 0 else ~low_lane
            zero = jnp.zeros_like(k)
            scores = jnp.where(live[...] > 0, dot_cols(jnp.where(keep, k, zero), q), NEG_FILL)
            probs = jnp.exp(scores - lse[pl.ds(2 * p + h, 1), :])
            up = dot_cols(jnp.where(keep, v, zero), g)
            inner_sum = jnp.sum(probs * up, axis=0, keepdims=True)
            grad_scores = (probs * (up - inner_sum)).astype(BF16)
            for at, calls in under.items():
                if at % 2 == h:
                    pl.when(p == at // 2)(in_order(*calls))
            results.append((dot_rows(k, grad_scores), dot(grad_scores, q), dot(probs.astype(BF16), g)))
        (q_0, k_0, v_0), (q_1, k_1, v_1) = results
        d_q = jnp.where(rows_of(q_0.shape) < HEAD_DIM, q_0, q_1) * scale
        d_qkv[:, pl.ds(start, 128)] = d_q.T.astype(BF16)
        d_qkv[:, pl.ds(feat + start, 128)] = jnp.where(low_lane, k_0, k_1).astype(BF16)
        d_qkv[:, pl.ds(2 * feat + start, 128)] = jnp.where(low_lane, v_0, v_1).astype(BF16)

    under = {
        4: [(sums_2.fold,)],
        5: [(sum_1.turn, 3), (sum_qkv[0].first,)],
        8: [(sums_2.last,), (sum_1.turn, 1)],
        9: [(sum_qkv[1].first,)],
        10: [(sum_1.turn, 2), (sum_1.cross,)],
    }

    def group(i, _):
        def one(j, _):
            pair(2 * i + j)
            return 0

        lax.fori_loop(0, 2, one, 0)
        for t in range(3):
            cols = pl.ds(pl.multiple_of(t * feat + i * TILE, TILE), TILE)
            part = dot(turned[...], d_qkv[:, cols])
            g_qkv[i, :, :, :, :, :, pl.ds(t * TILE, TILE)] = part.astype(BF16).reshape(
                g_qkv.shape[1:-1] + (TILE,)
            )
        for at in range(GROUPS):
            pl.when(i == at)(sum_qkv[at].send_all)
        return 0

    lax.fori_loop(0, GROUPS, group, 0)
    thirds_0, thirds_1, thirds_2 = sum_qkv
    sum_1.turn(0)
    tally(0, d_qkv[:, 0:feat].astype(F32))
    tally(1, d_qkv[:, 2 * feat : 3 * feat].astype(F32))
    thirds_2.first()
    in_order((sum_1.fold,), (sum_o.along_z,))()
    grad_tokens = x.reshape(4, length // 4, feat)
    token_copies = [page_copy(grad_tokens, tokens_out, ts, tr, j) for j in range(3)]
    token_own = pltpu.make_async_copy(grad_tokens.at[me], tokens_out.at[me], local.at[19])

    def token_grad(i, _):
        block = block_of(me ^ (3 - i), length // 4)
        total = grad[block, :]
        for t in range(3):
            total += dot_cols(
                d_qkv[block, t * feat : (t + 1) * feat], wb[(t + 1) * feat : (t + 2) * feat, :]
            )
        x[block, :] = total.astype(BF16)
        for j in range(3):
            pl.when(i == 2 - j)(in_order((token_copies[j].start,)))
        return 0

    lax.fori_loop(0, 4, token_grad, 0)
    g_small[:, :, :, :, 0:8, :] = pack_rows(sums[...], feat // 32, 32).reshape(4, 2, 2, 2, 8, 128)
    for i in range(4):
        part = sums1[:, i * (inner_width // 4) : (i + 1) * (inner_width // 4)]
        g_small[i, :, :, :, 8:16, :] = pack_rows(part, inner_width // 32, 8).reshape(2, 2, 2, 8, 128)
    sum_small.send_all()
    token_own.start()
    in_order(
        (sum_small.first,),
        (thirds_0.along_z,),
        (thirds_1.along_z,),
        (sum_1.last,),
        (sum_o.last,),
        (sum_small.along_z,),
        (thirds_2.along_z,),
        (thirds_0.last,),
        (thirds_1.last,),
        (sum_small.last,),
        (thirds_2.last,),
    )()
    for copy in layer_copies + token_copies:
        copy.wait()
    layer_own.wait()
    token_own.wait()
    for one in reduces:
        one.finish()


def backward(saved, weights, grad_pages, layer_slots, slots, live, tokens_shape):
    w_q, w_1, w_2 = weights[0], weights[4], weights[5]
    qkv, lse, x, att, normed1, low, act, slope, normed2, factors, bias = saved
    length, feat = low.shape
    inner_width = act.shape[1]
    anywhere = pl.BlockSpec(memory_space=pl.ANY)
    vmem = pl.BlockSpec(memory_space=pltpu.VMEM)
    grid = (4, 2, 2, 2)
    small, inner, outer = (feat // 32, feat), (feat // 32, inner_width), (inner_width // 32, feat)
    sizes = [outer, inner] + [small] * 4 + [(16, 128)]
    scratch = [
        ((length, 3 * feat), BF16),
        ((length, feat), BF16),
        ((length, feat), BF16),
        ((length, feat), F32),
        ((length, feat), BF16),
        ((length, inner_width), BF16),
        ((length, inner_width), BF16),
        ((length, feat), F32),
        ((grad_pages.shape[0] * grad_pages.shape[1], feat), BF16),
        (grid + inner, BF16),
        ((inner_width, feat), BF16),
        ((feat, length), BF16),
        ((length, 3 * feat), BF16),
        (grid + outer, BF16),
        (grid + inner, BF16),
        (grid + small, BF16),
        ((GROUPS,) + grid + small, BF16),
        (grid + (16, 128), BF16),
        ((8, feat), F32),
        ((8, inner_width), F32),
    ]
    bufs, sems = [], []
    for i, size in enumerate(sizes):
        bufs += reduce_mid_bufs(*size) if i < 2 else reduce_bufs(*size)
        sems += reduce_mid_sems() if i < 2 else reduce_sems()
    outs = [(grad_pages.shape, BF16, anywhere), (tokens_shape, BF16, anywhere)]
    outs += [(small, F32, vmem)] * 4 + [(inner, F32, vmem), (outer, F32, vmem), ((16, 128), F32, vmem)]
    return pl.pallas_call(
        backward_kernel,
        out_shape=[jax.ShapeDtypeStruct(shape, kind) for shape, kind, _ in outs],
        in_specs=[anywhere, vmem] + [anywhere] * 7 + [vmem, vmem] + [anywhere] * 8 + [vmem, vmem],
        out_specs=[spec for _, _, spec in outs],
        scratch_shapes=[pltpu.VMEM(shape, kind) for shape, kind in scratch]
        + [DMA((20,)), DMA((3,)), DMA((3,)), DMA((3,)), DMA((3,))]
        + bufs
        + sems,
        compiler_params=pltpu.CompilerParams(
            collective_id=1, has_side_effects=True, vmem_limit_bytes=VMEM_LIMIT
        ),
        name="backward",
    )(*saved, *weights, grad_pages, layer_slots, slots, live)


LARGE = (0, 2, 3, 5, 9, 11)
SMALL_ORDER = (1, 4, 6, 7, 8, 12, 13, 14, 10)


def finish_kernel(count, sizes, *refs):
    ins, small, outs = refs[:count], refs[count], refs[count + 1 : 2 * count + 1]
    vectors, stages, sems = refs[2 * count + 1 :][: len(sizes)], refs[-count - 1 : -1], refs[-1]
    inward = [pltpu.make_async_copy(i, s, sems.at[0, n]) for n, (i, s) in enumerate(zip(ins, stages))]
    outward = [pltpu.make_async_copy(s, o, sems.at[1, n]) for n, (s, o) in enumerate(zip(stages, outs))]
    for copy in inward:
        copy.start()
    for row, (size, ref) in enumerate(zip(sizes, vectors)):
        ref[...] = small[row : row + 1, 0:size].reshape(size)
    for first, second in zip(inward, outward):
        first.wait()
        second.start()
    for copy in outward:
        copy.wait()


def finish(arrays, small, sizes):
    count = len(arrays)
    anywhere = pl.BlockSpec(memory_space=pl.ANY)
    vmem = pl.BlockSpec(memory_space=pltpu.VMEM)

    def body(*refs):
        finish_kernel(count, sizes, *refs)

    return pl.pallas_call(
        body,
        out_shape=[jax.ShapeDtypeStruct(a.shape, a.dtype) for a in arrays]
        + [jax.ShapeDtypeStruct((size,), F32) for size in sizes],
        in_specs=[anywhere] * count + [vmem],
        out_specs=[anywhere] * count + [vmem] * len(sizes),
        scratch_shapes=[pltpu.VMEM(a.shape, a.dtype) for a in arrays] + [DMA((2, count))],
        compiler_params=pltpu.CompilerParams(vmem_limit_bytes=VMEM_LIMIT),
        name="finish",
    )(*arrays, small)


def by_kernels(tokens, band_ids, page_mask, weights, grad_output):
    large = [weights[i] for i in LARGE]
    vectors = [weights[i] for i in SMALL_ORDER]
    got = forward(vectors, tokens, grad_output, band_ids, page_mask, *large)
    saved, full, (grad_slots, layer_slots, slots, live) = got[:11], got[11:17], got[17:]
    full = [w if i == 4 else w.reshape(-1, w.shape[-1]) for i, w in enumerate(full)]
    sums = backward(saved, full, grad_slots, layer_slots, slots, live, tokens.shape)
    results = finish(sums[:8], sums[8], [v.shape[0] for v in vectors])
    grads = dict(zip(LARGE + SMALL_ORDER, results[2:]))
    return tuple(results[:2]) + tuple(grads[i] for i in range(len(weights)))


def per_device(hand_made, *args):
    tokens, band_ids, band_counts, page_mask = args[:4]
    weights, grad_output = args[4:19], args[19]
    if hand_made:
        return by_kernels(tokens, band_ids, page_mask, weights, grad_output)
    bands = lax.axis_size("band")
    slot_cap = grad_output.shape[1]
    pages = tokens.shape[0] // bands
    full = [lax.all_gather(w, BOTH, axis=0, tiled=True) for w in weights]
    first = lax.axis_index("band") * pages
    ids = lax.dynamic_slice_in_dim(band_ids, first, pages, 0)
    live = lax.dynamic_slice_in_dim(page_mask, first, pages, 0) > 0
    slots = page_slots(ids, bands, slot_cap)
    layer_slots, grad_in, grads = layer_pages(
        to_pages(tokens), slots, live, to_pages(grad_output), full
    )
    return (from_pages(layer_slots), from_pages(grad_in)) + tuple(
        lax.psum_scatter(g, BOTH, scatter_dimension=0, tiled=True) for g in grads
    )


def solution(mesh):
    hand_made = dict(mesh.shape) == {"page": 8, "band": 4}
    shard = P(BOTH)
    rows = P(BOTH, None)
    tokens = P("page", "band", None)
    page = P("page", None)
    weights = (rows, shard, rows, rows, shard, rows, shard, shard, shard)
    weights = weights + (rows, shard, rows, shard, shard, shard)

    def step(*args):
        return per_device(hand_made, *args)

    return jax.shard_map(
        step,
        mesh=mesh,
        in_specs=(tokens, page, page, page) + weights + (tokens,),
        out_specs=(tokens, tokens) + weights,
        check_vma=False,
    )
```
